32 devices in a mesh: shard: 4 (over z), ctx: 8 (over y, x, core).
Axes of the slice: x: 2, y: 2, z: 4, core: 2. Of those that a mesh axis runs over, the one named last changes fastest.
Arguments:
- tokens: bfloat16 [8, 1024, 512], P('shard', 'ctx'), may hold values from -6 to 6
- lengths: int32 [8], P('shard'), may hold values from 256 to 1024, as said below
- expert_picks: int32 [8, 1024, 8], P('shard', 'ctx'), may hold values from 0 to 23, all different within a row
- first_gain: float32 [512], P('shard'), may hold values from 0.5 to 1.5
- first_bias: float32 [512], P('shard'), may hold values from -0.625 to 0.625
- kv_weight: float32 [512, 128], P('shard'), may hold values from -0.25 to 0.25
- query_weight: float32 [512, 1536], P('shard'), may hold values from -0.25 to 0.25
- router_weight: float32 [512, 24], P('shard'), may hold values from -0.125 to 0.125
- output_weight: float32 [1536, 512], P('shard'), may hold values from -16 to 16
- second_gain: float32 [512], P('shard'), may hold values from 0.5 to 1.5
- second_bias: float32 [512], P('shard'), may hold values from -0.625 to 0.625
- inner_weight: float32 [512, 2048], P('shard'), may hold values from -0.25 to 0.25
- inner_bias: float32 [2048], P('shard'), may hold values from -1.25 to 1.25
- outer_weight: float32 [2048, 512], P('shard'), may hold values from -0.125 to 0.125
- outer_bias: float32 [512], P('shard'), may hold values from -1.25 to 1.25
- cotangent: bfloat16 [8, 1024, 512], P('shard', 'ctx'), may hold values from -6 to 6
Outputs:
- layer_out: bfloat16 [8, 1024, 512], P('shard', 'ctx')
- input_grad: float32 [8, 1024, 512], P('shard', 'ctx')
- first_gain_grad: float32 [512], P('shard')
- first_bias_grad: float32 [512], P('shard')
- kv_weight_grad: float32 [512, 128], P('shard')
- query_weight_grad: float32 [512, 1536], P('shard')
- router_weight_grad: float32 [512, 24], P('shard')
- output_weight_grad: float32 [1536, 512], P('shard')
- second_gain_grad: float32 [512], P('shard')
- second_bias_grad: float32 [512], P('shard')
- inner_weight_grad: float32 [512, 2048], P('shard')
- inner_bias_grad: float32 [2048], P('shard')
- outer_weight_grad: float32 [2048, 512], P('shard')
- outer_bias_grad: float32 [512], P('shard')
The draws below stay inside these ranges and needn't reach their ends.
Inputs may be any that keep to these rules, and one draw needn't show every extreme that they name: `lengths`: of the 2 slots at each index of shard, one has length exactly 1024. `expert_picks`: each token names 8 different experts.
All inputs are finite; a program needn't handle non-finite values.
Results may differ from the reference program's by a relative error of at most 0.019.
Values may be sent and summed in bfloat16 or wider, within the bound.
A program may use at most 128 MiB of HBM per device.

```python
import jax
import jax.numpy as jnp
from jax import lax

D = 512
HS = 64
E = 24
TOP = 8
FF = 2048
SLOTS_DEV = 2
SEG = 128
HALF = 64
SLOT = 1024
SLOTS = 8


def draw_lengths(key, part):
    key_len = jax.random.fold_in(key, 11)
    key_full = jax.random.fold_in(key, 12)
    random_lengths = jax.random.randint(key_len, (SLOTS,), SLOT // 4, SLOT + 1)
    full_pick = jax.random.randint(key_full, (SLOTS // SLOTS_DEV,), 0, SLOTS_DEV)
    slot_ids = jnp.arange(SLOTS)
    chosen = full_pick[slot_ids // SLOTS_DEV]
    return jnp.where(slot_ids % SLOTS_DEV == chosen, SLOT, random_lengths).astype(jnp.int32)


def strengthened(drawn, key, source, target, shards_of, factor):
    owner, partner = [(jnp.arange(drawn.shape[axis_at]) // (drawn.shape[axis_at] // shards_of)).reshape([-1 if axis == axis_at else 1 for axis in range(drawn.ndim)]) for axis_at in (source, target)]
    chosen = jax.random.permutation(key, shards_of)[partner]
    strong = (owner == chosen) | (owner == (partner + shards_of // 2) % shards_of)
    return jnp.where(strong, factor * drawn, drawn)


def level_of(own_key, shape, cuts, smallest, top_value):
    factor_of, own = 1.0, jax.random.fold_in(own_key, 6)
    for position, blocks in cuts:
        draws = jnp.exp(jax.random.uniform(jax.random.fold_in(own, position), (blocks,), jnp.float32, smallest / len(cuts), top_value / len(cuts)))
        factor_of = factor_of * jnp.repeat(draws, shape[position] // blocks).reshape([-1 if axis == position else 1 for axis in range(len(shape))])
    return factor_of


def choose_distinct(stream_key, rows, number_of, top, lift):
    sequence = jax.random.permutation(jax.random.fold_in(stream_key, 1), number_of)
    favour = sequence
    for power in range(3):
        favour = favour * favour // number_of
    favour = favour * lift // number_of
    tickets = jax.random.randint(jax.random.fold_in(stream_key, 2), (rows, number_of), 0, 4096) + favour
    sure = jax.random.permutation(jax.random.fold_in(stream_key, 3), rows)[jnp.arange(number_of) % rows]
    tickets = jnp.where(jnp.arange(rows)[:, None] == sure[None, :], 1 << 14, tickets)
    score = tickets * number_of + jnp.arange(number_of)
    return lax.top_k(score.astype(jnp.int32), top)[1].astype(jnp.int32)


def scatter_about(key, dims, scale, most, pieces=(), kind=jnp.bfloat16):
    loudness = level_of(key, dims, pieces, -0.22, 0.18) if pieces else 1.0
    drawn = jax.random.normal(key, dims, jnp.float32) * scale * loudness
    return jnp.minimum(jnp.maximum(drawn, -most), most).astype(kind)


def gaussian_with(key, shape, spread, reach, shards, heavy, kind=jnp.bfloat16):
    entries = spread * jax.random.normal(key, shape, jnp.float32)
    if shards:
        entries = entries * level_of(key, shape, shards, -0.22, 0.18)
    return jnp.clip(strengthened(entries, jax.random.fold_in(key, 3), *heavy), -reach, reach).astype(kind)


def setup_inputs(seed: int = 0) -> dict:
    seeds = jax.random.split(jax.random.key(seed), 17)
    return {
        "tokens": scatter_about(seeds[0], (SLOTS, SLOT, D), 1.0, 6.0, ((0, 4), (1, 8))),
        "lengths": draw_lengths(jax.random.fold_in(seeds[16], 71), 0),
        "expert_picks": choose_distinct(seeds[2], SLOTS * SLOT, E, TOP, 2730).reshape((SLOTS, SLOT, TOP)),
        "first_gain": jnp.clip(1.0 + 0.1 * jax.random.normal(seeds[3], (D,), jnp.float32), 0.5, 1.5),
        "first_bias": scatter_about(seeds[4], (D,), 0.1, 0.625, ((0, 4),), jnp.float32),
        "kv_weight": scatter_about(seeds[5], (D, 2 * HS), D ** -0.5, 0.25, ((0, 4),), jnp.float32),
        "query_weight": scatter_about(seeds[6], (D, E * HS), D ** -0.5, 0.25, ((0, 4),), jnp.float32),
        "router_weight": scatter_about(seeds[7], (D, E), (0.5 * D ** -0.5), 0.125, ((0, 4),), jnp.float32),
        "output_weight": scatter_about(seeds[8], (E * HS, D), ((TOP * SLOT / (16 * HS)) ** 0.5), 16.0, ((0, 4),), jnp.float32),
        "second_gain": jnp.clip(1.0 + 0.1 * jax.random.normal(seeds[9], (D,), jnp.float32), 0.5, 1.5),
        "second_bias": scatter_about(seeds[10], (D,), 0.1, 0.625, ((0, 4),), jnp.float32),
        "inner_weight": scatter_about(seeds[11], (D, FF), D ** -0.5, 0.25, ((0, 4),), jnp.float32),
        "inner_bias": scatter_about(seeds[12], (FF,), 0.2, 1.25, ((0, 4),), jnp.float32),
        "outer_weight": scatter_about(seeds[13], (FF, D), FF ** -0.5, 0.125, ((0, 4),), jnp.float32),
        "outer_bias": scatter_about(seeds[14], (D,), 0.2, 1.25, ((0, 4),), jnp.float32),
        "cotangent": gaussian_with(seeds[15], (SLOTS, SLOT, D), 1.0, 6.0, ((0, 4), (1, 8)), (1, 2, 8, 2.0)),
    }


@jax.custom_vjp
def low(v):
    return lax.optimization_barrier(v.astype(jnp.bfloat16)).astype(jnp.float32)

@jax.custom_vjp
def low_back(v):
    return v

def low_keep(v):
    return (low(v), None)

def low_pass(kept, grad):
    return (grad,)

def back_keep(v):
    return (v, None)

def back_low(kept, grad):
    return (low(grad),)
low.defvjp(low_keep, low_pass)
low_back.defvjp(back_keep, back_low)
NORM_EPS = 1e-05
PRECISE = lax.Precision.HIGHEST

def layer_norm(inputs, gain_vec, bias_vec):
    row_mean = lax.optimization_barrier(jnp.mean(inputs, axis=-1, keepdims=True))
    centered = inputs - row_mean
    row_var = lax.optimization_barrier(jnp.mean(centered * centered, axis=-1, keepdims=True))
    return centered * lax.rsqrt(row_var + NORM_EPS) * gain_vec + bias_vec

def dealt_positions():
    rows = jnp.arange(SLOT, dtype=jnp.int32)
    device = rows // SEG
    offset = rows % SEG
    return jnp.where(offset < HALF, device * HALF + offset, SLOT - (device + 2) * HALF + offset).astype(jnp.int32)

def attend(queries, keyval, lengths):
    positions = dealt_positions()

    def one_slot(operands):
        query_slot, kv_slot, length = operands
        key_rows = kv_slot[:, :HS]
        value_rows = kv_slot[:, HS:]
        slot_len = query_slot.shape[0]
        block_len = min(512, slot_len)
        key_pos = positions

        @jax.checkpoint
        def one_block(block_ops):
            query_block, row_begin = block_ops
            query_pos = lax.dynamic_slice_in_dim(positions, row_begin, block_len)
            raw_scores = jnp.einsum('qjd,kd->qjk', query_block, key_rows, precision=PRECISE) * HS ** (-0.5)
            scores = low_back(raw_scores)
            allowed = (key_pos[None, :] <= query_pos[:, None]) & (key_pos[None, :] < length)
            scores = jnp.where(allowed[:, None, :], scores, -jnp.inf)
            row_max = lax.optimization_barrier(jnp.max(scores, axis=-1, keepdims=True))
            exp_scores = jnp.exp(scores - row_max)
            attn_prob = exp_scores / lax.optimization_barrier(jnp.sum(exp_scores, axis=-1, keepdims=True))
            return jnp.einsum('qjk,kd->qjd', low(attn_prob), value_rows, precision=PRECISE)
        begins = (jnp.arange(slot_len // block_len) * block_len).astype(jnp.int32)
        mapped = lax.map(one_block, (query_slot.reshape(slot_len // block_len, block_len, TOP, HS), begins))
        return mapped.reshape(slot_len, TOP, HS)
    return lax.map(one_slot, (queries, keyval, lengths))

def forward(tokens, params, expert_picks, lengths):
    gain_one, bias_one, kv_w, query_w, router_w, output_w, gain_two, bias_two, inner_w, inner_b, outer_w, outer_b = [low(item) for item in params]
    slot_count, slot_len, model_width = tokens.shape
    flat_in = tokens.reshape(-1, model_width)
    normed = low(layer_norm(flat_in, gain_one, bias_one))
    keyval = low(low_back(jnp.dot(normed, kv_w, precision=PRECISE)))
    query_all = jnp.dot(normed, query_w, precision=PRECISE).reshape(-1, E, HS)
    choose = (expert_picks.reshape(-1, TOP)[:, :, None] == jnp.arange(E, dtype=jnp.int32)[None, None, :]).astype(jnp.float32)
    queries = low(low_back(jnp.einsum('tje,ted->tjd', choose, query_all, precision=PRECISE)))
    logits = low_back(jnp.dot(normed, router_w, precision=PRECISE))
    picked = jnp.einsum('tje,te->tj', choose, logits, precision=PRECISE)
    gate_probs = jax.nn.softmax(picked, axis=-1)
    head_out = attend(queries.reshape(slot_count, slot_len, TOP, HS), keyval.reshape(slot_count, slot_len, 2 * HS), lengths)
    head_out = low_back(head_out.reshape(-1, TOP, HS))
    mixed = jnp.einsum('tje,tjd->ted', choose, gate_probs[:, :, None] * head_out, precision=PRECISE)
    mixed = low(mixed.reshape(-1, E * HS))
    branch = low_back(jnp.dot(mixed, output_w, precision=PRECISE))
    residual = flat_in + branch
    normed_two = low(layer_norm(residual, gain_two, bias_two))
    hidden = low_back(jnp.dot(normed_two, inner_w, precision=PRECISE) + inner_b)
    act = low(jax.nn.gelu(hidden, approximate=True))
    final_sum = residual + jnp.dot(act, outer_w, precision=PRECISE) + outer_b
    positions = dealt_positions()
    valid = (positions[None, :] < lengths[:, None]).astype(jnp.float32)
    return final_sum.reshape(slot_count, slot_len, model_width) * valid[:, :, None]

def reference(tokens, lengths, expert_picks, first_gain, first_bias, kv_weight, query_weight, router_weight, output_weight, second_gain, second_bias, inner_weight, inner_bias, outer_weight, outer_bias, cotangent):
    params = (first_gain.astype(jnp.float32), first_bias.astype(jnp.float32), kv_weight.astype(jnp.float32), query_weight.astype(jnp.float32), router_weight.astype(jnp.float32), output_weight.astype(jnp.float32), second_gain.astype(jnp.float32), second_bias.astype(jnp.float32), inner_weight.astype(jnp.float32), inner_bias.astype(jnp.float32), outer_weight.astype(jnp.float32), outer_bias.astype(jnp.float32))

    def wrapped(token_vals, param_vals):
        return forward(token_vals, param_vals, expert_picks, lengths)
    result, pull = jax.vjp(wrapped, tokens.astype(jnp.float32), params)
    token_grad, param_grads = pull(cotangent.astype(jnp.float32))
    return (result.astype(jnp.bfloat16), token_grad, param_grads[0], param_grads[1], param_grads[2], param_grads[3], param_grads[4], param_grads[5], param_grads[6], param_grads[7], param_grads[8], param_grads[9], param_grads[10], param_grads[11])
```

```python
import functools

import jax
import jax.numpy as jnp
from jax import lax
from jax.experimental import pallas as pl
from jax.experimental.pallas import tpu as pltpu
from jax.sharding import PartitionSpec as P

HS = 64
E = 24
TOP = 8
NORM_EPS = 1e-05
NEG_LARGE = -1e30
BF16 = jnp.bfloat16
F32 = jnp.float32
PANEL = 512
VMEM_BYTES = 63 * 1024 * 1024
GELU_C = 0.7978845608028654
GELU_A = 0.044715


def dot(left, right):
    return jnp.dot(left, right, preferred_element_type=F32)


def dot_t(left, right):
    return lax.dot_general(left, right, (((1,), (1,)), ((), ())), preferred_element_type=F32)


class Net:
    def __init__(self, shards, ctxs, group, send_sem, recv_sem):
        self.shards, self.ctxs, self.group = shards, ctxs, group
        self.pairs = group // 2
        self.groups = ctxs // group
        self.z = lax.axis_index("shard")
        self.i = lax.axis_index("ctx")
        self.core = self.i % 2
        self.chip = (self.i % group) // 2
        self.grp = self.i // group
        self.mine = self.core * self.pairs + self.chip
        self.send_sem, self.recv_sem = send_sem, recv_sem
        self.used = 0
        self.sent = []

    def far(self, step):
        return (self.z + step) % self.shards

    def src(self, step):
        return (self.z + self.shards - step) % self.shards

    def chip_to(self, step):
        return (self.chip + step) % self.pairs

    def chip_from(self, step):
        return (self.chip + self.pairs - step) % self.pairs

    def same_core(self, chip):
        return self.grp * self.group + chip * 2 + self.core

    def sibling(self):
        return self.i + 1 - 2 * self.core

    def slot(self):
        self.used += 1
        return self.used - 1

    def copy(self, src, dst, slot, z, i):
        return pltpu.make_async_remote_copy(
            src_ref=src,
            dst_ref=dst,
            send_sem=self.send_sem.at[slot],
            recv_sem=self.recv_sem.at[slot],
            device_id={"shard": z, "ctx": i},
            device_id_type=pl.DeviceIdType.MESH,
        )

    def send(self, src, dst, z, i):
        slot = self.slot()
        one = self.copy(src, dst, slot, z, i)
        one.start()
        self.sent.append(one)
        return slot

    def wait(self, slot, dst):
        self.copy(dst, dst, slot, self.z, self.i).wait_recv()

    def finish(self):
        for one in self.sent:
            one.wait_send()
        self.sent = []

    def greet(self):
        barrier = pltpu.get_barrier_semaphore()
        count = 0
        for step in range(1, self.ctxs):
            peer = (self.i + step) % self.ctxs
            pl.semaphore_signal(
                barrier,
                inc=1,
                device_id={"shard": self.z, "ctx": peer},
                device_id_type=pl.DeviceIdType.MESH,
            )
            count += 1
        for step in range(1, self.shards):
            pl.semaphore_signal(
                barrier,
                inc=1,
                device_id={"shard": self.far(step), "ctx": self.i},
                device_id_type=pl.DeviceIdType.MESH,
            )
            count += 1
        pl.semaphore_wait(barrier, count)


class Gather:
    def __init__(self, net, buf):
        self.net, self.buf = net, buf
        self.rows = buf.shape[1]
        self.piece = self.rows // net.group
        self.half = self.rows // 2

    def part(self, z, core, chip):
        first = pl.multiple_of((core * self.net.pairs + chip) * self.piece, self.piece)
        return self.buf.at[z, pl.ds(first, self.piece)]

    def core_part(self, z, core):
        return self.buf.at[z, pl.ds(pl.multiple_of(core * self.half, self.half), self.half)]

    def start(self):
        net = self.net
        own = self.part(net.z, net.core, net.chip)
        self.z_slots = [net.send(own, own, net.far(k), net.i) for k in range(1, net.shards)]

    def spread(self):
        net = self.net
        self.p_slots = []
        for k in range(1, net.shards):
            piece = self.part(net.src(k), net.core, net.chip)
            net.wait(self.z_slots[k - 1], piece)
            self.p_slots.append(
                [
                    net.send(piece, piece, net.z, net.same_core(net.chip_to(q)))
                    for q in range(1, net.pairs)
                ]
            )

    def share(self):
        net = self.net
        self.c_slots = []
        for k in range(1, net.shards):
            for q in range(1, net.pairs):
                net.wait(self.p_slots[k - 1][q - 1], self.part(net.src(k), net.core, net.chip_from(q)))
            block = self.core_part(net.src(k), net.core)
            self.c_slots.append(net.send(block, block, net.z, net.sibling()))

    def finish(self):
        net = self.net
        for k in range(1, net.shards):
            net.wait(self.c_slots[k - 1], self.core_part(net.src(k), 1 - net.core))


class Reduce:
    def __init__(self, net, grad, from_core, from_chip, from_group, from_far, out):
        self.net, self.grad = net, grad
        self.from_core, self.from_chip, self.from_group, self.from_far = (
            from_core,
            from_chip,
            from_group,
            from_far,
        )
        self.out = out
        self.rows, self.width = grad.shape[1], grad.shape[2]
        self.piece = self.rows // net.group
        self.half = self.rows // 2

    def first(self, core, chip):
        return pl.multiple_of((core * self.net.pairs + chip) * self.piece, self.piece)

    def core_rows(self, core):
        return pl.ds(pl.multiple_of(core * self.half, self.half), self.half)

    def start(self):
        net = self.net
        self.c_slot = net.send(
            self.grad.at[:, self.core_rows(1 - net.core)], self.from_core, net.z, net.sibling()
        )

    def add_core(self):
        net = self.net
        net.wait(self.c_slot, self.from_core)
        lines = 16
        base = pl.multiple_of(net.core * self.half, self.half)

        def one(step, carry):
            at = pl.multiple_of(step * lines, lines)
            rows = pl.ds(pl.multiple_of(base + at, lines), lines)
            for z in range(net.shards):
                self.grad[z, rows] = (
                    self.grad[z, rows].astype(F32)
                    + self.from_core[z, pl.ds(at, lines)].astype(F32)
                ).astype(BF16)
            return carry

        lax.fori_loop(0, self.half // lines, one, 0)
        self.p_slots = [
            net.send(
                self.grad.at[:, pl.ds(self.first(net.core, net.chip_to(q)), self.piece)],
                self.from_chip.at[q - 1],
                net.z,
                net.same_core(net.chip_to(q)),
            )
            for q in range(1, net.pairs)
        ]

    def total(self, parts):
        net = self.net
        lines = 16
        base = self.first(net.core, net.chip)

        def one(step, carry):
            at = pl.multiple_of(step * lines, lines)
            rows = pl.ds(pl.multiple_of(base + at, lines), lines)
            for z in range(net.shards):
                value = self.grad[z, rows].astype(F32)
                for part in range(parts.shape[0]):
                    value = value + parts[part, z, pl.ds(at, lines)].astype(F32)
                self.grad[z, rows] = value.astype(BF16)
            return carry

        lax.fori_loop(0, self.piece // lines, one, 0)

    def add_chip(self):
        net = self.net
        for q in range(1, net.pairs):
            net.wait(self.p_slots[q - 1], self.from_chip.at[q - 1])
        self.total(self.from_chip)
        own = pl.ds(self.first(net.core, net.chip), self.piece)
        step, at = 1, 0
        while step < net.groups:
            peer = net.i + net.group * step * (1 - 2 * ((net.grp // step) % 2))
            slot = net.send(self.grad.at[:, own], self.from_group.at[at], net.z, peer)
            net.wait(slot, self.from_group.at[at])
            net.sent.pop().wait_send()
            self.total(self.from_group.at[at : at + 1])
            step, at = step * 2, at + 1
        self.z_slots = [
            net.send(self.grad.at[net.far(k), own], self.from_far.at[k - 1], net.far(k), net.i)
            for k in range(1, net.shards)
        ]

    def add_far(self):
        net = self.net
        for k in range(1, net.shards):
            net.wait(self.z_slots[k - 1], self.from_far.at[k - 1])
        own = pl.ds(self.first(net.core, net.chip), self.piece)
        value = self.grad[net.z, own].astype(F32)
        for k in range(1, net.shards):
            value = value + self.from_far[k - 1].astype(F32)
        self.out[own, :] = value.astype(BF16)
        piece = self.out.at[own]
        self.o_slots = [
            net.send(piece, piece, net.z, net.same_core(net.chip_to(q))) for q in range(1, net.pairs)
        ]

    def share(self):
        net = self.net
        for q in range(1, net.pairs):
            net.wait(
                self.o_slots[q - 1],
                self.out.at[pl.ds(self.first(net.core, net.chip_from(q)), self.piece)],
            )
        block = self.out.at[self.core_rows(net.core)]
        self.s_slot = net.send(block, block, net.z, net.sibling())

    def finish(self):
        net = self.net
        net.wait(self.s_slot, self.out.at[self.core_rows(1 - net.core)])


def layer_kernel(
    shards,
    ctxs,
    group,
    len_ref,
    x_ref,
    cot_ref,
    picks_ref,
    g1_ref,
    b1_ref,
    g2_ref,
    b2_ref,
    bo_ref,
    bi_ref,
    wq_hbm,
    wkv_hbm,
    wr_hbm,
    wo_hbm,
    wi_hbm,
    wout_hbm,
    out_ref,
    gin_ref,
    two_out,
    q_out,
    kv_out,
    vec_out,
    wq_st,
    wkv_st,
    wr_st,
    wi_st,
    stage,
    w1,
    w2,
    vecs,
    normed,
    normed_t,
    q_t,
    sel_a,
    heads_t,
    small,
    kvall,
    kvt,
    qpad,
    ghpad,
    hrow,
    linv,
    ebuf,
    dkv,
    from_kv,
    mixed_t,
    xhat2,
    n2,
    n2_t,
    gfin_low,
    biases,
    g_t,
    two_g,
    two_core,
    two_chip,
    two_group,
    two_far,
    qg,
    qg_core,
    qg_chip,
    qg_group,
    qg_far,
    kg,
    kg_core,
    kg_chip,
    kg_group,
    kg_far,
    vec_g,
    vec_near,
    vec_far,
    local_sem,
    send_sem,
    recv_sem,
):
    net = Net(shards, ctxs, group, send_sem, recv_sem)
    z, c = net.z, net.i
    tokens, width = x_ref.shape
    seg = tokens // 2
    half = seg // 2
    blocks = 2 * ctxs
    ws = width // shards
    wos = E * HS // shards
    fs = wout_hbm.shape[0]
    off_out = wos
    off_in = wos + fs
    scale = HS ** (-0.5)
    panels = 4
    chunks = fs * shards // PANEL
    per_chunk = PANEL // fs

    wo_st, wout_st = stage.at[0:wos], stage.at[wos : wos + fs]
    resid, acc_a, acc_b = (stage.at[k * tokens : (k + 1) * tokens] for k in range(3))
    loads = []
    for at, (src, dst) in enumerate(
        (
            (wq_hbm, wq_st),
            (wkv_hbm, wkv_st),
            (wr_hbm, wr_st),
            (wo_hbm, wo_st),
            (wi_hbm, wi_st),
            (wout_hbm, wout_st),
        )
    ):
        one = pltpu.make_async_copy(src, dst, local_sem.at[at])
        one.start()
        loads.append(one)

    own_vec = vecs.at[z]
    own_vec[...] = jnp.zeros(own_vec.shape, F32)
    for row, ref in enumerate((g1_ref, b1_ref, g2_ref, b2_ref, bo_ref, bi_ref)):
        own_vec[row : row + 1, 0 : ref.shape[1]] = ref[...].astype(BF16).astype(F32)
    for one in loads[:3]:
        one.wait()
    w1[z, :, 0 : E * HS] = wq_st[...].astype(BF16)
    w1[z, :, E * HS : E * HS + 2 * HS] = wkv_st[...].astype(BF16)
    w1[z, :, E * HS + 2 * HS :] = jnp.zeros((ws, 128), BF16)
    w1[z, :, E * HS + 2 * HS : E * HS + 2 * HS + E] = wr_st[...].astype(BF16)

    net.greet()
    first_gather = Gather(net, w1)
    first_gather.start()
    vec_slots = [net.send(own_vec, own_vec, net.far(k), net.i) for k in range(1, shards)]
    for one in loads[3:]:
        one.wait()
    w2[z, 0:wos] = wo_st[...].astype(BF16)
    w2[z, off_out : off_out + fs] = wout_st[...].astype(BF16)
    for panel in range(panels):
        w2[z, off_in + panel * ws : off_in + (panel + 1) * ws] = wi_st[
            :, panel * PANEL : (panel + 1) * PANEL
        ].astype(BF16)
    second_gather = Gather(net, w2)
    second_gather.start()

    x = x_ref[...].astype(F32)
    mean1 = jnp.mean(x, axis=1, keepdims=True)
    cen = x - mean1
    small[0, :, 0:1] = lax.rsqrt(jnp.mean(cen * cen, axis=1, keepdims=True) + NORM_EPS)
    small[0, :, 2:3] = mean1

    def first_hat():
        return (x_ref[...].astype(F32) - small[0, :, 2:3]) * small[0, :, 0:1]

    first_gather.spread()
    for k in range(1, shards):
        net.wait(vec_slots[k - 1], vecs.at[net.src(k)])

    def whole(row, part):
        return jnp.concatenate([vecs[s, row : row + 1, 0:part] for s in range(shards)], axis=1)

    gain1, bias1 = whole(0, ws), whole(1, ws)
    gain2, bias2, bias_out = whole(2, ws), whole(3, ws), whole(4, ws)
    bias_in = whole(5, fs)
    for chunk in range(chunks):
        biases[chunk : chunk + 1, :] = bias_in[:, chunk * PANEL : (chunk + 1) * PANEL]
    norm_value = first_hat() * gain1 + bias1
    normed[...] = norm_value.astype(BF16)
    normed_t[...] = norm_value.T.astype(BF16)
    first_gather.share()
    first_gather.finish()

    def w1_tile(first, size):
        return w1[:, :, first : first + size].reshape(width, size)

    kvr = dot(normed[...], w1_tile(E * HS, 256))
    kv_own = kvr[:, 0 : 2 * HS].astype(BF16)
    for h in range(2):
        block = c if h == 0 else blocks - 1 - c
        for s in range(2):
            kvall[block, s] = kv_own[s * seg + h * half : s * seg + (h + 1) * half]
    kv_slots = []
    for step in range(1, ctxs):
        peer = (c + step) % ctxs
        pair = []
        for h in range(2):
            ref = kvall.at[c if h == 0 else blocks - 1 - c]
            pair.append(net.send(ref, ref, z, peer))
        kv_slots.append(pair)
    kv_sent = net.sent[-2 * (ctxs - 1) :]
    del net.sent[-2 * (ctxs - 1) :]

    second_gather.spread()

    logits_t = kvr[:, 2 * HS : 2 * HS + 128].T
    eye = (
        lax.broadcasted_iota(jnp.int32, (TOP, TOP), 0)
        == lax.broadcasted_iota(jnp.int32, (TOP, TOP), 1)
    ).astype(F32)
    picks = dot_t(eye, picks_ref[...].astype(F32))
    small_p = jnp.full((TOP, tokens), 0.0, F32)
    for e in range(E):
        small_p = jnp.where(picks == float(e), logits_t[e : e + 1, :], small_p)
    top = jnp.max(small_p, axis=0, keepdims=True)
    gexp = jnp.exp(small_p - top)
    gates = gexp / jnp.sum(gexp, axis=0, keepdims=True)
    small[1, 0:TOP, 0:tokens] = gates
    small[1, TOP : 2 * TOP, 0:tokens] = picks

    def query_tile(n, carry):
        cols = pl.ds(pl.multiple_of(n * 256, 256), 256)
        value = dot(normed[...], w1[:, :, cols].reshape(width, 256))
        value = value.astype(BF16).astype(F32).T
        for k in range(4):
            q_t[n * 4 + k] = value[k * HS : (k + 1) * HS]
        return carry

    lax.fori_loop(0, E * HS // 256, query_tile, 0)

    def choose(src, store):
        def one(j, carry):
            pick = small[1, pl.ds(TOP + j, 1), 0:tokens]
            value = jnp.zeros((HS, tokens), F32)
            for e in range(E):
                value = jnp.where(pick == float(e), src[e], value)
            store(j, value)
            return carry

        lax.fori_loop(0, TOP, one, 0)

    def spread_back(src, store):
        def one(e, carry):
            value = jnp.zeros((HS, tokens), F32)
            for j in range(TOP):
                pick = small[1, TOP + j : TOP + j + 1, 0:tokens]
                value = jnp.where(pick == e.astype(F32), src[j], value)
            store(e, value)
            return carry

        lax.fori_loop(0, E, one, 0)

    low_lane = lax.broadcasted_iota(jnp.int32, (HS, 2 * half), 1) < half

    def swap(one, two):
        return (
            jnp.where(low_lane, one, pltpu.roll(two, half, 1)),
            jnp.where(low_lane, pltpu.roll(one, half, 1), two),
        )

    def store_query(j, value):
        sel_a[j] = value * scale

    choose(q_t, store_query)
    for s in range(2):
        for pair in range(TOP // 2):
            halves = swap(
                sel_a[2 * pair, :, s * seg : (s + 1) * seg],
                sel_a[2 * pair + 1, :, s * seg : (s + 1) * seg],
            )
            for h in range(2):
                qpad[2 * s + h, 0:HS, pair * 128 : (pair + 1) * 128] = halves[h].astype(BF16)
    for sh in range(4):
        qpad[sh, HS:, :] = jnp.zeros((HS, TOP * half), BF16)
        ghpad[sh, 0:HS, :] = jnp.zeros((HS, TOP * half), BF16)

    for step in range(1, ctxs):
        source = (c + ctxs - step) % ctxs
        net.wait(kv_slots[step - 1][0], kvall.at[source])
        net.wait(kv_slots[step - 1][1], kvall.at[blocks - 1 - source])

    def turn(block, carry):
        both = kvall[block].reshape(2 * half, 2 * HS)
        kvt[block] = both.astype(F32).T.astype(BF16)
        dkv[block] = jnp.zeros((2, half, 2 * HS), F32)
        return carry

    lax.fori_loop(0, blocks, turn, 0)

    lanes = TOP * half
    offset = lax.broadcasted_iota(jnp.int32, (1, lanes), 1) % half
    key_row = lax.broadcasted_iota(jnp.int32, (half, lanes), 0)

    def place(h):
        if h == 0:
            return c, c + 1, blocks - c
        return blocks - 1 - c, blocks - c, 0

    def fold(value, op):
        parts = [value[8 * k : 8 * k + 8] for k in range(half // 8)]
        while len(parts) > 1:
            parts = [op(parts[k], parts[k + 1]) for k in range(0, len(parts), 2)]
        return parts[0]

    def masked(block, s, sh, limit):
        scores = dot(kvall[block, s], qpad[sh])
        return jnp.where(key_row <= limit - block * half, scores, NEG_LARGE)

    for s in range(2):
        length = len_ref[s]
        for h in range(2):
            sh = 2 * s + h
            position, count, base = place(h)
            limit = jnp.minimum(position * half + offset, length - 1)

            def score_step(block, top, s=s, sh=sh, limit=limit):
                return jnp.maximum(top, fold(masked(block, s, sh, limit), jnp.maximum))

            top = lax.fori_loop(0, count, score_step, jnp.full((8, lanes), NEG_LARGE, F32))
            top = jnp.max(top, axis=0, keepdims=True)
            acc_a[0:HS, :] = jnp.zeros((HS, lanes), F32)

            def value_step(block, total, s=s, sh=sh, limit=limit, top=top, base=base):
                expd = jnp.exp(masked(block, s, sh, limit) - top)
                low = expd.astype(BF16)
                ebuf[s, base + block] = low
                acc_a[0:HS, :] += dot(kvt[block, HS:, s * half : (s + 1) * half], low)
                return total + fold(expd, jnp.add)

            total = lax.fori_loop(0, count, value_step, jnp.zeros((8, lanes), F32))
            inverse = 1.0 / jnp.sum(total, axis=0, keepdims=True)
            linv[sh] = jnp.broadcast_to(inverse, (8, lanes))
            hrow[sh] = acc_a[0:HS, :] * inverse
    second_gather.share()

    for s in range(2):
        for pair in range(TOP // 2):
            both = swap(
                hrow[2 * s, :, pair * 128 : (pair + 1) * 128],
                hrow[2 * s + 1, :, pair * 128 : (pair + 1) * 128],
            )
            for k in range(2):
                heads_t[2 * pair + k, :, s * seg : (s + 1) * seg] = both[k]
    for j in range(TOP):
        sel_a[j] = heads_t[j] * small[1, j : j + 1, 0:tokens]

    def store_mixed(e, value):
        mixed_t[e] = value.astype(BF16)

    spread_back(sel_a, store_mixed)
    second_gather.finish()

    experts = E // shards
    acc_a[...] = x_ref[...].astype(F32)

    def project(s, carry):
        part = mixed_t[pl.ds(s * experts, experts)].reshape(wos, tokens)
        acc_a[...] += dot(part.astype(F32).T.astype(BF16), w2[s, 0:wos])
        return carry

    lax.fori_loop(0, shards, project, 0)
    residual = acc_a[...]
    resid[...] = residual
    cen = residual - jnp.mean(residual, axis=1, keepdims=True)
    rstd2 = lax.rsqrt(jnp.mean(cen * cen, axis=1, keepdims=True) + NORM_EPS)
    small[0, :, 1:2] = rstd2
    cen = cen * rstd2
    xhat2[...] = cen
    cen = cen * gain2 + bias2
    n2[...] = cen.astype(BF16)
    n2_t[...] = cen.T.astype(BF16)

    row = lax.broadcasted_iota(jnp.int32, (tokens, 1), 0)
    inner_row = row % seg
    pos = jnp.where(
        inner_row < half, c * half + inner_row, blocks * half - (c + 2) * half + inner_row
    )
    valid = (pos < jnp.where(row < seg, len_ref[0], len_ref[1])).astype(F32)
    gfin_low[...] = (cot_ref[...].astype(F32) * valid).astype(BF16)
    acc_a[...] = jnp.zeros((tokens, width), F32)
    acc_b[...] = jnp.zeros((tokens, width), F32)
    vec_g[...] = jnp.zeros(vec_g.shape, F32)

    def feed(f, carry):
        rows_in = pl.ds(pl.multiple_of(off_in + f * ws, 16), ws)
        w_in = w2[:, rows_in].reshape(width, PANEL)
        w_out = w2[pl.ds(f * per_chunk, per_chunk), off_out : off_out + fs].reshape(PANEL, width)
        hidden = dot(n2[...], w_in) + biases[pl.ds(f, 1), :]
        square = hidden * hidden
        tanh = jnp.tanh(GELU_C * hidden * (1.0 + GELU_A * square))
        act = (0.5 * hidden * (1.0 + tanh)).astype(BF16)
        slope = 0.5 * (1.0 + tanh) + 0.5 * GELU_C * hidden * (1.0 - tanh * tanh) * (
            1.0 + 3.0 * GELU_A * square
        )
        gfin = gfin_low[...]
        acc_a[...] += dot(act, w_out)
        grad_hidden = (slope * dot_t(gfin, w_out)).astype(BF16)
        vec_g[pl.ds(5 + f, 1), :] = jnp.sum(grad_hidden.astype(F32), axis=0, keepdims=True)
        grad_outer = dot(act.astype(F32).T.astype(BF16), gfin).astype(BF16)
        two_g[pl.ds(f * per_chunk, per_chunk), off_out : off_out + fs] = grad_outer.reshape(
            per_chunk, fs, width
        )
        grad_inner = dot(n2_t[...], grad_hidden).astype(BF16)
        two_g[:, rows_in] = grad_inner.reshape(shards, ws, PANEL)
        acc_b[...] += dot_t(grad_hidden, w_in)
        return carry

    lax.fori_loop(0, chunks, feed, 0)
    out_ref[...] = (valid * (resid[...] + acc_a[...] + bias_out)).astype(BF16)
    gfin = cot_ref[...].astype(F32) * valid
    vec_g[4:5, :] = jnp.sum(gfin, axis=0, keepdims=True)
    grad_n2 = acc_b[...]
    vec_g[3:4, :] = jnp.sum(grad_n2, axis=0, keepdims=True)
    vec_g[2:3, :] = jnp.sum(grad_n2 * xhat2[...], axis=0, keepdims=True)
    grad_hat = grad_n2 * gain2
    grad_hat = grad_hat - jnp.mean(grad_hat, axis=1, keepdims=True)
    grad_hat = grad_hat - xhat2[...] * jnp.mean(grad_hat * xhat2[...], axis=1, keepdims=True)
    grad_residual = gfin + grad_hat * small[0, :, 1:2]
    resid[...] = grad_residual
    n2[...] = grad_residual.astype(BF16)

    def branch(s, carry):
        part = mixed_t[pl.ds(s * experts, experts)].reshape(wos, tokens)
        two_g[s, 0:wos] = dot(part, n2[...]).astype(BF16)
        grad = dot_t(w2[s, 0:wos], n2[...])
        q_t[pl.ds(s * experts, experts)] = grad.reshape(experts, HS, tokens)
        return carry

    lax.fori_loop(0, shards, branch, 0)
    two = Reduce(net, two_g, two_core, two_chip, two_group, two_far, two_out)
    two.start()

    def store_head_grad(j, value):
        sel_a[j] = value * small[1, pl.ds(j, 1), 0:tokens]
        small[1, pl.ds(2 * TOP + j, 1), 0:tokens] = jnp.sum(
            value * heads_t[j], axis=0, keepdims=True
        )

    choose(q_t, store_head_grad)
    gates = small[1, 0:TOP, 0:tokens]
    grad_gates = small[1, 2 * TOP : 3 * TOP, 0:tokens]
    grad_picked = gates * (grad_gates - jnp.sum(gates * grad_gates, axis=0, keepdims=True))
    picks = small[1, TOP : 2 * TOP, 0:tokens]
    g_t[E * HS + 2 * HS :, :] = jnp.zeros((128, tokens), BF16)
    grad_logits = [
        jnp.sum(jnp.where(picks == float(e), grad_picked, 0.0), axis=0, keepdims=True)
        for e in range(E)
    ]
    grad_logits += [jnp.zeros((1, tokens), F32)] * (32 - E)
    g_t[E * HS + 2 * HS : E * HS + 2 * HS + 32, :] = jnp.concatenate(grad_logits, axis=0).astype(
        BF16
    )
    for s in range(2):
        for pair in range(TOP // 2):
            halves = swap(
                sel_a[2 * pair, :, s * seg : (s + 1) * seg],
                sel_a[2 * pair + 1, :, s * seg : (s + 1) * seg],
            )
            at = pair * 128
            for h in range(2):
                sh = 2 * s + h
                grad = (halves[h] * linv[sh, 0:1, at : at + 128]).astype(BF16)
                ghpad[sh, HS:, at : at + 128] = grad
                linv[sh, 1:2, at : at + 128] = jnp.sum(
                    grad.astype(F32) * hrow[sh, :, at : at + 128], axis=0, keepdims=True
                )
    two.add_core()

    for s in range(2):
        for h in range(2):
            sh = 2 * s + h
            position, count, base = place(h)
            delta = linv[sh, 1:2, :]
            acc_a[0:HS, :] = jnp.zeros((HS, lanes), F32)

            def grad_step(block, carry, s=s, sh=sh, base=base, delta=delta):
                expd = ebuf[s, base + block]
                grad_prob = dot(kvall[block, s], ghpad[sh])
                grad_score = (expd.astype(F32) * (grad_prob - delta)).astype(BF16)
                dkv[block, s] += dot_t(expd, ghpad[sh]) + dot_t(grad_score, qpad[sh])
                acc_a[0:HS, :] += dot(kvt[block, 0:HS, s * half : (s + 1) * half], grad_score)
                return carry

            lax.fori_loop(0, count, grad_step, 0)
            hrow[sh] = acc_a[0:HS, :] * scale

    for one in kv_sent:
        one.wait_send()

    def lower(block, carry):
        kvall[block] = dkv[block].astype(BF16)
        return carry

    lax.fori_loop(0, blocks, lower, 0)
    dkv_slots = []
    for step in range(1, ctxs):
        peer = (c + step) % ctxs
        pair = []
        for h in range(2):
            ref = kvall.at[peer if h == 0 else blocks - 1 - peer]
            pair.append(net.send(ref, from_kv.at[step - 1, h], z, peer))
        dkv_slots.append(pair)

    for s in range(2):
        for pair in range(TOP // 2):
            both = swap(
                hrow[2 * s, :, pair * 128 : (pair + 1) * 128],
                hrow[2 * s + 1, :, pair * 128 : (pair + 1) * 128],
            )
            for k in range(2):
                q_t[2 * pair + k, :, s * seg : (s + 1) * seg] = both[k]

    def store_grad_query(e, value):
        g_t[pl.ds(pl.multiple_of(e * HS, HS), HS), :] = value.astype(BF16)

    spread_back(q_t, store_grad_query)

    def query_grad(n, carry):
        at = pl.ds(pl.multiple_of(n * 256, 256), 256)
        grad = dot_t(normed_t[...], g_t[at, :]).astype(BF16)
        qg[:, :, at] = grad.reshape(shards, ws, 256)
        return carry

    lax.fori_loop(0, E * HS // 256, query_grad, 0)
    first_q = Reduce(net, qg, qg_core, qg_chip, qg_group, qg_far, q_out)
    first_q.start()
    two.add_chip()

    heads_t[...] = jnp.zeros(heads_t.shape, F32)

    def norm_grad(n, carry):
        at = pl.ds(pl.multiple_of(n * 256, 256), 256)
        part = dot(w1[:, :, at].reshape(width, 256), g_t[at, :])
        heads_t[...] += part.reshape(heads_t.shape)
        return carry

    lax.fori_loop(0, E * HS // 256, norm_grad, 0)
    first_q.add_core()

    for step in range(1, ctxs):
        for h in range(2):
            net.wait(dkv_slots[step - 1][h], from_kv.at[step - 1, h])
    for h in range(2):
        block = c if h == 0 else blocks - 1 - c
        value = dkv[block]
        for step in range(1, ctxs):
            value = value + from_kv[step - 1, h].astype(F32)
        for s in range(2):
            acc_a[s * seg + h * half : s * seg + (h + 1) * half, 0:128] = value[s]
    g_t[E * HS : E * HS + 2 * HS, :] = acc_a[:, 0:128].T.astype(BF16)
    tail = g_t[E * HS :, :]
    kg[...] = dot_t(normed_t[...], tail).astype(BF16).reshape(shards, ws, 256)
    first_kv = Reduce(net, kg, kg_core, kg_chip, kg_group, kg_far, kv_out)
    first_kv.start()
    part = heads_t[...].reshape(width, tokens) + dot(w1_tile(E * HS, 256), tail)
    grad_normed = part.T
    vec_g[1:2, :] = jnp.sum(grad_normed, axis=0, keepdims=True)
    hat = first_hat()
    vec_g[0:1, :] = jnp.sum(grad_normed * hat, axis=0, keepdims=True)
    vec_slots = []
    for step in range(1, ctxs):
        vec_slots.append(net.send(vec_g, vec_near.at[step - 1], z, (c + step) % ctxs))
    vec_sent = net.sent[-(ctxs - 1) :]
    del net.sent[-(ctxs - 1) :]
    grad_hat = grad_normed * gain1
    grad_hat = grad_hat - jnp.mean(grad_hat, axis=1, keepdims=True)
    grad_hat = grad_hat - hat * jnp.mean(grad_hat * hat, axis=1, keepdims=True)
    gin_ref[...] = resid[...] + grad_hat * small[0, :, 0:1]

    two.add_far()
    first_kv.add_core()
    for step in range(1, ctxs):
        net.wait(vec_slots[step - 1], vec_near.at[step - 1])
    for one in vec_sent:
        one.wait_send()
    value = vec_g[...]
    for step in range(1, ctxs):
        value = value + vec_near[step - 1]
    vec_g[...] = value
    far_slots = [
        net.send(vec_g, vec_far.at[k - 1], net.far(k), net.i) for k in range(1, shards)
    ]
    first_q.add_chip()
    two.share()
    first_kv.add_chip()
    for k in range(1, shards):
        net.wait(far_slots[k - 1], vec_far.at[k - 1])
    value = vec_g[...]
    for k in range(1, shards):
        value = value + vec_far[k - 1]
    first_kv.add_far()
    first_q.add_far()
    vec_out[...] = jnp.zeros(vec_out.shape, F32)
    for at in range(5):
        part = jnp.zeros((1, ws), F32)
        for s in range(shards):
            part = jnp.where(z == s, value[at : at + 1, s * ws : (s + 1) * ws], part)
        vec_out[at : at + 1, 0:ws] = part
    part = jnp.zeros((1, fs), F32)
    for s in range(shards):
        first = (s % per_chunk) * fs
        line = 5 + s // per_chunk
        part = jnp.where(z == s, value[line : line + 1, first : first + fs], part)
    vec_out[5:6, 0:fs] = part
    first_kv.share()
    first_q.share()
    two.finish()
    first_kv.finish()
    first_q.finish()
    net.finish()


def unpack_kernel(
    ws,
    wos,
    fs,
    out_in,
    gin_in,
    two_in,
    q_in,
    kv_in,
    vec_in,
    out_ref,
    gin_ref,
    g1_ref,
    b1_ref,
    kv_ref,
    q_ref,
    r_ref,
    wo_ref,
    g2_ref,
    b2_ref,
    wi_ref,
    bi_ref,
    wout_ref,
    bo_ref,
):
    out_ref[...] = out_in[...]
    gin_ref[...] = gin_in[...]
    for row, ref in enumerate((g1_ref, b1_ref, g2_ref, b2_ref, bo_ref, bi_ref)):
        ref[...] = vec_in[row : row + 1, 0 : ref.shape[1]]
    q_ref[...] = q_in[...].astype(F32)
    kv_ref[...] = kv_in[:, 0 : 2 * HS].astype(F32)
    r_ref[...] = kv_in[:, 2 * HS : 2 * HS + E].astype(F32)
    wo_ref[...] = two_in[0:wos].astype(F32)
    wout_ref[...] = two_in[wos : wos + fs].astype(F32)
    for panel in range(4):
        first = wos + fs + panel * ws
        wi_ref[:, panel * PANEL : (panel + 1) * PANEL] = two_in[first : first + ws].astype(F32)


def on_device(
    shards,
    ctxs,
    tokens,
    lengths,
    expert_picks,
    first_gain,
    first_bias,
    kv_weight,
    query_weight,
    router_weight,
    output_weight,
    second_gain,
    second_bias,
    inner_weight,
    inner_bias,
    outer_weight,
    outer_bias,
    cotangent,
):
    slots, seg, width = tokens.shape
    count = slots * seg
    half = seg // 2
    blocks = 2 * ctxs
    lanes = TOP * half
    ws = width // shards
    wos = output_weight.shape[0]
    fs = outer_weight.shape[0]
    group = min(ctxs, ws // 16)
    pairs, groups = group // 2, ctxs // group
    rounds = groups.bit_length() - 1
    rows_two = wos + fs + 4 * ws
    wide_one = E * HS + 256

    vmem = pl.BlockSpec(memory_space=pltpu.VMEM)
    smem = pl.BlockSpec(memory_space=pltpu.SMEM)
    anywhere = pl.BlockSpec(memory_space=pl.ANY)

    def reduce_scratch(rows, wide):
        piece = rows // group
        return [
            pltpu.VMEM((shards, rows, wide), BF16),
            pltpu.VMEM((shards, rows // 2, wide), BF16),
            pltpu.VMEM((max(pairs - 1, 1), shards, piece, wide), BF16),
            pltpu.VMEM((rounds, shards, piece, wide), BF16)
            if rounds
            else pltpu.VMEM((16, 128), BF16),
            pltpu.VMEM((shards - 1, piece, wide), BF16),
        ]

    copies = (
        2 * (shards - 1) * (pairs + 1)
        + (shards - 1)
        + 4 * (ctxs - 1)
        + 3 * (2 + 2 * (pairs - 1) + rounds + shards - 1)
        + (ctxs - 1)
        + (shards - 1)
    )
    scratch = [
        pltpu.VMEM(query_weight.shape, F32),
        pltpu.VMEM(kv_weight.shape, F32),
        pltpu.VMEM(router_weight.shape, F32),
        pltpu.VMEM(inner_weight.shape, F32),
        pltpu.VMEM((max(wos + fs, 3 * count), width), F32),
        pltpu.VMEM((shards, ws, wide_one), BF16),
        pltpu.VMEM((shards, rows_two, PANEL), BF16),
        pltpu.VMEM((shards, 8, fs), F32),
        pltpu.VMEM((count, width), BF16),
        pltpu.VMEM((width, count), BF16),
        pltpu.VMEM((E, HS, count), F32),
        pltpu.VMEM((TOP, HS, count), F32),
        pltpu.VMEM((TOP, HS, count), F32),
        pltpu.VMEM((2, count, count), F32),
        pltpu.VMEM((blocks, slots, half, 2 * HS), BF16),
        pltpu.VMEM((blocks, 2 * HS, slots * half), BF16),
        pltpu.VMEM((4, 2 * HS, lanes), BF16),
        pltpu.VMEM((4, 2 * HS, lanes), BF16),
        pltpu.VMEM((4, HS, lanes), F32),
        pltpu.VMEM((4, 8, lanes), F32),
        pltpu.VMEM((slots, blocks + 1, half, lanes), BF16),
        pltpu.VMEM((blocks, slots, half, 2 * HS), F32),
        pltpu.VMEM((ctxs - 1, 2, slots, half, 2 * HS), BF16),
        pltpu.VMEM((E, HS, count), BF16),
        pltpu.VMEM((count, width), F32),
        pltpu.VMEM((count, width), BF16),
        pltpu.VMEM((width, count), BF16),
        pltpu.VMEM((count, width), BF16),
        pltpu.VMEM((8, PANEL), F32),
        pltpu.VMEM((wide_one, count), BF16),
        *reduce_scratch(rows_two, PANEL),
        *reduce_scratch(ws, E * HS),
        *reduce_scratch(ws, 256),
        pltpu.VMEM((16, width), F32),
        pltpu.VMEM((ctxs - 1, 16, width), F32),
        pltpu.VMEM((shards - 1, 16, width), F32),
        pltpu.SemaphoreType.DMA((6,)),
        pltpu.SemaphoreType.DMA((copies,)),
        pltpu.SemaphoreType.DMA((copies,)),
    ]
    results = pl.pallas_call(
        functools.partial(layer_kernel, shards, ctxs, group),
        out_shape=(
            jax.ShapeDtypeStruct((count, width), BF16),
            jax.ShapeDtypeStruct((count, width), F32),
            jax.ShapeDtypeStruct((rows_two, PANEL), BF16),
            jax.ShapeDtypeStruct((ws, E * HS), BF16),
            jax.ShapeDtypeStruct((ws, 256), BF16),
            jax.ShapeDtypeStruct((8, fs), F32),
        ),
        in_specs=[smem] + [vmem] * 9 + [anywhere] * 6,
        out_specs=tuple([vmem] * 6),
        scratch_shapes=scratch,
        compiler_params=pltpu.CompilerParams(
            collective_id=0, has_side_effects=True, vmem_limit_bytes=VMEM_BYTES
        ),
        name="layer",
    )(
        lengths,
        tokens.reshape(count, width),
        cotangent.reshape(count, width),
        expert_picks.reshape(count, TOP),
        first_gain.reshape(1, ws),
        first_bias.reshape(1, ws),
        second_gain.reshape(1, ws),
        second_bias.reshape(1, ws),
        outer_bias.reshape(1, ws),
        inner_bias.reshape(1, fs),
        query_weight,
        kv_weight,
        router_weight,
        output_weight,
        inner_weight,
        outer_weight,
    )
    vec_shape = jax.ShapeDtypeStruct((1, ws), F32)
    final = pl.pallas_call(
        functools.partial(unpack_kernel, ws, wos, fs),
        out_shape=(
            jax.ShapeDtypeStruct((count, width), BF16),
            jax.ShapeDtypeStruct((count, width), F32),
            vec_shape,
            vec_shape,
            jax.ShapeDtypeStruct(kv_weight.shape, F32),
            jax.ShapeDtypeStruct(query_weight.shape, F32),
            jax.ShapeDtypeStruct(router_weight.shape, F32),
            jax.ShapeDtypeStruct(output_weight.shape, F32),
            vec_shape,
            vec_shape,
            jax.ShapeDtypeStruct(inner_weight.shape, F32),
            jax.ShapeDtypeStruct((1, fs), F32),
            jax.ShapeDtypeStruct(outer_weight.shape, F32),
            vec_shape,
        ),
        in_specs=[vmem] * 6,
        out_specs=tuple([vmem] * 14),
        name="unpack",
    )(*results)
    shapes = (
        tokens.shape,
        tokens.shape,
        first_gain.shape,
        first_bias.shape,
        kv_weight.shape,
        query_weight.shape,
        router_weight.shape,
        output_weight.shape,
        second_gain.shape,
        second_bias.shape,
        inner_weight.shape,
        inner_bias.shape,
        outer_weight.shape,
        outer_bias.shape,
    )
    return tuple(value.reshape(shape) for value, shape in zip(final, shapes))


def solution(mesh):
    rows = P("shard", "ctx", None)
    vec, mat = P("shard"), P("shard", None)
    return jax.shard_map(
        functools.partial(on_device, mesh.shape["shard"], mesh.shape["ctx"]),
        mesh=mesh,
        in_specs=(
            rows,
            vec,
            rows,
            vec,
            vec,
            mat,
            mat,
            mat,
            mat,
            vec,
            vec,
            mat,
            vec,
            mat,
            vec,
            rows,
        ),
        out_specs=(
            rows,
            rows,
            vec,
            vec,
            mat,
            mat,
            mat,
            mat,
            vec,
            vec,
            mat,
            vec,
            mat,
            vec,
        ),
        check_vma=False,
    )
```

```python
import functools

import jax
import jax.numpy as jnp
from jax import lax
from jax.experimental import pallas as pl
from jax.experimental.pallas import tpu as pltpu
from jax.sharding import PartitionSpec as P

HS = 64
E = 24
TOP = 8
NORM_EPS = 1e-05
NEG_LARGE = -1e30
BF16 = jnp.bfloat16
F32 = jnp.float32
PANEL = 512
UNIT = 128
GELU_C = 0.7978845608028654
GELU_A = 0.044715
MESH = pl.DeviceIdType.MESH


def dot(left, right):
    return jnp.dot(left, right, preferred_element_type=F32)


def dot_t(left, right):
    return lax.dot_general(left, right, (((1,), (1,)), ((), ())), preferred_element_type=F32)


def many(first, size, step):
    return pl.ds(pl.multiple_of(first, step), size)


class Net:
    def __init__(self, shards, ctxs, group, send_sem, recv_sem):
        self.shards, self.ctxs, self.group = shards, ctxs, group
        self.pairs = group // 2
        self.groups = ctxs // group
        self.dims = self.pairs.bit_length() - 1
        self.z = lax.axis_index("shard")
        self.i = lax.axis_index("ctx")
        self.core = self.i % 2
        self.chip = (self.i % group) // 2
        self.grp = self.i // group
        self.send_sem, self.recv_sem = send_sem, recv_sem
        self.used = 0
        self.sent = []
        flip_low = self.chip + 1 - 2 * (self.chip % 2)
        if self.dims == 2:
            flip_high = self.chip + 2 - 4 * (self.chip // 2)
            self.chip_a = self.core * flip_high + (1 - self.core) * flip_low
            self.chip_b = self.core * flip_low + (1 - self.core) * flip_high
            self.chip_ab = self.pairs - 1 - self.chip
        elif self.dims == 1:
            self.chip_b = flip_low

    def far(self, step):
        return (self.z + step) % self.shards

    def src(self, step):
        return (self.z + self.shards - step) % self.shards

    def peer(self, chip):
        return self.grp * self.group + chip * 2 + self.core

    def sibling(self):
        return self.i + 1 - 2 * self.core

    def copy(self, src, dst, slot, z, i):
        return pltpu.make_async_remote_copy(
            src_ref=src,
            dst_ref=dst,
            send_sem=self.send_sem.at[slot],
            recv_sem=self.recv_sem.at[slot],
            device_id={"shard": z, "ctx": i},
            device_id_type=MESH,
        )

    def send(self, src, dst, z, i):
        slot = self.used
        self.used += 1
        one = self.copy(src, dst, slot, z, i)
        one.start()
        self.sent.append(one)
        return slot

    def wait(self, slot, dst):
        self.copy(dst, dst, slot, self.z, self.i).wait_recv()

    def finish(self):
        for one in self.sent:
            one.wait_send()
        self.sent = []

    def greet(self):
        barrier = pltpu.get_barrier_semaphore()
        for step in range(1, self.ctxs):
            pl.semaphore_signal(
                barrier,
                inc=1,
                device_id={"shard": self.z, "ctx": (self.i + step) % self.ctxs},
                device_id_type=MESH,
            )
        for step in range(1, self.shards):
            pl.semaphore_signal(
                barrier,
                inc=1,
                device_id={"shard": self.far(step), "ctx": self.i},
                device_id_type=MESH,
            )

    def greeted(self):
        pl.semaphore_wait(pltpu.get_barrier_semaphore(), self.ctxs + self.shards - 2)


class Spread:
    def __init__(self, net, ref):
        self.net, self.ref = net, ref
        self.piece = ref.shape[0] // net.group
        self.half = ref.shape[0] // 2

    def part(self, chip):
        first = (self.net.core * self.net.pairs + chip) * self.piece
        return self.ref.at[many(first, self.piece, self.piece)]

    def block(self, core):
        return self.ref.at[many(core * self.half, self.half, self.half)]

    def begin(self):
        net = self.net
        own = self.part(net.chip)
        if net.dims == 2:
            self.to_a = net.send(own, own, net.z, net.peer(net.chip_a))
        if net.dims:
            self.to_b = net.send(own, own, net.z, net.peer(net.chip_b))

    def pass_on(self):
        net = self.net
        if net.dims == 2:
            got = self.part(net.chip_a)
            net.wait(self.to_a, got)
            self.on = net.send(got, got, net.z, net.peer(net.chip_b))

    def share(self):
        net = self.net
        if net.dims:
            net.wait(self.to_b, self.part(net.chip_b))
        if net.dims == 2:
            net.wait(self.on, self.part(net.chip_ab))
        block = self.block(net.core)
        self.to_core = net.send(block, block, net.z, net.sibling())

    def end(self):
        self.net.wait(self.to_core, self.block(1 - self.net.core))


class Gather:
    def __init__(self, net, buf):
        self.net, self.buf = net, buf
        self.spreads = [Spread(net, buf.at[net.src(k)]) for k in range(1, net.shards)]

    def start(self):
        net = self.net
        own = Spread(net, self.buf.at[net.z]).part(net.chip)
        self.slots = [net.send(own, own, net.far(k), net.i) for k in range(1, net.shards)]

    def begin(self):
        for slot, spread in zip(self.slots, self.spreads):
            self.net.wait(slot, spread.part(self.net.chip))
            spread.begin()

    def pass_on(self):
        for spread in self.spreads:
            spread.pass_on()

    def share(self):
        for spread in self.spreads:
            spread.share()

    def end(self):
        for spread in self.spreads:
            spread.end()


class CoreGather:
    def __init__(self, net, buf):
        self.net, self.buf = net, buf
        self.spreads = [Spread(net, buf.at[net.src(k)]) for k in range(1, net.shards)]

    def start(self):
        net = self.net
        own = Spread(net, self.buf.at[net.z]).block(net.core)
        self.slots = [net.send(own, own, net.far(k), net.i) for k in range(1, net.shards)]

    def share(self):
        net = self.net
        for slot, spread in zip(self.slots, self.spreads):
            block = spread.block(net.core)
            net.wait(slot, block)
            spread.to_core = net.send(block, block, net.z, net.sibling())

    def end(self):
        for spread in self.spreads:
            spread.end()


class Reduce:
    def __init__(
        self, net, grad, from_core, from_a, from_b, from_group, from_far, out, far_first, store
    ):
        self.net, self.grad, self.out, self.far_first = net, grad, out, far_first
        self.store = store
        self.from_core, self.from_a, self.from_b = from_core, from_a, from_b
        self.from_group, self.from_far = from_group, from_far
        self.piece = grad.shape[1] // net.group
        self.half = grad.shape[1] // 2
        self.spread = Spread(net, out)
        near = [self.take_a, self.take_b] if net.dims == 2 else [self.take_b]
        steps = [self.take_far] + near if far_first else near + [self.take_far]
        self.steps = [self.start, self.take_core] + steps
        self.steps[-1] = functools.partial(self.last, self.steps[-1])
        if net.dims == 2:
            self.steps.append(self.spread.pass_on)
        self.steps += [self.spread.share, self.finish]
        self.stage = 0

    def advance(self, times=1):
        for _ in range(times):
            if self.stage < len(self.steps):
                self.steps[self.stage]()
                self.stage += 1

    def last(self, step):
        step()
        self.spread.begin()

    def finish(self):
        self.spread.end()
        self.store.start()

    def first(self, chip):
        return (self.net.core * self.net.pairs + chip) * self.piece

    def rows(self, chip):
        return many(self.first(chip), self.piece, self.piece)

    def planes(self, after_far):
        if after_far:
            return [(self.net.z, 0)]
        return [(s, s) for s in range(self.net.shards)]

    def add(self, first, count, planes, parts):
        lines = 16

        def one(step, carry):
            at = pl.multiple_of(step * lines, lines)
            rows = many(first + at, lines, lines)
            for here, there in planes:
                value = self.grad[here, rows].astype(F32)
                for part in parts:
                    value = value + part[there, pl.ds(at, lines)].astype(F32)
                self.grad[here, rows] = value.astype(BF16)
            return carry

        lax.fori_loop(0, count // lines, one, 0)

    def cut(self, rows, after_far):
        if after_far:
            return self.grad.at[pl.ds(self.net.z, 1), rows]
        return self.grad.at[:, rows]

    def start(self):
        net = self.net
        away = many((1 - net.core) * self.half, self.half, self.half)
        self.to_core = net.send(self.grad.at[:, away], self.from_core, net.z, net.sibling())

    def take_core(self):
        net = self.net
        net.wait(self.to_core, self.from_core)
        self.add(net.core * self.half, self.half, self.planes(False), [self.from_core])
        if self.far_first:
            own = many(net.core * self.half, self.half, self.half)
            self.send_far(own)
        else:
            self.send_near(False)

    def send_near(self, after_far):
        net = self.net
        if net.dims == 2:
            self.to_a = [
                net.send(
                    self.cut(self.rows(chip), after_far),
                    self.from_a.at[k],
                    net.z,
                    net.peer(net.chip_a),
                )
                for k, chip in enumerate((net.chip_a, net.chip_ab))
            ]
        elif net.dims == 1:
            self.send_b(after_far)

    def send_b(self, after_far):
        net = self.net
        self.to_b = net.send(
            self.cut(self.rows(net.chip_b), after_far), self.from_b, net.z, net.peer(net.chip_b)
        )

    def take_a(self):
        net = self.net
        for k, chip in ((1, net.chip_b), (0, net.chip)):
            net.wait(self.to_a[k], self.from_a.at[k])
            self.add(self.first(chip), self.piece, self.planes(self.far_first), [self.from_a.at[k]])
            if k:
                self.send_b(self.far_first)

    def take_b(self):
        net = self.net
        if net.dims:
            net.wait(self.to_b, self.from_b)
            self.add(
                self.first(net.chip), self.piece, self.planes(self.far_first), [self.from_b]
            )
        own = self.rows(net.chip)
        step, at = 1, 0
        while step < net.groups:
            peer = net.i + net.group * step * (1 - 2 * ((net.grp // step) % 2))
            slot = net.send(self.cut(own, self.far_first), self.from_group.at[at], net.z, peer)
            net.wait(slot, self.from_group.at[at])
            net.sent.pop().wait_send()
            self.add(
                self.first(net.chip),
                self.piece,
                self.planes(self.far_first),
                [self.from_group.at[at]],
            )
            step, at = step * 2, at + 1
        if self.far_first:
            self.out[own, :] = self.grad[net.z, own]
        else:
            self.send_far(own)

    def send_far(self, own):
        net = self.net
        self.own = own
        self.to_far = [
            net.send(
                self.grad.at[pl.ds(net.far(k), 1), own],
                self.from_far.at[pl.ds(k - 1, 1)],
                net.far(k),
                net.i,
            )
            for k in range(1, net.shards)
        ]

    def take_far(self):
        net = self.net
        for k in range(1, net.shards):
            net.wait(self.to_far[k - 1], self.from_far.at[pl.ds(k - 1, 1)])
        parts = [self.from_far.at[pl.ds(k, 1)] for k in range(net.shards - 1)]
        if self.far_first:
            self.add(net.core * self.half, self.half, self.planes(True), parts)
            self.send_near(True)
        else:
            self.add(self.first(net.chip), self.piece, self.planes(True), parts)
            self.out[self.own, :] = self.grad[net.z, self.own]


def reduce_scratch(shards, group, rounds, rows, wide, far_first, lead=()):
    pairs = group // 2
    piece, half = rows // group, rows // 2
    far_rows = half if far_first else piece
    planes = 1 if far_first else shards
    tiny = (*lead, 1, 16, 128)
    return [
        pltpu.VMEM((*lead, shards, rows, wide), BF16),
        pltpu.VMEM((*lead, shards, half, wide), BF16),
        pltpu.VMEM((*lead, 2, planes, piece, wide) if pairs == 4 else tiny, BF16),
        pltpu.VMEM((*lead, planes, piece, wide), BF16),
        pltpu.VMEM((*lead, rounds, planes, piece, wide) if rounds else tiny, BF16),
        pltpu.VMEM((*lead, shards - 1, far_rows, wide), BF16),
    ]


def reduce_copies(shards, group, rounds):
    pairs = group // 2
    near = {1: 0, 2: 1, 4: 3}[pairs]
    return 2 * (near + 1) + rounds + shards - 1


def layer_kernel(
    shards,
    ctxs,
    group,
    chunk_far,
    len_ref,
    x_hbm,
    cot_hbm,
    picks_hbm,
    g1_hbm,
    b1_hbm,
    g2_hbm,
    b2_hbm,
    bo_hbm,
    bi_hbm,
    wq_hbm,
    wkv_hbm,
    wr_hbm,
    wo_hbm,
    wi_hbm,
    wout_hbm,
    out_hbm,
    gin_hbm,
    chunk_hbm,
    wo_hbm_out,
    q_hbm,
    kv_hbm,
    x_ref,
    cot_ref,
    picks_ref,
    g1_ref,
    b1_ref,
    g2_ref,
    b2_ref,
    bo_ref,
    bi_ref,
    wq_st,
    wkv_st,
    wr_st,
    wi_st,
    stage,
    wk,
    wq,
    wo,
    wc,
    vecs,
    normed,
    normed_t,
    q_t,
    sel_a,
    heads_t,
    small,
    kvall,
    kvt,
    pads,
    hrow,
    linv,
    ebuf,
    dkv,
    from_sib,
    from_kv,
    mixed_t,
    xhat2,
    n2,
    n2_t,
    gfin_low,
    biases,
    g_t,
    gc,
    gc_core,
    gc_a,
    gc_b,
    gc_group,
    gc_far,
    go,
    go_core,
    go_a,
    go_b,
    go_group,
    go_far,
    gq,
    gq_core,
    gq_a,
    gq_b,
    gq_group,
    gq_far,
    gk,
    gk_core,
    gk_a,
    gk_b,
    gk_group,
    gk_far,
    out_ref,
    gin_ref,
    chunk_out,
    wo_out,
    q_out,
    kv_out,
    vec_g,
    local_sem,
    send_sem,
    recv_sem,
):
    net = Net(shards, ctxs, group, send_sem, recv_sem)
    z, c = net.z, net.i
    tokens, width = x_ref.shape
    seg = tokens // 2
    half = seg // 2
    blocks = 2 * ctxs
    ws = width // shards
    wos = wo.shape[1]
    fs = wout_hbm.shape[0]
    scale = HS ** (-0.5)
    chunks = fs // UNIT
    panels = shards * UNIT // PANEL
    per_panel = PANEL // UNIT
    lanes = TOP * half
    wide = E * HS
    vec_line = E
    bias_line = vec_line + 5
    per_unit = UNIT // ws
    near_steps = ctxs // 2

    def local(src, dst, at):
        return pltpu.make_async_copy(src, dst, local_sem.at[at])

    net.greet()
    wo_st, wout_st = stage.at[0:wos], stage.at[wos : wos + fs]
    resid, acc_a, acc_b = (stage.at[k * tokens : (k + 1) * tokens] for k in range(3))
    loads = {}
    for at, (src, dst) in enumerate(
        (
            (wkv_hbm, wkv_st),
            (wr_hbm, wr_st),
            (wq_hbm, wq_st),
            (g1_hbm, g1_ref),
            (b1_hbm, b1_ref),
            (g2_hbm, g2_ref),
            (b2_hbm, b2_ref),
            (bo_hbm, bo_ref),
            (bi_hbm, bi_ref),
            (x_hbm, x_ref),
            (picks_hbm, picks_ref),
            (wo_hbm, wo_st),
            (wi_hbm, wi_st),
            (wout_hbm, wout_st),
            (cot_hbm, cot_ref),
        )
    ):
        loads[id(dst)] = local(src, dst, at)
        loads[id(dst)].start()
    loads[id(wkv_st)].wait()
    loads[id(wr_st)].wait()
    wk[z, :, 0 : 2 * HS] = wkv_st[...].astype(BF16)
    padded = jnp.concatenate([wr_st[...], jnp.zeros((128 - E, ws), F32)], axis=0)
    wk[z, :, 2 * HS :] = padded.T.astype(BF16)
    own_vec = vecs.at[z]
    own_vec[...] = jnp.zeros(own_vec.shape, F32)
    for row, ref in enumerate((g1_ref, b1_ref, g2_ref, b2_ref, bo_ref, bi_ref)):
        loads[id(ref)].wait()
        own_vec[row : row + 1, 0 : ref.shape[1]] = ref[...].astype(BF16).astype(F32)
    net.greeted()
    gather_k, gather_q, gather_o = CoreGather(net, wk), Gather(net, wq), Gather(net, wo)
    gather_c = [Gather(net, wc.at[k]) for k in range(chunks)]
    gather_k.start()
    vec_slots = [net.send(own_vec, own_vec, net.far(k), net.i) for k in range(1, shards)]
    loads[id(wq_st)].wait()
    wq[z] = wq_st[...].astype(BF16)
    gather_q.start()

    loads[id(x_ref)].wait()
    x = x_ref[...].astype(F32)
    mean1 = jnp.mean(x, axis=1, keepdims=True)
    cen = x - mean1
    small[0, :, 0:1] = lax.rsqrt(jnp.mean(cen * cen, axis=1, keepdims=True) + NORM_EPS)
    small[0, :, 2:3] = mean1

    def first_hat():
        return (x_ref[...].astype(F32) - small[0, :, 2:3]) * small[0, :, 0:1]

    for ref in (wo_st, wi_st, wout_st):
        loads[id(ref)].wait()
    wo[z] = wo_st[...].astype(BF16)
    for k in range(chunks):
        wc[k, z, 0:UNIT] = wout_st[k * UNIT : (k + 1) * UNIT].astype(BF16)
        for s in range(shards):
            first = UNIT + (s // per_panel) * ws
            at = (s % per_panel) * UNIT
            wc[k, z, first : first + ws, at : at + UNIT] = wi_st[
                :, s * fs + k * UNIT : s * fs + (k + 1) * UNIT
            ].astype(BF16)
    gather_k.share()
    for k in range(1, shards):
        net.wait(vec_slots[k - 1], vecs.at[net.src(k)])

    def whole(row):
        return jnp.concatenate([vecs[s, row : row + 1, 0:ws] for s in range(shards)], axis=1)

    gain1, bias1, gain2, bias2, bias_out = (whole(row) for row in range(5))
    for k in range(chunks):
        for p in range(panels):
            biases[k * panels + p : k * panels + p + 1, :] = jnp.concatenate(
                [
                    vecs[s, 5:6, k * UNIT : (k + 1) * UNIT]
                    for s in range(p * per_panel, (p + 1) * per_panel)
                ],
                axis=1,
            )
    norm_value = first_hat() * gain1 + bias1
    normed[...] = norm_value.astype(BF16)
    normed_t[...] = norm_value.T.astype(BF16)
    gather_k.end()

    kvr = dot(normed[...], wk[...].reshape(width, 256))
    kv_own = kvr[:, 0 : 2 * HS].astype(BF16)

    def at_block(ref, block):
        return ref.at[block // 2, :, block % 2]

    def my_block(h):
        return c if h == 0 else blocks - 1 - c

    def core_blocks(ref, core):
        return ref.at[0:near_steps, :, core], ref.at[near_steps:ctxs, :, 1 - core]

    for h in range(2):
        block = my_block(h)
        for s in range(2):
            first = s * seg + h * half
            kvall[block // 2, s, block % 2] = kv_own[first : first + half]
    kv_first = len(net.sent)
    kv_slots = []
    for step in range(1, near_steps):
        kv_slots.append(
            [
                net.send(at_block(kvall, block), at_block(kvall, block), z, (c + 2 * step) % ctxs)
                for block in (c, blocks - 1 - c)
            ]
        )
    kv_sent = net.sent[kv_first:]
    del net.sent[kv_first:]
    gather_q.begin()
    gather_o.start()
    logits_t = kvr[:, 2 * HS : 2 * HS + 128].T
    loads[id(picks_ref)].wait()
    picks = jnp.concatenate([picks_ref[0], picks_ref[1]], axis=1).astype(F32)
    picked = jnp.zeros((TOP, tokens), F32)
    for e in range(E):
        picked = jnp.where(picks == float(e), logits_t[e : e + 1, :], picked)
    top = jnp.max(picked, axis=0, keepdims=True)
    gexp = jnp.exp(picked - top)
    small[1, 0:TOP, 0:tokens] = gexp / jnp.sum(gexp, axis=0, keepdims=True)
    small[1, TOP : 2 * TOP, 0:tokens] = picks
    for step in range(1, near_steps):
        source = (c + ctxs - 2 * step) % ctxs
        for slot, block in zip(kv_slots[step - 1], (source, blocks - 1 - source)):
            net.wait(slot, at_block(kvall, block))
    kv_cross = [net.send(part, part, z, net.sibling()) for part in core_blocks(kvall, net.core)]
    kv_sent += net.sent[-2:]
    del net.sent[-2:]
    gather_q.pass_on()
    gather_c[0].start()
    for slot, part in zip(kv_cross, core_blocks(kvall, 1 - net.core)):
        net.wait(slot, part)

    def turn(step, carry):
        for s in range(2):
            keys = kvall[step, s].reshape(2 * half, 2 * HS)
            kvt[step, s] = keys.astype(F32).T.astype(BF16)
            dkv[step, s] = jnp.zeros((2 * half, 2 * HS), F32)
        return carry

    lax.fori_loop(0, ctxs, turn, 0)
    gather_q.share()
    gather_o.begin()
    if chunks > 1:
        gather_c[1].start()
    gather_q.end()

    def query_tile(n, carry):
        cols = many(n * 256, 256, 256)
        value = dot(normed[...], wq[:, :, cols].reshape(width, 256))
        value = value.astype(BF16).astype(F32).T
        for k in range(4):
            q_t[n * 4 + k] = value[k * HS : (k + 1) * HS]
        return carry

    lax.fori_loop(0, wide // 256, query_tile, 0)

    def choose(src, store):
        def one(j, carry):
            pick = small[1, pl.ds(TOP + j, 1), 0:tokens]
            value = jnp.zeros((HS, tokens), F32)
            for e in range(E):
                value = jnp.where(pick == float(e), src[e], value)
            store(j, value)
            return carry

        lax.fori_loop(0, TOP, one, 0)

    def spread_back(src, store):
        def one(e, carry):
            value = jnp.zeros((HS, tokens), F32)
            for j in range(TOP):
                pick = small[1, TOP + j : TOP + j + 1, 0:tokens]
                value = jnp.where(pick == e.astype(F32), src[j], value)
            store(e, value)
            return carry

        lax.fori_loop(0, E, one, 0)

    low_lane = lax.broadcasted_iota(jnp.int32, (HS, 2 * half), 1) < half

    def swap(one, two):
        return (
            jnp.where(low_lane, one, pltpu.roll(two, half, 1)),
            jnp.where(low_lane, pltpu.roll(one, half, 1), two),
        )

    def store_query(j, value):
        sel_a[j] = value * scale

    def serve(*calls):
        for k, call in calls:
            if k < chunks:
                getattr(gather_c[k], call)()

    gather_o.pass_on()
    serve((0, "begin"), (2, "start"))
    choose(q_t, store_query)
    for s in range(2):
        for pair in range(TOP // 2):
            halves = swap(
                sel_a[2 * pair, :, s * seg : (s + 1) * seg],
                sel_a[2 * pair + 1, :, s * seg : (s + 1) * seg],
            )
            for h in range(2):
                pads[2 * s + h, 0:HS, pair * 128 : (pair + 1) * 128] = halves[h].astype(BF16)
    for sh in range(4):
        pads[sh, HS:, 0:lanes] = jnp.zeros((HS, lanes), BF16)
        pads[sh, 0:HS, lanes:] = jnp.zeros((HS, lanes), BF16)

    gather_o.share()
    serve((0, "pass_on"), (1, "begin"), (3, "start"))

    offset = lax.broadcasted_iota(jnp.int32, (1, lanes), 1) % half
    key_row = lax.broadcasted_iota(jnp.int32, (2 * half, lanes), 0)

    def place(h):
        if h == 1:
            return (blocks - c + 1) // 2, 0
        return (c + 2) // 2, (blocks - c + 1) // 2

    def fold(value, op):
        parts = [value[8 * k : 8 * k + 8] for k in range(value.shape[0] // 8)]
        while len(parts) > 1:
            parts = [op(parts[k], parts[k + 1]) for k in range(0, len(parts), 2)]
        return parts[0]

    def keys_of(step, s):
        return kvall[step, s].reshape(2 * half, 2 * HS)

    def attend(h):
        count, base = place(h)
        limits = [
            jnp.minimum(my_block(h) * half + offset, len_ref[s] - 1) for s in range(2)
        ]

        def masked(step, s):
            scores = dot(keys_of(step, s), pads[2 * s + h, :, 0:lanes])
            return jnp.where(key_row <= limits[s] - step * 2 * half, scores, NEG_LARGE)

        def score_step(step, tops):
            return tuple(
                jnp.maximum(tops[s], fold(masked(step, s), jnp.maximum)) for s in range(2)
            )

        start = jnp.full((8, lanes), NEG_LARGE, F32)
        tops = lax.fori_loop(0, count, score_step, (start, start))
        tops = [jnp.max(top, axis=0, keepdims=True) for top in tops]
        if h == 1:
            serve((0, "share"), (1, "pass_on"), (2, "begin"))
        for s in range(2):
            hrow[2 * s + h] = jnp.zeros((HS, lanes), F32)

        def value_step(step, totals):
            result = []
            for s in range(2):
                expd = jnp.exp(masked(step, s) - tops[s])
                low = expd.astype(BF16)
                ebuf[s, base + step] = low
                hrow[2 * s + h] += dot(kvt[step, s, HS:], low)
                result.append(totals[s] + fold(expd, jnp.add))
            return tuple(result)

        start = jnp.zeros((8, lanes), F32)
        totals = lax.fori_loop(0, count, value_step, (start, start))
        for s in range(2):
            inverse = 1.0 / jnp.sum(totals[s], axis=0, keepdims=True)
            linv[2 * s + h] = jnp.broadcast_to(inverse, (8, lanes))
            hrow[2 * s + h] = hrow[2 * s + h] * inverse

    attend(1)
    serve((1, "share"), (2, "pass_on"), (3, "begin"))
    attend(0)
    serve((2, "share"), (3, "pass_on"))

    for s in range(2):
        for pair in range(TOP // 2):
            both = swap(
                hrow[2 * s, :, pair * 128 : (pair + 1) * 128],
                hrow[2 * s + 1, :, pair * 128 : (pair + 1) * 128],
            )
            for k in range(2):
                heads_t[2 * pair + k, :, s * seg : (s + 1) * seg] = both[k]
    for j in range(TOP):
        sel_a[j] = heads_t[j] * small[1, j : j + 1, 0:tokens]

    def store_mixed(e, value):
        mixed_t[e] = value.astype(BF16)

    spread_back(sel_a, store_mixed)
    gather_o.end()
    serve((3, "share"))

    experts = E // shards
    acc_a[...] = x_ref[...].astype(F32)

    def project(s, carry):
        part = mixed_t[pl.ds(s * experts, experts)].reshape(wos, tokens)
        acc_a[...] += dot(part.astype(F32).T.astype(BF16), wo[s])
        return carry

    lax.fori_loop(0, shards, project, 0)
    residual = acc_a[...]
    resid[...] = residual
    cen = residual - jnp.mean(residual, axis=1, keepdims=True)
    rstd2 = lax.rsqrt(jnp.mean(cen * cen, axis=1, keepdims=True) + NORM_EPS)
    small[0, :, 1:2] = rstd2
    cen = cen * rstd2
    xhat2[...] = cen
    cen = cen * gain2 + bias2
    n2[...] = cen.astype(BF16)
    n2_t[...] = cen.T.astype(BF16)

    row = lax.broadcasted_iota(jnp.int32, (tokens, 1), 0)
    inner_row = row % seg
    pos = jnp.where(
        inner_row < half, c * half + inner_row, blocks * half - (c + 2) * half + inner_row
    )
    valid = (pos < jnp.where(row < seg, len_ref[0], len_ref[1])).astype(F32)
    loads[id(cot_ref)].wait()
    gfin_low[...] = (cot_ref[...].astype(F32) * valid).astype(BF16)
    acc_a[...] = jnp.zeros((tokens, width), F32)
    acc_b[...] = jnp.zeros((tokens, width), F32)
    vec_g[...] = jnp.zeros(vec_g.shape, F32)

    def feed(k, p):
        rows_in = slice(UNIT + p * ws, UNIT + (p + 1) * ws)
        planes = slice(p * per_panel, (p + 1) * per_panel)
        w_in = wc[k, :, rows_in].reshape(width, PANEL)
        w_out = wc[k, planes, 0:UNIT].reshape(PANEL, width)
        line = k * panels + p
        hidden = dot(n2[...], w_in) + biases[line : line + 1, :]
        square = hidden * hidden
        tanh = jnp.tanh(GELU_C * hidden * (1.0 + GELU_A * square))
        act = (0.5 * hidden * (1.0 + tanh)).astype(BF16)
        slope = 0.5 * (1.0 + tanh) + 0.5 * GELU_C * hidden * (1.0 - tanh * tanh) * (
            1.0 + 3.0 * GELU_A * square
        )
        gfin = gfin_low[...]
        acc_a[...] += dot(act, w_out)
        grad_hidden = (slope * dot_t(gfin, w_out)).astype(BF16)
        total = jnp.sum(grad_hidden.astype(F32), axis=0, keepdims=True)
        for a in range(per_panel):
            for q in range(per_unit):
                at = bias_line + k * per_unit + q
                first = (p * per_panel + a) * ws
                vec_g[at : at + 1, first : first + ws] = total[
                    :, a * UNIT + q * ws : a * UNIT + (q + 1) * ws
                ]
        grad_outer = dot(act.astype(F32).T.astype(BF16), gfin).astype(BF16)
        gc[k, planes, 0:UNIT] = grad_outer.reshape(per_panel, UNIT, width)
        grad_inner = dot(n2_t[...], grad_hidden).astype(BF16)
        gc[k, :, rows_in] = grad_inner.reshape(shards, ws, PANEL)
        acc_b[...] += dot_t(grad_hidden, w_in)

    outs = [local(out_ref, out_hbm, 15), local(gin_ref, gin_hbm, 16)]

    def reduction(refs, out, hbm, at, far_first):
        store = local(out, hbm, at)
        outs.append(store)
        return Reduce(net, *refs, out, far_first, store)

    reduce_c = [
        reduction(
            [ref.at[k] for ref in (gc, gc_core, gc_a, gc_b, gc_group, gc_far)],
            chunk_out.at[k],
            chunk_hbm.at[k],
            20 + k,
            chunk_far[k],
        )
        for k in range(chunks)
    ]
    for k in range(chunks):
        gather_c[k].end()
        for p in range(panels):
            feed(k, p)
        reduce_c[k].advance()
        if k:
            reduce_c[k - 1].advance()
    out_ref[...] = (valid * (resid[...] + acc_a[...] + bias_out)).astype(BF16)
    outs[0].start()
    gfin = cot_ref[...].astype(F32) * valid
    vec_g[vec_line + 4 : vec_line + 5, :] = jnp.sum(gfin, axis=0, keepdims=True)
    grad_n2 = acc_b[...]
    vec_g[vec_line + 3 : vec_line + 4, :] = jnp.sum(grad_n2, axis=0, keepdims=True)
    vec_g[vec_line + 2 : vec_line + 3, :] = jnp.sum(grad_n2 * xhat2[...], axis=0, keepdims=True)
    grad_hat = grad_n2 * gain2
    grad_hat = grad_hat - jnp.mean(grad_hat, axis=1, keepdims=True)
    grad_hat = grad_hat - xhat2[...] * jnp.mean(grad_hat * xhat2[...], axis=1, keepdims=True)
    grad_residual = gfin + grad_hat * small[0, :, 1:2]
    resid[...] = grad_residual
    n2[...] = grad_residual.astype(BF16)
    reduce_c[chunks - 1].advance()

    def branch(s, carry):
        part = mixed_t[pl.ds(s * experts, experts)].reshape(wos, tokens)
        go[s] = dot(part, n2[...]).astype(BF16)
        grad = dot_t(wo[s], n2[...])
        q_t[pl.ds(s * experts, experts)] = grad.reshape(experts, HS, tokens)
        return carry

    lax.fori_loop(0, shards, branch, 0)
    reduce_o = reduction(
        (go, go_core, go_a, go_b, go_group, go_far), wo_out, wo_hbm_out, 17, False
    )
    reduce_o.advance()

    def store_head_grad(j, value):
        sel_a[j] = value * small[1, pl.ds(j, 1), 0:tokens]
        small[1, pl.ds(2 * TOP + j, 1), 0:tokens] = jnp.sum(
            value * heads_t[j], axis=0, keepdims=True
        )

    choose(q_t, store_head_grad)
    reduce_c[0].advance()
    gates = small[1, 0:TOP, 0:tokens]
    grad_gates = small[1, 2 * TOP : 3 * TOP, 0:tokens]
    grad_picked = gates * (grad_gates - jnp.sum(gates * grad_gates, axis=0, keepdims=True))
    picks = small[1, TOP : 2 * TOP, 0:tokens]
    g_t[wide + 2 * HS :, :] = jnp.zeros((128, tokens), BF16)
    grad_logits = [
        jnp.sum(jnp.where(picks == float(e), grad_picked, 0.0), axis=0, keepdims=True)
        for e in range(E)
    ]
    grad_logits += [jnp.zeros((1, tokens), F32)] * (32 - E)
    g_t[wide + 2 * HS : wide + 2 * HS + 32, :] = jnp.concatenate(grad_logits, axis=0).astype(BF16)
    for s in range(2):
        for pair in range(TOP // 2):
            halves = swap(
                sel_a[2 * pair, :, s * seg : (s + 1) * seg],
                sel_a[2 * pair + 1, :, s * seg : (s + 1) * seg],
            )
            at = pair * 128
            for h in range(2):
                sh = 2 * s + h
                grad = (halves[h] * linv[sh, 0:1, at : at + 128]).astype(BF16)
                pads[sh, HS:, lanes + at : lanes + at + 128] = grad
                linv[sh, 1:2, at : at + 128] = jnp.sum(
                    grad.astype(F32) * hrow[sh, :, at : at + 128], axis=0, keepdims=True
                )
    reduce_o.advance()
    reduce_c[1 % chunks].advance()

    def attend_back(h):
        count, base = place(h)
        deltas = [linv[2 * s + h, 1:2, :] for s in range(2)]
        for s in range(2):
            hrow[2 * s + h] = jnp.zeros((HS, lanes), F32)

        def grad_step(step, carry):
            for s in range(2):
                sh = 2 * s + h
                expd = ebuf[s, base + step]
                grad_prob = dot(keys_of(step, s), pads[sh, :, lanes:])
                grad_score = (expd.astype(F32) * (grad_prob - deltas[s])).astype(BF16)
                dkv[step, s] += dot_t(jnp.concatenate([grad_score, expd], axis=1), pads[sh])
                hrow[sh] += dot(kvt[step, s, 0:HS], grad_score)
            return carry

        lax.fori_loop(0, count, grad_step, 0)

    attend_back(1)
    for k in range(chunks):
        reduce_c[k].advance()
    attend_back(0)

    for one in kv_sent:
        one.wait_send()

    def lower(step, carry):
        kvall[step] = dkv[step].astype(BF16).reshape(2, 2, half, 2 * HS)
        return carry

    lax.fori_loop(0, ctxs, lower, 0)
    dkv_cross = [
        net.send(part, from_sib.at[k], z, net.sibling())
        for k, part in enumerate(core_blocks(kvall, 1 - net.core))
    ]
    for s in range(2):
        for pair in range(TOP // 2):
            both = swap(
                hrow[2 * s, :, pair * 128 : (pair + 1) * 128],
                hrow[2 * s + 1, :, pair * 128 : (pair + 1) * 128],
            )
            for k in range(2):
                q_t[2 * pair + k, :, s * seg : (s + 1) * seg] = both[k] * scale

    def store_grad_query(e, value):
        g_t[many(e * HS, HS, HS), :] = value.astype(BF16)

    spread_back(q_t, store_grad_query)

    for k in range(2):
        net.wait(dkv_cross[k], from_sib.at[k])

    def add_sibling(step, carry):
        for k, sub in enumerate((net.core, 1 - net.core)):
            at = step + k * near_steps
            rows = many(sub * half, half, half)
            for s in range(2):
                value = dkv[at, s, rows] + from_sib[k, step, s].astype(F32)
                dkv[at, s, rows] = value
                kvall[at, s, sub] = value.astype(BF16)
        return carry

    lax.fori_loop(0, near_steps, add_sibling, 0)
    dkv_slots = []
    for step in range(1, near_steps):
        peer = (c + 2 * step) % ctxs
        dkv_slots.append(
            [
                net.send(at_block(kvall, block), from_kv.at[step - 1, h], z, peer)
                for h, block in enumerate((peer, blocks - 1 - peer))
            ]
        )

    def query_grad(n, carry):
        at = many(n * 256, 256, 256)
        grad = dot_t(normed_t[...], g_t[at, :]).astype(BF16)
        gq[:, :, at] = grad.reshape(shards, ws, 256)
        return carry

    lax.fori_loop(0, wide // 256, query_grad, 0)
    reduce_q = reduction((gq, gq_core, gq_a, gq_b, gq_group, gq_far), q_out, q_hbm, 18, False)
    reduce_q.advance()
    reduce_o.advance()

    heads_t[...] = jnp.zeros(heads_t.shape, F32)

    def norm_grad(n, carry):
        at = many(n * 256, 256, 256)
        part = dot(wq[:, :, at].reshape(width, 256), g_t[at, :])
        heads_t[...] += part.reshape(heads_t.shape)
        return carry

    lax.fori_loop(0, wide // 256, norm_grad, 0)
    reduce_q.advance()
    for step in range(1, near_steps):
        for h in range(2):
            net.wait(dkv_slots[step - 1][h], from_kv.at[step - 1, h])
    for h in range(2):
        block = my_block(h)
        for s in range(2):
            value = dkv[block // 2, s, many((block % 2) * half, half, half)]
            for step in range(1, near_steps):
                value = value + from_kv[step - 1, h, s].astype(F32)
            first = s * seg + h * half
            acc_a[first : first + half, 0:128] = value
    g_t[wide : wide + 2 * HS, :] = acc_a[:, 0:128].T.astype(BF16)
    tail = g_t[wide:, :]
    part = heads_t[...].reshape(width, tokens) + dot(wk[...].reshape(width, 256), tail)
    grad_normed = part.T
    hat = first_hat()
    vec_g[vec_line : vec_line + 1, :] = jnp.sum(grad_normed * hat, axis=0, keepdims=True)
    vec_g[vec_line + 1 : vec_line + 2, :] = jnp.sum(grad_normed, axis=0, keepdims=True)
    tail_grad = dot_t(normed_t[...], tail)
    gk[:, :, 0 : 2 * HS] = tail_grad[:, 0 : 2 * HS].astype(BF16).reshape(shards, ws, 2 * HS)
    tail_grad = tail_grad[:, 2 * HS :] + vec_g[...].T
    gk[:, :, 2 * HS :] = tail_grad.astype(BF16).reshape(shards, ws, 128)
    reduce_k = reduction((gk, gk_core, gk_a, gk_b, gk_group, gk_far), kv_out, kv_hbm, 19, False)
    reduce_k.advance()
    grad_hat = grad_normed * gain1
    grad_hat = grad_hat - jnp.mean(grad_hat, axis=1, keepdims=True)
    grad_hat = grad_hat - hat * jnp.mean(grad_hat * hat, axis=1, keepdims=True)
    gin_ref[...] = resid[...] + grad_hat * small[0, :, 0:1]
    outs[1].start()

    everything = [*reduce_c, reduce_o, reduce_q, reduce_k]
    while any(one.stage < len(one.steps) for one in everything):
        for one in everything:
            one.advance()
    net.finish()
    for one in outs:
        one.wait()


def unpack_kernel(shards, *refs):
    ins, outs = refs[0:6], refs[6:20]
    in_st, out_st, sem = refs[20:26], refs[26:40], refs[40]
    loads = [pltpu.make_async_copy(a, b, sem.at[k]) for k, (a, b) in enumerate(zip(ins, in_st))]
    stores = [
        pltpu.make_async_copy(in_st[k] if k < 2 else out_st[k], outs[k], sem.at[6 + k])
        for k in range(14)
    ]
    for k in (2, 3, 4, 5, 1, 0):
        loads[k].start()
    chunk_in, wo_in, q_in, kv_in = in_st[2:]
    g1_ref, b1_ref, kv_ref, q_ref, r_ref, wo_ref, g2_ref, b2_ref = out_st[2:10]
    wi_ref, bi_ref, wout_ref, bo_ref = out_st[10:]
    ws, fs = q_ref.shape[0], wout_ref.shape[0]
    per_panel = PANEL // UNIT
    loads[2].wait()
    for k in range(chunk_in.shape[0]):
        wout_ref[k * UNIT : (k + 1) * UNIT, :] = chunk_in[k, 0:UNIT].astype(F32)
    stores[12].start()
    for k in range(chunk_in.shape[0]):
        for s in range(shards):
            first = UNIT + (s // per_panel) * ws
            at = (s % per_panel) * UNIT
            wi_ref[:, s * fs + k * UNIT : s * fs + (k + 1) * UNIT] = chunk_in[
                k, first : first + ws, at : at + UNIT
            ].astype(F32)
    stores[10].start()
    loads[3].wait()
    wo_ref[...] = wo_in[...].astype(F32)
    stores[7].start()
    loads[4].wait()
    q_ref[...] = q_in[...].astype(F32)
    stores[5].start()
    loads[5].wait()
    kv_ref[...] = kv_in[:, 0 : 2 * HS].astype(F32)
    stores[4].start()
    turned = kv_in[:, 2 * HS :].astype(F32).T
    r_ref[...] = turned[0:E]
    stores[6].start()
    for row, at, ref in (
        (0, 2, g1_ref),
        (1, 3, b1_ref),
        (2, 8, g2_ref),
        (3, 9, b2_ref),
        (4, 13, bo_ref),
    ):
        ref[...] = turned[E + row : E + row + 1]
        stores[at].start()
    for line in range(fs // ws):
        bi_ref[:, line * ws : (line + 1) * ws] = turned[E + 5 + line : E + 6 + line]
    stores[11].start()
    loads[1].wait()
    stores[1].start()
    loads[0].wait()
    stores[0].start()
    for one in stores:
        one.wait()


def on_device(
    shards,
    ctxs,
    tokens,
    lengths,
    expert_picks,
    first_gain,
    first_bias,
    kv_weight,
    query_weight,
    router_weight,
    output_weight,
    second_gain,
    second_bias,
    inner_weight,
    inner_bias,
    outer_weight,
    outer_bias,
    cotangent,
):
    slots, seg, width = tokens.shape
    count = slots * seg
    half = seg // 2
    lanes = TOP * half
    ws = width // shards
    wos = output_weight.shape[0]
    fs = outer_weight.shape[0]
    group = min(ctxs, ws // 16, 8)
    pairs, groups = group // 2, ctxs // group
    rounds = groups.bit_length() - 1
    chunks = fs // UNIT
    panels = shards * UNIT // PANEL
    chunk_rows = UNIT + panels * ws
    wide = E * HS
    chunk_far = [False] * chunks
    shapes_mid = (
        jax.ShapeDtypeStruct((count, width), BF16),
        jax.ShapeDtypeStruct((count, width), F32),
        jax.ShapeDtypeStruct((chunks, chunk_rows, PANEL), BF16),
        jax.ShapeDtypeStruct((wos, width), BF16),
        jax.ShapeDtypeStruct((ws, wide), BF16),
        jax.ShapeDtypeStruct((ws, 256), BF16),
    )

    smem = pl.BlockSpec(memory_space=pltpu.SMEM)
    anywhere = pl.BlockSpec(memory_space=pl.ANY)
    spread = {1: 0, 2: 1, 4: 3}[pairs]
    copies = (
        (3 + chunks) * (shards - 1) * (spread + 2)
        + (3 + chunks) * (reduce_copies(shards, group, rounds) + 1)
        + 4 * (ctxs // 2 - 1)
        + 4
        + (shards - 1)
    )
    scratch = [
        pltpu.VMEM((count, width), BF16),
        pltpu.VMEM((count, width), BF16),
        pltpu.VMEM((slots, TOP, seg), jnp.int32),
        *[pltpu.VMEM((1, ws), F32)] * 5,
        pltpu.VMEM((1, fs), F32),
        pltpu.VMEM(query_weight.shape, F32),
        pltpu.VMEM(kv_weight.shape, F32),
        pltpu.VMEM((E, ws), F32),
        pltpu.VMEM(inner_weight.shape, F32),
        pltpu.VMEM((max(wos + fs, 3 * count), width), F32),
        pltpu.VMEM((shards, ws, 256), BF16),
        pltpu.VMEM((shards, ws, wide), BF16),
        pltpu.VMEM((shards, wos, width), BF16),
        pltpu.VMEM((chunks, shards, chunk_rows, PANEL), BF16),
        pltpu.VMEM((shards, 8, fs), F32),
        pltpu.VMEM((count, width), BF16),
        pltpu.VMEM((width, count), BF16),
        pltpu.VMEM((E, HS, count), F32),
        pltpu.VMEM((TOP, HS, count), F32),
        pltpu.VMEM((TOP, HS, count), F32),
        pltpu.VMEM((2, count, count), F32),
        pltpu.VMEM((ctxs, slots, 2, half, 2 * HS), BF16),
        pltpu.VMEM((ctxs, slots, 2 * HS, 2 * half), BF16),
        pltpu.VMEM((4, 2 * HS, 2 * lanes), BF16),
        pltpu.VMEM((4, HS, lanes), F32),
        pltpu.VMEM((4, 8, lanes), F32),
        pltpu.VMEM((slots, ctxs + 1, 2 * half, lanes), BF16),
        pltpu.VMEM((ctxs, slots, 2 * half, 2 * HS), F32),
        pltpu.VMEM((2, ctxs // 2, slots, half, 2 * HS), BF16),
        pltpu.VMEM((ctxs // 2 - 1, 2, slots, half, 2 * HS), BF16),
        pltpu.VMEM((E, HS, count), BF16),
        pltpu.VMEM((count, width), F32),
        pltpu.VMEM((count, width), BF16),
        pltpu.VMEM((width, count), BF16),
        pltpu.VMEM((count, width), BF16),
        pltpu.VMEM((8, PANEL), F32),
        pltpu.VMEM((wide + 256, count), BF16),
        *reduce_scratch(shards, group, rounds, chunk_rows, PANEL, False, (chunks,)),
        *reduce_scratch(shards, group, rounds, wos, width, False),
        *reduce_scratch(shards, group, rounds, ws, wide, False),
        *reduce_scratch(shards, group, rounds, ws, 256, False),
        *[pltpu.VMEM(one.shape, one.dtype) for one in shapes_mid],
        pltpu.VMEM((128, width), F32),
        pltpu.SemaphoreType.DMA((20 + chunks,)),
        pltpu.SemaphoreType.DMA((copies,)),
        pltpu.SemaphoreType.DMA((copies,)),
    ]
    results = pl.pallas_call(
        functools.partial(layer_kernel, shards, ctxs, group, chunk_far),
        out_shape=shapes_mid,
        in_specs=[smem] + [anywhere] * 15,
        out_specs=tuple([anywhere] * 6),
        scratch_shapes=scratch,
        compiler_params=pltpu.CompilerParams(
            collective_id=0, has_side_effects=True, vmem_limit_bytes=63 * 1024 * 1024
        ),
        name="layer",
    )(
        lengths,
        tokens.reshape(count, width),
        cotangent.reshape(count, width),
        jnp.swapaxes(expert_picks, 1, 2),
        first_gain.reshape(1, ws),
        first_bias.reshape(1, ws),
        second_gain.reshape(1, ws),
        second_bias.reshape(1, ws),
        outer_bias.reshape(1, ws),
        inner_bias.reshape(1, fs),
        query_weight,
        kv_weight,
        router_weight.T,
        output_weight,
        inner_weight,
        outer_weight,
    )
    vec_shape = jax.ShapeDtypeStruct((1, ws), F32)
    shapes_out = (
        jax.ShapeDtypeStruct((count, width), BF16),
        jax.ShapeDtypeStruct((count, width), F32),
        vec_shape,
        vec_shape,
        jax.ShapeDtypeStruct(kv_weight.shape, F32),
        jax.ShapeDtypeStruct(query_weight.shape, F32),
        jax.ShapeDtypeStruct((E, ws), F32),
        jax.ShapeDtypeStruct(output_weight.shape, F32),
        vec_shape,
        vec_shape,
        jax.ShapeDtypeStruct(inner_weight.shape, F32),
        jax.ShapeDtypeStruct((1, fs), F32),
        jax.ShapeDtypeStruct(outer_weight.shape, F32),
        vec_shape,
    )
    final = pl.pallas_call(
        functools.partial(unpack_kernel, shards),
        out_shape=shapes_out,
        in_specs=[anywhere] * 6,
        out_specs=tuple([anywhere] * 14),
        scratch_shapes=[pltpu.VMEM(one.shape, one.dtype) for one in (*shapes_mid, *shapes_out)]
        + [pltpu.SemaphoreType.DMA((20,))],
        name="unpack",
    )(*results)
    final = list(final)
    final[6] = final[6].T
    shapes = (
        tokens.shape,
        tokens.shape,
        first_gain.shape,
        first_bias.shape,
        kv_weight.shape,
        query_weight.shape,
        router_weight.shape,
        output_weight.shape,
        second_gain.shape,
        second_bias.shape,
        inner_weight.shape,
        inner_bias.shape,
        outer_weight.shape,
        outer_bias.shape,
    )
    return tuple(value.reshape(shape) for value, shape in zip(final, shapes))


def solution(mesh):
    rows = P("shard", "ctx", None)
    vec, mat = P("shard"), P("shard", None)
    return jax.shard_map(
        functools.partial(on_device, mesh.shape["shard"], mesh.shape["ctx"]),
        mesh=mesh,
        in_specs=(
            rows,
            vec,
            rows,
            vec,
            vec,
            mat,
            mat,
            mat,
            mat,
            vec,
            vec,
            mat,
            vec,
            mat,
            vec,
            rows,
        ),
        out_specs=(
            rows,
            rows,
            vec,
            vec,
            mat,
            mat,
            mat,
            mat,
            vec,
            vec,
            mat,
            vec,
            mat,
            vec,
        ),
        check_vma=False,
    )
```

```python
import functools

import jax
import jax.numpy as jnp
from jax import lax
from jax.experimental import pallas as pl
from jax.experimental.pallas import tpu as pltpu
from jax.sharding import PartitionSpec as P

HS = 64
E = 24
TOP = 8
NORM_EPS = 1e-05
NEG_LARGE = -1e30
BF16 = jnp.bfloat16
F32 = jnp.float32
PANEL = 512
UNIT = 128
GELU_C = 0.7978845608028654
GELU_A = 0.044715
MESH = pl.DeviceIdType.MESH
RING = 40


def dot(left, right):
    return jnp.dot(left, right, preferred_element_type=F32)


def dot_t(left, right):
    return lax.dot_general(left, right, (((1,), (1,)), ((), ())), preferred_element_type=F32)


def many(first, size, step):
    return pl.ds(pl.multiple_of(first, step), size)


class Net:
    def __init__(self, shards, ctxs, group, send_sem, recv_sem):
        self.shards, self.ctxs, self.group = shards, ctxs, group
        self.pairs = group // 2
        self.groups = ctxs // group
        self.dims = self.pairs.bit_length() - 1
        self.z = lax.axis_index("shard")
        self.i = lax.axis_index("ctx")
        self.core = self.i % 2
        self.chip = (self.i % group) // 2
        self.grp = self.i // group
        self.send_sem, self.recv_sem = send_sem, recv_sem
        self.arrivals = 0
        self.starts = 0
        self.ring = [[] for _ in range(RING)]
        flip_low = self.chip + 1 - 2 * (self.chip % 2)
        if self.dims == 2:
            flip_high = self.chip + 2 - 4 * (self.chip // 2)
            self.chip_a = self.core * flip_high + (1 - self.core) * flip_low
            self.chip_b = self.core * flip_low + (1 - self.core) * flip_high
            self.chip_ab = self.pairs - 1 - self.chip
        elif self.dims == 1:
            self.chip_b = flip_low

    def far(self, step):
        return (self.z + step) % self.shards

    def src(self, step):
        return (self.z + self.shards - step) % self.shards

    def peer(self, chip):
        return self.grp * self.group + chip * 2 + self.core

    def sibling(self):
        return self.i + 1 - 2 * self.core

    def copy(self, src, dst, sent, arrived, z, i):
        return pltpu.make_async_remote_copy(
            src_ref=src,
            dst_ref=dst,
            send_sem=self.send_sem.at[sent],
            recv_sem=self.recv_sem.at[arrived],
            device_id={"shard": z, "ctx": i},
            device_id_type=MESH,
        )

    def arrival(self):
        self.arrivals += 1
        return self.arrivals - 1

    def send(self, src, dst, arrived, z, i):
        slot = self.starts % RING
        self.starts += 1
        if self.ring[slot]:
            self.left(self.ring[slot])
        one = self.ring[slot] = [self.copy(src, dst, slot, arrived, z, i)]
        one[0].start()
        return one

    def left(self, one):
        if one:
            one.pop().wait_send()

    def wait(self, arrived, dst):
        self.copy(dst, dst, 0, arrived, self.z, self.i).wait_recv()

    def finish(self):
        for one in self.ring:
            self.left(one)

    def greet(self):
        barrier = pltpu.get_barrier_semaphore()
        for step in range(1, self.ctxs):
            pl.semaphore_signal(
                barrier,
                inc=1,
                device_id={"shard": self.z, "ctx": (self.i + step) % self.ctxs},
                device_id_type=MESH,
            )
        for step in range(1, self.shards):
            pl.semaphore_signal(
                barrier,
                inc=1,
                device_id={"shard": self.far(step), "ctx": self.i},
                device_id_type=MESH,
            )

    def greeted(self):
        pl.semaphore_wait(pltpu.get_barrier_semaphore(), self.ctxs + self.shards - 2)


class Spread:
    def __init__(self, net, refs, all_of):
        self.net, self.refs, self.all_of = net, refs, all_of
        self.piece = refs[0].shape[0] // net.group
        self.half = refs[0].shape[0] // 2

    def part(self, chip):
        return many((self.net.core * self.net.pairs + chip) * self.piece, self.piece, self.piece)

    def block(self, core):
        return many(core * self.half, self.half, self.half)

    def give(self, rows, peer):
        arrived = self.net.arrival()
        for ref in self.refs:
            self.net.send(ref.at[rows], ref.at[rows], arrived, self.net.z, peer)
        return arrived

    def begin(self):
        net = self.net
        own = self.part(net.chip)
        if net.dims == 2:
            self.to_a = self.give(own, net.peer(net.chip_a))
        if net.dims:
            self.to_b = self.give(own, net.peer(net.chip_b))

    def pass_on(self):
        net = self.net
        if net.dims == 2:
            got = self.part(net.chip_a)
            net.wait(self.to_a, self.all_of(got))
            self.on = self.give(got, net.peer(net.chip_b))

    def share(self):
        net = self.net
        if net.dims:
            net.wait(self.to_b, self.all_of(self.part(net.chip_b)))
        if net.dims == 2:
            net.wait(self.on, self.all_of(self.part(net.chip_ab)))
        self.cross()

    def cross(self):
        self.to_core = self.give(self.block(self.net.core), self.net.sibling())

    def end(self):
        self.net.wait(self.to_core, self.all_of(self.block(1 - self.net.core)))


class Gather:
    def __init__(self, net, buf, by_core=False):
        self.net, self.buf, self.by_core = net, buf, by_core
        planes = [buf.at[net.src(k)] for k in range(1, net.shards)]
        self.spread = Spread(net, planes, lambda rows: buf.at[0 : net.shards - 1, rows])
        self.pass_on, self.share, self.end = self.spread.pass_on, self.spread.share, self.spread.end
        self.rows = self.spread.block(net.core) if by_core else self.spread.part(net.chip)

    def start(self):
        net = self.net
        own = self.buf.at[net.z, self.rows]
        self.far = net.arrival()
        for k in range(1, net.shards):
            net.send(own, own, self.far, net.far(k), net.i)

    def begin(self):
        self.net.wait(self.far, self.spread.all_of(self.rows))
        if self.by_core:
            self.spread.cross()
        else:
            self.spread.begin()


class Reduce:
    def __init__(
        self, net, grad, from_core, from_a, from_b, from_group, from_far, out, far_first, store
    ):
        self.net, self.grad, self.out, self.far_first = net, grad, out, far_first
        self.store = store
        self.from_core, self.from_a, self.from_b = from_core, from_a, from_b
        self.from_group, self.from_far = from_group, from_far
        self.piece = grad.shape[1] // net.group
        self.half = grad.shape[1] // 2
        self.spread = Spread(net, [out], lambda rows: out.at[rows])
        near = [self.take_a, self.take_b] if net.dims == 2 else [self.take_b]
        steps = [self.take_far] + near if far_first else near + [self.take_far]
        self.steps = [self.start, self.take_core] + steps
        self.steps[-1] = functools.partial(self.last, self.steps[-1])
        if net.dims == 2:
            self.steps.append(self.spread.pass_on)
        self.steps += [self.spread.share, self.finish]
        self.stage = 0

    def advance(self, times=1):
        for _ in range(times):
            if self.stage < len(self.steps):
                self.steps[self.stage]()
                self.stage += 1

    def last(self, step):
        step()
        self.spread.begin()

    def finish(self):
        self.spread.end()
        self.store.start()

    def first(self, chip):
        return (self.net.core * self.net.pairs + chip) * self.piece

    def rows(self, chip):
        return many(self.first(chip), self.piece, self.piece)

    def planes(self, after_far):
        if after_far:
            return [(self.net.z, 0)]
        return [(s, s) for s in range(self.net.shards)]

    def add(self, first, count, planes, parts):
        lines = 16

        def one(step, carry):
            at = pl.multiple_of(step * lines, lines)
            rows = many(first + at, lines, lines)
            for here, there in planes:
                value = self.grad[here, rows].astype(F32)
                for part in parts:
                    value = value + part[there, pl.ds(at, lines)].astype(F32)
                self.grad[here, rows] = value.astype(BF16)
            return carry

        lax.fori_loop(0, count // lines, one, 0)

    def cut(self, rows, after_far):
        if after_far:
            return self.grad.at[pl.ds(self.net.z, 1), rows]
        return self.grad.at[:, rows]

    def start(self):
        net = self.net
        away = many((1 - net.core) * self.half, self.half, self.half)
        self.to_core = net.arrival()
        net.send(self.grad.at[:, away], self.from_core, self.to_core, net.z, net.sibling())

    def take_core(self):
        net = self.net
        net.wait(self.to_core, self.from_core)
        self.add(net.core * self.half, self.half, self.planes(False), [self.from_core])
        if self.far_first:
            own = many(net.core * self.half, self.half, self.half)
            self.send_far(own)
        else:
            self.send_near(False)

    def send_near(self, after_far):
        net = self.net
        if net.dims == 2:
            self.to_a = [net.arrival(), net.arrival()]
            for k, chip in ((1, net.chip_ab), (0, net.chip_a)):
                net.send(
                    self.cut(self.rows(chip), after_far),
                    self.from_a.at[k],
                    self.to_a[k],
                    net.z,
                    net.peer(net.chip_a),
                )
        elif net.dims == 1:
            self.send_b(after_far)

    def send_b(self, after_far):
        net = self.net
        self.to_b = net.arrival()
        rows = self.rows(net.chip_b)
        net.send(
            self.cut(rows, after_far), self.from_b, self.to_b, net.z, net.peer(net.chip_b)
        )

    def take_a(self):
        net = self.net
        for k, chip in ((1, net.chip_b), (0, net.chip)):
            net.wait(self.to_a[k], self.from_a.at[k])
            self.add(self.first(chip), self.piece, self.planes(self.far_first), [self.from_a.at[k]])
            if k:
                self.send_b(self.far_first)

    def take_b(self):
        net = self.net
        if net.dims:
            net.wait(self.to_b, self.from_b)
            self.add(
                self.first(net.chip), self.piece, self.planes(self.far_first), [self.from_b]
            )
        own = self.rows(net.chip)
        step, at = 1, 0
        while step < net.groups:
            peer = net.i + net.group * step * (1 - 2 * ((net.grp // step) % 2))
            arrived = net.arrival()
            one = net.send(
                self.cut(own, self.far_first), self.from_group.at[at], arrived, net.z, peer
            )
            net.wait(arrived, self.from_group.at[at])
            net.left(one)
            self.add(
                self.first(net.chip),
                self.piece,
                self.planes(self.far_first),
                [self.from_group.at[at]],
            )
            step, at = step * 2, at + 1
        if self.far_first:
            self.out[own, :] = self.grad[net.z, own]
        else:
            self.send_far(own)

    def send_far(self, own):
        net = self.net
        self.own = own
        self.to_far = net.arrival()
        for k in range(1, net.shards):
            net.send(
                self.grad.at[pl.ds(net.far(k), 1), own],
                self.from_far.at[pl.ds(k - 1, 1)],
                self.to_far,
                net.far(k),
                net.i,
            )

    def take_far(self):
        net = self.net
        net.wait(self.to_far, self.from_far)
        parts = [self.from_far.at[pl.ds(k, 1)] for k in range(net.shards - 1)]
        if self.far_first:
            self.add(net.core * self.half, self.half, self.planes(True), parts)
            self.send_near(True)
        else:
            self.add(self.first(net.chip), self.piece, self.planes(True), parts)
            self.out[self.own, :] = self.grad[net.z, self.own]


def reduce_scratch(shards, group, rounds, rows, wide, far_first):
    pairs = group // 2
    piece, half = rows // group, rows // 2
    planes = 1 if far_first else shards
    tiny = (1, 16, 128)
    return [
        pltpu.VMEM((shards, rows, wide), BF16),
        pltpu.VMEM((shards, half, wide), BF16),
        pltpu.VMEM((2, planes, piece, wide) if pairs == 4 else tiny, BF16),
        pltpu.VMEM((planes, piece, wide), BF16),
        pltpu.VMEM((rounds, planes, piece, wide) if rounds else tiny, BF16),
        pltpu.VMEM((shards - 1, half if far_first else piece, wide), BF16),
    ]


def layer_kernel(
    shards,
    ctxs,
    group,
    chunk_far,
    len_ref,
    x_hbm,
    cot_hbm,
    picks_hbm,
    g1_hbm,
    b1_hbm,
    g2_hbm,
    b2_hbm,
    bo_hbm,
    bi_hbm,
    wq_hbm,
    wkv_hbm,
    wr_hbm,
    wo_hbm,
    wi_hbm,
    wout_hbm,
    out_hbm,
    gin_hbm,
    chunk_hbm,
    wo_hbm_out,
    q_hbm,
    kv_hbm,
    x_ref,
    cot_ref,
    picks_ref,
    g1_ref,
    b1_ref,
    g2_ref,
    b2_ref,
    bo_ref,
    bi_ref,
    wq_st,
    wkv_st,
    wr_st,
    wi_st,
    stage,
    wk,
    wq,
    wo,
    wc,
    vec_st,
    vecs,
    normed,
    normed_t,
    q_t,
    sel_a,
    heads_t,
    small,
    kvall,
    kvt,
    pads,
    hrow,
    linv,
    ebuf,
    dkv,
    from_sib,
    from_kv,
    mixed_t,
    xhat2,
    n2,
    n2_t,
    gfin_low,
    biases,
    g_t,
    sums_c,
    sums_o,
    sums_q,
    sums_k,
    out_ref,
    gin_ref,
    chunk_out,
    wo_out,
    q_out,
    kv_out,
    vec_g,
    local_sem,
    send_sem,
    recv_sem,
):
    net = Net(shards, ctxs, group, send_sem, recv_sem)
    z, c = net.z, net.i
    tokens, width = x_ref.shape
    seg = tokens // 2
    half = seg // 2
    blocks = 2 * ctxs
    ws = width // shards
    wos = wo.shape[1]
    fs = wout_hbm.shape[0]
    scale = HS ** (-0.5)
    chunks = fs // UNIT
    panels = shards * UNIT // PANEL
    per_panel = PANEL // UNIT
    lanes = TOP * half
    wide = E * HS
    gc, go, gq, gk = [one[0] for one in sums_c], sums_o[0], sums_q[0], sums_k[0]
    vec_line = E
    bias_line = vec_line + 5
    per_unit = UNIT // ws
    near_steps = ctxs // 2

    def local(src, dst, at):
        return pltpu.make_async_copy(src, dst, local_sem.at[at])

    net.greet()
    wo_st, wout_st = stage.at[0:wos], stage.at[wos : wos + fs]
    resid, acc_a, acc_b = (stage.at[k * tokens : (k + 1) * tokens] for k in range(3))
    loads = {}
    for at, (src, dst) in enumerate(
        (
            (wkv_hbm, wkv_st),
            (wr_hbm, wr_st),
            (wq_hbm, wq_st),
            (g1_hbm, g1_ref),
            (b1_hbm, b1_ref),
            (g2_hbm, g2_ref),
            (b2_hbm, b2_ref),
            (bo_hbm, bo_ref),
            (bi_hbm, bi_ref),
            (x_hbm, x_ref),
            (picks_hbm, picks_ref),
            (wo_hbm, wo_st),
            (wi_hbm, wi_st),
            (wout_hbm, wout_st),
            (cot_hbm, cot_ref),
        )
    ):
        loads[id(dst)] = local(src, dst, at)
        loads[id(dst)].start()
    loads[id(wkv_st)].wait()
    wk[z] = wkv_st[...].astype(BF16)
    vec_st[...] = jnp.zeros(vec_st.shape, F32)
    for row, ref in enumerate((g1_ref, b1_ref, g2_ref, b2_ref, bo_ref)):
        loads[id(ref)].wait()
        vec_st[row : row + 1, 0:ws] = ref[...]
    loads[id(bi_ref)].wait()
    for k in range(chunks):
        vec_st[5 + k : 6 + k, :] = bi_ref[:, k * UNIT : (k + 1) * UNIT]
    own_vec = vecs.at[z]
    own_vec[...] = vec_st[...].astype(BF16)
    net.greeted()
    gather_k, gather_q, gather_o = Gather(net, wk, True), Gather(net, wq), Gather(net, wo)
    gather_c = [Gather(net, wc.at[k]) for k in range(chunks)]
    gather_k.start()
    vec_slot = net.arrival()
    for k in range(1, shards):
        net.send(own_vec, own_vec, vec_slot, net.far(k), net.i)
    loads[id(wq_st)].wait()
    loads[id(wr_st)].wait()
    wq[z, :, 0:wide] = wq_st[...].astype(BF16)
    padded = jnp.concatenate([wr_st[...], jnp.zeros((128 - E, ws), F32)], axis=0)
    wq[z, :, wide:] = padded.T.astype(BF16)
    gather_q.start()

    loads[id(x_ref)].wait()
    x = x_ref[...].astype(F32)
    mean1 = jnp.mean(x, axis=1, keepdims=True)
    cen = x - mean1
    small[0, :, 0:1] = lax.rsqrt(jnp.mean(cen * cen, axis=1, keepdims=True) + NORM_EPS)
    small[0, :, 2:3] = mean1

    def first_hat():
        return (x_ref[...].astype(F32) - small[0, :, 2:3]) * small[0, :, 0:1]

    for ref in (wo_st, wi_st, wout_st):
        loads[id(ref)].wait()
    wo[z] = wo_st[...].astype(BF16)
    for k in range(chunks):
        wc[k, z, 0:UNIT] = wout_st[k * UNIT : (k + 1) * UNIT].astype(BF16)
        for s in range(shards):
            first = UNIT + (s // per_panel) * ws
            at = (s % per_panel) * UNIT
            wc[k, z, first : first + ws, at : at + UNIT] = wi_st[
                :, s * fs + k * UNIT : s * fs + (k + 1) * UNIT
            ].astype(BF16)
    gather_k.begin()
    net.wait(vec_slot, vecs.at[0 : shards - 1])

    vec_all = [vecs[s].astype(F32) for s in range(shards)]

    def whole(row):
        return jnp.concatenate([one[row : row + 1, 0:ws] for one in vec_all], axis=1)

    gain1, bias1, gain2, bias2, bias_out = (whole(row) for row in range(5))
    for k in range(chunks):
        for p in range(panels):
            biases[k * panels + p : k * panels + p + 1, :] = jnp.concatenate(
                [one[5 + k : 6 + k] for one in vec_all[p * per_panel : (p + 1) * per_panel]],
                axis=1,
            )
    norm_value = first_hat() * gain1 + bias1
    normed[...] = norm_value.astype(BF16)
    normed_t[...] = norm_value.T.astype(BF16)
    gather_k.end()

    kv_own = dot(normed[...], wk[...].reshape(width, 2 * HS)).astype(BF16)

    def at_block(ref, block):
        return ref.at[block // 2, :, block % 2]

    def my_block(h):
        return c if h == 0 else blocks - 1 - c

    def core_blocks(ref, core):
        return ref.at[0:near_steps, :, core], ref.at[near_steps:ctxs, :, 1 - core]

    for h in range(2):
        block = my_block(h)
        for s in range(2):
            first = s * seg + h * half
            kvall[block // 2, s, block % 2] = kv_own[first : first + half]
    kv_slot, kv_cross = net.arrival(), net.arrival()
    kv_sent = []
    for step in range(1, near_steps):
        for block in (c, blocks - 1 - c):
            ref = at_block(kvall, block)
            kv_sent.append(net.send(ref, ref, kv_slot, z, (c + 2 * step) % ctxs))
    gather_o.start()
    gather_q.begin()
    gather_c[0].start()
    net.wait(kv_slot, kvall.at[0 : near_steps - 1])
    for part in core_blocks(kvall, net.core):
        kv_sent.append(net.send(part, part, kv_cross, z, net.sibling()))
    gather_q.pass_on()
    net.wait(kv_cross, kvall.at[0:near_steps])

    def turn(step, carry):
        for s in range(2):
            keys = kvall[step, s].reshape(2 * half, 2 * HS)
            kvt[step, s] = keys.astype(F32).T.astype(BF16)
            dkv[step, s] = jnp.zeros((2 * half, 2 * HS), F32)
        return carry

    lax.fori_loop(0, ctxs, turn, 0)

    def serve(*calls):
        for k, call in calls:
            if k < chunks:
                getattr(gather_c[k], call)()

    gather_o.begin()
    serve((1, "start"))
    gather_q.share()
    serve((0, "begin"), (2, "start"))
    gather_q.end()

    logits_t = dot(normed[...], wq[:, :, wide:].reshape(width, 128)).T
    loads[id(picks_ref)].wait()
    picks = jnp.concatenate([picks_ref[0], picks_ref[1]], axis=1).astype(F32)
    picked = jnp.zeros((TOP, tokens), F32)
    for e in range(E):
        picked = jnp.where(picks == float(e), logits_t[e : e + 1, :], picked)
    top = jnp.max(picked, axis=0, keepdims=True)
    gexp = jnp.exp(picked - top)
    small[1, 0:TOP, 0:tokens] = gexp / jnp.sum(gexp, axis=0, keepdims=True)
    small[1, TOP : 2 * TOP, 0:tokens] = picks

    def query_tile(n, carry):
        cols = many(n * 256, 256, 256)
        value = dot(normed[...], wq[:, :, cols].reshape(width, 256))
        value = value.astype(BF16).astype(F32).T
        for k in range(4):
            q_t[n * 4 + k] = value[k * HS : (k + 1) * HS]
        return carry

    lax.fori_loop(0, wide // 256, query_tile, 0)

    def choose(src, store):
        def one(j, carry):
            pick = small[1, pl.ds(TOP + j, 1), 0:tokens]
            value = jnp.zeros((HS, tokens), F32)
            for e in range(E):
                value = jnp.where(pick == float(e), src[e], value)
            store(j, value)
            return carry

        lax.fori_loop(0, TOP, one, 0)

    def spread_back(src, store):
        def one(e, carry):
            value = jnp.zeros((HS, tokens), F32)
            for j in range(TOP):
                pick = small[1, TOP + j : TOP + j + 1, 0:tokens]
                value = jnp.where(pick == e.astype(F32), src[j], value)
            store(e, value)
            return carry

        lax.fori_loop(0, E, one, 0)

    low_lane = lax.broadcasted_iota(jnp.int32, (HS, 2 * half), 1) < half

    def swap(one, two):
        return (
            jnp.where(low_lane, one, pltpu.roll(two, half, 1)),
            jnp.where(low_lane, pltpu.roll(one, half, 1), two),
        )

    def store_query(j, value):
        sel_a[j] = value * scale

    gather_o.pass_on()
    serve((3, "start"))
    choose(q_t, store_query)
    for s in range(2):
        for pair in range(TOP // 2):
            halves = swap(
                sel_a[2 * pair, :, s * seg : (s + 1) * seg],
                sel_a[2 * pair + 1, :, s * seg : (s + 1) * seg],
            )
            for h in range(2):
                pads[2 * s + h, 0:HS, pair * 128 : (pair + 1) * 128] = halves[h].astype(BF16)
    for sh in range(4):
        pads[sh, HS:, 0:lanes] = jnp.zeros((HS, lanes), BF16)
        pads[sh, 0:HS, lanes:] = jnp.zeros((HS, lanes), BF16)

    serve((1, "begin"))
    serve((0, "pass_on"))

    offset = lax.broadcasted_iota(jnp.int32, (1, lanes), 1) % half
    key_row = lax.broadcasted_iota(jnp.int32, (2 * half, lanes), 0)

    def place(h):
        if h == 1:
            return (blocks - c + 1) // 2, 0
        return (c + 2) // 2, (blocks - c + 1) // 2

    def fold(value, op):
        parts = [value[8 * k : 8 * k + 8] for k in range(value.shape[0] // 8)]
        while len(parts) > 1:
            parts = [op(parts[k], parts[k + 1]) for k in range(0, len(parts), 2)]
        return parts[0]

    def keys_of(step, s):
        return kvall[step, s].reshape(2 * half, 2 * HS)

    def attend(h):
        count, base = place(h)
        limits = [
            jnp.minimum(my_block(h) * half + offset, len_ref[s] - 1) for s in range(2)
        ]

        def masked(step, s):
            scores = dot(keys_of(step, s), pads[2 * s + h, :, 0:lanes])
            return jnp.where(key_row <= limits[s] - step * 2 * half, scores, NEG_LARGE)

        def score_step(step, tops):
            return tuple(
                jnp.maximum(tops[s], fold(masked(step, s), jnp.maximum)) for s in range(2)
            )

        start = jnp.full((8, lanes), NEG_LARGE, F32)
        tops = lax.fori_loop(0, count, score_step, (start, start))
        tops = [jnp.max(top, axis=0, keepdims=True) for top in tops]
        if h == 1:
            gather_o.share()
            serve((2, "begin"))
        for s in range(2):
            hrow[2 * s + h] = jnp.zeros((HS, lanes), F32)

        def value_step(step, totals):
            result = []
            for s in range(2):
                expd = jnp.exp(masked(step, s) - tops[s])
                low = expd.astype(BF16)
                ebuf[s, base + step] = low
                hrow[2 * s + h] += dot(kvt[step, s, HS:], low)
                result.append(totals[s] + fold(expd, jnp.add))
            return tuple(result)

        start = jnp.zeros((8, lanes), F32)
        totals = lax.fori_loop(0, count, value_step, (start, start))
        for s in range(2):
            inverse = 1.0 / jnp.sum(totals[s], axis=0, keepdims=True)
            linv[2 * s + h] = jnp.broadcast_to(inverse, (8, lanes))
            hrow[2 * s + h] = hrow[2 * s + h] * inverse

    attend(1)
    serve((0, "share"), (1, "pass_on"), (3, "begin"))
    attend(0)
    serve((2, "pass_on"), (1, "share"))

    for s in range(2):
        for pair in range(TOP // 2):
            both = swap(
                hrow[2 * s, :, pair * 128 : (pair + 1) * 128],
                hrow[2 * s + 1, :, pair * 128 : (pair + 1) * 128],
            )
            for k in range(2):
                heads_t[2 * pair + k, :, s * seg : (s + 1) * seg] = both[k]
    for j in range(TOP):
        sel_a[j] = heads_t[j] * small[1, j : j + 1, 0:tokens]

    def store_mixed(e, value):
        mixed_t[e] = value.astype(BF16)

    spread_back(sel_a, store_mixed)
    gather_o.end()
    experts = E // shards
    acc_a[...] = x_ref[...].astype(F32)

    def project(s, carry):
        part = mixed_t[pl.ds(s * experts, experts)].reshape(wos, tokens)
        acc_a[...] += dot(part.astype(F32).T.astype(BF16), wo[s])
        return carry

    lax.fori_loop(0, shards, project, 0)
    residual = acc_a[...]
    resid[...] = residual
    cen = residual - jnp.mean(residual, axis=1, keepdims=True)
    rstd2 = lax.rsqrt(jnp.mean(cen * cen, axis=1, keepdims=True) + NORM_EPS)
    small[0, :, 1:2] = rstd2
    cen = cen * rstd2
    xhat2[...] = cen
    cen = cen * gain2 + bias2
    n2[...] = cen.astype(BF16)
    n2_t[...] = cen.T.astype(BF16)

    row = lax.broadcasted_iota(jnp.int32, (tokens, 1), 0)
    inner_row = row % seg
    pos = jnp.where(
        inner_row < half, c * half + inner_row, blocks * half - (c + 2) * half + inner_row
    )
    valid = (pos < jnp.where(row < seg, len_ref[0], len_ref[1])).astype(F32)
    loads[id(cot_ref)].wait()
    gfin_low[...] = (cot_ref[...].astype(F32) * valid).astype(BF16)
    acc_a[...] = jnp.zeros((tokens, width), F32)
    acc_b[...] = jnp.zeros((tokens, width), F32)
    vec_g[...] = jnp.zeros(vec_g.shape, F32)

    def feed(k, p):
        rows_in = slice(UNIT + p * ws, UNIT + (p + 1) * ws)
        planes = slice(p * per_panel, (p + 1) * per_panel)
        w_in = wc[k, :, rows_in].reshape(width, PANEL)
        w_out = wc[k, planes, 0:UNIT].reshape(PANEL, width)
        line = k * panels + p
        hidden = dot(n2[...], w_in) + biases[line : line + 1, :]
        square = hidden * hidden
        tanh = jnp.tanh(GELU_C * hidden * (1.0 + GELU_A * square))
        act = (0.5 * hidden * (1.0 + tanh)).astype(BF16)
        slope = 0.5 * (1.0 + tanh) + 0.5 * GELU_C * hidden * (1.0 - tanh * tanh) * (
            1.0 + 3.0 * GELU_A * square
        )
        gfin = gfin_low[...]
        acc_a[...] += dot(act, w_out)
        grad_hidden = (slope * dot_t(gfin, w_out)).astype(BF16)
        total = jnp.sum(grad_hidden.astype(F32), axis=0, keepdims=True)
        for a in range(per_panel):
            for q in range(per_unit):
                at = bias_line + k * per_unit + q
                first = (p * per_panel + a) * ws
                vec_g[at : at + 1, first : first + ws] = total[
                    :, a * UNIT + q * ws : a * UNIT + (q + 1) * ws
                ]
        grad_outer = dot(act.astype(F32).T.astype(BF16), gfin).astype(BF16)
        gc[k][planes, 0:UNIT] = grad_outer.reshape(per_panel, UNIT, width)
        grad_inner = dot(n2_t[...], grad_hidden).astype(BF16)
        gc[k][:, rows_in] = grad_inner.reshape(shards, ws, PANEL)
        acc_b[...] += dot_t(grad_hidden, w_in)

    outs = [local(out_ref, out_hbm, 15), local(gin_ref, gin_hbm, 16)]

    def reduction(refs, out, hbm, at, far_first):
        store = local(out, hbm, at)
        outs.append(store)
        return Reduce(net, *refs, out, far_first, store)

    reduce_c = [
        reduction(sums_c[k], chunk_out.at[k], chunk_hbm.at[k], 20 + k, chunk_far[k])
        for k in range(chunks)
    ]
    for k in range(chunks):
        if k == 0:
            serve((3, "pass_on"), (2, "share"))
        if k == 1:
            serve((3, "share"))
        gather_c[k].end()
        for p in range(panels):
            feed(k, p)
        reduce_c[k].advance()
        if k > 1:
            reduce_c[k - 2].advance()
    out_ref[...] = (valid * (resid[...] + acc_a[...] + bias_out)).astype(BF16)
    outs[0].start()
    gfin = cot_ref[...].astype(F32) * valid
    vec_g[vec_line + 4 : vec_line + 5, :] = jnp.sum(gfin, axis=0, keepdims=True)
    grad_n2 = acc_b[...]
    vec_g[vec_line + 3 : vec_line + 4, :] = jnp.sum(grad_n2, axis=0, keepdims=True)
    vec_g[vec_line + 2 : vec_line + 3, :] = jnp.sum(grad_n2 * xhat2[...], axis=0, keepdims=True)
    grad_hat = grad_n2 * gain2
    grad_hat = grad_hat - jnp.mean(grad_hat, axis=1, keepdims=True)
    grad_hat = grad_hat - xhat2[...] * jnp.mean(grad_hat * xhat2[...], axis=1, keepdims=True)
    grad_residual = gfin + grad_hat * small[0, :, 1:2]
    resid[...] = grad_residual
    n2[...] = grad_residual.astype(BF16)
    if chunks > 1:
        reduce_c[chunks - 2].advance()

    def branch(s, carry):
        part = mixed_t[pl.ds(s * experts, experts)].reshape(wos, tokens)
        go[s] = dot(part, n2[...]).astype(BF16)
        grad = dot_t(wo[s], n2[...])
        q_t[pl.ds(s * experts, experts)] = grad.reshape(experts, HS, tokens)
        return carry

    lax.fori_loop(0, shards, branch, 0)
    reduce_o = reduction(sums_o, wo_out, wo_hbm_out, 17, False)
    reduce_o.advance()
    reduce_c[chunks - 1].advance()

    def store_head_grad(j, value):
        sel_a[j] = value * small[1, pl.ds(j, 1), 0:tokens]
        small[1, pl.ds(2 * TOP + j, 1), 0:tokens] = jnp.sum(
            value * heads_t[j], axis=0, keepdims=True
        )

    choose(q_t, store_head_grad)
    gates = small[1, 0:TOP, 0:tokens]
    grad_gates = small[1, 2 * TOP : 3 * TOP, 0:tokens]
    grad_picked = gates * (grad_gates - jnp.sum(gates * grad_gates, axis=0, keepdims=True))
    picks = small[1, TOP : 2 * TOP, 0:tokens]
    g_t[wide : wide + 128, :] = jnp.zeros((128, tokens), BF16)
    grad_logits = [
        jnp.sum(jnp.where(picks == float(e), grad_picked, 0.0), axis=0, keepdims=True)
        for e in range(E)
    ]
    grad_logits += [jnp.zeros((1, tokens), F32)] * (32 - E)
    g_t[wide : wide + 32, :] = jnp.concatenate(grad_logits, axis=0).astype(BF16)
    for s in range(2):
        for pair in range(TOP // 2):
            halves = swap(
                sel_a[2 * pair, :, s * seg : (s + 1) * seg],
                sel_a[2 * pair + 1, :, s * seg : (s + 1) * seg],
            )
            at = pair * 128
            for h in range(2):
                sh = 2 * s + h
                grad = (halves[h] * linv[sh, 0:1, at : at + 128]).astype(BF16)
                pads[sh, HS:, lanes + at : lanes + at + 128] = grad
                linv[sh, 1:2, at : at + 128] = jnp.sum(
                    grad.astype(F32) * hrow[sh, :, at : at + 128], axis=0, keepdims=True
                )
    reduce_o.advance()

    def attend_back(h):
        count, base = place(h)
        deltas = [linv[2 * s + h, 1:2, :] for s in range(2)]
        for s in range(2):
            hrow[2 * s + h] = jnp.zeros((HS, lanes), F32)

        def grad_step(step, carry):
            for s in range(2):
                sh = 2 * s + h
                expd = ebuf[s, base + step]
                grad_prob = dot(keys_of(step, s), pads[sh, :, lanes:])
                grad_score = (expd.astype(F32) * (grad_prob - deltas[s])).astype(BF16)
                dkv[step, s] += dot_t(jnp.concatenate([grad_score, expd], axis=1), pads[sh])
                hrow[sh] += dot(kvt[step, s, 0:HS], grad_score)
            return carry

        lax.fori_loop(0, count, grad_step, 0)

    attend_back(1)
    attend_back(0)

    for one in kv_sent:
        net.left(one)

    def lower(step, carry):
        kvall[step] = dkv[step].astype(BF16).reshape(2, 2, half, 2 * HS)
        return carry

    lax.fori_loop(0, ctxs, lower, 0)
    dkv_cross, dkv_near = net.arrival(), net.arrival()
    for k, part in enumerate(core_blocks(kvall, 1 - net.core)):
        net.send(part, from_sib.at[k], dkv_cross, z, net.sibling())
    for s in range(2):
        for pair in range(TOP // 2):
            both = swap(
                hrow[2 * s, :, pair * 128 : (pair + 1) * 128],
                hrow[2 * s + 1, :, pair * 128 : (pair + 1) * 128],
            )
            for k in range(2):
                q_t[2 * pair + k, :, s * seg : (s + 1) * seg] = both[k] * scale

    def store_grad_query(e, value):
        g_t[many(e * HS, HS, HS), :] = value.astype(BF16)

    spread_back(q_t, store_grad_query)

    net.wait(dkv_cross, from_sib)

    def add_sibling(step, carry):
        for k, sub in enumerate((net.core, 1 - net.core)):
            at = step + k * near_steps
            rows = many(sub * half, half, half)
            for s in range(2):
                value = dkv[at, s, rows] + from_sib[k, step, s].astype(F32)
                dkv[at, s, rows] = value
                kvall[at, s, sub] = value.astype(BF16)
        return carry

    lax.fori_loop(0, near_steps, add_sibling, 0)
    for step in range(1, near_steps):
        peer = (c + 2 * step) % ctxs
        for h, block in enumerate((peer, blocks - 1 - peer)):
            net.send(at_block(kvall, block), from_kv.at[step - 1, h], dkv_near, z, peer)

    def query_grad(n, carry):
        at = many(n * 256, 256, 256)
        grad = dot_t(normed_t[...], g_t[at, :]).astype(BF16)
        gq[:, :, at] = grad.reshape(shards, ws, 256)
        return carry

    lax.fori_loop(0, wide // 256, query_grad, 0)
    reduce_q = reduction(sums_q, q_out, q_hbm, 18, False)
    reduce_q.advance()

    heads_t[...] = jnp.zeros(heads_t.shape, F32)

    def norm_grad(n, carry):
        at = many(n * 256, 256, 256)
        part = dot(wq[:, :, at].reshape(width, 256), g_t[at, :])
        heads_t[...] += part.reshape(heads_t.shape)
        return carry

    lax.fori_loop(0, wide // 256, norm_grad, 0)
    part = dot(wq[:, :, wide:].reshape(width, 128), g_t[wide : wide + 128, :])
    heads_t[...] += part.reshape(heads_t.shape)
    reduce_q.advance()
    net.wait(dkv_near, from_kv)
    for h in range(2):
        block = my_block(h)
        for s in range(2):
            value = dkv[block // 2, s, many((block % 2) * half, half, half)]
            for step in range(1, near_steps):
                value = value + from_kv[step - 1, h, s].astype(F32)
            first = s * seg + h * half
            acc_a[first : first + half, 0:128] = value
    grad_kv = acc_a[:, 0:128].T.astype(BF16)
    part = heads_t[...].reshape(width, tokens) + dot(wk[...].reshape(width, 2 * HS), grad_kv)
    grad_normed = part.T
    hat = first_hat()
    vec_g[vec_line : vec_line + 1, :] = jnp.sum(grad_normed * hat, axis=0, keepdims=True)
    vec_g[vec_line + 1 : vec_line + 2, :] = jnp.sum(grad_normed, axis=0, keepdims=True)
    value = dot_t(normed_t[...], grad_kv)
    gk[:, :, 0 : 2 * HS] = value.astype(BF16).reshape(shards, ws, 2 * HS)
    value = dot_t(normed_t[...], g_t[wide:, :]) + vec_g[...].T
    gk[:, :, 2 * HS :] = value.astype(BF16).reshape(shards, ws, 128)
    reduce_k = reduction(sums_k, kv_out, kv_hbm, 19, False)
    reduce_k.advance()
    grad_hat = grad_normed * gain1
    grad_hat = grad_hat - jnp.mean(grad_hat, axis=1, keepdims=True)
    grad_hat = grad_hat - hat * jnp.mean(grad_hat * hat, axis=1, keepdims=True)
    gin_ref[...] = resid[...] + grad_hat * small[0, :, 0:1]
    outs[1].start()

    everything = [*reduce_c, reduce_o, reduce_q, reduce_k]
    while any(one.stage < len(one.steps) for one in everything):
        for one in everything:
            one.advance()
    net.finish()
    for one in outs:
        one.wait()


def unpack_kernel(shards, *refs):
    ins, outs = refs[0:6], refs[6:20]
    in_st, out_st, sem = refs[20:26], refs[26:40], refs[40]
    loads = [pltpu.make_async_copy(a, b, sem.at[k]) for k, (a, b) in enumerate(zip(ins, in_st))]
    stores = [
        pltpu.make_async_copy(in_st[k] if k < 2 else out_st[k], outs[k], sem.at[6 + k])
        for k in range(14)
    ]
    for k in (2, 3, 4, 5, 1, 0):
        loads[k].start()
    chunk_in, wo_in, q_in, kv_in = in_st[2:]
    g1_ref, b1_ref, kv_ref, q_ref, r_ref, wo_ref, g2_ref, b2_ref = out_st[2:10]
    wi_ref, bi_ref, wout_ref, bo_ref = out_st[10:]
    ws, fs = q_ref.shape[0], wout_ref.shape[0]
    per_panel = PANEL // UNIT
    loads[2].wait()
    for k in range(chunk_in.shape[0]):
        wout_ref[k * UNIT : (k + 1) * UNIT, :] = chunk_in[k, 0:UNIT].astype(F32)
    stores[12].start()
    for k in range(chunk_in.shape[0]):
        for s in range(shards):
            first = UNIT + (s // per_panel) * ws
            at = (s % per_panel) * UNIT
            wi_ref[:, s * fs + k * UNIT : s * fs + (k + 1) * UNIT] = chunk_in[
                k, first : first + ws, at : at + UNIT
            ].astype(F32)
    stores[10].start()
    loads[3].wait()
    wo_ref[...] = wo_in[...].astype(F32)
    stores[7].start()
    loads[4].wait()
    q_ref[...] = q_in[...].astype(F32)
    stores[5].start()
    loads[5].wait()
    kv_ref[...] = kv_in[:, 0 : 2 * HS].astype(F32)
    stores[4].start()
    turned = kv_in[:, 2 * HS :].astype(F32).T
    r_ref[...] = turned[0:E]
    stores[6].start()
    for row, at, ref in (
        (0, 2, g1_ref),
        (1, 3, b1_ref),
        (2, 8, g2_ref),
        (3, 9, b2_ref),
        (4, 13, bo_ref),
    ):
        ref[...] = turned[E + row : E + row + 1]
        stores[at].start()
    for line in range(fs // ws):
        bi_ref[:, line * ws : (line + 1) * ws] = turned[E + 5 + line : E + 6 + line]
    stores[11].start()
    loads[1].wait()
    stores[1].start()
    loads[0].wait()
    stores[0].start()
    for one in stores:
        one.wait()


def on_device(
    shards,
    ctxs,
    tokens,
    lengths,
    expert_picks,
    first_gain,
    first_bias,
    kv_weight,
    query_weight,
    router_weight,
    output_weight,
    second_gain,
    second_bias,
    inner_weight,
    inner_bias,
    outer_weight,
    outer_bias,
    cotangent,
):
    slots, seg, width = tokens.shape
    count = slots * seg
    half = seg // 2
    lanes = TOP * half
    ws = width // shards
    wos = output_weight.shape[0]
    fs = outer_weight.shape[0]
    group = min(ctxs, ws // 16, 8)
    pairs, groups = group // 2, ctxs // group
    rounds = groups.bit_length() - 1
    chunks = fs // UNIT
    panels = shards * UNIT // PANEL
    chunk_rows = UNIT + panels * ws
    wide = E * HS
    chunk_far = [k < chunks // 2 for k in range(chunks)]
    shapes_mid = (
        jax.ShapeDtypeStruct((count, width), BF16),
        jax.ShapeDtypeStruct((count, width), F32),
        jax.ShapeDtypeStruct((chunks, chunk_rows, PANEL), BF16),
        jax.ShapeDtypeStruct((wos, width), BF16),
        jax.ShapeDtypeStruct((ws, wide), BF16),
        jax.ShapeDtypeStruct((ws, 256), BF16),
    )

    smem = pl.BlockSpec(memory_space=pltpu.SMEM)
    anywhere = pl.BlockSpec(memory_space=pl.ANY)
    arrivals = 2 + (2 + chunks) * 5 + 1 + 4 + (3 + chunks) * (9 + rounds)
    scratch = [
        pltpu.VMEM((count, width), BF16),
        pltpu.VMEM((count, width), BF16),
        pltpu.VMEM((slots, TOP, seg), jnp.int32),
        *[pltpu.VMEM((1, ws), F32)] * 5,
        pltpu.VMEM((1, fs), F32),
        pltpu.VMEM(query_weight.shape, F32),
        pltpu.VMEM(kv_weight.shape, F32),
        pltpu.VMEM((E, ws), F32),
        pltpu.VMEM(inner_weight.shape, F32),
        pltpu.VMEM((max(wos + fs, 3 * count), width), F32),
        pltpu.VMEM((shards, ws, 2 * HS), BF16),
        pltpu.VMEM((shards, ws, wide + 128), BF16),
        pltpu.VMEM((shards, wos, width), BF16),
        pltpu.VMEM((chunks, shards, chunk_rows, PANEL), BF16),
        pltpu.VMEM((16, UNIT), F32),
        pltpu.VMEM((shards, 16, UNIT), BF16),
        pltpu.VMEM((count, width), BF16),
        pltpu.VMEM((width, count), BF16),
        pltpu.VMEM((E, HS, count), F32),
        pltpu.VMEM((TOP, HS, count), F32),
        pltpu.VMEM((TOP, HS, count), F32),
        pltpu.VMEM((2, count, count), F32),
        pltpu.VMEM((ctxs, slots, 2, half, 2 * HS), BF16),
        pltpu.VMEM((ctxs, slots, 2 * HS, 2 * half), BF16),
        pltpu.VMEM((4, 2 * HS, 2 * lanes), BF16),
        pltpu.VMEM((4, HS, lanes), F32),
        pltpu.VMEM((4, 8, lanes), F32),
        pltpu.VMEM((slots, ctxs + 1, 2 * half, lanes), BF16),
        pltpu.VMEM((ctxs, slots, 2 * half, 2 * HS), F32),
        pltpu.VMEM((2, ctxs // 2, slots, half, 2 * HS), BF16),
        pltpu.VMEM((ctxs // 2 - 1, 2, slots, half, 2 * HS), BF16),
        pltpu.VMEM((E, HS, count), BF16),
        pltpu.VMEM((count, width), F32),
        pltpu.VMEM((count, width), BF16),
        pltpu.VMEM((width, count), BF16),
        pltpu.VMEM((count, width), BF16),
        pltpu.VMEM((8, PANEL), F32),
        pltpu.VMEM((wide + 128, count), BF16),
        [
            reduce_scratch(shards, group, rounds, chunk_rows, PANEL, chunk_far[k])
            for k in range(chunks)
        ],
        reduce_scratch(shards, group, rounds, wos, width, False),
        reduce_scratch(shards, group, rounds, ws, wide, False),
        reduce_scratch(shards, group, rounds, ws, 256, False),
        *[pltpu.VMEM(one.shape, one.dtype) for one in shapes_mid],
        pltpu.VMEM((128, width), F32),
        pltpu.SemaphoreType.DMA((20 + chunks,)),
        pltpu.SemaphoreType.DMA((RING,)),
        pltpu.SemaphoreType.DMA((arrivals,)),
    ]
    results = pl.pallas_call(
        functools.partial(layer_kernel, shards, ctxs, group, chunk_far),
        out_shape=shapes_mid,
        in_specs=[smem] + [anywhere] * 15,
        out_specs=tuple([anywhere] * 6),
        scratch_shapes=scratch,
        compiler_params=pltpu.CompilerParams(
            collective_id=0, has_side_effects=True, vmem_limit_bytes=63 * 1024 * 1024
        ),
        name="layer",
    )(
        lengths,
        tokens.reshape(count, width),
        cotangent.reshape(count, width),
        jnp.swapaxes(expert_picks, 1, 2),
        first_gain.reshape(1, ws),
        first_bias.reshape(1, ws),
        second_gain.reshape(1, ws),
        second_bias.reshape(1, ws),
        outer_bias.reshape(1, ws),
        inner_bias.reshape(1, fs),
        query_weight,
        kv_weight,
        router_weight.T,
        output_weight,
        inner_weight,
        outer_weight,
    )
    vec_shape = jax.ShapeDtypeStruct((1, ws), F32)
    shapes_out = (
        jax.ShapeDtypeStruct((count, width), BF16),
        jax.ShapeDtypeStruct((count, width), F32),
        vec_shape,
        vec_shape,
        jax.ShapeDtypeStruct(kv_weight.shape, F32),
        jax.ShapeDtypeStruct(query_weight.shape, F32),
        jax.ShapeDtypeStruct((E, ws), F32),
        jax.ShapeDtypeStruct(output_weight.shape, F32),
        vec_shape,
        vec_shape,
        jax.ShapeDtypeStruct(inner_weight.shape, F32),
        jax.ShapeDtypeStruct((1, fs), F32),
        jax.ShapeDtypeStruct(outer_weight.shape, F32),
        vec_shape,
    )
    final = pl.pallas_call(
        functools.partial(unpack_kernel, shards),
        out_shape=shapes_out,
        in_specs=[anywhere] * 6,
        out_specs=tuple([anywhere] * 14),
        scratch_shapes=[pltpu.VMEM(one.shape, one.dtype) for one in (*shapes_mid, *shapes_out)]
        + [pltpu.SemaphoreType.DMA((20,))],
        name="unpack",
    )(*results)
    final = list(final)
    final[6] = final[6].T
    shapes = (
        tokens.shape,
        tokens.shape,
        first_gain.shape,
        first_bias.shape,
        kv_weight.shape,
        query_weight.shape,
        router_weight.shape,
        output_weight.shape,
        second_gain.shape,
        second_bias.shape,
        inner_weight.shape,
        inner_bias.shape,
        outer_weight.shape,
        outer_bias.shape,
    )
    return tuple(value.reshape(shape) for value, shape in zip(final, shapes))


def solution(mesh):
    rows = P("shard", "ctx", None)
    vec, mat = P("shard"), P("shard", None)
    return jax.shard_map(
        functools.partial(on_device, mesh.shape["shard"], mesh.shape["ctx"]),
        mesh=mesh,
        in_specs=(
            rows,
            vec,
            rows,
            vec,
            vec,
            mat,
            mat,
            mat,
            mat,
            vec,
            vec,
            mat,
            vec,
            mat,
            vec,
            rows,
        ),
        out_specs=(
            rows,
            rows,
            vec,
            vec,
            mat,
            mat,
            mat,
            mat,
            vec,
            vec,
            mat,
            vec,
            mat,
            vec,
        ),
        check_vma=False,
    )
```

```python
import functools

import jax
import jax.numpy as jnp
from jax import lax
from jax.experimental import pallas as pl
from jax.experimental.pallas import tpu as pltpu
from jax.sharding import PartitionSpec as P

HS = 64
E = 24
TOP = 8
NORM_EPS = 1e-05
NEG_LARGE = -1e30
BF16 = jnp.bfloat16
F32 = jnp.float32
PANEL = 512
UNIT = 128
GELU_C = 0.7978845608028654
GELU_A = 0.044715
MESH = pl.DeviceIdType.MESH
RING = 40


def dot(left, right):
    return jnp.dot(left, right, preferred_element_type=F32)


def dot_t(left, right):
    return lax.dot_general(left, right, (((1,), (1,)), ((), ())), preferred_element_type=F32)


def many(first, size, step):
    return pl.ds(pl.multiple_of(first, step), size)


class Net:
    def __init__(self, shards, ctxs, group, send_sem, recv_sem):
        self.shards, self.ctxs, self.group = shards, ctxs, group
        self.pairs = group // 2
        self.groups = ctxs // group
        self.dims = self.pairs.bit_length() - 1
        self.z = lax.axis_index("shard")
        self.i = lax.axis_index("ctx")
        self.core = self.i % 2
        self.chip = (self.i % group) // 2
        self.grp = self.i // group
        self.send_sem, self.recv_sem = send_sem, recv_sem
        self.arrivals = 0
        self.starts = 0
        self.ring = [[] for _ in range(RING)]
        flip_low = self.chip + 1 - 2 * (self.chip % 2)
        if self.dims == 2:
            flip_high = self.chip + 2 - 4 * (self.chip // 2)
            self.chip_a = self.core * flip_high + (1 - self.core) * flip_low
            self.chip_b = self.core * flip_low + (1 - self.core) * flip_high
            self.chip_ab = self.pairs - 1 - self.chip
        elif self.dims == 1:
            self.chip_b = flip_low

    def far(self, step):
        return (self.z + step) % self.shards

    def src(self, step):
        return (self.z + self.shards - step) % self.shards

    def peer(self, chip):
        return self.grp * self.group + chip * 2 + self.core

    def sibling(self):
        return self.i + 1 - 2 * self.core

    def copy(self, src, dst, sent, arrived, z, i):
        return pltpu.make_async_remote_copy(
            src_ref=src,
            dst_ref=dst,
            send_sem=self.send_sem.at[sent],
            recv_sem=self.recv_sem.at[arrived],
            device_id={"shard": z, "ctx": i},
            device_id_type=MESH,
        )

    def arrival(self):
        self.arrivals += 1
        return self.arrivals - 1

    def send(self, src, dst, arrived, z, i):
        slot = self.starts % RING
        self.starts += 1
        if self.ring[slot]:
            self.left(self.ring[slot])
        one = self.ring[slot] = [self.copy(src, dst, slot, arrived, z, i)]
        one[0].start()
        return one

    def left(self, one):
        if one:
            one.pop().wait_send()

    def wait(self, arrived, dst):
        self.copy(dst, dst, 0, arrived, self.z, self.i).wait_recv()

    def finish(self):
        for one in self.ring:
            self.left(one)

    def greet(self):
        barrier = pltpu.get_barrier_semaphore()
        for step in range(1, self.ctxs):
            pl.semaphore_signal(
                barrier,
                inc=1,
                device_id={"shard": self.z, "ctx": (self.i + step) % self.ctxs},
                device_id_type=MESH,
            )
        for step in range(1, self.shards):
            pl.semaphore_signal(
                barrier,
                inc=1,
                device_id={"shard": self.far(step), "ctx": self.i},
                device_id_type=MESH,
            )

    def greeted(self):
        pl.semaphore_wait(pltpu.get_barrier_semaphore(), self.ctxs + self.shards - 2)


class Spread:
    def __init__(self, net, refs, all_of):
        self.net, self.refs, self.all_of = net, refs, all_of
        self.piece = refs[0].shape[0] // net.group
        self.half = refs[0].shape[0] // 2

    def part(self, chip):
        return many((self.net.core * self.net.pairs + chip) * self.piece, self.piece, self.piece)

    def block(self, core):
        return many(core * self.half, self.half, self.half)

    def give(self, rows, peer):
        arrived = self.net.arrival()
        for ref in self.refs:
            self.net.send(ref.at[rows], ref.at[rows], arrived, self.net.z, peer)
        return arrived

    def begin(self):
        net = self.net
        own = self.part(net.chip)
        if net.dims == 2:
            self.to_a = self.give(own, net.peer(net.chip_a))
        if net.dims:
            self.to_b = self.give(own, net.peer(net.chip_b))

    def pass_on(self):
        net = self.net
        if net.dims == 2:
            got = self.part(net.chip_a)
            net.wait(self.to_a, self.all_of(got))
            self.on = self.give(got, net.peer(net.chip_b))

    def share(self):
        net = self.net
        if net.dims:
            net.wait(self.to_b, self.all_of(self.part(net.chip_b)))
        if net.dims == 2:
            net.wait(self.on, self.all_of(self.part(net.chip_ab)))
        self.cross()

    def cross(self):
        self.to_core = self.give(self.block(self.net.core), self.net.sibling())

    def end(self):
        self.net.wait(self.to_core, self.all_of(self.block(1 - self.net.core)))


class Gather:
    def __init__(self, net, buf, by_core=False):
        self.net, self.buf, self.by_core = net, buf, by_core
        planes = [buf.at[net.src(k)] for k in range(1, net.shards)]
        self.spread = Spread(net, planes, lambda rows: buf.at[0 : net.shards - 1, rows])
        self.pass_on, self.share, self.end = self.spread.pass_on, self.spread.share, self.spread.end
        self.rows = self.spread.block(net.core) if by_core else self.spread.part(net.chip)

    def start(self):
        net = self.net
        own = self.buf.at[net.z, self.rows]
        self.far = net.arrival()
        for k in range(1, net.shards):
            net.send(own, own, self.far, net.far(k), net.i)

    def begin(self):
        self.net.wait(self.far, self.spread.all_of(self.rows))
        if self.by_core:
            self.spread.cross()
        else:
            self.spread.begin()


class Reduce:
    def __init__(
        self, net, grad, from_core, from_a, from_b, from_group, from_far, out, far_first, store
    ):
        self.net, self.grad, self.out, self.far_first = net, grad, out, far_first
        self.store = store
        self.from_core, self.from_a, self.from_b = from_core, from_a, from_b
        self.from_group, self.from_far = from_group, from_far
        self.piece = grad.shape[1] // net.group
        self.half = grad.shape[1] // 2
        self.spread = Spread(net, [out], lambda rows: out.at[rows])
        near = [self.take_a, self.take_b] if net.dims == 2 else [self.take_b]
        steps = [self.take_far] + near if far_first else near + [self.take_far]
        self.steps = [self.start, self.take_core] + steps
        self.steps[-1] = functools.partial(self.last, self.steps[-1])
        if net.dims == 2:
            self.steps.append(self.spread.pass_on)
        self.steps += [self.spread.share, self.finish]
        self.stage = 0

    def advance(self, times=1):
        for _ in range(times):
            if self.stage < len(self.steps):
                self.steps[self.stage]()
                self.stage += 1

    def last(self, step):
        step()
        self.spread.begin()

    def finish(self):
        self.spread.end()
        self.store.start()

    def first(self, chip):
        return (self.net.core * self.net.pairs + chip) * self.piece

    def rows(self, chip):
        return many(self.first(chip), self.piece, self.piece)

    def planes(self, after_far):
        if after_far:
            return [(self.net.z, 0)]
        return [(s, s) for s in range(self.net.shards)]

    def add(self, first, count, planes, parts):
        lines = 16

        def one(step, carry):
            at = pl.multiple_of(step * lines, lines)
            rows = many(first + at, lines, lines)
            for here, there in planes:
                value = self.grad[here, rows].astype(F32)
                for part in parts:
                    value = value + part[there, pl.ds(at, lines)].astype(F32)
                self.grad[here, rows] = value.astype(BF16)
            return carry

        lax.fori_loop(0, count // lines, one, 0)

    def cut(self, rows, after_far):
        if after_far:
            return self.grad.at[pl.ds(self.net.z, 1), rows]
        return self.grad.at[:, rows]

    def start(self):
        net = self.net
        away = many((1 - net.core) * self.half, self.half, self.half)
        self.to_core = net.arrival()
        net.send(self.grad.at[:, away], self.from_core, self.to_core, net.z, net.sibling())

    def take_core(self):
        net = self.net
        net.wait(self.to_core, self.from_core)
        self.add(net.core * self.half, self.half, self.planes(False), [self.from_core])
        if self.far_first:
            own = many(net.core * self.half, self.half, self.half)
            self.send_far(own)
        else:
            self.send_near(False)

    def send_near(self, after_far):
        net = self.net
        if net.dims == 2:
            self.to_a = [net.arrival(), net.arrival()]
            for k, chip in ((1, net.chip_ab), (0, net.chip_a)):
                net.send(
                    self.cut(self.rows(chip), after_far),
                    self.from_a.at[k],
                    self.to_a[k],
                    net.z,
                    net.peer(net.chip_a),
                )
        elif net.dims == 1:
            self.send_b(after_far)

    def send_b(self, after_far):
        net = self.net
        self.to_b = net.arrival()
        rows = self.rows(net.chip_b)
        net.send(
            self.cut(rows, after_far), self.from_b, self.to_b, net.z, net.peer(net.chip_b)
        )

    def take_a(self):
        net = self.net
        for k, chip in ((1, net.chip_b), (0, net.chip)):
            net.wait(self.to_a[k], self.from_a.at[k])
            self.add(self.first(chip), self.piece, self.planes(self.far_first), [self.from_a.at[k]])
            if k:
                self.send_b(self.far_first)

    def take_b(self):
        net = self.net
        if net.dims:
            net.wait(self.to_b, self.from_b)
            self.add(
                self.first(net.chip), self.piece, self.planes(self.far_first), [self.from_b]
            )
        own = self.rows(net.chip)
        step, at = 1, 0
        while step < net.groups:
            peer = net.i + net.group * step * (1 - 2 * ((net.grp // step) % 2))
            arrived = net.arrival()
            one = net.send(
                self.cut(own, self.far_first), self.from_group.at[at], arrived, net.z, peer
            )
            net.wait(arrived, self.from_group.at[at])
            net.left(one)
            self.add(
                self.first(net.chip),
                self.piece,
                self.planes(self.far_first),
                [self.from_group.at[at]],
            )
            step, at = step * 2, at + 1
        if self.far_first:
            self.out[own, :] = self.grad[net.z, own]
        else:
            self.send_far(own)

    def send_far(self, own):
        net = self.net
        self.own = own
        self.to_far = net.arrival()
        for k in range(1, net.shards):
            net.send(
                self.grad.at[pl.ds(net.far(k), 1), own],
                self.from_far.at[pl.ds(k - 1, 1)],
                self.to_far,
                net.far(k),
                net.i,
            )

    def take_far(self):
        net = self.net
        net.wait(self.to_far, self.from_far)
        parts = [self.from_far.at[pl.ds(k, 1)] for k in range(net.shards - 1)]
        if self.far_first:
            self.add(net.core * self.half, self.half, self.planes(True), parts)
            self.send_near(True)
        else:
            self.add(self.first(net.chip), self.piece, self.planes(True), parts)
            self.out[self.own, :] = self.grad[net.z, self.own]


def reduce_scratch(shards, group, rounds, rows, wide, far_first):
    pairs = group // 2
    piece, half = rows // group, rows // 2
    planes = 1 if far_first else shards
    tiny = (1, 16, 128)
    return [
        pltpu.VMEM((shards, rows, wide), BF16),
        pltpu.VMEM((shards, half, wide), BF16),
        pltpu.VMEM((2, planes, piece, wide) if pairs == 4 else tiny, BF16),
        pltpu.VMEM((planes, piece, wide), BF16),
        pltpu.VMEM((rounds, planes, piece, wide) if rounds else tiny, BF16),
        pltpu.VMEM((shards - 1, half if far_first else piece, wide), BF16),
    ]


def layer_kernel(
    shards,
    ctxs,
    group,
    chunk_far,
    len_ref,
    x_hbm,
    cot_hbm,
    picks_hbm,
    g1_hbm,
    b1_hbm,
    g2_hbm,
    b2_hbm,
    bo_hbm,
    bi_hbm,
    wq_hbm,
    wkv_hbm,
    wr_hbm,
    wo_hbm,
    wi_hbm,
    wout_hbm,
    out_hbm,
    gin_hbm,
    chunk_hbm,
    wo_hbm_out,
    q_hbm,
    kv_hbm,
    x_ref,
    cot_ref,
    picks_ref,
    g1_ref,
    b1_ref,
    g2_ref,
    b2_ref,
    bo_ref,
    bi_ref,
    wq_st,
    wkv_st,
    wr_st,
    wi_st,
    stage,
    wk,
    wqs,
    wo,
    wc,
    vec_st,
    vecs,
    normed,
    normed_t,
    q_t,
    sel_a,
    heads_t,
    small,
    kvall,
    kvt,
    pads,
    hrow,
    linv,
    sbuf,
    ebuf,
    dkv,
    from_sib,
    from_kv,
    mixed_t,
    xhat2,
    n2,
    n2_t,
    gfin_low,
    biases,
    g_t,
    sums_c,
    sums_o,
    sums_q,
    sums_k,
    out_ref,
    gin_ref,
    chunk_out,
    wo_out,
    q_out,
    kv_out,
    vec_g,
    local_sem,
    send_sem,
    recv_sem,
):
    net = Net(shards, ctxs, group, send_sem, recv_sem)
    z, c = net.z, net.i
    tokens, width = x_ref.shape
    seg = tokens // 2
    half = seg // 2
    blocks = 2 * ctxs
    ws = width // shards
    wos = wo.shape[1]
    fs = wout_hbm.shape[0]
    scale = HS ** (-0.5)
    chunks = fs // UNIT
    panels = shards * UNIT // PANEL
    per_panel = PANEL // UNIT
    lanes = TOP * half
    wide = E * HS
    split = wide // 2
    gc, go, gq, gk = [one[0] for one in sums_c], sums_o[0], sums_q[0], sums_k[0]
    vec_line = E
    bias_line = vec_line + 5
    per_unit = UNIT // ws
    near_steps = ctxs // 2

    def local(src, dst, at):
        return pltpu.make_async_copy(src, dst, local_sem.at[at])

    net.greet()
    wo_st, wout_st = stage.at[0:wos], stage.at[wos : wos + fs]
    resid, acc_a, acc_b = (stage.at[k * tokens : (k + 1) * tokens] for k in range(3))
    loads = {}
    for at, (src, dst) in enumerate(
        (
            (wkv_hbm, wkv_st),
            (wr_hbm, wr_st),
            (wq_hbm, wq_st),
            (g1_hbm, g1_ref),
            (b1_hbm, b1_ref),
            (g2_hbm, g2_ref),
            (b2_hbm, b2_ref),
            (bo_hbm, bo_ref),
            (bi_hbm, bi_ref),
            (x_hbm, x_ref),
            (picks_hbm, picks_ref),
            (wo_hbm, wo_st),
            (wi_hbm, wi_st),
            (wout_hbm, wout_st),
            (cot_hbm, cot_ref),
        )
    ):
        loads[id(dst)] = local(src, dst, at)
        loads[id(dst)].start()
    loads[id(wkv_st)].wait()
    wk[z] = wkv_st[...].astype(BF16)
    vec_st[...] = jnp.zeros(vec_st.shape, F32)
    for row, ref in enumerate((g1_ref, b1_ref, g2_ref, b2_ref, bo_ref)):
        loads[id(ref)].wait()
        vec_st[row : row + 1, 0:ws] = ref[...]
    loads[id(bi_ref)].wait()
    for k in range(chunks):
        vec_st[5 + k : 6 + k, :] = bi_ref[:, k * UNIT : (k + 1) * UNIT]
    own_vec = vecs.at[z]
    own_vec[...] = vec_st[...].astype(BF16)
    net.greeted()
    gather_k, gather_o = Gather(net, wk, True), Gather(net, wo)
    gather_q = [Gather(net, one) for one in wqs]
    gather_c = [Gather(net, wc.at[k]) for k in range(chunks)]
    gather_k.start()
    vec_slot = net.arrival()
    for k in range(1, shards):
        net.send(own_vec, own_vec, vec_slot, net.far(k), net.i)
    loads[id(wq_st)].wait()
    loads[id(wr_st)].wait()
    for k in range(2):
        wqs[k][z, :, 0:split] = wq_st[:, k * split : (k + 1) * split].astype(BF16)
    padded = jnp.concatenate([wr_st[...], jnp.zeros((128 - E, ws), F32)], axis=0)
    wqs[1][z, :, split:] = padded.T.astype(BF16)
    for one in gather_q:
        one.start()

    loads[id(x_ref)].wait()
    x = x_ref[...].astype(F32)
    mean1 = jnp.mean(x, axis=1, keepdims=True)
    cen = x - mean1
    small[0, :, 0:1] = lax.rsqrt(jnp.mean(cen * cen, axis=1, keepdims=True) + NORM_EPS)
    small[0, :, 2:3] = mean1

    def first_hat():
        return (x_ref[...].astype(F32) - small[0, :, 2:3]) * small[0, :, 0:1]

    for ref in (wo_st, wi_st, wout_st):
        loads[id(ref)].wait()
    wo[z] = wo_st[...].astype(BF16)
    for k in range(chunks):
        wc[k, z, 0:UNIT] = wout_st[k * UNIT : (k + 1) * UNIT].astype(BF16)
        for s in range(shards):
            first = UNIT + (s // per_panel) * ws
            at = (s % per_panel) * UNIT
            wc[k, z, first : first + ws, at : at + UNIT] = wi_st[
                :, s * fs + k * UNIT : s * fs + (k + 1) * UNIT
            ].astype(BF16)
    gather_k.begin()
    net.wait(vec_slot, vecs.at[0 : shards - 1])

    vec_all = [vecs[s].astype(F32) for s in range(shards)]

    def whole(row):
        return jnp.concatenate([one[row : row + 1, 0:ws] for one in vec_all], axis=1)

    gain1, bias1, gain2, bias2, bias_out = (whole(row) for row in range(5))
    for k in range(chunks):
        for p in range(panels):
            biases[k * panels + p : k * panels + p + 1, :] = jnp.concatenate(
                [one[5 + k : 6 + k] for one in vec_all[p * per_panel : (p + 1) * per_panel]],
                axis=1,
            )
    norm_value = first_hat() * gain1 + bias1
    normed[...] = norm_value.astype(BF16)
    normed_t[...] = norm_value.T.astype(BF16)
    gather_q[0].begin()
    gather_k.end()

    kv_own = dot(normed[...], wk[...].reshape(width, 2 * HS)).astype(BF16)

    def at_block(ref, block):
        return ref.at[block // 2, :, block % 2]

    def my_block(h):
        return c if h == 0 else blocks - 1 - c

    def core_blocks(ref, core):
        return ref.at[0:near_steps, :, core], ref.at[near_steps:ctxs, :, 1 - core]

    for h in range(2):
        block = my_block(h)
        for s in range(2):
            first = s * seg + h * half
            kvall[block // 2, s, block % 2] = kv_own[first : first + half]
    kv_slot, kv_cross = net.arrival(), net.arrival()
    kv_sent = []
    for step in range(1, near_steps):
        for block in (c, blocks - 1 - c):
            ref = at_block(kvall, block)
            kv_sent.append(net.send(ref, ref, kv_slot, z, (c + 2 * step) % ctxs))
    gather_q[1].begin()
    gather_o.start()
    gather_q[0].pass_on()
    net.wait(kv_slot, kvall.at[0 : near_steps - 1])
    for part in core_blocks(kvall, net.core):
        kv_sent.append(net.send(part, part, kv_cross, z, net.sibling()))
    gather_q[1].pass_on()
    gather_c[0].start()
    gather_q[0].share()
    net.wait(kv_cross, kvall.at[0:near_steps])

    def turn(step, carry):
        for s in range(2):
            keys = kvall[step, s].reshape(2 * half, 2 * HS)
            kvt[step, s] = keys.astype(F32).T.astype(BF16)
            dkv[step, s] = jnp.zeros((2 * half, 2 * HS), F32)
        return carry

    lax.fori_loop(0, ctxs, turn, 0, unroll=4)

    def serve(*calls):
        for k, call in calls:
            if k < chunks:
                getattr(gather_c[k], call)()

    gather_o.begin()
    serve((1, "start"))
    gather_q[0].end()

    def project_queries(part):
        def query_tile(n, carry):
            cols = many(n * 256, 256, 256)
            value = dot(normed[...], wqs[part][:, :, cols].reshape(width, 256))
            value = value.astype(BF16).astype(F32).T
            for k in range(4):
                q_t[part * (E // 2) + n * 4 + k] = value[k * HS : (k + 1) * HS]
            return carry

        lax.fori_loop(0, split // 256, query_tile, 0, unroll=True)

    project_queries(0)
    gather_q[1].share()
    serve((0, "begin"), (2, "start"))
    gather_q[1].end()
    project_queries(1)

    logits_t = dot(normed[...], wqs[1][:, :, split:].reshape(width, 128)).T
    loads[id(picks_ref)].wait()
    picks = jnp.concatenate([picks_ref[0], picks_ref[1]], axis=1).astype(F32)
    picked = jnp.zeros((TOP, tokens), F32)
    for e in range(E):
        picked = jnp.where(picks == float(e), logits_t[e : e + 1, :], picked)
    top = jnp.max(picked, axis=0, keepdims=True)
    gexp = jnp.exp(picked - top)
    small[1, 0:TOP, 0:tokens] = gexp / jnp.sum(gexp, axis=0, keepdims=True)
    small[1, TOP : 2 * TOP, 0:tokens] = picks

    def choose(src, store):
        def one(j, carry):
            pick = small[1, pl.ds(TOP + j, 1), 0:tokens]
            value = jnp.zeros((HS, tokens), F32)
            for e in range(E):
                value = jnp.where(pick == float(e), src[e], value)
            store(j, value)
            return carry

        lax.fori_loop(0, TOP, one, 0, unroll=2)

    def spread_back(src, store):
        def one(e, carry):
            value = jnp.zeros((HS, tokens), F32)
            for j in range(TOP):
                pick = small[1, TOP + j : TOP + j + 1, 0:tokens]
                value = jnp.where(pick == e.astype(F32), src[j], value)
            store(e, value)
            return carry

        lax.fori_loop(0, E, one, 0, unroll=4)

    low_lane = lax.broadcasted_iota(jnp.int32, (HS, 2 * half), 1) < half

    def swap(one, two):
        return (
            jnp.where(low_lane, one, pltpu.roll(two, half, 1)),
            jnp.where(low_lane, pltpu.roll(one, half, 1), two),
        )

    def store_query(j, value):
        sel_a[j] = value * scale

    gather_o.pass_on()
    serve((3, "start"))
    choose(q_t, store_query)
    for s in range(2):
        for pair in range(TOP // 2):
            halves = swap(
                sel_a[2 * pair, :, s * seg : (s + 1) * seg],
                sel_a[2 * pair + 1, :, s * seg : (s + 1) * seg],
            )
            for h in range(2):
                pads[2 * s + h, 0:HS, pair * 128 : (pair + 1) * 128] = halves[h].astype(BF16)
    for sh in range(4):
        pads[sh, HS:, 0:lanes] = jnp.zeros((HS, lanes), BF16)
        pads[sh, 0:HS, lanes:] = jnp.zeros((HS, lanes), BF16)

    serve((1, "begin"))
    serve((0, "pass_on"))

    offset = lax.broadcasted_iota(jnp.int32, (1, lanes), 1) % half
    key_row = lax.broadcasted_iota(jnp.int32, (4 * half, lanes), 0)
    keep_scores = sbuf.shape[1] > 1

    def place(h):
        last = (blocks - c + 3) // 4
        if h == 1:
            return last, 0
        return (c + 4) // 4, last

    def fold(value, op):
        parts = [value[8 * k : 8 * k + 8] for k in range(value.shape[0] // 8)]
        while len(parts) > 1:
            parts = [op(parts[k], parts[k + 1]) for k in range(0, len(parts), 2)]
        return parts[0]

    def keys_of(step, s):
        return kvall[pl.ds(2 * step, 2), s].reshape(4 * half, 2 * HS)

    def turned(step, s, rows):
        return jnp.concatenate([kvt[2 * step + k, s, rows] for k in range(2)], axis=1)

    def attend(h):
        count, base = place(h)
        limits = [
            jnp.minimum(my_block(h) * half + offset, len_ref[s] - 1) for s in range(2)
        ]

        def masked(step, s):
            scores = dot(keys_of(step, s), pads[2 * s + h, :, 0:lanes])
            return jnp.where(key_row <= limits[s] - step * 4 * half, scores, NEG_LARGE)

        def score_step(step, tops):
            result = []
            for s in range(2):
                scores = masked(step, s)
                if keep_scores:
                    sbuf[s, step] = scores
                result.append(jnp.maximum(tops[s], fold(scores, jnp.maximum)))
            return tuple(result)

        start = jnp.full((8, lanes), NEG_LARGE, F32)
        tops = lax.fori_loop(0, count, score_step, (start, start))
        tops = [jnp.max(top, axis=0, keepdims=True) for top in tops]
        if h == 1:
            gather_o.share()
            serve((2, "begin"))
        for s in range(2):
            hrow[2 * s + h] = jnp.zeros((HS, lanes), F32)

        def value_step(step, totals):
            result = []
            for s in range(2):
                total = totals[s]
                scores = None if keep_scores else masked(step, s)
                for k in range(2):
                    rows = slice(2 * half * k, 2 * half * (k + 1))
                    part = sbuf[s, step, rows] if keep_scores else scores[rows]
                    expd = jnp.exp(part - tops[s])
                    ebuf[s, base + step, rows] = expd.astype(BF16)
                    total = total + fold(expd, jnp.add)
                hrow[2 * s + h] += dot(turned(step, s, slice(HS, 2 * HS)), ebuf[s, base + step])
                result.append(total)
            return tuple(result)

        start = jnp.zeros((8, lanes), F32)
        totals = lax.fori_loop(0, count, value_step, (start, start))
        for s in range(2):
            inverse = 1.0 / jnp.sum(totals[s], axis=0, keepdims=True)
            linv[2 * s + h] = jnp.broadcast_to(inverse, (8, lanes))
            hrow[2 * s + h] = hrow[2 * s + h] * inverse

    attend(1)
    serve((0, "share"), (1, "pass_on"), (3, "begin"))
    attend(0)
    serve((2, "pass_on"), (1, "share"))

    for s in range(2):
        for pair in range(TOP // 2):
            both = swap(
                hrow[2 * s, :, pair * 128 : (pair + 1) * 128],
                hrow[2 * s + 1, :, pair * 128 : (pair + 1) * 128],
            )
            for k in range(2):
                heads_t[2 * pair + k, :, s * seg : (s + 1) * seg] = both[k]
    for j in range(TOP):
        sel_a[j] = heads_t[j] * small[1, j : j + 1, 0:tokens]

    def store_mixed(e, value):
        mixed_t[e] = value.astype(BF16)

    spread_back(sel_a, store_mixed)
    gather_o.end()
    experts = E // shards
    acc_a[...] = x_ref[...].astype(F32)

    def project(s, carry):
        part = mixed_t[pl.ds(s * experts, experts)].reshape(wos, tokens)
        acc_a[...] += dot(part.astype(F32).T.astype(BF16), wo[s])
        return carry

    lax.fori_loop(0, shards, project, 0, unroll=True)
    residual = acc_a[...]
    resid[...] = residual
    cen = residual - jnp.mean(residual, axis=1, keepdims=True)
    rstd2 = lax.rsqrt(jnp.mean(cen * cen, axis=1, keepdims=True) + NORM_EPS)
    small[0, :, 1:2] = rstd2
    cen = cen * rstd2
    xhat2[...] = cen
    cen = cen * gain2 + bias2
    n2[...] = cen.astype(BF16)
    n2_t[...] = cen.T.astype(BF16)

    row = lax.broadcasted_iota(jnp.int32, (tokens, 1), 0)
    inner_row = row % seg
    pos = jnp.where(
        inner_row < half, c * half + inner_row, blocks * half - (c + 2) * half + inner_row
    )
    valid = (pos < jnp.where(row < seg, len_ref[0], len_ref[1])).astype(F32)
    loads[id(cot_ref)].wait()
    gfin_low[...] = (cot_ref[...].astype(F32) * valid).astype(BF16)
    acc_a[...] = jnp.zeros((tokens, width), F32)
    acc_b[...] = jnp.zeros((tokens, width), F32)
    vec_g[...] = jnp.zeros(vec_g.shape, F32)

    def feed(k, p):
        rows_in = slice(UNIT + p * ws, UNIT + (p + 1) * ws)
        planes = slice(p * per_panel, (p + 1) * per_panel)
        w_in = wc[k, :, rows_in].reshape(width, PANEL)
        w_out = wc[k, planes, 0:UNIT].reshape(PANEL, width)
        line = k * panels + p
        hidden = dot(n2[...], w_in) + biases[line : line + 1, :]
        square = hidden * hidden
        tanh = jnp.tanh(GELU_C * hidden * (1.0 + GELU_A * square))
        act = (0.5 * hidden * (1.0 + tanh)).astype(BF16)
        slope = 0.5 * (1.0 + tanh) + 0.5 * GELU_C * hidden * (1.0 - tanh * tanh) * (
            1.0 + 3.0 * GELU_A * square
        )
        gfin = gfin_low[...]
        acc_a[...] += dot(act, w_out)
        grad_hidden = (slope * dot_t(gfin, w_out)).astype(BF16)
        total = jnp.sum(grad_hidden.astype(F32), axis=0, keepdims=True)
        for a in range(per_panel):
            for q in range(per_unit):
                at = bias_line + k * per_unit + q
                first = (p * per_panel + a) * ws
                vec_g[at : at + 1, first : first + ws] = total[
                    :, a * UNIT + q * ws : a * UNIT + (q + 1) * ws
                ]
        grad_outer = dot(act.astype(F32).T.astype(BF16), gfin).astype(BF16)
        gc[k][planes, 0:UNIT] = grad_outer.reshape(per_panel, UNIT, width)
        grad_inner = dot(n2_t[...], grad_hidden).astype(BF16)
        gc[k][:, rows_in] = grad_inner.reshape(shards, ws, PANEL)
        acc_b[...] += dot_t(grad_hidden, w_in)

    outs = [local(out_ref, out_hbm, 15), local(gin_ref, gin_hbm, 16)]

    def reduction(refs, out, hbm, at, far_first):
        store = local(out, hbm, at)
        outs.append(store)
        return Reduce(net, *refs, out, far_first, store)

    reduce_c = [
        reduction(sums_c[k], chunk_out.at[k], chunk_hbm.at[k], 20 + k, chunk_far[k])
        for k in range(chunks)
    ]
    for k in range(chunks):
        if k == 0:
            serve((3, "pass_on"), (2, "share"))
        if k == 1:
            serve((3, "share"))
        gather_c[k].end()
        for p in range(panels):
            feed(k, p)
        reduce_c[k].advance()
        if k > 1:
            reduce_c[k - 2].advance()
    out_ref[...] = (valid * (resid[...] + acc_a[...] + bias_out)).astype(BF16)
    outs[0].start()
    gfin = cot_ref[...].astype(F32) * valid
    vec_g[vec_line + 4 : vec_line + 5, :] = jnp.sum(gfin, axis=0, keepdims=True)
    grad_n2 = acc_b[...]
    vec_g[vec_line + 3 : vec_line + 4, :] = jnp.sum(grad_n2, axis=0, keepdims=True)
    vec_g[vec_line + 2 : vec_line + 3, :] = jnp.sum(grad_n2 * xhat2[...], axis=0, keepdims=True)
    grad_hat = grad_n2 * gain2
    grad_hat = grad_hat - jnp.mean(grad_hat, axis=1, keepdims=True)
    grad_hat = grad_hat - xhat2[...] * jnp.mean(grad_hat * xhat2[...], axis=1, keepdims=True)
    grad_residual = gfin + grad_hat * small[0, :, 1:2]
    resid[...] = grad_residual
    n2[...] = grad_residual.astype(BF16)
    if chunks > 1:
        reduce_c[chunks - 2].advance()

    def branch(s, carry):
        part = mixed_t[pl.ds(s * experts, experts)].reshape(wos, tokens)
        go[s] = dot(part, n2[...]).astype(BF16)
        grad = dot_t(wo[s], n2[...])
        q_t[pl.ds(s * experts, experts)] = grad.reshape(experts, HS, tokens)
        return carry

    lax.fori_loop(0, shards, branch, 0, unroll=2)
    reduce_o = reduction(sums_o, wo_out, wo_hbm_out, 17, False)
    reduce_o.advance()
    reduce_c[chunks - 1].advance()

    def store_head_grad(j, value):
        sel_a[j] = value * small[1, pl.ds(j, 1), 0:tokens]
        small[1, pl.ds(2 * TOP + j, 1), 0:tokens] = jnp.sum(
            value * heads_t[j], axis=0, keepdims=True
        )

    choose(q_t, store_head_grad)
    gates = small[1, 0:TOP, 0:tokens]
    grad_gates = small[1, 2 * TOP : 3 * TOP, 0:tokens]
    grad_picked = gates * (grad_gates - jnp.sum(gates * grad_gates, axis=0, keepdims=True))
    picks = small[1, TOP : 2 * TOP, 0:tokens]
    g_t[wide : wide + 128, :] = jnp.zeros((128, tokens), BF16)
    grad_logits = [
        jnp.sum(jnp.where(picks == float(e), grad_picked, 0.0), axis=0, keepdims=True)
        for e in range(E)
    ]
    grad_logits += [jnp.zeros((1, tokens), F32)] * (32 - E)
    g_t[wide : wide + 32, :] = jnp.concatenate(grad_logits, axis=0).astype(BF16)
    for s in range(2):
        for pair in range(TOP // 2):
            halves = swap(
                sel_a[2 * pair, :, s * seg : (s + 1) * seg],
                sel_a[2 * pair + 1, :, s * seg : (s + 1) * seg],
            )
            at = pair * 128
            for h in range(2):
                sh = 2 * s + h
                grad = (halves[h] * linv[sh, 0:1, at : at + 128]).astype(BF16)
                pads[sh, HS:, lanes + at : lanes + at + 128] = grad
                linv[sh, 1:2, at : at + 128] = jnp.sum(
                    grad.astype(F32) * hrow[sh, :, at : at + 128], axis=0, keepdims=True
                )
    reduce_o.advance()

    def attend_back(h):
        count, base = place(h)
        deltas = [linv[2 * s + h, 1:2, :] for s in range(2)]
        for s in range(2):
            hrow[2 * s + h] = jnp.zeros((HS, lanes), F32)

        def grad_step(step, carry):
            for s in range(2):
                sh = 2 * s + h
                parts = []
                for k in range(2):
                    expd = ebuf[s, base + step, 2 * half * k : 2 * half * (k + 1)]
                    keys = kvall[2 * step + k, s].reshape(2 * half, 2 * HS)
                    grad_prob = dot(keys, pads[sh, :, lanes:])
                    parts.append((expd.astype(F32) * (grad_prob - deltas[s])).astype(BF16))
                grad_score = jnp.concatenate(parts, axis=0)
                grad = dot_t(grad_score, pads[sh, :, 0:lanes])
                grad = grad + dot_t(ebuf[s, base + step], pads[sh, :, lanes:])
                dkv[pl.ds(2 * step, 2), s] += grad.reshape(2, 2 * half, 2 * HS)
                hrow[sh] += dot(turned(step, s, slice(0, HS)), grad_score)
            return carry

        lax.fori_loop(0, count, grad_step, 0)

    attend_back(1)
    for k in range(chunks // 2, chunks):
        reduce_c[k].advance()
    attend_back(0)

    for one in kv_sent:
        net.left(one)

    def lower(step, carry):
        kvall[step] = dkv[step].astype(BF16).reshape(2, 2, half, 2 * HS)
        return carry

    lax.fori_loop(0, ctxs, lower, 0)
    dkv_cross, dkv_near = net.arrival(), net.arrival()
    for k, part in enumerate(core_blocks(kvall, 1 - net.core)):
        net.send(part, from_sib.at[k], dkv_cross, z, net.sibling())
    for s in range(2):
        for pair in range(TOP // 2):
            both = swap(
                hrow[2 * s, :, pair * 128 : (pair + 1) * 128],
                hrow[2 * s + 1, :, pair * 128 : (pair + 1) * 128],
            )
            for k in range(2):
                q_t[2 * pair + k, :, s * seg : (s + 1) * seg] = both[k] * scale

    def store_grad_query(e, value):
        g_t[many(e * HS, HS, HS), :] = value.astype(BF16)

    spread_back(q_t, store_grad_query)

    def query_grad(n, carry):
        at = many(n * 256, 256, 256)
        grad = dot_t(normed_t[...], g_t[at, :]).astype(BF16)
        gq[:, :, at] = grad.reshape(shards, ws, 256)
        return carry

    lax.fori_loop(0, wide // 256, query_grad, 0, unroll=3)
    reduce_q = reduction(sums_q, q_out, q_hbm, 18, False)
    reduce_q.advance()

    net.wait(dkv_cross, from_sib)

    def add_sibling(step, carry):
        for k, sub in enumerate((net.core, 1 - net.core)):
            at = step + k * near_steps
            rows = many(sub * half, half, half)
            for s in range(2):
                value = dkv[at, s, rows] + from_sib[k, step, s].astype(F32)
                dkv[at, s, rows] = value
                kvall[at, s, sub] = value.astype(BF16)
        return carry

    lax.fori_loop(0, near_steps, add_sibling, 0)
    for step in range(1, near_steps):
        peer = (c + 2 * step) % ctxs
        for h, block in enumerate((peer, blocks - 1 - peer)):
            net.send(at_block(kvall, block), from_kv.at[step - 1, h], dkv_near, z, peer)

    reduce_o.advance()
    part = dot(wqs[0][...].reshape(width, split), g_t[0:split, :])
    part = part + dot(wqs[1][...].reshape(width, split + 128), g_t[split:, :])
    heads_t[...] = part.reshape(heads_t.shape)
    reduce_q.advance()
    for k in range(chunks // 2, chunks):
        reduce_c[k].advance()
    net.wait(dkv_near, from_kv)
    for h in range(2):
        block = my_block(h)
        for s in range(2):
            value = dkv[block // 2, s, many((block % 2) * half, half, half)]
            for step in range(1, near_steps):
                value = value + from_kv[step - 1, h, s].astype(F32)
            first = s * seg + h * half
            acc_a[first : first + half, 0:128] = value
    grad_kv = acc_a[:, 0:128].T.astype(BF16)
    part = heads_t[...].reshape(width, tokens) + dot(wk[...].reshape(width, 2 * HS), grad_kv)
    grad_normed = part.T
    hat = first_hat()
    vec_g[vec_line : vec_line + 1, :] = jnp.sum(grad_normed * hat, axis=0, keepdims=True)
    vec_g[vec_line + 1 : vec_line + 2, :] = jnp.sum(grad_normed, axis=0, keepdims=True)
    value = dot_t(normed_t[...], grad_kv)
    gk[:, :, 0 : 2 * HS] = value.astype(BF16).reshape(shards, ws, 2 * HS)
    value = dot_t(normed_t[...], g_t[wide:, :]) + vec_g[...].T
    gk[:, :, 2 * HS :] = value.astype(BF16).reshape(shards, ws, 128)
    reduce_k = reduction(sums_k, kv_out, kv_hbm, 19, False)
    reduce_k.advance()
    grad_hat = grad_normed * gain1
    grad_hat = grad_hat - jnp.mean(grad_hat, axis=1, keepdims=True)
    grad_hat = grad_hat - hat * jnp.mean(grad_hat * hat, axis=1, keepdims=True)
    gin_ref[...] = resid[...] + grad_hat * small[0, :, 0:1]
    outs[1].start()

    everything = [reduce_k, reduce_q, reduce_o, *reduce_c[chunks // 2 :], *reduce_c[: chunks // 2]]
    while any(one.stage < len(one.steps) for one in everything):
        for one in everything:
            one.advance()
    net.finish()
    for one in outs:
        one.wait()


def unpack_kernel(shards, *refs):
    ins, outs = refs[0:6], refs[6:20]
    in_st, out_st, sem = refs[20:26], refs[26:40], refs[40]
    loads = [pltpu.make_async_copy(a, b, sem.at[k]) for k, (a, b) in enumerate(zip(ins, in_st))]
    stores = [
        pltpu.make_async_copy(in_st[k] if k < 2 else out_st[k], outs[k], sem.at[6 + k])
        for k in range(14)
    ]
    for k in (2, 3, 4, 5, 1, 0):
        loads[k].start()
    chunk_in, wo_in, q_in, kv_in = in_st[2:]
    g1_ref, b1_ref, kv_ref, q_ref, r_ref, wo_ref, g2_ref, b2_ref = out_st[2:10]
    wi_ref, bi_ref, wout_ref, bo_ref = out_st[10:]
    ws, fs = q_ref.shape[0], wout_ref.shape[0]
    per_panel = PANEL // UNIT
    loads[2].wait()
    for k in range(chunk_in.shape[0]):
        wout_ref[k * UNIT : (k + 1) * UNIT, :] = chunk_in[k, 0:UNIT].astype(F32)
    stores[12].start()
    for k in range(chunk_in.shape[0]):
        for s in range(shards):
            first = UNIT + (s // per_panel) * ws
            at = (s % per_panel) * UNIT
            wi_ref[:, s * fs + k * UNIT : s * fs + (k + 1) * UNIT] = chunk_in[
                k, first : first + ws, at : at + UNIT
            ].astype(F32)
    stores[10].start()
    loads[3].wait()
    wo_ref[...] = wo_in[...].astype(F32)
    stores[7].start()
    loads[4].wait()
    q_ref[...] = q_in[...].astype(F32)
    stores[5].start()
    loads[5].wait()
    kv_ref[...] = kv_in[:, 0 : 2 * HS].astype(F32)
    stores[4].start()
    turned = kv_in[:, 2 * HS :].astype(F32).T
    r_ref[...] = turned[0:E]
    stores[6].start()
    for row, at, ref in (
        (0, 2, g1_ref),
        (1, 3, b1_ref),
        (2, 8, g2_ref),
        (3, 9, b2_ref),
        (4, 13, bo_ref),
    ):
        ref[...] = turned[E + row : E + row + 1]
        stores[at].start()
    for line in range(fs // ws):
        bi_ref[:, line * ws : (line + 1) * ws] = turned[E + 5 + line : E + 6 + line]
    stores[11].start()
    loads[1].wait()
    stores[1].start()
    loads[0].wait()
    stores[0].start()
    for one in stores:
        one.wait()


def on_device(
    shards,
    ctxs,
    tokens,
    lengths,
    expert_picks,
    first_gain,
    first_bias,
    kv_weight,
    query_weight,
    router_weight,
    output_weight,
    second_gain,
    second_bias,
    inner_weight,
    inner_bias,
    outer_weight,
    outer_bias,
    cotangent,
):
    slots, seg, width = tokens.shape
    count = slots * seg
    half = seg // 2
    lanes = TOP * half
    ws = width // shards
    wos = output_weight.shape[0]
    fs = outer_weight.shape[0]
    group = min(ctxs, ws // 16, 8)
    pairs, groups = group // 2, ctxs // group
    rounds = groups.bit_length() - 1
    chunks = fs // UNIT
    panels = shards * UNIT // PANEL
    chunk_rows = UNIT + panels * ws
    wide = E * HS
    chunk_far = [k < chunks // 2 for k in range(chunks)]
    keep_scores = ctxs * seg * slots * lanes * 4 <= 8 * 1024 * 1024
    shapes_mid = (
        jax.ShapeDtypeStruct((count, width), BF16),
        jax.ShapeDtypeStruct((count, width), F32),
        jax.ShapeDtypeStruct((chunks, chunk_rows, PANEL), BF16),
        jax.ShapeDtypeStruct((wos, width), BF16),
        jax.ShapeDtypeStruct((ws, wide), BF16),
        jax.ShapeDtypeStruct((ws, 256), BF16),
    )

    smem = pl.BlockSpec(memory_space=pltpu.SMEM)
    anywhere = pl.BlockSpec(memory_space=pl.ANY)
    arrivals = 2 + (3 + chunks) * 5 + 1 + 4 + (3 + chunks) * (9 + rounds)
    scratch = [
        pltpu.VMEM((count, width), BF16),
        pltpu.VMEM((count, width), BF16),
        pltpu.VMEM((slots, TOP, seg), jnp.int32),
        *[pltpu.VMEM((1, ws), F32)] * 5,
        pltpu.VMEM((1, fs), F32),
        pltpu.VMEM(query_weight.shape, F32),
        pltpu.VMEM(kv_weight.shape, F32),
        pltpu.VMEM((E, ws), F32),
        pltpu.VMEM(inner_weight.shape, F32),
        pltpu.VMEM((max(wos + fs, 3 * count), width), F32),
        pltpu.VMEM((shards, ws, 2 * HS), BF16),
        [pltpu.VMEM((shards, ws, wide // 2 + 128 * k), BF16) for k in range(2)],
        pltpu.VMEM((shards, wos, width), BF16),
        pltpu.VMEM((chunks, shards, chunk_rows, PANEL), BF16),
        pltpu.VMEM((16, UNIT), F32),
        pltpu.VMEM((shards, 16, UNIT), BF16),
        pltpu.VMEM((count, width), BF16),
        pltpu.VMEM((width, count), BF16),
        pltpu.VMEM((E, HS, count), F32),
        pltpu.VMEM((TOP, HS, count), F32),
        pltpu.VMEM((TOP, HS, count), F32),
        pltpu.VMEM((2, count, count), F32),
        pltpu.VMEM((ctxs, slots, 2, half, 2 * HS), BF16),
        pltpu.VMEM((ctxs, slots, 2 * HS, 2 * half), BF16),
        pltpu.VMEM((4, 2 * HS, 2 * lanes), BF16),
        pltpu.VMEM((4, HS, lanes), F32),
        pltpu.VMEM((4, 8, lanes), F32),
        pltpu.VMEM((slots, ctxs // 2, 4 * half, lanes) if keep_scores else (1, 1, 8, 128), F32),
        pltpu.VMEM((slots, ctxs // 2 + 1, 4 * half, lanes), BF16),
        pltpu.VMEM((ctxs, slots, 2 * half, 2 * HS), F32),
        pltpu.VMEM((2, ctxs // 2, slots, half, 2 * HS), BF16),
        pltpu.VMEM((ctxs // 2 - 1, 2, slots, half, 2 * HS), BF16),
        pltpu.VMEM((E, HS, count), BF16),
        pltpu.VMEM((count, width), F32),
        pltpu.VMEM((count, width), BF16),
        pltpu.VMEM((width, count), BF16),
        pltpu.VMEM((count, width), BF16),
        pltpu.VMEM((8, PANEL), F32),
        pltpu.VMEM((wide + 128, count), BF16),
        [
            reduce_scratch(shards, group, rounds, chunk_rows, PANEL, chunk_far[k])
            for k in range(chunks)
        ],
        reduce_scratch(shards, group, rounds, wos, width, False),
        reduce_scratch(shards, group, rounds, ws, wide, False),
        reduce_scratch(shards, group, rounds, ws, 256, False),
        *[pltpu.VMEM(one.shape, one.dtype) for one in shapes_mid],
        pltpu.VMEM((128, width), F32),
        pltpu.SemaphoreType.DMA((20 + chunks,)),
        pltpu.SemaphoreType.DMA((RING,)),
        pltpu.SemaphoreType.DMA((arrivals,)),
    ]
    results = pl.pallas_call(
        functools.partial(layer_kernel, shards, ctxs, group, chunk_far),
        out_shape=shapes_mid,
        in_specs=[smem] + [anywhere] * 15,
        out_specs=tuple([anywhere] * 6),
        scratch_shapes=scratch,
        compiler_params=pltpu.CompilerParams(
            collective_id=0, has_side_effects=True, vmem_limit_bytes=63 * 1024 * 1024
        ),
        name="layer",
    )(
        lengths,
        tokens.reshape(count, width),
        cotangent.reshape(count, width),
        jnp.swapaxes(expert_picks, 1, 2),
        first_gain.reshape(1, ws),
        first_bias.reshape(1, ws),
        second_gain.reshape(1, ws),
        second_bias.reshape(1, ws),
        outer_bias.reshape(1, ws),
        inner_bias.reshape(1, fs),
        query_weight,
        kv_weight,
        router_weight.T,
        output_weight,
        inner_weight,
        outer_weight,
    )
    vec_shape = jax.ShapeDtypeStruct((1, ws), F32)
    shapes_out = (
        jax.ShapeDtypeStruct((count, width), BF16),
        jax.ShapeDtypeStruct((count, width), F32),
        vec_shape,
        vec_shape,
        jax.ShapeDtypeStruct(kv_weight.shape, F32),
        jax.ShapeDtypeStruct(query_weight.shape, F32),
        jax.ShapeDtypeStruct((E, ws), F32),
        jax.ShapeDtypeStruct(output_weight.shape, F32),
        vec_shape,
        vec_shape,
        jax.ShapeDtypeStruct(inner_weight.shape, F32),
        jax.ShapeDtypeStruct((1, fs), F32),
        jax.ShapeDtypeStruct(outer_weight.shape, F32),
        vec_shape,
    )
    final = pl.pallas_call(
        functools.partial(unpack_kernel, shards),
        out_shape=shapes_out,
        in_specs=[anywhere] * 6,
        out_specs=tuple([anywhere] * 14),
        scratch_shapes=[pltpu.VMEM(one.shape, one.dtype) for one in (*shapes_mid, *shapes_out)]
        + [pltpu.SemaphoreType.DMA((20,))],
        name="unpack",
    )(*results)
    final = list(final)
    final[6] = final[6].T
    shapes = (
        tokens.shape,
        tokens.shape,
        first_gain.shape,
        first_bias.shape,
        kv_weight.shape,
        query_weight.shape,
        router_weight.shape,
        output_weight.shape,
        second_gain.shape,
        second_bias.shape,
        inner_weight.shape,
        inner_bias.shape,
        outer_weight.shape,
        outer_bias.shape,
    )
    return tuple(value.reshape(shape) for value, shape in zip(final, shapes))


def solution(mesh):
    rows = P("shard", "ctx", None)
    vec, mat = P("shard"), P("shard", None)
    return jax.shard_map(
        functools.partial(on_device, mesh.shape["shard"], mesh.shape["ctx"]),
        mesh=mesh,
        in_specs=(
            rows,
            vec,
            rows,
            vec,
            vec,
            mat,
            mat,
            mat,
            mat,
            vec,
            vec,
            mat,
            vec,
            mat,
            vec,
            rows,
        ),
        out_specs=(
            rows,
            rows,
            vec,
            vec,
            mat,
            mat,
            mat,
            mat,
            vec,
            vec,
            mat,
            vec,
            mat,
            vec,
        ),
        check_vma=False,
    )
```

```python
import functools

import jax
import jax.numpy as jnp
from jax import lax
from jax.experimental import pallas as pl
from jax.experimental.pallas import tpu as pltpu
from jax.sharding import PartitionSpec as P

HS = 64
E = 24
TOP = 8
NORM_EPS = 1e-05
NEG_LARGE = -1e30
BF16 = jnp.bfloat16
F32 = jnp.float32
PANEL = 512
UNIT = 128
GELU_C = 0.7978845608028654
GELU_A = 0.044715
MESH = pl.DeviceIdType.MESH
RING = 40
START, CORE, NEAR_A, NEAR_B, FAR_0, FAR_1, FAR_2, PASS, SHARE, END = range(10)


def dot(left, right):
    return jnp.dot(left, right, preferred_element_type=F32)


def dot_t(left, right):
    return lax.dot_general(left, right, (((1,), (1,)), ((), ())), preferred_element_type=F32)


def many(first, size, step):
    return pl.ds(pl.multiple_of(first, step), size)


class Net:
    def __init__(self, shards, ctxs, group, send_sem, recv_sem):
        self.shards, self.ctxs, self.group = shards, ctxs, group
        self.pairs = group // 2
        self.groups = ctxs // group
        self.dims = self.pairs.bit_length() - 1
        self.z = lax.axis_index("shard")
        self.i = lax.axis_index("ctx")
        self.core = self.i % 2
        self.chip = (self.i % group) // 2
        self.grp = self.i // group
        self.send_sem, self.recv_sem = send_sem, recv_sem
        self.arrivals = 0
        self.starts = 0
        self.ring = [[] for _ in range(RING)]
        flip_low = self.chip + 1 - 2 * (self.chip % 2)
        if self.dims == 2:
            flip_high = self.chip + 2 - 4 * (self.chip // 2)
            self.chip_a = self.core * flip_high + (1 - self.core) * flip_low
            self.chip_b = self.core * flip_low + (1 - self.core) * flip_high
            self.chip_ab = self.pairs - 1 - self.chip
        elif self.dims == 1:
            self.chip_b = flip_low

    def far(self, step):
        return (self.z + step) % self.shards

    def src(self, step):
        return (self.z + self.shards - step) % self.shards

    def peer(self, chip):
        return self.grp * self.group + chip * 2 + self.core

    def sibling(self):
        return self.i + 1 - 2 * self.core

    def copy(self, src, dst, sent, arrived, z, i):
        return pltpu.make_async_remote_copy(
            src_ref=src,
            dst_ref=dst,
            send_sem=self.send_sem.at[sent],
            recv_sem=self.recv_sem.at[arrived],
            device_id={"shard": z, "ctx": i},
            device_id_type=MESH,
        )

    def arrival(self):
        self.arrivals += 1
        return self.arrivals - 1

    def send(self, src, dst, arrived, z, i):
        slot = self.starts % RING
        self.starts += 1
        if self.ring[slot]:
            self.left(self.ring[slot])
        one = self.ring[slot] = [self.copy(src, dst, slot, arrived, z, i)]
        one[0].start()
        return one

    def left(self, one):
        if one:
            one.pop().wait_send()

    def wait(self, arrived, dst):
        self.copy(dst, dst, 0, arrived, self.z, self.i).wait_recv()

    def finish(self):
        for one in self.ring:
            self.left(one)

    def greet(self):
        barrier = pltpu.get_barrier_semaphore()
        for step in range(1, self.ctxs):
            pl.semaphore_signal(
                barrier,
                inc=1,
                device_id={"shard": self.z, "ctx": (self.i + step) % self.ctxs},
                device_id_type=MESH,
            )
        for step in range(1, self.shards):
            pl.semaphore_signal(
                barrier,
                inc=1,
                device_id={"shard": self.far(step), "ctx": self.i},
                device_id_type=MESH,
            )

    def greeted(self):
        pl.semaphore_wait(pltpu.get_barrier_semaphore(), self.ctxs + self.shards - 2)


class Spread:
    def __init__(self, net, refs, all_of, at_once=False, straight=False):
        self.net, self.refs, self.all_of, self.at_once = net, refs, all_of, at_once
        self.straight = straight
        self.piece = refs[0].shape[0] // net.group
        self.half = refs[0].shape[0] // 2

    def part(self, chip):
        return many((self.net.core * self.net.pairs + chip) * self.piece, self.piece, self.piece)

    def block(self, core):
        return many(core * self.half, self.half, self.half)

    def give(self, rows, peer):
        arrived = self.net.arrival()
        for ref in self.refs:
            self.net.send(ref.at[rows], ref.at[rows], arrived, self.net.z, peer)
        return arrived

    def begin(self):
        net = self.net
        own = self.part(net.chip)
        if self.at_once:
            self.to_all = net.arrival()
            (ref,) = self.refs
            for step in range(1, net.group):
                peer = net.grp * net.group + (net.i + step) % net.group
                net.send(ref.at[own], ref.at[own], self.to_all, net.z, peer)
            return
        if net.dims == 2:
            self.to_a = self.give(own, net.peer(net.chip_a))
        if net.dims:
            self.to_b = self.give(own, net.peer(net.chip_b))
        if net.dims == 2 and self.straight:
            self.on = self.give(own, net.peer(net.chip_ab))

    def pass_on(self):
        net = self.net
        if net.dims == 2 and not self.straight:
            got = self.part(net.chip_a)
            net.wait(self.to_a, self.all_of(got))
            self.on = self.give(got, net.peer(net.chip_b))

    def share(self):
        net = self.net
        if net.dims:
            net.wait(self.to_b, self.all_of(self.part(net.chip_b)))
        if net.dims == 2:
            if self.straight:
                net.wait(self.to_a, self.all_of(self.part(net.chip_a)))
            net.wait(self.on, self.all_of(self.part(net.chip_ab)))
        self.cross()

    def cross(self):
        self.to_core = self.give(self.block(self.net.core), self.net.sibling())

    def end(self):
        if self.at_once:
            count = self.piece * (self.net.group - 1)
            self.net.wait(self.to_all, self.all_of(pl.ds(0, count)))
        else:
            self.net.wait(self.to_core, self.all_of(self.block(1 - self.net.core)))


class Gather:
    def __init__(self, net, buf, by_core=False):
        self.net, self.buf, self.by_core = net, buf, by_core
        planes = [buf.at[net.src(k)] for k in range(1, net.shards)]
        self.spread = Spread(net, planes, lambda rows: buf.at[0 : net.shards - 1, rows])
        self.rows = self.spread.block(net.core) if by_core else self.spread.part(net.chip)

    def start(self):
        net = self.net
        own = self.buf.at[net.z, self.rows]
        self.far = net.arrival()
        for k in range(1, net.shards):
            net.send(own, own, self.far, net.far(k), net.i)

    def begin(self):
        self.net.wait(self.far, self.spread.all_of(self.rows))
        if self.by_core:
            self.spread.cross()
        else:
            self.spread.begin()

    def pass_on(self):
        if not self.by_core:
            self.spread.pass_on()

    def share(self):
        if not self.by_core:
            self.spread.share()

    def end(self):
        self.spread.end()


class Absent:
    def start(self):
        pass

    begin = pass_on = share = end = start

    def to(self, name):
        pass


class Reduce:
    def __init__(self, net, buffers, out, far_first, halving, at_once, straight, store):
        self.net, self.out, self.store = net, out, store
        self.grad, self.from_core, self.from_a, self.from_b = buffers[0:4]
        self.from_group, self.from_far = buffers[4:6]
        self.far_first, self.halving = far_first, halving
        self.piece = self.grad.shape[1] // net.group
        self.half = self.grad.shape[1] // 2
        self.spread = Spread(net, [out], lambda rows: out.at[rows], at_once, straight)
        near = [(NEAR_B, self.take_b)]
        if net.dims == 2:
            near = [(NEAR_A, self.take_a)] + near
        if halving:
            rounds = net.shards.bit_length() - 1
            far = [(FAR_0 + k, functools.partial(self.take_half, k)) for k in range(rounds)]
        else:
            far = [(FAR_0, self.take_far)]
        steps = far + near if far_first else near + far
        name, step = steps[-1]
        steps[-1] = (name, functools.partial(self.last, step))
        after = [(PASS, self.spread.pass_on), (SHARE, self.spread.share)]
        after = [] if at_once else after if net.dims == 2 else after[1:]
        self.steps = [(START, self.start), (CORE, self.take_core), *steps, *after]
        self.steps.append((END, self.finish))
        far, near = [FAR_0, FAR_1, FAR_2], [NEAR_A, NEAR_B]
        order = far + near if far_first else near + far
        order = [START, CORE, *order, PASS, SHARE, END]
        self.rank = {name: k for k, name in enumerate(order)}

    def to(self, name):
        while self.steps and self.rank[self.steps[0][0]] <= self.rank[name]:
            self.steps.pop(0)[1]()

    def last(self, step):
        step()
        self.spread.begin()

    def finish(self):
        self.spread.end()
        self.store.start()

    def first(self, chip):
        return (self.net.core * self.net.pairs + chip) * self.piece

    def rows(self, chip):
        return many(self.first(chip), self.piece, self.piece)

    def planes(self, after_far):
        if after_far:
            return [(self.net.z, 0)]
        return [(s, s) for s in range(self.net.shards)]

    def add(self, first, count, planes, parts):
        lines = 16

        def one(step, carry):
            at = pl.multiple_of(step * lines, lines)
            rows = many(first + at, lines, lines)
            for here, there in planes:
                value = self.grad[here, rows].astype(F32)
                for part in parts:
                    value = value + part[there, pl.ds(at, lines)].astype(F32)
                self.grad[here, rows] = value.astype(BF16)
            return carry

        lax.fori_loop(0, count // lines, one, 0)

    def cut(self, rows, after_far):
        if after_far:
            return self.grad.at[pl.ds(self.net.z, 1), rows]
        return self.grad.at[:, rows]

    def start(self):
        net = self.net
        away = many((1 - net.core) * self.half, self.half, self.half)
        self.to_core = net.arrival()
        net.send(self.grad.at[:, away], self.from_core, self.to_core, net.z, net.sibling())

    def take_core(self):
        net = self.net
        net.wait(self.to_core, self.from_core)
        self.add(net.core * self.half, self.half, self.planes(False), [self.from_core])
        if self.far_first:
            own = many(net.core * self.half, self.half, self.half)
            self.send_far(own)
        else:
            self.send_near(False)

    def send_near(self, after_far):
        net = self.net
        if net.dims == 2:
            self.to_a = [net.arrival(), net.arrival()]
            for k, chip in ((1, net.chip_ab), (0, net.chip_a)):
                net.send(
                    self.cut(self.rows(chip), after_far),
                    self.from_a.at[k],
                    self.to_a[k],
                    net.z,
                    net.peer(net.chip_a),
                )
        elif net.dims == 1:
            self.send_b(after_far)

    def send_b(self, after_far):
        net = self.net
        self.to_b = net.arrival()
        rows = self.rows(net.chip_b)
        net.send(
            self.cut(rows, after_far), self.from_b, self.to_b, net.z, net.peer(net.chip_b)
        )

    def take_a(self):
        net = self.net
        for k, chip in ((1, net.chip_b), (0, net.chip)):
            net.wait(self.to_a[k], self.from_a.at[k])
            self.add(self.first(chip), self.piece, self.planes(self.far_first), [self.from_a.at[k]])
            if k:
                self.send_b(self.far_first)

    def take_b(self):
        net = self.net
        if net.dims:
            net.wait(self.to_b, self.from_b)
            self.add(
                self.first(net.chip), self.piece, self.planes(self.far_first), [self.from_b]
            )
        own = self.rows(net.chip)
        step, at = 1, 0
        while step < net.groups:
            peer = net.i + net.group * step * (1 - 2 * ((net.grp // step) % 2))
            arrived = net.arrival()
            one = net.send(
                self.cut(own, self.far_first), self.from_group.at[at], arrived, net.z, peer
            )
            net.wait(arrived, self.from_group.at[at])
            net.left(one)
            self.add(
                self.first(net.chip),
                self.piece,
                self.planes(self.far_first),
                [self.from_group.at[at]],
            )
            step, at = step * 2, at + 1
        if self.far_first:
            self.out[own, :] = self.grad[net.z, own]
        else:
            self.send_far(own)

    def send_far(self, own):
        net = self.net
        self.own = own
        if self.halving:
            self.send_half(0)
            return
        self.to_far = net.arrival()
        for k in range(1, net.shards):
            net.send(
                self.grad.at[pl.ds(net.far(k), 1), own],
                self.from_far.at[pl.ds(k - 1, 1)],
                self.to_far,
                net.far(k),
                net.i,
            )

    def half_at(self, turn):
        step = 1 << turn
        count = self.net.shards // (2 * step)
        return step, count, self.net.shards - 2 * count

    def send_half(self, turn):
        net = self.net
        step, count, at = self.half_at(turn)
        partner = net.z + step * (1 - 2 * ((net.z // step) % 2))
        self.to_far = net.arrival()
        for k in range(count):
            plane = partner % (2 * step) + 2 * step * k
            net.send(
                self.grad.at[pl.ds(plane, 1), self.own],
                self.from_far.at[pl.ds(at + k, 1)],
                self.to_far,
                partner,
                net.i,
            )

    def take_half(self, turn):
        net = self.net
        step, count, at = self.half_at(turn)
        parts = self.from_far.at[pl.ds(at, count)]
        net.wait(self.to_far, parts)
        planes = [(net.z % (2 * step) + 2 * step * k, k) for k in range(count)]
        first, size = (
            (net.core * self.half, self.half)
            if self.far_first
            else (self.first(net.chip), self.piece)
        )
        self.add(first, size, planes, [parts])
        if count > 1:
            self.send_half(turn + 1)
        else:
            self.far_done()

    def take_far(self):
        net = self.net
        net.wait(self.to_far, self.from_far)
        parts = [self.from_far.at[pl.ds(k, 1)] for k in range(net.shards - 1)]
        if self.far_first:
            self.add(net.core * self.half, self.half, self.planes(True), parts)
        else:
            self.add(self.first(net.chip), self.piece, self.planes(True), parts)
        self.far_done()

    def far_done(self):
        if self.far_first:
            self.send_near(True)
        else:
            self.out[self.own, :] = self.grad[self.net.z, self.own]


def reduce_scratch(shards, group, rounds, rows, wide, far_first):
    pairs = group // 2
    piece, half = rows // group, rows // 2
    planes = 1 if far_first else shards
    tiny = (1, 16, 128)
    return [
        pltpu.VMEM((shards, rows, wide), BF16),
        pltpu.VMEM((shards, half, wide), BF16),
        pltpu.VMEM((2, planes, piece, wide) if pairs == 4 else tiny, BF16),
        pltpu.VMEM((planes, piece, wide), BF16),
        pltpu.VMEM((rounds, planes, piece, wide) if rounds else tiny, BF16),
        pltpu.VMEM((shards - 1, half if far_first else piece, wide), BF16),
    ]


def layer_kernel(
    shards,
    ctxs,
    group,
    chunk_far,
    len_ref,
    x_hbm,
    cot_hbm,
    picks_hbm,
    g1_hbm,
    b1_hbm,
    g2_hbm,
    b2_hbm,
    bo_hbm,
    bi_hbm,
    wq_hbm,
    wkv_hbm,
    wr_hbm,
    wo_hbm,
    wi_hbm,
    wout_hbm,
    out_hbm,
    gin_hbm,
    chunk_hbm,
    wo_hbm_out,
    q_hbm,
    kv_hbm,
    x_ref,
    cot_ref,
    picks_ref,
    g1_ref,
    b1_ref,
    g2_ref,
    b2_ref,
    bo_ref,
    bi_ref,
    wq_st,
    wkv_st,
    wr_st,
    wi_st,
    stage,
    wk,
    wqs,
    wo,
    wc,
    vec_st,
    vecs,
    normed,
    normed_t,
    q_t,
    sel_a,
    heads_t,
    small,
    kvall,
    kvt,
    pads,
    hrow,
    linv,
    sbuf,
    ebuf,
    dkv,
    from_sib,
    from_kv,
    mixed_t,
    xhat2,
    n2,
    n2_t,
    gfin_low,
    biases,
    g_t,
    sums_c,
    sums_o,
    sums_q,
    sums_k,
    out_ref,
    gin_ref,
    chunk_out,
    wo_out,
    q_out,
    kv_out,
    vec_g,
    local_sem,
    send_sem,
    recv_sem,
):
    net = Net(shards, ctxs, group, send_sem, recv_sem)
    z, c = net.z, net.i
    tokens, width = x_ref.shape
    seg = tokens // 2
    half = seg // 2
    blocks = 2 * ctxs
    ws = width // shards
    wos = wo.shape[1]
    fs = wout_hbm.shape[0]
    scale = HS ** (-0.5)
    chunks = fs // UNIT
    panels = shards * UNIT // PANEL
    per_panel = PANEL // UNIT
    lanes = TOP * half
    wide = E * HS
    split = wide // 2
    sum_c, sum_q = [one[0] for one in sums_c], [one[0] for one in sums_q]
    sum_o, sum_k = sums_o[0], sums_k[0]
    vec_line = E
    bias_line = vec_line + 5
    per_unit = UNIT // ws
    near_steps = ctxs // 2

    def local(src, dst, at):
        return pltpu.make_async_copy(src, dst, local_sem.at[at])

    net.greet()
    wo_st, wout_st = stage.at[0:wos], stage.at[wos : wos + fs]
    resid, acc_a, acc_b = (stage.at[k * tokens : (k + 1) * tokens] for k in range(3))
    loads = {}
    for at, (src, dst) in enumerate(
        (
            (wkv_hbm, wkv_st),
            (wr_hbm, wr_st),
            (wq_hbm, wq_st),
            (g1_hbm, g1_ref),
            (b1_hbm, b1_ref),
            (g2_hbm, g2_ref),
            (b2_hbm, b2_ref),
            (bo_hbm, bo_ref),
            (bi_hbm, bi_ref),
            (x_hbm, x_ref),
            (picks_hbm, picks_ref),
            (wo_hbm, wo_st),
            (wi_hbm, wi_st),
            (wout_hbm, wout_st),
            (cot_hbm, cot_ref),
        )
    ):
        loads[id(dst)] = local(src, dst, at)
        loads[id(dst)].start()
    loads[id(wkv_st)].wait()
    wk[z] = wkv_st[...].astype(BF16)
    vec_st[...] = jnp.zeros(vec_st.shape, F32)
    for row, ref in enumerate((g1_ref, b1_ref, g2_ref, b2_ref, bo_ref)):
        loads[id(ref)].wait()
        vec_st[row : row + 1, 0:ws] = ref[...]
    loads[id(bi_ref)].wait()
    for k in range(chunks):
        vec_st[5 + k : 6 + k, :] = bi_ref[:, k * UNIT : (k + 1) * UNIT]
    own_vec = vecs.at[z]
    own_vec[...] = vec_st[...].astype(BF16)
    net.greeted()
    gather_k, gather_o = Gather(net, wk, True), Gather(net, wo)
    gather_q = [Gather(net, one) for one in wqs]
    gather_c = [Gather(net, wc.at[k], k == chunks - 1) for k in range(chunks)]
    gather_k.start()
    vec_slot = net.arrival()
    for k in range(1, shards):
        net.send(own_vec, own_vec, vec_slot, net.far(k), net.i)
    loads[id(wq_st)].wait()
    loads[id(wr_st)].wait()
    for k in range(2):
        wqs[k][z, :, 0:split] = wq_st[:, k * split : (k + 1) * split].astype(BF16)
    padded = jnp.concatenate([wr_st[...], jnp.zeros((128 - E, ws), F32)], axis=0)
    wqs[1][z, :, split:] = padded.T.astype(BF16)
    for one in gather_q:
        one.start()

    loads[id(x_ref)].wait()
    x = x_ref[...].astype(F32)
    mean1 = jnp.mean(x, axis=1, keepdims=True)
    cen = x - mean1
    small[0, :, 0:1] = lax.rsqrt(jnp.mean(cen * cen, axis=1, keepdims=True) + NORM_EPS)
    small[0, :, 2:3] = mean1

    def first_hat():
        return (x_ref[...].astype(F32) - small[0, :, 2:3]) * small[0, :, 0:1]

    for ref in (wo_st, wi_st, wout_st):
        loads[id(ref)].wait()
    wo[z] = wo_st[...].astype(BF16)
    for k in range(chunks):
        wc[k, z, 0:UNIT] = wout_st[k * UNIT : (k + 1) * UNIT].astype(BF16)
        for s in range(shards):
            first = UNIT + (s // per_panel) * ws
            at = (s % per_panel) * UNIT
            wc[k, z, first : first + ws, at : at + UNIT] = wi_st[
                :, s * fs + k * UNIT : s * fs + (k + 1) * UNIT
            ].astype(BF16)
    gather_k.begin()
    net.wait(vec_slot, vecs.at[0 : shards - 1])

    vec_all = [vecs[s].astype(F32) for s in range(shards)]

    def whole(row):
        return jnp.concatenate([one[row : row + 1, 0:ws] for one in vec_all], axis=1)

    gain1, bias1, gain2, bias2, bias_out = (whole(row) for row in range(5))
    for k in range(chunks):
        for p in range(panels):
            biases[k * panels + p : k * panels + p + 1, :] = jnp.concatenate(
                [one[5 + k : 6 + k] for one in vec_all[p * per_panel : (p + 1) * per_panel]],
                axis=1,
            )
    norm_value = first_hat() * gain1 + bias1
    normed[...] = norm_value.astype(BF16)
    normed_t[...] = norm_value.T.astype(BF16)
    gather_q[0].begin()
    def at_block(ref, block):
        return ref.at[block // 2, :, block % 2]

    def my_block(h):
        return c if h == 0 else blocks - 1 - c

    def core_blocks(ref, core):
        return ref.at[0:near_steps, :, core], ref.at[near_steps:ctxs, :, 1 - core]

    kv_slot, kv_cross, dkv_cross, dkv_near = (net.arrival() for _ in range(4))
    kv_sent = []

    def do_kvproj():
        kv_own = dot(normed[...], wk[...].reshape(width, 2 * HS)).astype(BF16)

        for h in range(2):
            block = my_block(h)
            for s in range(2):
                first = s * seg + h * half
                kvall[block // 2, s, block % 2] = kv_own[first : first + half]
        for step in range(1, near_steps):
            for block in (c, blocks - 1 - c):
                ref = at_block(kvall, block)
                kv_sent.append(net.send(ref, ref, kv_slot, z, (c + 2 * step) % ctxs))

    def do_kvcross():
        net.wait(kv_slot, kvall.at[0 : near_steps - 1])
        for part in core_blocks(kvall, net.core):
            kv_sent.append(net.send(part, part, kv_cross, z, net.sibling()))

    def do_kvwait():
        net.wait(kv_cross, kvall.at[0:near_steps])

    def do_turn():
        def turn(step, carry):
            for s in range(2):
                keys = kvall[step, s].reshape(2 * half, 2 * HS)
                kvt[step, s] = keys.astype(F32).T.astype(BF16)
                dkv[step, s] = jnp.zeros((2 * half, 2 * HS), F32)
            return carry

        lax.fori_loop(0, ctxs, turn, 0, unroll=4)

    def project_queries(part):
        def query_tile(n, carry):
            cols = many(n * 256, 256, 256)
            value = dot(normed[...], wqs[part][:, :, cols].reshape(width, 256))
            value = value.astype(BF16).astype(F32).T
            for k in range(4):
                q_t[part * (E // 2) + n * 4 + k] = value[k * HS : (k + 1) * HS]
            return carry

        lax.fori_loop(0, split // 256, query_tile, 0, unroll=True)

    def do_gates():
        logits_t = dot(normed[...], wqs[1][:, :, split:].reshape(width, 128)).T
        loads[id(picks_ref)].wait()
        picks = jnp.concatenate([picks_ref[0], picks_ref[1]], axis=1).astype(F32)
        picked = jnp.zeros((TOP, tokens), F32)
        for e in range(E):
            picked = jnp.where(picks == float(e), logits_t[e : e + 1, :], picked)
        top = jnp.max(picked, axis=0, keepdims=True)
        gexp = jnp.exp(picked - top)
        small[1, 0:TOP, 0:tokens] = gexp / jnp.sum(gexp, axis=0, keepdims=True)
        small[1, TOP : 2 * TOP, 0:tokens] = picks

    def choose(src, store):
        def one(j, carry):
            pick = small[1, pl.ds(TOP + j, 1), 0:tokens]
            value = jnp.zeros((HS, tokens), F32)
            for e in range(E):
                value = jnp.where(pick == float(e), src[e], value)
            store(j, value)
            return carry

        lax.fori_loop(0, TOP, one, 0, unroll=2)

    def spread_back(src, store):
        def one(e, carry):
            value = jnp.zeros((HS, tokens), F32)
            for j in range(TOP):
                pick = small[1, TOP + j : TOP + j + 1, 0:tokens]
                value = jnp.where(pick == e.astype(F32), src[j], value)
            store(e, value)
            return carry

        lax.fori_loop(0, E, one, 0, unroll=4)

    low_lane = lax.broadcasted_iota(jnp.int32, (HS, 2 * half), 1) < half

    def swap(one, two):
        return (
            jnp.where(low_lane, one, pltpu.roll(two, half, 1)),
            jnp.where(low_lane, pltpu.roll(one, half, 1), two),
        )

    def store_query(j, value):
        sel_a[j] = value * scale

    def do_choose():
        choose(q_t, store_query)
        for s in range(2):
            for pair in range(TOP // 2):
                halves = swap(
                    sel_a[2 * pair, :, s * seg : (s + 1) * seg],
                    sel_a[2 * pair + 1, :, s * seg : (s + 1) * seg],
                )
                for h in range(2):
                    pads[2 * s + h, 0:HS, pair * 128 : (pair + 1) * 128] = halves[h].astype(BF16)
        for sh in range(4):
            pads[sh, HS:, 0:lanes] = jnp.zeros((HS, lanes), BF16)
            pads[sh, 0:HS, lanes:] = jnp.zeros((HS, lanes), BF16)

    offset = lax.broadcasted_iota(jnp.int32, (1, lanes), 1) % half
    key_row = lax.broadcasted_iota(jnp.int32, (4 * half, lanes), 0)
    keep_scores = sbuf.shape[1] > 1

    def place(h):
        last = (blocks - c + 3) // 4
        if h == 1:
            return last, 0
        return (c + 4) // 4, last

    def fold(value, op):
        parts = [value[8 * k : 8 * k + 8] for k in range(value.shape[0] // 8)]
        while len(parts) > 1:
            parts = [op(parts[k], parts[k + 1]) for k in range(0, len(parts), 2)]
        return parts[0]

    def keys_of(step, s):
        return kvall[pl.ds(2 * step, 2), s].reshape(4 * half, 2 * HS)

    def turned(step, s, rows):
        return jnp.concatenate([kvt[2 * step + k, s, rows] for k in range(2)], axis=1)

    tops_of = {}

    def masked(step, s, h):
        limit = jnp.minimum(my_block(h) * half + offset, len_ref[s] - 1)
        scores = dot(keys_of(step, s), pads[2 * s + h, :, 0:lanes])
        return jnp.where(key_row <= limit - step * 4 * half, scores, NEG_LARGE)

    def find_tops(h):
        def score_step(step, tops):
            result = []
            for s in range(2):
                scores = masked(step, s, h)
                if keep_scores:
                    sbuf[s, step] = scores
                result.append(jnp.maximum(tops[s], fold(scores, jnp.maximum)))
            return tuple(result)

        start = jnp.full((8, lanes), NEG_LARGE, F32)
        tops = lax.fori_loop(0, place(h)[0], score_step, (start, start))
        tops_of[h] = [jnp.max(top, axis=0, keepdims=True) for top in tops]

    def weigh(h):
        count, base = place(h)
        for s in range(2):
            hrow[2 * s + h] = jnp.zeros((HS, lanes), F32)

        def value_step(step, totals):
            result = []
            for s in range(2):
                total = totals[s]
                scores = None if keep_scores else masked(step, s, h)
                for k in range(2):
                    rows = slice(2 * half * k, 2 * half * (k + 1))
                    part = sbuf[s, step, rows] if keep_scores else scores[rows]
                    expd = jnp.exp(part - tops_of[h][s])
                    ebuf[s, base + step, rows] = expd.astype(BF16)
                    total = total + fold(expd, jnp.add)
                hrow[2 * s + h] += dot(turned(step, s, slice(HS, 2 * HS)), ebuf[s, base + step])
                result.append(total)
            return tuple(result)

        start = jnp.zeros((8, lanes), F32)
        totals = lax.fori_loop(0, count, value_step, (start, start))
        for s in range(2):
            inverse = 1.0 / jnp.sum(totals[s], axis=0, keepdims=True)
            linv[2 * s + h] = jnp.broadcast_to(inverse, (8, lanes))
            hrow[2 * s + h] = hrow[2 * s + h] * inverse

    def do_mix():
        for s in range(2):
            for pair in range(TOP // 2):
                both = swap(
                    hrow[2 * s, :, pair * 128 : (pair + 1) * 128],
                    hrow[2 * s + 1, :, pair * 128 : (pair + 1) * 128],
                )
                for k in range(2):
                    heads_t[2 * pair + k, :, s * seg : (s + 1) * seg] = both[k]
        for j in range(TOP):
            sel_a[j] = heads_t[j] * small[1, j : j + 1, 0:tokens]

        def store_mixed(e, value):
            mixed_t[e] = value.astype(BF16)

        spread_back(sel_a, store_mixed)

    experts = E // shards
    row = lax.broadcasted_iota(jnp.int32, (tokens, 1), 0)
    inner_row = row % seg
    pos = jnp.where(
        inner_row < half, c * half + inner_row, blocks * half - (c + 2) * half + inner_row
    )
    valid = (pos < jnp.where(row < seg, len_ref[0], len_ref[1])).astype(F32)

    def do_project():
        acc_a[...] = x_ref[...].astype(F32)

        def project(s, carry):
            part = mixed_t[pl.ds(s * experts, experts)].reshape(wos, tokens)
            acc_a[...] += dot(part.astype(F32).T.astype(BF16), wo[s])
            return carry

        lax.fori_loop(0, shards, project, 0, unroll=True)
        residual = acc_a[...]
        resid[...] = residual
        cen = residual - jnp.mean(residual, axis=1, keepdims=True)
        rstd2 = lax.rsqrt(jnp.mean(cen * cen, axis=1, keepdims=True) + NORM_EPS)
        small[0, :, 1:2] = rstd2
        cen = cen * rstd2
        xhat2[...] = cen
        cen = cen * gain2 + bias2
        n2[...] = cen.astype(BF16)
        n2_t[...] = cen.T.astype(BF16)

        loads[id(cot_ref)].wait()
        gfin_low[...] = (cot_ref[...].astype(F32) * valid).astype(BF16)
        acc_a[...] = jnp.zeros((tokens, width), F32)
        acc_b[...] = jnp.zeros((tokens, width), F32)
        vec_g[...] = jnp.zeros(vec_g.shape, F32)

    def feed(k, p):
        rows_in = slice(UNIT + p * ws, UNIT + (p + 1) * ws)
        planes = slice(p * per_panel, (p + 1) * per_panel)
        w_in = wc[k, :, rows_in].reshape(width, PANEL)
        w_out = wc[k, planes, 0:UNIT].reshape(PANEL, width)
        line = k * panels + p
        hidden = dot(n2[...], w_in) + biases[line : line + 1, :]
        square = hidden * hidden
        tanh = jnp.tanh(GELU_C * hidden * (1.0 + GELU_A * square))
        act = (0.5 * hidden * (1.0 + tanh)).astype(BF16)
        slope = 0.5 * (1.0 + tanh) + 0.5 * GELU_C * hidden * (1.0 - tanh * tanh) * (
            1.0 + 3.0 * GELU_A * square
        )
        gfin = gfin_low[...]
        acc_a[...] += dot(act, w_out)
        grad_hidden = (slope * dot_t(gfin, w_out)).astype(BF16)
        total = jnp.sum(grad_hidden.astype(F32), axis=0, keepdims=True)
        for a in range(per_panel):
            for q in range(per_unit):
                at = bias_line + k * per_unit + q
                first = (p * per_panel + a) * ws
                vec_g[at : at + 1, first : first + ws] = total[
                    :, a * UNIT + q * ws : a * UNIT + (q + 1) * ws
                ]
        grad_outer = dot(act.astype(F32).T.astype(BF16), gfin).astype(BF16)
        sum_c[k][planes, 0:UNIT] = grad_outer.reshape(per_panel, UNIT, width)
        grad_inner = dot(n2_t[...], grad_hidden).astype(BF16)
        sum_c[k][:, rows_in] = grad_inner.reshape(shards, ws, PANEL)
        acc_b[...] += dot_t(grad_hidden, w_in)

    outs = [local(out_ref, out_hbm, 15), local(gin_ref, gin_hbm, 16)]

    def reduction(
        refs, out, hbm, at, far_first=False, halving=False, at_once=False, straight=False
    ):
        store = local(out, hbm, at)
        outs.append(store)
        return Reduce(net, refs, out, far_first, halving, at_once, straight, store)

    reduce_c = [
        reduction(sums_c[k], chunk_out.at[k], chunk_hbm.at[k], 20 + k, chunk_far[k], True)
        for k in range(chunks)
    ]
    reduce_o = reduction(sums_o, wo_out, wo_hbm_out, 17, straight=False)
    reduce_q = [
        reduction(
            sums_q[k],
            q_out[k],
            q_hbm.at[:, k * split : (k + 1) * split],
            20 + chunks + k,
            straight=True,
        )
        for k in range(2)
    ]
    reduce_k = reduction(sums_k, kv_out, kv_hbm, 19, at_once=True)

    def do_norm2():
        out_ref[...] = (valid * (resid[...] + acc_a[...] + bias_out)).astype(BF16)
        outs[0].start()
        gfin = cot_ref[...].astype(F32) * valid
        vec_g[vec_line + 4 : vec_line + 5, :] = jnp.sum(gfin, axis=0, keepdims=True)
        grad_n2 = acc_b[...]
        vec_g[vec_line + 3 : vec_line + 4, :] = jnp.sum(grad_n2, axis=0, keepdims=True)
        vec_g[vec_line + 2 : vec_line + 3, :] = jnp.sum(grad_n2 * xhat2[...], axis=0, keepdims=True)
        grad_hat = grad_n2 * gain2
        grad_hat = grad_hat - jnp.mean(grad_hat, axis=1, keepdims=True)
        grad_hat = grad_hat - xhat2[...] * jnp.mean(grad_hat * xhat2[...], axis=1, keepdims=True)
        grad_residual = gfin + grad_hat * small[0, :, 1:2]
        resid[...] = grad_residual
        n2[...] = grad_residual.astype(BF16)

    def do_branch():
        def branch(s, carry):
            part = mixed_t[pl.ds(s * experts, experts)].reshape(wos, tokens)
            sum_o[s] = dot(part, n2[...]).astype(BF16)
            grad = dot_t(wo[s], n2[...])
            q_t[pl.ds(s * experts, experts)] = grad.reshape(experts, HS, tokens)
            return carry

        lax.fori_loop(0, shards, branch, 0, unroll=2)

    def do_heads():
        def store_head_grad(j, value):
            sel_a[j] = value * small[1, pl.ds(j, 1), 0:tokens]
            small[1, pl.ds(2 * TOP + j, 1), 0:tokens] = jnp.sum(
                value * heads_t[j], axis=0, keepdims=True
            )

        choose(q_t, store_head_grad)
        gates = small[1, 0:TOP, 0:tokens]
        grad_gates = small[1, 2 * TOP : 3 * TOP, 0:tokens]
        grad_picked = gates * (grad_gates - jnp.sum(gates * grad_gates, axis=0, keepdims=True))
        picks = small[1, TOP : 2 * TOP, 0:tokens]
        g_t[wide : wide + 128, :] = jnp.zeros((128, tokens), BF16)
        grad_logits = [
            jnp.sum(jnp.where(picks == float(e), grad_picked, 0.0), axis=0, keepdims=True)
            for e in range(E)
        ]
        grad_logits += [jnp.zeros((1, tokens), F32)] * (32 - E)
        g_t[wide : wide + 32, :] = jnp.concatenate(grad_logits, axis=0).astype(BF16)
        for s in range(2):
            for pair in range(TOP // 2):
                halves = swap(
                    sel_a[2 * pair, :, s * seg : (s + 1) * seg],
                    sel_a[2 * pair + 1, :, s * seg : (s + 1) * seg],
                )
                at = pair * 128
                for h in range(2):
                    sh = 2 * s + h
                    grad = (halves[h] * linv[sh, 0:1, at : at + 128]).astype(BF16)
                    pads[sh, HS:, lanes + at : lanes + at + 128] = grad
                    linv[sh, 1:2, at : at + 128] = jnp.sum(
                        grad.astype(F32) * hrow[sh, :, at : at + 128], axis=0, keepdims=True
                    )

    def attend_back(h):
        count, base = place(h)
        deltas = [linv[2 * s + h, 1:2, :] for s in range(2)]
        for s in range(2):
            hrow[2 * s + h] = jnp.zeros((HS, lanes), F32)

        def grad_step(step, carry):
            for s in range(2):
                sh = 2 * s + h
                parts = []
                for k in range(2):
                    expd = ebuf[s, base + step, 2 * half * k : 2 * half * (k + 1)]
                    keys = kvall[2 * step + k, s].reshape(2 * half, 2 * HS)
                    grad_prob = dot(keys, pads[sh, :, lanes:])
                    parts.append((expd.astype(F32) * (grad_prob - deltas[s])).astype(BF16))
                grad_score = jnp.concatenate(parts, axis=0)
                grad = dot_t(grad_score, pads[sh, :, 0:lanes])
                grad = grad + dot_t(ebuf[s, base + step], pads[sh, :, lanes:])
                dkv[pl.ds(2 * step, 2), s] += grad.reshape(2, 2 * half, 2 * HS)
                hrow[sh] += dot(turned(step, s, slice(0, HS)), grad_score)
            return carry

        lax.fori_loop(0, count, grad_step, 0)

    def do_dsend():
        for one in kv_sent:
            net.left(one)

        def lower(step, carry):
            kvall[step] = dkv[step].astype(BF16).reshape(2, 2, half, 2 * HS)
            return carry

        lax.fori_loop(0, ctxs, lower, 0)
        for k, part in enumerate(core_blocks(kvall, 1 - net.core)):
            net.send(part, from_sib.at[k], dkv_cross, z, net.sibling())

    def do_gradq():
        for s in range(2):
            for pair in range(TOP // 2):
                both = swap(
                    hrow[2 * s, :, pair * 128 : (pair + 1) * 128],
                    hrow[2 * s + 1, :, pair * 128 : (pair + 1) * 128],
                )
                for k in range(2):
                    q_t[2 * pair + k, :, s * seg : (s + 1) * seg] = both[k] * scale

        def store_grad_query(e, value):
            g_t[many(e * HS, HS, HS), :] = value.astype(BF16)

        spread_back(q_t, store_grad_query)

    def query_grads(part):
        def query_grad(n, carry):
            rows = many(part * split + n * 256, 256, 256)
            grad = dot_t(normed_t[...], g_t[rows, :]).astype(BF16)
            sum_q[part][:, :, many(n * 256, 256, 256)] = grad.reshape(shards, ws, 256)
            return carry

        lax.fori_loop(0, split // 256, query_grad, 0, unroll=True)

    def do_dnear():
        net.wait(dkv_cross, from_sib)

        def add_sibling(step, carry):
            for k, sub in enumerate((net.core, 1 - net.core)):
                at = step + k * near_steps
                rows = many(sub * half, half, half)
                for s in range(2):
                    value = dkv[at, s, rows] + from_sib[k, step, s].astype(F32)
                    dkv[at, s, rows] = value
                    kvall[at, s, sub] = value.astype(BF16)
            return carry

        lax.fori_loop(0, near_steps, add_sibling, 0)
        for step in range(1, near_steps):
            peer = (c + 2 * step) % ctxs
            for h, block in enumerate((peer, blocks - 1 - peer)):
                net.send(at_block(kvall, block), from_kv.at[step - 1, h], dkv_near, z, peer)

    def do_ngrad():
        part = dot(wqs[0][...].reshape(width, split), g_t[0:split, :])
        part = part + dot(wqs[1][...].reshape(width, split + 128), g_t[split:, :])
        heads_t[...] = part.reshape(heads_t.shape)

    def do_dwait():
        net.wait(dkv_near, from_kv)

    def do_kvgrad():
        for h in range(2):
            block = my_block(h)
            for s in range(2):
                value = dkv[block // 2, s, many((block % 2) * half, half, half)]
                for step in range(1, near_steps):
                    value = value + from_kv[step - 1, h, s].astype(F32)
                first = s * seg + h * half
                acc_a[first : first + half, 0:128] = value
        grad_kv = acc_a[:, 0:128].T.astype(BF16)
        part = heads_t[...].reshape(width, tokens) + dot(wk[...].reshape(width, 2 * HS), grad_kv)
        grad_normed = part.T
        hat = first_hat()
        vec_g[vec_line : vec_line + 1, :] = jnp.sum(grad_normed * hat, axis=0, keepdims=True)
        vec_g[vec_line + 1 : vec_line + 2, :] = jnp.sum(grad_normed, axis=0, keepdims=True)
        value = dot_t(normed_t[...], grad_kv)
        sum_k[:, :, 0 : 2 * HS] = value.astype(BF16).reshape(shards, ws, 2 * HS)
        value = dot_t(normed_t[...], g_t[wide:, :]) + vec_g[...].T
        sum_k[:, :, 2 * HS :] = value.astype(BF16).reshape(shards, ws, 128)
        acc_b[...] = grad_normed

    def do_gin():
        hat = first_hat()
        grad_normed = acc_b[...]
        grad_hat = grad_normed * gain1
        grad_hat = grad_hat - jnp.mean(grad_hat, axis=1, keepdims=True)
        grad_hat = grad_hat - hat * jnp.mean(grad_hat * hat, axis=1, keepdims=True)
        gin_ref[...] = resid[...] + grad_hat * small[0, :, 0:1]
        outs[1].start()

    def feed_all(k):
        if k < chunks:
            for p in range(panels):
                feed(k, p)

    absent = [Absent()] * 4
    gc0, gc1, gc2, gc3 = (gather_c + absent)[0:4]
    rc0, rc1, rc2, rc3 = (reduce_c + absent)[0:4]
    (gq0, gq1), (rq0, rq1) = gather_q, reduce_q
    go, gk, ro, rk = gather_o, gather_k, reduce_o, reduce_k
    gk.end()
    do_kvproj()
    go.start()
    gq1.begin()
    gq0.pass_on()
    gc0.start()
    do_kvcross()
    gq1.pass_on()
    gc1.start()
    go.begin()
    gc2.start()
    gq0.share()
    do_kvwait()
    do_turn()
    gc0.begin()
    gq0.end()
    project_queries(0)
    gq1.share()
    gc1.begin()
    gq1.end()
    gc3.start()
    project_queries(1)
    do_gates()
    go.pass_on()
    gc2.begin()
    do_choose()
    gc0.pass_on()
    find_tops(1)
    go.share()
    gc1.pass_on()
    weigh(1)
    gc0.share()
    gc2.pass_on()
    find_tops(0)
    weigh(0)
    gc1.share()
    do_mix()
    go.end()
    do_project()
    gc2.share()
    gc0.end()
    feed_all(0)
    rc0.to(START)
    gc3.begin()
    gc3.pass_on()
    gc3.share()
    gc1.end()
    feed_all(1)
    rc1.to(START)
    gc2.end()
    feed_all(2)
    rc2.to(START)
    rc0.to(CORE)
    gc3.end()
    feed_all(3)
    rc3.to(START)
    rc1.to(CORE)
    do_norm2()
    rc2.to(CORE)
    do_branch()
    ro.to(START)
    rc3.to(CORE)
    do_heads()
    attend_back(1)
    attend_back(0)
    ro.to(CORE)
    do_dsend()
    do_gradq()
    query_grads(0)
    rq0.to(START)
    query_grads(1)
    rq1.to(START)
    rc2.to(NEAR_A)
    rc3.to(NEAR_A)
    do_dnear()
    do_ngrad()
    rc0.to(FAR_0)
    rc1.to(FAR_0)
    ro.to(NEAR_A)
    rc2.to(NEAR_B)
    rc3.to(NEAR_B)
    rq0.to(CORE)
    rq1.to(CORE)
    do_dwait()
    do_kvgrad()
    rk.to(START)
    do_gin()
    rk.to(CORE)
    rc0.to(FAR_1)
    rc1.to(FAR_1)
    ro.to(NEAR_B)
    rq0.to(NEAR_A)
    rq1.to(NEAR_A)
    rc2.to(FAR_0)
    rc3.to(FAR_0)
    rc0.to(NEAR_A)
    rc1.to(NEAR_A)
    rk.to(NEAR_A)
    rq0.to(NEAR_B)
    rq1.to(NEAR_B)
    ro.to(FAR_0)
    rc0.to(NEAR_B)
    rc1.to(NEAR_B)
    rc2.to(FAR_1)
    rc3.to(FAR_1)
    rk.to(NEAR_B)
    ro.to(PASS)
    rc0.to(PASS)
    rc1.to(PASS)
    rc2.to(PASS)
    rc3.to(PASS)
    rq0.to(FAR_0)
    rq1.to(FAR_0)
    rk.to(FAR_0)
    ro.to(SHARE)
    rc0.to(SHARE)
    rc1.to(SHARE)
    rc2.to(SHARE)
    rc3.to(SHARE)
    rq0.to(PASS)
    rq1.to(PASS)
    rc1.to(END)
    rc2.to(END)
    rc0.to(END)
    rc3.to(END)
    rq0.to(SHARE)
    rq1.to(SHARE)
    rk.to(END)
    ro.to(END)
    rq0.to(END)
    rq1.to(END)
    for one in (*reduce_c, ro, *reduce_q, rk):
        one.to(END)
    net.finish()
    for one in outs:
        one.wait()


def unpack_kernel(shards, *refs):
    ins, outs = refs[0:6], refs[6:20]
    in_st, out_st, sem = refs[20:26], refs[26:40], refs[40]
    chunks = ins[2].shape[0]
    copy = pltpu.make_async_copy
    loads = [copy(a, b, sem.at[k]) for k, (a, b) in enumerate(zip(ins, in_st)) if k != 2]
    loads.insert(2, None)
    stores = {
        k: copy(in_st[k] if k < 2 else out_st[k], outs[k], sem.at[6 + k])
        for k in range(14)
        if k != 12
    }
    chunk_in, wo_in, q_in, kv_in = in_st[2:]
    g1_ref, b1_ref, kv_ref, q_ref, r_ref, wo_ref, g2_ref, b2_ref = out_st[2:10]
    wi_ref, bi_ref, wout_ref, bo_ref = out_st[10:]
    ws, fs = q_ref.shape[0], wout_ref.shape[0]
    per_panel = PANEL // UNIT
    chunk_loads = [
        copy(ins[2].at[k], chunk_in.at[k], sem.at[20 + k]) for k in range(chunks)
    ]
    for one in chunk_loads:
        one.start()
    for k in (3, 4, 5, 1, 0):
        loads[k].start()
    for k in range(chunks):
        chunk_loads[k].wait()
        rows = slice(k * UNIT, (k + 1) * UNIT)
        wout_ref[rows, :] = chunk_in[k, 0:UNIT].astype(F32)
        stores[20 + k] = copy(wout_ref.at[rows], outs[12].at[rows], sem.at[20 + chunks + k])
        stores[20 + k].start()
        for s in range(shards):
            first = UNIT + (s // per_panel) * ws
            at = (s % per_panel) * UNIT
            wi_ref[:, s * fs + k * UNIT : s * fs + (k + 1) * UNIT] = chunk_in[
                k, first : first + ws, at : at + UNIT
            ].astype(F32)
    stores[10].start()
    loads[3].wait()
    wo_ref[...] = wo_in[...].astype(F32)
    stores[7].start()
    loads[4].wait()
    q_ref[...] = q_in[...].astype(F32)
    stores[5].start()
    loads[5].wait()
    kv_ref[...] = kv_in[:, 0 : 2 * HS].astype(F32)
    stores[4].start()
    turned = kv_in[:, 2 * HS :].astype(F32).T
    r_ref[...] = turned[0:E]
    stores[6].start()
    for row, at, ref in (
        (0, 2, g1_ref),
        (1, 3, b1_ref),
        (2, 8, g2_ref),
        (3, 9, b2_ref),
        (4, 13, bo_ref),
    ):
        ref[...] = turned[E + row : E + row + 1]
        stores[at].start()
    for line in range(fs // ws):
        bi_ref[:, line * ws : (line + 1) * ws] = turned[E + 5 + line : E + 6 + line]
    stores[11].start()
    loads[1].wait()
    stores[1].start()
    loads[0].wait()
    stores[0].start()
    for one in stores.values():
        one.wait()


def on_device(
    shards,
    ctxs,
    tokens,
    lengths,
    expert_picks,
    first_gain,
    first_bias,
    kv_weight,
    query_weight,
    router_weight,
    output_weight,
    second_gain,
    second_bias,
    inner_weight,
    inner_bias,
    outer_weight,
    outer_bias,
    cotangent,
):
    slots, seg, width = tokens.shape
    count = slots * seg
    half = seg // 2
    lanes = TOP * half
    ws = width // shards
    wos = output_weight.shape[0]
    fs = outer_weight.shape[0]
    group = min(ctxs, ws // 16, 8)
    pairs, groups = group // 2, ctxs // group
    rounds = groups.bit_length() - 1
    chunks = fs // UNIT
    panels = shards * UNIT // PANEL
    chunk_rows = UNIT + panels * ws
    wide = E * HS
    chunk_far = [k < 2 for k in range(chunks)]
    keep_scores = ctxs * seg * slots * lanes * 4 <= 8 * 1024 * 1024
    shapes_mid = (
        jax.ShapeDtypeStruct((count, width), BF16),
        jax.ShapeDtypeStruct((count, width), F32),
        jax.ShapeDtypeStruct((chunks, chunk_rows, PANEL), BF16),
        jax.ShapeDtypeStruct((wos, width), BF16),
        jax.ShapeDtypeStruct((ws, wide), BF16),
        jax.ShapeDtypeStruct((ws, 256), BF16),
    )

    smem = pl.BlockSpec(memory_space=pltpu.SMEM)
    anywhere = pl.BlockSpec(memory_space=pl.ANY)
    arrivals = 2 + (3 + chunks) * 5 + 1 + 4 + (4 + chunks) * (8 + rounds + shards.bit_length() - 1)
    scratch = [
        pltpu.VMEM((count, width), BF16),
        pltpu.VMEM((count, width), BF16),
        pltpu.VMEM((slots, TOP, seg), jnp.int32),
        *[pltpu.VMEM((1, ws), F32)] * 5,
        pltpu.VMEM((1, fs), F32),
        pltpu.VMEM(query_weight.shape, F32),
        pltpu.VMEM(kv_weight.shape, F32),
        pltpu.VMEM((E, ws), F32),
        pltpu.VMEM(inner_weight.shape, F32),
        pltpu.VMEM((max(wos + fs, 3 * count), width), F32),
        pltpu.VMEM((shards, ws, 2 * HS), BF16),
        [pltpu.VMEM((shards, ws, wide // 2 + 128 * k), BF16) for k in range(2)],
        pltpu.VMEM((shards, wos, width), BF16),
        pltpu.VMEM((chunks, shards, chunk_rows, PANEL), BF16),
        pltpu.VMEM((16, UNIT), F32),
        pltpu.VMEM((shards, 16, UNIT), BF16),
        pltpu.VMEM((count, width), BF16),
        pltpu.VMEM((width, count), BF16),
        pltpu.VMEM((E, HS, count), F32),
        pltpu.VMEM((TOP, HS, count), F32),
        pltpu.VMEM((TOP, HS, count), F32),
        pltpu.VMEM((2, count, count), F32),
        pltpu.VMEM((ctxs, slots, 2, half, 2 * HS), BF16),
        pltpu.VMEM((ctxs, slots, 2 * HS, 2 * half), BF16),
        pltpu.VMEM((4, 2 * HS, 2 * lanes), BF16),
        pltpu.VMEM((4, HS, lanes), F32),
        pltpu.VMEM((4, 8, lanes), F32),
        pltpu.VMEM((slots, ctxs // 2, 4 * half, lanes) if keep_scores else (1, 1, 8, 128), F32),
        pltpu.VMEM((slots, ctxs // 2 + 1, 4 * half, lanes), BF16),
        pltpu.VMEM((ctxs, slots, 2 * half, 2 * HS), F32),
        pltpu.VMEM((2, ctxs // 2, slots, half, 2 * HS), BF16),
        pltpu.VMEM((ctxs // 2 - 1, 2, slots, half, 2 * HS), BF16),
        pltpu.VMEM((E, HS, count), BF16),
        pltpu.VMEM((count, width), F32),
        pltpu.VMEM((count, width), BF16),
        pltpu.VMEM((width, count), BF16),
        pltpu.VMEM((count, width), BF16),
        pltpu.VMEM((8, PANEL), F32),
        pltpu.VMEM((wide + 128, count), BF16),
        [
            reduce_scratch(shards, group, rounds, chunk_rows, PANEL, chunk_far[k])
            for k in range(chunks)
        ],
        reduce_scratch(shards, group, rounds, wos, width, False),
        [reduce_scratch(shards, group, rounds, ws, wide // 2, False) for _ in range(2)],
        reduce_scratch(shards, group, rounds, ws, 256, False),
        *[pltpu.VMEM(one.shape, one.dtype) for one in shapes_mid[0:4]],
        [pltpu.VMEM((ws, wide // 2), BF16) for _ in range(2)],
        pltpu.VMEM((ws, 256), BF16),
        pltpu.VMEM((128, width), F32),
        pltpu.SemaphoreType.DMA((22 + chunks,)),
        pltpu.SemaphoreType.DMA((RING,)),
        pltpu.SemaphoreType.DMA((arrivals,)),
    ]
    results = pl.pallas_call(
        functools.partial(layer_kernel, shards, ctxs, group, chunk_far),
        out_shape=shapes_mid,
        in_specs=[smem] + [anywhere] * 15,
        out_specs=tuple([anywhere] * 6),
        scratch_shapes=scratch,
        compiler_params=pltpu.CompilerParams(
            collective_id=0, has_side_effects=True, vmem_limit_bytes=63 * 1024 * 1024
        ),
        name="layer",
    )(
        lengths,
        tokens.reshape(count, width),
        cotangent.reshape(count, width),
        jnp.swapaxes(expert_picks, 1, 2),
        first_gain.reshape(1, ws),
        first_bias.reshape(1, ws),
        second_gain.reshape(1, ws),
        second_bias.reshape(1, ws),
        outer_bias.reshape(1, ws),
        inner_bias.reshape(1, fs),
        query_weight,
        kv_weight,
        router_weight.T,
        output_weight,
        inner_weight,
        outer_weight,
    )
    vec_shape = jax.ShapeDtypeStruct((1, ws), F32)
    shapes_out = (
        jax.ShapeDtypeStruct((count, width), BF16),
        jax.ShapeDtypeStruct((count, width), F32),
        vec_shape,
        vec_shape,
        jax.ShapeDtypeStruct(kv_weight.shape, F32),
        jax.ShapeDtypeStruct(query_weight.shape, F32),
        jax.ShapeDtypeStruct((E, ws), F32),
        jax.ShapeDtypeStruct(output_weight.shape, F32),
        vec_shape,
        vec_shape,
        jax.ShapeDtypeStruct(inner_weight.shape, F32),
        jax.ShapeDtypeStruct((1, fs), F32),
        jax.ShapeDtypeStruct(outer_weight.shape, F32),
        vec_shape,
    )
    final = pl.pallas_call(
        functools.partial(unpack_kernel, shards),
        out_shape=shapes_out,
        in_specs=[anywhere] * 6,
        out_specs=tuple([anywhere] * 14),
        scratch_shapes=[pltpu.VMEM(one.shape, one.dtype) for one in (*shapes_mid, *shapes_out)]
        + [pltpu.SemaphoreType.DMA((20 + 2 * chunks,))],
        name="unpack",
    )(*results)
    final = list(final)
    final[6] = final[6].T
    shapes = (
        tokens.shape,
        tokens.shape,
        first_gain.shape,
        first_bias.shape,
        kv_weight.shape,
        query_weight.shape,
        router_weight.shape,
        output_weight.shape,
        second_gain.shape,
        second_bias.shape,
        inner_weight.shape,
        inner_bias.shape,
        outer_weight.shape,
        outer_bias.shape,
    )
    return tuple(value.reshape(shape) for value, shape in zip(final, shapes))


def solution(mesh):
    rows = P("shard", "ctx", None)
    vec, mat = P("shard"), P("shard", None)
    return jax.shard_map(
        functools.partial(on_device, mesh.shape["shard"], mesh.shape["ctx"]),
        mesh=mesh,
        in_specs=(
            rows,
            vec,
            rows,
            vec,
            vec,
            mat,
            mat,
            mat,
            mat,
            vec,
            vec,
            mat,
            vec,
            mat,
            vec,
            rows,
        ),
        out_specs=(
            rows,
            rows,
            vec,
            vec,
            mat,
            mat,
            mat,
            mat,
            vec,
            vec,
            mat,
            vec,
            mat,
            vec,
        ),
        check_vma=False,
    )
```

```python
import functools

import jax
import jax.numpy as jnp
from jax import lax
from jax.experimental import pallas as pl
from jax.experimental.pallas import tpu as pltpu
from jax.sharding import PartitionSpec as P

HS = 64
E = 24
TOP = 8
NORM_EPS = 1e-05
NEG_LARGE = -1e30
BF16 = jnp.bfloat16
F32 = jnp.float32
PANEL = 512
UNIT = 128
GELU_C = 0.7978845608028654
GELU_A = 0.044715
MESH = pl.DeviceIdType.MESH
RING = 40
START, CORE, NEAR_A, NEAR_B, FAR_0, FAR_1, FAR_2, PASS, SHARE, END = range(10)


def dot(left, right):
    return jnp.dot(left, right, preferred_element_type=F32)


def dot_t(left, right):
    return lax.dot_general(left, right, (((1,), (1,)), ((), ())), preferred_element_type=F32)


def many(first, size, step):
    return pl.ds(pl.multiple_of(first, step), size)


class Net:
    def __init__(self, shards, ctxs, group, send_sem, recv_sem):
        self.shards, self.ctxs, self.group = shards, ctxs, group
        self.pairs = group // 2
        self.groups = ctxs // group
        self.dims = self.pairs.bit_length() - 1
        self.z = lax.axis_index("shard")
        self.i = lax.axis_index("ctx")
        self.core = self.i % 2
        self.chip = (self.i % group) // 2
        self.grp = self.i // group
        self.send_sem, self.recv_sem = send_sem, recv_sem
        self.arrivals = 0
        self.starts = 0
        self.ring = [[] for _ in range(RING)]
        flip_low = self.chip + 1 - 2 * (self.chip % 2)
        if self.dims == 2:
            flip_high = self.chip + 2 - 4 * (self.chip // 2)
            self.chip_a = self.core * flip_high + (1 - self.core) * flip_low
            self.chip_b = self.core * flip_low + (1 - self.core) * flip_high
            self.chip_ab = self.pairs - 1 - self.chip
        elif self.dims == 1:
            self.chip_b = flip_low

    def far(self, step):
        return (self.z + step) % self.shards

    def src(self, step):
        return (self.z + self.shards - step) % self.shards

    def peer(self, chip):
        return self.grp * self.group + chip * 2 + self.core

    def sibling(self):
        return self.i + 1 - 2 * self.core

    def copy(self, src, dst, sent, arrived, z, i):
        return pltpu.make_async_remote_copy(
            src_ref=src,
            dst_ref=dst,
            send_sem=self.send_sem.at[sent],
            recv_sem=self.recv_sem.at[arrived],
            device_id={"shard": z, "ctx": i},
            device_id_type=MESH,
        )

    def arrival(self):
        self.arrivals += 1
        return self.arrivals - 1

    def send(self, src, dst, arrived, z, i):
        slot = self.starts % RING
        self.starts += 1
        if self.ring[slot]:
            self.left(self.ring[slot])
        one = self.ring[slot] = [self.copy(src, dst, slot, arrived, z, i)]
        one[0].start()
        return one

    def left(self, one):
        if one:
            one.pop().wait_send()

    def wait(self, arrived, dst):
        self.copy(dst, dst, 0, arrived, self.z, self.i).wait_recv()

    def finish(self):
        for one in self.ring:
            self.left(one)

    def greet(self):
        barrier = pltpu.get_barrier_semaphore()
        for step in range(1, self.ctxs):
            pl.semaphore_signal(
                barrier,
                inc=1,
                device_id={"shard": self.z, "ctx": (self.i + step) % self.ctxs},
                device_id_type=MESH,
            )
        for step in range(1, self.shards):
            pl.semaphore_signal(
                barrier,
                inc=1,
                device_id={"shard": self.far(step), "ctx": self.i},
                device_id_type=MESH,
            )

    def greeted(self):
        pl.semaphore_wait(pltpu.get_barrier_semaphore(), self.ctxs + self.shards - 2)


class Spread:
    def __init__(self, net, refs, all_of, at_once=False, straight=False):
        self.net, self.refs, self.all_of, self.at_once = net, refs, all_of, at_once
        self.straight = straight
        self.piece = refs[0].shape[0] // net.group
        self.half = refs[0].shape[0] // 2

    def part(self, chip):
        return many((self.net.core * self.net.pairs + chip) * self.piece, self.piece, self.piece)

    def block(self, core):
        return many(core * self.half, self.half, self.half)

    def give(self, rows, peer):
        arrived = self.net.arrival()
        for ref in self.refs:
            self.net.send(ref.at[rows], ref.at[rows], arrived, self.net.z, peer)
        return arrived

    def begin(self):
        net = self.net
        own = self.part(net.chip)
        if self.at_once:
            self.to_all = net.arrival()
            (ref,) = self.refs
            for step in range(1, net.group):
                peer = net.grp * net.group + (net.i + step) % net.group
                net.send(ref.at[own], ref.at[own], self.to_all, net.z, peer)
            return
        if net.dims == 2:
            self.to_a = self.give(own, net.peer(net.chip_a))
        if net.dims:
            self.to_b = self.give(own, net.peer(net.chip_b))
        if net.dims == 2 and self.straight:
            self.on = self.give(own, net.peer(net.chip_ab))

    def pass_on(self):
        net = self.net
        if net.dims == 2 and not self.straight:
            got = self.part(net.chip_a)
            net.wait(self.to_a, self.all_of(got))
            self.on = self.give(got, net.peer(net.chip_b))

    def share(self):
        net = self.net
        if net.dims:
            net.wait(self.to_b, self.all_of(self.part(net.chip_b)))
        if net.dims == 2:
            if self.straight:
                net.wait(self.to_a, self.all_of(self.part(net.chip_a)))
            net.wait(self.on, self.all_of(self.part(net.chip_ab)))
        self.cross()

    def cross(self):
        self.to_core = self.give(self.block(self.net.core), self.net.sibling())

    def end(self):
        if self.at_once:
            count = self.piece * (self.net.group - 1)
            self.net.wait(self.to_all, self.all_of(pl.ds(0, count)))
        else:
            self.net.wait(self.to_core, self.all_of(self.block(1 - self.net.core)))


class Gather:
    def __init__(self, net, buf, by_core=False):
        self.net, self.buf, self.by_core = net, buf, by_core
        planes = [buf.at[net.src(k)] for k in range(1, net.shards)]
        self.spread = Spread(net, planes, lambda rows: buf.at[0 : net.shards - 1, rows])
        self.rows = self.spread.block(net.core) if by_core else self.spread.part(net.chip)

    def start(self):
        net = self.net
        own = self.buf.at[net.z, self.rows]
        self.far = net.arrival()
        for k in range(1, net.shards):
            net.send(own, own, self.far, net.far(k), net.i)

    def begin(self):
        self.net.wait(self.far, self.spread.all_of(self.rows))
        if self.by_core:
            self.spread.cross()
        else:
            self.spread.begin()

    def pass_on(self):
        if not self.by_core:
            self.spread.pass_on()

    def share(self):
        if not self.by_core:
            self.spread.share()

    def end(self):
        self.spread.end()


class Absent:
    def start(self):
        pass

    begin = pass_on = share = end = start

    def to(self, name):
        pass


class Reduce:
    def __init__(self, net, buffers, out, far_first, halving, at_once, straight, store):
        self.net, self.out, self.store = net, out, store
        self.grad, self.from_core, self.from_a, self.from_b = buffers[0:4]
        self.from_group, self.from_far = buffers[4:6]
        self.far_first, self.halving = far_first, halving
        self.piece = self.grad.shape[1] // net.group
        self.half = self.grad.shape[1] // 2
        self.spread = Spread(net, [out], lambda rows: out.at[rows], at_once, straight)
        near = [(NEAR_B, self.take_b)]
        if net.dims == 2:
            near = [(NEAR_A, self.take_a)] + near
        if halving:
            rounds = net.shards.bit_length() - 1
            far = [(FAR_0 + k, functools.partial(self.take_half, k)) for k in range(rounds)]
        else:
            far = [(FAR_0, self.take_far)]
        steps = far + near if far_first else near + far
        name, step = steps[-1]
        steps[-1] = (name, functools.partial(self.last, step))
        after = [(PASS, self.spread.pass_on), (SHARE, self.spread.share)]
        after = [] if at_once else after if net.dims == 2 else after[1:]
        self.steps = [(START, self.start), (CORE, self.take_core), *steps, *after]
        self.steps.append((END, self.finish))
        far, near = [FAR_0, FAR_1, FAR_2], [NEAR_A, NEAR_B]
        order = far + near if far_first else near + far
        order = [START, CORE, *order, PASS, SHARE, END]
        self.rank = {name: k for k, name in enumerate(order)}

    def to(self, name):
        while self.steps and self.rank[self.steps[0][0]] <= self.rank[name]:
            self.steps.pop(0)[1]()

    def last(self, step):
        step()
        self.spread.begin()

    def finish(self):
        self.spread.end()
        self.store.start()

    def first(self, chip):
        return (self.net.core * self.net.pairs + chip) * self.piece

    def rows(self, chip):
        return many(self.first(chip), self.piece, self.piece)

    def planes(self, after_far):
        if after_far:
            return [(self.net.z, 0)]
        return [(s, s) for s in range(self.net.shards)]

    def add(self, first, count, planes, parts):
        lines = 16

        def one(step, carry):
            at = pl.multiple_of(step * lines, lines)
            rows = many(first + at, lines, lines)
            for here, there in planes:
                value = self.grad[here, rows].astype(F32)
                for part in parts:
                    value = value + part[there, pl.ds(at, lines)].astype(F32)
                self.grad[here, rows] = value.astype(BF16)
            return carry

        lax.fori_loop(0, count // lines, one, 0)

    def cut(self, rows, after_far):
        if after_far:
            return self.grad.at[pl.ds(self.net.z, 1), rows]
        return self.grad.at[:, rows]

    def start(self):
        net = self.net
        away = many((1 - net.core) * self.half, self.half, self.half)
        self.to_core = net.arrival()
        net.send(self.grad.at[:, away], self.from_core, self.to_core, net.z, net.sibling())

    def take_core(self):
        net = self.net
        net.wait(self.to_core, self.from_core)
        self.add(net.core * self.half, self.half, self.planes(False), [self.from_core])
        if self.far_first:
            own = many(net.core * self.half, self.half, self.half)
            self.send_far(own)
        else:
            self.send_near(False)

    def send_near(self, after_far):
        net = self.net
        if net.dims == 2:
            self.to_a = [net.arrival(), net.arrival()]
            for k, chip in ((1, net.chip_ab), (0, net.chip_a)):
                net.send(
                    self.cut(self.rows(chip), after_far),
                    self.from_a.at[k],
                    self.to_a[k],
                    net.z,
                    net.peer(net.chip_a),
                )
        elif net.dims == 1:
            self.send_b(after_far)

    def send_b(self, after_far):
        net = self.net
        self.to_b = net.arrival()
        rows = self.rows(net.chip_b)
        net.send(
            self.cut(rows, after_far), self.from_b, self.to_b, net.z, net.peer(net.chip_b)
        )

    def take_a(self):
        net = self.net
        for k, chip in ((1, net.chip_b), (0, net.chip)):
            net.wait(self.to_a[k], self.from_a.at[k])
            self.add(self.first(chip), self.piece, self.planes(self.far_first), [self.from_a.at[k]])
            if k:
                self.send_b(self.far_first)

    def take_b(self):
        net = self.net
        if net.dims:
            net.wait(self.to_b, self.from_b)
            self.add(
                self.first(net.chip), self.piece, self.planes(self.far_first), [self.from_b]
            )
        own = self.rows(net.chip)
        step, at = 1, 0
        while step < net.groups:
            peer = net.i + net.group * step * (1 - 2 * ((net.grp // step) % 2))
            arrived = net.arrival()
            one = net.send(
                self.cut(own, self.far_first), self.from_group.at[at], arrived, net.z, peer
            )
            net.wait(arrived, self.from_group.at[at])
            net.left(one)
            self.add(
                self.first(net.chip),
                self.piece,
                self.planes(self.far_first),
                [self.from_group.at[at]],
            )
            step, at = step * 2, at + 1
        if self.far_first:
            self.out[own, :] = self.grad[net.z, own]
        else:
            self.send_far(own)

    def send_far(self, own):
        net = self.net
        self.own = own
        if self.halving:
            self.send_half(0)
            return
        self.to_far = net.arrival()
        for k in range(1, net.shards):
            net.send(
                self.grad.at[pl.ds(net.far(k), 1), own],
                self.from_far.at[pl.ds(k - 1, 1)],
                self.to_far,
                net.far(k),
                net.i,
            )

    def half_at(self, turn):
        step = 1 << turn
        count = self.net.shards // (2 * step)
        return step, count, self.net.shards - 2 * count

    def send_half(self, turn):
        net = self.net
        step, count, at = self.half_at(turn)
        partner = net.z + step * (1 - 2 * ((net.z // step) % 2))
        self.to_far = net.arrival()
        for k in range(count):
            plane = partner % (2 * step) + 2 * step * k
            net.send(
                self.grad.at[pl.ds(plane, 1), self.own],
                self.from_far.at[pl.ds(at + k, 1)],
                self.to_far,
                partner,
                net.i,
            )

    def take_half(self, turn):
        net = self.net
        step, count, at = self.half_at(turn)
        parts = self.from_far.at[pl.ds(at, count)]
        net.wait(self.to_far, parts)
        planes = [(net.z % (2 * step) + 2 * step * k, k) for k in range(count)]
        first, size = (
            (net.core * self.half, self.half)
            if self.far_first
            else (self.first(net.chip), self.piece)
        )
        self.add(first, size, planes, [parts])
        if count > 1:
            self.send_half(turn + 1)
        else:
            self.far_done()

    def take_far(self):
        net = self.net
        net.wait(self.to_far, self.from_far)
        parts = [self.from_far.at[pl.ds(k, 1)] for k in range(net.shards - 1)]
        if self.far_first:
            self.add(net.core * self.half, self.half, self.planes(True), parts)
        else:
            self.add(self.first(net.chip), self.piece, self.planes(True), parts)
        self.far_done()

    def far_done(self):
        if self.far_first:
            self.send_near(True)
        else:
            self.out[self.own, :] = self.grad[self.net.z, self.own]


def reduce_scratch(shards, group, rounds, rows, wide, far_first):
    pairs = group // 2
    piece, half = rows // group, rows // 2
    planes = 1 if far_first else shards
    tiny = (1, 16, 128)
    return [
        pltpu.VMEM((shards, rows, wide), BF16),
        pltpu.VMEM((shards, half, wide), BF16),
        pltpu.VMEM((2, planes, piece, wide) if pairs == 4 else tiny, BF16),
        pltpu.VMEM((planes, piece, wide), BF16),
        pltpu.VMEM((rounds, planes, piece, wide) if rounds else tiny, BF16),
        pltpu.VMEM((shards - 1, half if far_first else piece, wide), BF16),
    ]


def layer_kernel(
    shards,
    ctxs,
    group,
    chunk_far,
    len_ref,
    x_hbm,
    cot_hbm,
    picks_hbm,
    g1_hbm,
    b1_hbm,
    g2_hbm,
    b2_hbm,
    bo_hbm,
    bi_hbm,
    wq_hbm,
    wkv_hbm,
    wr_hbm,
    wo_hbm,
    wi_hbm,
    wout_hbm,
    out_hbm,
    gin_hbm,
    chunk_hbm,
    wo_hbm_out,
    q_hbm,
    kv_hbm,
    x_ref,
    cot_ref,
    picks_ref,
    g1_ref,
    b1_ref,
    g2_ref,
    b2_ref,
    bo_ref,
    bi_ref,
    wq_st,
    wkv_st,
    wr_st,
    wi_st,
    stage,
    wk,
    wqs,
    wo,
    wc,
    vec_st,
    vecs,
    normed,
    normed_t,
    q_t,
    sel_a,
    heads_t,
    small,
    kvall,
    kvt,
    pads,
    hrow,
    linv,
    sbuf,
    ebuf,
    dkv,
    from_sib,
    from_kv,
    mixed_t,
    xhat2,
    n2,
    n2_t,
    gfin_low,
    biases,
    g_t,
    sums_c,
    sums_o,
    sums_q,
    sums_k,
    out_ref,
    gin_ref,
    chunk_out,
    wo_out,
    q_out,
    kv_out,
    vec_g,
    local_sem,
    send_sem,
    recv_sem,
):
    net = Net(shards, ctxs, group, send_sem, recv_sem)
    z, c = net.z, net.i
    tokens, width = x_ref.shape
    seg = tokens // 2
    half = seg // 2
    blocks = 2 * ctxs
    ws = width // shards
    wos = wo.shape[1]
    fs = wout_hbm.shape[0]
    scale = HS ** (-0.5)
    chunks = fs // UNIT
    panels = shards * UNIT // PANEL
    per_panel = PANEL // UNIT
    lanes = TOP * half
    wide = E * HS
    split = wide // 2
    sum_c, sum_q = [one[0] for one in sums_c], [one[0] for one in sums_q]
    sum_o, sum_k = sums_o[0], sums_k[0]
    vec_line = E
    bias_line = vec_line + 5
    per_unit = UNIT // ws
    near_steps = ctxs // 2

    def local(src, dst, at):
        return pltpu.make_async_copy(src, dst, local_sem.at[at])

    net.greet()
    wo_st, wout_st = stage.at[0:wos], stage.at[wos : wos + fs]
    resid, acc_a, acc_b = (stage.at[k * tokens : (k + 1) * tokens] for k in range(3))
    loads = {}
    for at, (src, dst) in enumerate(
        (
            (wkv_hbm, wkv_st),
            (wr_hbm, wr_st),
            (wq_hbm, wq_st),
            (g1_hbm, g1_ref),
            (b1_hbm, b1_ref),
            (g2_hbm, g2_ref),
            (b2_hbm, b2_ref),
            (bo_hbm, bo_ref),
            (bi_hbm, bi_ref),
            (x_hbm, x_ref),
            (picks_hbm, picks_ref),
            (wo_hbm, wo_st),
            (wi_hbm, wi_st),
            (wout_hbm, wout_st),
            (cot_hbm, cot_ref),
        )
    ):
        loads[id(dst)] = local(src, dst, at)
        loads[id(dst)].start()
    loads[id(wkv_st)].wait()
    wk[z] = wkv_st[...].astype(BF16)
    vec_st[...] = jnp.zeros(vec_st.shape, F32)
    for row, ref in enumerate((g1_ref, b1_ref, g2_ref, b2_ref, bo_ref)):
        loads[id(ref)].wait()
        vec_st[row : row + 1, 0:ws] = ref[...]
    loads[id(bi_ref)].wait()
    for k in range(chunks):
        vec_st[5 + k : 6 + k, :] = bi_ref[:, k * UNIT : (k + 1) * UNIT]
    own_vec = vecs.at[z]
    own_vec[...] = vec_st[...].astype(BF16)
    net.greeted()
    gather_k, gather_o = Gather(net, wk, True), Gather(net, wo)
    gather_q = [Gather(net, one) for one in wqs]
    gather_c = [Gather(net, wc.at[k], k == chunks - 1) for k in range(chunks)]
    gather_k.start()
    vec_slot = net.arrival()
    for k in range(1, shards):
        net.send(own_vec, own_vec, vec_slot, net.far(k), net.i)
    loads[id(wq_st)].wait()
    loads[id(wr_st)].wait()
    for k in range(2):
        wqs[k][z, :, 0:split] = wq_st[:, k * split : (k + 1) * split].astype(BF16)
    padded = jnp.concatenate([wr_st[...], jnp.zeros((128 - E, ws), F32)], axis=0)
    wqs[1][z, :, split:] = padded.T.astype(BF16)

    loads[id(x_ref)].wait()
    x = x_ref[...].astype(F32)
    mean1 = jnp.mean(x, axis=1, keepdims=True)
    cen = x - mean1
    small[0, :, 0:1] = lax.rsqrt(jnp.mean(cen * cen, axis=1, keepdims=True) + NORM_EPS)
    small[0, :, 2:3] = mean1

    def first_hat():
        return (x_ref[...].astype(F32) - small[0, :, 2:3]) * small[0, :, 0:1]

    for ref in (wo_st, wi_st, wout_st):
        loads[id(ref)].wait()
    wo[z] = wo_st[...].astype(BF16)
    for k in range(chunks):
        wc[k, z, 0:UNIT] = wout_st[k * UNIT : (k + 1) * UNIT].astype(BF16)
        for s in range(shards):
            first = UNIT + (s // per_panel) * ws
            at = (s % per_panel) * UNIT
            wc[k, z, first : first + ws, at : at + UNIT] = wi_st[
                :, s * fs + k * UNIT : s * fs + (k + 1) * UNIT
            ].astype(BF16)
    for one in gather_q:
        one.start()
    gather_k.begin()
    net.wait(vec_slot, vecs.at[0 : shards - 1])

    vec_all = [vecs[s].astype(F32) for s in range(shards)]

    def whole(row):
        return jnp.concatenate([one[row : row + 1, 0:ws] for one in vec_all], axis=1)

    gain1, bias1, gain2, bias2, bias_out = (whole(row) for row in range(5))
    for k in range(chunks):
        for p in range(panels):
            biases[k * panels + p : k * panels + p + 1, :] = jnp.concatenate(
                [one[5 + k : 6 + k] for one in vec_all[p * per_panel : (p + 1) * per_panel]],
                axis=1,
            )
    norm_value = first_hat() * gain1 + bias1
    normed[...] = norm_value.astype(BF16)
    normed_t[...] = norm_value.T.astype(BF16)
    gather_q[0].begin()
    def at_block(ref, block):
        return ref.at[block // 2, :, block % 2]

    def my_block(h):
        return c if h == 0 else blocks - 1 - c

    def core_blocks(ref, core):
        return ref.at[0:near_steps, :, core], ref.at[near_steps:ctxs, :, 1 - core]

    kv_slot, kv_cross, dkv_cross, dkv_near = (net.arrival() for _ in range(4))
    kv_sent = []

    def do_kvproj():
        kv_own = dot(normed[...], wk[...].reshape(width, 2 * HS)).astype(BF16)

        for h in range(2):
            block = my_block(h)
            for s in range(2):
                first = s * seg + h * half
                kvall[block // 2, s, block % 2] = kv_own[first : first + half]
        for step in range(1, near_steps):
            for block in (c, blocks - 1 - c):
                ref = at_block(kvall, block)
                kv_sent.append(net.send(ref, ref, kv_slot, z, (c + 2 * step) % ctxs))

    def do_kvcross():
        net.wait(kv_slot, kvall.at[0 : near_steps - 1])
        for part in core_blocks(kvall, net.core):
            kv_sent.append(net.send(part, part, kv_cross, z, net.sibling()))

    def do_kvwait():
        net.wait(kv_cross, kvall.at[0:near_steps])

    def do_turn():
        def turn(step, carry):
            for s in range(2):
                keys = kvall[step, s].reshape(2 * half, 2 * HS)
                kvt[step, s] = keys.astype(F32).T.astype(BF16)
                dkv[step, s] = jnp.zeros((2 * half, 2 * HS), F32)
            return carry

        lax.fori_loop(0, ctxs, turn, 0, unroll=4)

    def project_queries(part):
        def query_tile(n, carry):
            cols = many(n * 256, 256, 256)
            value = dot(normed[...], wqs[part][:, :, cols].reshape(width, 256))
            value = value.astype(BF16).astype(F32).T
            for k in range(4):
                q_t[part * (E // 2) + n * 4 + k] = value[k * HS : (k + 1) * HS]
            return carry

        lax.fori_loop(0, split // 256, query_tile, 0, unroll=True)

    def do_gates():
        logits_t = dot(normed[...], wqs[1][:, :, split:].reshape(width, 128)).T
        loads[id(picks_ref)].wait()
        picks = jnp.concatenate([picks_ref[0], picks_ref[1]], axis=1).astype(F32)
        picked = jnp.zeros((TOP, tokens), F32)
        for e in range(E):
            picked = jnp.where(picks == float(e), logits_t[e : e + 1, :], picked)
        top = jnp.max(picked, axis=0, keepdims=True)
        gexp = jnp.exp(picked - top)
        small[1, 0:TOP, 0:tokens] = gexp / jnp.sum(gexp, axis=0, keepdims=True)
        small[1, TOP : 2 * TOP, 0:tokens] = picks

    def choose(src, store):
        def one(j, carry):
            pick = small[1, pl.ds(TOP + j, 1), 0:tokens]
            value = jnp.zeros((HS, tokens), F32)
            for e in range(E):
                value = jnp.where(pick == float(e), src[e], value)
            store(j, value)
            return carry

        lax.fori_loop(0, TOP, one, 0, unroll=2)

    def spread_back(src, store):
        def one(e, carry):
            value = jnp.zeros((HS, tokens), F32)
            for j in range(TOP):
                pick = small[1, TOP + j : TOP + j + 1, 0:tokens]
                value = jnp.where(pick == e.astype(F32), src[j], value)
            store(e, value)
            return carry

        lax.fori_loop(0, E, one, 0, unroll=4)

    low_lane = lax.broadcasted_iota(jnp.int32, (HS, 2 * half), 1) < half

    def swap(one, two):
        return (
            jnp.where(low_lane, one, pltpu.roll(two, half, 1)),
            jnp.where(low_lane, pltpu.roll(one, half, 1), two),
        )

    def store_query(j, value):
        sel_a[j] = value * scale

    def do_choose():
        choose(q_t, store_query)
        for s in range(2):
            for pair in range(TOP // 2):
                halves = swap(
                    sel_a[2 * pair, :, s * seg : (s + 1) * seg],
                    sel_a[2 * pair + 1, :, s * seg : (s + 1) * seg],
                )
                for h in range(2):
                    pads[2 * s + h, 0:HS, pair * 128 : (pair + 1) * 128] = halves[h].astype(BF16)
        for sh in range(4):
            pads[sh, HS:, 0:lanes] = jnp.zeros((HS, lanes), BF16)
            pads[sh, 0:HS, lanes:] = jnp.zeros((HS, lanes), BF16)

    offset = lax.broadcasted_iota(jnp.int32, (1, lanes), 1) % half
    key_row = lax.broadcasted_iota(jnp.int32, (4 * half, lanes), 0)
    keep_scores = sbuf.shape[1] > 1

    def place(h):
        last = (blocks - c + 3) // 4
        if h == 1:
            return last, 0
        return (c + 4) // 4, last

    def fold(value, op):
        parts = [value[8 * k : 8 * k + 8] for k in range(value.shape[0] // 8)]
        while len(parts) > 1:
            parts = [op(parts[k], parts[k + 1]) for k in range(0, len(parts), 2)]
        return parts[0]

    def keys_of(step, s):
        return kvall[pl.ds(2 * step, 2), s].reshape(4 * half, 2 * HS)

    def turned(step, s, rows):
        return jnp.concatenate([kvt[2 * step + k, s, rows] for k in range(2)], axis=1)

    tops_of = {}

    def masked(step, s, h):
        limit = jnp.minimum(my_block(h) * half + offset, len_ref[s] - 1)
        scores = dot(keys_of(step, s), pads[2 * s + h, :, 0:lanes])
        return jnp.where(key_row <= limit - step * 4 * half, scores, NEG_LARGE)

    def find_tops(h):
        def score_step(step, tops):
            result = []
            for s in range(2):
                scores = masked(step, s, h)
                if keep_scores:
                    sbuf[s, step] = scores
                result.append(jnp.maximum(tops[s], fold(scores, jnp.maximum)))
            return tuple(result)

        start = jnp.full((8, lanes), NEG_LARGE, F32)
        tops = lax.fori_loop(0, place(h)[0], score_step, (start, start))
        tops_of[h] = [jnp.max(top, axis=0, keepdims=True) for top in tops]

    def weigh(h):
        count, base = place(h)
        for s in range(2):
            hrow[2 * s + h] = jnp.zeros((HS, lanes), F32)

        def value_step(step, totals):
            result = []
            for s in range(2):
                total = totals[s]
                scores = None if keep_scores else masked(step, s, h)
                for k in range(2):
                    rows = slice(2 * half * k, 2 * half * (k + 1))
                    part = sbuf[s, step, rows] if keep_scores else scores[rows]
                    expd = jnp.exp(part - tops_of[h][s])
                    ebuf[s, base + step, rows] = expd.astype(BF16)
                    total = total + fold(expd, jnp.add)
                hrow[2 * s + h] += dot(turned(step, s, slice(HS, 2 * HS)), ebuf[s, base + step])
                result.append(total)
            return tuple(result)

        start = jnp.zeros((8, lanes), F32)
        totals = lax.fori_loop(0, count, value_step, (start, start))
        for s in range(2):
            inverse = 1.0 / jnp.sum(totals[s], axis=0, keepdims=True)
            linv[2 * s + h] = jnp.broadcast_to(inverse, (8, lanes))
            hrow[2 * s + h] = hrow[2 * s + h] * inverse

    def do_mix():
        for s in range(2):
            for pair in range(TOP // 2):
                both = swap(
                    hrow[2 * s, :, pair * 128 : (pair + 1) * 128],
                    hrow[2 * s + 1, :, pair * 128 : (pair + 1) * 128],
                )
                for k in range(2):
                    heads_t[2 * pair + k, :, s * seg : (s + 1) * seg] = both[k]
        for j in range(TOP):
            sel_a[j] = heads_t[j] * small[1, j : j + 1, 0:tokens]

        def store_mixed(e, value):
            mixed_t[e] = value.astype(BF16)

        spread_back(sel_a, store_mixed)

    experts = E // shards
    row = lax.broadcasted_iota(jnp.int32, (tokens, 1), 0)
    inner_row = row % seg
    pos = jnp.where(
        inner_row < half, c * half + inner_row, blocks * half - (c + 2) * half + inner_row
    )
    valid = (pos < jnp.where(row < seg, len_ref[0], len_ref[1])).astype(F32)

    def do_project():
        acc_a[...] = x_ref[...].astype(F32)

        def project(s, carry):
            part = mixed_t[pl.ds(s * experts, experts)].reshape(wos, tokens)
            acc_a[...] += dot(part.astype(F32).T.astype(BF16), wo[s])
            return carry

        lax.fori_loop(0, shards, project, 0, unroll=True)
        residual = acc_a[...]
        resid[...] = residual
        cen = residual - jnp.mean(residual, axis=1, keepdims=True)
        rstd2 = lax.rsqrt(jnp.mean(cen * cen, axis=1, keepdims=True) + NORM_EPS)
        small[0, :, 1:2] = rstd2
        cen = cen * rstd2
        xhat2[...] = cen
        cen = cen * gain2 + bias2
        n2[...] = cen.astype(BF16)
        n2_t[...] = cen.T.astype(BF16)

        loads[id(cot_ref)].wait()
        gfin_low[...] = (cot_ref[...].astype(F32) * valid).astype(BF16)
        acc_a[...] = jnp.zeros((tokens, width), F32)
        acc_b[...] = jnp.zeros((tokens, width), F32)
        vec_g[...] = jnp.zeros(vec_g.shape, F32)

    def feed(k, p):
        rows_in = slice(UNIT + p * ws, UNIT + (p + 1) * ws)
        planes = slice(p * per_panel, (p + 1) * per_panel)
        w_in = wc[k, :, rows_in].reshape(width, PANEL)
        w_out = wc[k, planes, 0:UNIT].reshape(PANEL, width)
        line = k * panels + p
        hidden = dot(n2[...], w_in) + biases[line : line + 1, :]
        square = hidden * hidden
        tanh = jnp.tanh(GELU_C * hidden * (1.0 + GELU_A * square))
        act = (0.5 * hidden * (1.0 + tanh)).astype(BF16)
        slope = 0.5 * (1.0 + tanh) + 0.5 * GELU_C * hidden * (1.0 - tanh * tanh) * (
            1.0 + 3.0 * GELU_A * square
        )
        gfin = gfin_low[...]
        acc_a[...] += dot(act, w_out)
        grad_hidden = (slope * dot_t(gfin, w_out)).astype(BF16)
        total = jnp.sum(grad_hidden.astype(F32), axis=0, keepdims=True)
        for a in range(per_panel):
            for q in range(per_unit):
                at = bias_line + k * per_unit + q
                first = (p * per_panel + a) * ws
                vec_g[at : at + 1, first : first + ws] = total[
                    :, a * UNIT + q * ws : a * UNIT + (q + 1) * ws
                ]
        grad_outer = dot(act.astype(F32).T.astype(BF16), gfin).astype(BF16)
        sum_c[k][planes, 0:UNIT] = grad_outer.reshape(per_panel, UNIT, width)
        grad_inner = dot(n2_t[...], grad_hidden).astype(BF16)
        sum_c[k][:, rows_in] = grad_inner.reshape(shards, ws, PANEL)
        acc_b[...] += dot_t(grad_hidden, w_in)

    outs = [local(out_ref, out_hbm, 15), local(gin_ref, gin_hbm, 16)]

    def reduction(
        refs, out, hbm, at, far_first=False, halving=False, at_once=False, straight=False
    ):
        store = local(out, hbm, at)
        outs.append(store)
        return Reduce(net, refs, out, far_first, halving, at_once, straight, store)

    reduce_c = [
        reduction(sums_c[k], chunk_out.at[k], chunk_hbm.at[k], 20 + k, chunk_far[k], True)
        for k in range(chunks)
    ]
    reduce_o = reduction(sums_o, wo_out, wo_hbm_out, 17, straight=False)
    reduce_q = [
        reduction(
            sums_q[k],
            q_out[k],
            q_hbm.at[:, k * split : (k + 1) * split],
            20 + chunks + k,
            straight=True,
        )
        for k in range(2)
    ]
    reduce_k = reduction(sums_k, kv_out, kv_hbm, 19, at_once=True)

    def do_norm2():
        out_ref[...] = (valid * (resid[...] + acc_a[...] + bias_out)).astype(BF16)
        outs[0].start()
        gfin = cot_ref[...].astype(F32) * valid
        vec_g[vec_line + 4 : vec_line + 5, :] = jnp.sum(gfin, axis=0, keepdims=True)
        grad_n2 = acc_b[...]
        vec_g[vec_line + 3 : vec_line + 4, :] = jnp.sum(grad_n2, axis=0, keepdims=True)
        vec_g[vec_line + 2 : vec_line + 3, :] = jnp.sum(grad_n2 * xhat2[...], axis=0, keepdims=True)
        grad_hat = grad_n2 * gain2
        grad_hat = grad_hat - jnp.mean(grad_hat, axis=1, keepdims=True)
        grad_hat = grad_hat - xhat2[...] * jnp.mean(grad_hat * xhat2[...], axis=1, keepdims=True)
        grad_residual = gfin + grad_hat * small[0, :, 1:2]
        resid[...] = grad_residual
        n2[...] = grad_residual.astype(BF16)

    def do_branch():
        def branch(s, carry):
            part = mixed_t[pl.ds(s * experts, experts)].reshape(wos, tokens)
            sum_o[s] = dot(part, n2[...]).astype(BF16)
            grad = dot_t(wo[s], n2[...])
            q_t[pl.ds(s * experts, experts)] = grad.reshape(experts, HS, tokens)
            return carry

        lax.fori_loop(0, shards, branch, 0, unroll=2)

    def do_heads():
        def store_head_grad(j, value):
            sel_a[j] = value * small[1, pl.ds(j, 1), 0:tokens]
            small[1, pl.ds(2 * TOP + j, 1), 0:tokens] = jnp.sum(
                value * heads_t[j], axis=0, keepdims=True
            )

        choose(q_t, store_head_grad)
        gates = small[1, 0:TOP, 0:tokens]
        grad_gates = small[1, 2 * TOP : 3 * TOP, 0:tokens]
        grad_picked = gates * (grad_gates - jnp.sum(gates * grad_gates, axis=0, keepdims=True))
        picks = small[1, TOP : 2 * TOP, 0:tokens]
        g_t[wide : wide + 128, :] = jnp.zeros((128, tokens), BF16)
        grad_logits = [
            jnp.sum(jnp.where(picks == float(e), grad_picked, 0.0), axis=0, keepdims=True)
            for e in range(E)
        ]
        grad_logits += [jnp.zeros((1, tokens), F32)] * (32 - E)
        g_t[wide : wide + 32, :] = jnp.concatenate(grad_logits, axis=0).astype(BF16)
        for s in range(2):
            for pair in range(TOP // 2):
                halves = swap(
                    sel_a[2 * pair, :, s * seg : (s + 1) * seg],
                    sel_a[2 * pair + 1, :, s * seg : (s + 1) * seg],
                )
                at = pair * 128
                for h in range(2):
                    sh = 2 * s + h
                    grad = (halves[h] * linv[sh, 0:1, at : at + 128]).astype(BF16)
                    pads[sh, HS:, lanes + at : lanes + at + 128] = grad
                    linv[sh, 1:2, at : at + 128] = jnp.sum(
                        grad.astype(F32) * hrow[sh, :, at : at + 128], axis=0, keepdims=True
                    )

    def attend_back(h):
        count, base = place(h)
        deltas = [linv[2 * s + h, 1:2, :] for s in range(2)]
        for s in range(2):
            hrow[2 * s + h] = jnp.zeros((HS, lanes), F32)

        def grad_step(step, carry):
            for s in range(2):
                sh = 2 * s + h
                parts = []
                for k in range(2):
                    expd = ebuf[s, base + step, 2 * half * k : 2 * half * (k + 1)]
                    keys = kvall[2 * step + k, s].reshape(2 * half, 2 * HS)
                    grad_prob = dot(keys, pads[sh, :, lanes:])
                    parts.append((expd.astype(F32) * (grad_prob - deltas[s])).astype(BF16))
                grad_score = jnp.concatenate(parts, axis=0)
                grad = dot_t(grad_score, pads[sh, :, 0:lanes])
                grad = grad + dot_t(ebuf[s, base + step], pads[sh, :, lanes:])
                dkv[pl.ds(2 * step, 2), s] += grad.reshape(2, 2 * half, 2 * HS)
                hrow[sh] += dot(turned(step, s, slice(0, HS)), grad_score)
            return carry

        lax.fori_loop(0, count, grad_step, 0)

    def do_dsend():
        for one in kv_sent:
            net.left(one)

        def lower(step, carry):
            kvall[step] = dkv[step].astype(BF16).reshape(2, 2, half, 2 * HS)
            return carry

        lax.fori_loop(0, ctxs, lower, 0)
        for k, part in enumerate(core_blocks(kvall, 1 - net.core)):
            net.send(part, from_sib.at[k], dkv_cross, z, net.sibling())

    def do_gradq():
        for s in range(2):
            for pair in range(TOP // 2):
                both = swap(
                    hrow[2 * s, :, pair * 128 : (pair + 1) * 128],
                    hrow[2 * s + 1, :, pair * 128 : (pair + 1) * 128],
                )
                for k in range(2):
                    q_t[2 * pair + k, :, s * seg : (s + 1) * seg] = both[k] * scale

        def store_grad_query(e, value):
            g_t[many(e * HS, HS, HS), :] = value.astype(BF16)

        spread_back(q_t, store_grad_query)

    def query_grads(part):
        def query_grad(n, carry):
            rows = many(part * split + n * 256, 256, 256)
            grad = dot_t(normed_t[...], g_t[rows, :]).astype(BF16)
            sum_q[part][:, :, many(n * 256, 256, 256)] = grad.reshape(shards, ws, 256)
            return carry

        lax.fori_loop(0, split // 256, query_grad, 0, unroll=True)

    def do_dnear():
        net.wait(dkv_cross, from_sib)

        def add_sibling(step, carry):
            for k, sub in enumerate((net.core, 1 - net.core)):
                at = step + k * near_steps
                rows = many(sub * half, half, half)
                for s in range(2):
                    value = dkv[at, s, rows] + from_sib[k, step, s].astype(F32)
                    dkv[at, s, rows] = value
                    kvall[at, s, sub] = value.astype(BF16)
            return carry

        lax.fori_loop(0, near_steps, add_sibling, 0)
        for step in range(1, near_steps):
            peer = (c + 2 * step) % ctxs
            for h, block in enumerate((peer, blocks - 1 - peer)):
                net.send(at_block(kvall, block), from_kv.at[step - 1, h], dkv_near, z, peer)

    def do_ngrad():
        part = dot(wqs[0][...].reshape(width, split), g_t[0:split, :])
        part = part + dot(wqs[1][...].reshape(width, split + 128), g_t[split:, :])
        heads_t[...] = part.reshape(heads_t.shape)

    def do_dwait():
        net.wait(dkv_near, from_kv)

    def do_kvgrad():
        for h in range(2):
            block = my_block(h)
            for s in range(2):
                value = dkv[block // 2, s, many((block % 2) * half, half, half)]
                for step in range(1, near_steps):
                    value = value + from_kv[step - 1, h, s].astype(F32)
                first = s * seg + h * half
                acc_a[first : first + half, 0:128] = value
        grad_kv = acc_a[:, 0:128].T.astype(BF16)
        part = heads_t[...].reshape(width, tokens) + dot(wk[...].reshape(width, 2 * HS), grad_kv)
        grad_normed = part.T
        hat = first_hat()
        vec_g[vec_line : vec_line + 1, :] = jnp.sum(grad_normed * hat, axis=0, keepdims=True)
        vec_g[vec_line + 1 : vec_line + 2, :] = jnp.sum(grad_normed, axis=0, keepdims=True)
        value = dot_t(normed_t[...], grad_kv)
        sum_k[:, :, 0 : 2 * HS] = value.astype(BF16).reshape(shards, ws, 2 * HS)
        value = dot_t(normed_t[...], g_t[wide:, :]) + vec_g[...].T
        sum_k[:, :, 2 * HS :] = value.astype(BF16).reshape(shards, ws, 128)
        acc_b[...] = grad_normed

    def do_gin():
        hat = first_hat()
        grad_normed = acc_b[...]
        grad_hat = grad_normed * gain1
        grad_hat = grad_hat - jnp.mean(grad_hat, axis=1, keepdims=True)
        grad_hat = grad_hat - hat * jnp.mean(grad_hat * hat, axis=1, keepdims=True)
        gin_ref[...] = resid[...] + grad_hat * small[0, :, 0:1]
        outs[1].start()

    def feed_all(k):
        if k < chunks:
            for p in range(panels):
                feed(k, p)

    absent = [Absent()] * 4
    gc0, gc1, gc2, gc3 = (gather_c + absent)[0:4]
    rc0, rc1, rc2, rc3 = (reduce_c + absent)[0:4]
    (gq0, gq1), (rq0, rq1) = gather_q, reduce_q
    go, gk, ro, rk = gather_o, gather_k, reduce_o, reduce_k
    gk.end()
    do_kvproj()
    go.start()
    gq1.begin()
    gq0.pass_on()
    gc0.start()
    do_kvcross()
    gq1.pass_on()
    gc1.start()
    go.begin()
    gc2.start()
    gq0.share()
    do_kvwait()
    do_turn()
    gc0.begin()
    gq0.end()
    project_queries(0)
    gq1.share()
    gc1.begin()
    gq1.end()
    gc3.start()
    project_queries(1)
    do_gates()
    go.pass_on()
    gc2.begin()
    do_choose()
    gc0.pass_on()
    find_tops(1)
    gc1.pass_on()
    weigh(1)
    go.share()
    gc2.pass_on()
    find_tops(0)
    weigh(0)
    gc0.share()
    do_mix()
    go.end()
    do_project()
    gc1.share()
    gc0.end()
    feed_all(0)
    gc2.share()
    rc0.to(START)
    gc3.begin()
    gc3.pass_on()
    gc3.share()
    gc1.end()
    feed_all(1)
    rc1.to(START)
    gc2.end()
    feed_all(2)
    rc2.to(START)
    rc0.to(CORE)
    gc3.end()
    feed_all(3)
    rc3.to(START)
    rc1.to(CORE)
    do_norm2()
    rc2.to(CORE)
    do_branch()
    ro.to(START)
    rc3.to(CORE)
    do_heads()
    attend_back(1)
    attend_back(0)
    ro.to(CORE)
    do_dsend()
    do_gradq()
    query_grads(0)
    rq0.to(START)
    query_grads(1)
    rq1.to(START)
    rc2.to(NEAR_A)
    rc3.to(NEAR_A)
    do_dnear()
    do_ngrad()
    rc0.to(FAR_0)
    rc1.to(FAR_0)
    ro.to(NEAR_A)
    rc2.to(NEAR_B)
    rc3.to(NEAR_B)
    rq0.to(CORE)
    rq1.to(CORE)
    do_dwait()
    do_kvgrad()
    rk.to(START)
    do_gin()
    rk.to(CORE)
    rc0.to(FAR_1)
    rc1.to(FAR_1)
    ro.to(NEAR_B)
    rq0.to(NEAR_A)
    rq1.to(NEAR_A)
    rc2.to(FAR_0)
    rc3.to(FAR_0)
    rc0.to(NEAR_A)
    rc1.to(NEAR_A)
    rk.to(NEAR_A)
    rq0.to(NEAR_B)
    rq1.to(NEAR_B)
    ro.to(FAR_0)
    rc0.to(NEAR_B)
    rc1.to(NEAR_B)
    rc2.to(FAR_1)
    rc3.to(FAR_1)
    rk.to(NEAR_B)
    ro.to(PASS)
    rc0.to(PASS)
    rc1.to(PASS)
    rc2.to(PASS)
    rc3.to(PASS)
    rq0.to(FAR_0)
    rq1.to(FAR_0)
    rk.to(FAR_0)
    ro.to(SHARE)
    rc0.to(SHARE)
    rc1.to(SHARE)
    rc2.to(SHARE)
    rc3.to(SHARE)
    rq0.to(PASS)
    rq1.to(PASS)
    rc1.to(END)
    rc2.to(END)
    rc0.to(END)
    rc3.to(END)
    rq0.to(SHARE)
    rq1.to(SHARE)
    rk.to(END)
    ro.to(END)
    rq0.to(END)
    rq1.to(END)
    for one in (*reduce_c, ro, *reduce_q, rk):
        one.to(END)
    net.finish()
    for one in outs:
        one.wait()


def unpack_kernel(shards, *refs):
    ins, outs = refs[0:6], refs[6:20]
    in_st, out_st, sem = refs[20:26], refs[26:40], refs[40]
    chunks = ins[2].shape[0]
    copy = pltpu.make_async_copy
    loads = [copy(a, b, sem.at[k]) for k, (a, b) in enumerate(zip(ins, in_st)) if k != 2]
    loads.insert(2, None)
    stores = {
        k: copy(in_st[k] if k < 2 else out_st[k], outs[k], sem.at[6 + k])
        for k in range(14)
        if k != 12
    }
    chunk_in, wo_in, q_in, kv_in = in_st[2:]
    g1_ref, b1_ref, kv_ref, q_ref, r_ref, wo_ref, g2_ref, b2_ref = out_st[2:10]
    wi_ref, bi_ref, wout_ref, bo_ref = out_st[10:]
    ws, fs = q_ref.shape[0], wout_ref.shape[0]
    per_panel = PANEL // UNIT
    chunk_loads = [
        copy(ins[2].at[k], chunk_in.at[k], sem.at[20 + k]) for k in range(chunks)
    ]
    for one in chunk_loads:
        one.start()
    for k in (3, 4, 5, 1, 0):
        loads[k].start()
    for k in range(chunks):
        chunk_loads[k].wait()
        rows = slice(k * UNIT, (k + 1) * UNIT)
        wout_ref[rows, :] = chunk_in[k, 0:UNIT].astype(F32)
        stores[20 + k] = copy(wout_ref.at[rows], outs[12].at[rows], sem.at[20 + chunks + k])
        stores[20 + k].start()
        for s in range(shards):
            first = UNIT + (s // per_panel) * ws
            at = (s % per_panel) * UNIT
            wi_ref[:, s * fs + k * UNIT : s * fs + (k + 1) * UNIT] = chunk_in[
                k, first : first + ws, at : at + UNIT
            ].astype(F32)
    stores[10].start()
    loads[3].wait()
    wo_ref[...] = wo_in[...].astype(F32)
    stores[7].start()
    loads[4].wait()
    q_ref[...] = q_in[...].astype(F32)
    stores[5].start()
    loads[5].wait()
    kv_ref[...] = kv_in[:, 0 : 2 * HS].astype(F32)
    stores[4].start()
    turned = kv_in[:, 2 * HS :].astype(F32).T
    r_ref[...] = turned[0:E]
    stores[6].start()
    for row, at, ref in (
        (0, 2, g1_ref),
        (1, 3, b1_ref),
        (2, 8, g2_ref),
        (3, 9, b2_ref),
        (4, 13, bo_ref),
    ):
        ref[...] = turned[E + row : E + row + 1]
        stores[at].start()
    for line in range(fs // ws):
        bi_ref[:, line * ws : (line + 1) * ws] = turned[E + 5 + line : E + 6 + line]
    stores[11].start()
    loads[1].wait()
    stores[1].start()
    loads[0].wait()
    stores[0].start()
    for one in stores.values():
        one.wait()


def on_device(
    shards,
    ctxs,
    tokens,
    lengths,
    expert_picks,
    first_gain,
    first_bias,
    kv_weight,
    query_weight,
    router_weight,
    output_weight,
    second_gain,
    second_bias,
    inner_weight,
    inner_bias,
    outer_weight,
    outer_bias,
    cotangent,
):
    slots, seg, width = tokens.shape
    count = slots * seg
    half = seg // 2
    lanes = TOP * half
    ws = width // shards
    wos = output_weight.shape[0]
    fs = outer_weight.shape[0]
    group = min(ctxs, ws // 16, 8)
    pairs, groups = group // 2, ctxs // group
    rounds = groups.bit_length() - 1
    chunks = fs // UNIT
    panels = shards * UNIT // PANEL
    chunk_rows = UNIT + panels * ws
    wide = E * HS
    chunk_far = [k < 2 for k in range(chunks)]
    keep_scores = ctxs * seg * slots * lanes * 4 <= 8 * 1024 * 1024
    shapes_mid = (
        jax.ShapeDtypeStruct((count, width), BF16),
        jax.ShapeDtypeStruct((count, width), F32),
        jax.ShapeDtypeStruct((chunks, chunk_rows, PANEL), BF16),
        jax.ShapeDtypeStruct((wos, width), BF16),
        jax.ShapeDtypeStruct((ws, wide), BF16),
        jax.ShapeDtypeStruct((ws, 256), BF16),
    )

    smem = pl.BlockSpec(memory_space=pltpu.SMEM)
    anywhere = pl.BlockSpec(memory_space=pl.ANY)
    arrivals = 2 + (3 + chunks) * 5 + 1 + 4 + (4 + chunks) * (8 + rounds + shards.bit_length() - 1)
    scratch = [
        pltpu.VMEM((count, width), BF16),
        pltpu.VMEM((count, width), BF16),
        pltpu.VMEM((slots, TOP, seg), jnp.int32),
        *[pltpu.VMEM((1, ws), F32)] * 5,
        pltpu.VMEM((1, fs), F32),
        pltpu.VMEM(query_weight.shape, F32),
        pltpu.VMEM(kv_weight.shape, F32),
        pltpu.VMEM((E, ws), F32),
        pltpu.VMEM(inner_weight.shape, F32),
        pltpu.VMEM((max(wos + fs, 3 * count), width), F32),
        pltpu.VMEM((shards, ws, 2 * HS), BF16),
        [pltpu.VMEM((shards, ws, wide // 2 + 128 * k), BF16) for k in range(2)],
        pltpu.VMEM((shards, wos, width), BF16),
        pltpu.VMEM((chunks, shards, chunk_rows, PANEL), BF16),
        pltpu.VMEM((16, UNIT), F32),
        pltpu.VMEM((shards, 16, UNIT), BF16),
        pltpu.VMEM((count, width), BF16),
        pltpu.VMEM((width, count), BF16),
        pltpu.VMEM((E, HS, count), F32),
        pltpu.VMEM((TOP, HS, count), F32),
        pltpu.VMEM((TOP, HS, count), F32),
        pltpu.VMEM((2, count, count), F32),
        pltpu.VMEM((ctxs, slots, 2, half, 2 * HS), BF16),
        pltpu.VMEM((ctxs, slots, 2 * HS, 2 * half), BF16),
        pltpu.VMEM((4, 2 * HS, 2 * lanes), BF16),
        pltpu.VMEM((4, HS, lanes), F32),
        pltpu.VMEM((4, 8, lanes), F32),
        pltpu.VMEM((slots, ctxs // 2, 4 * half, lanes) if keep_scores else (1, 1, 8, 128), F32),
        pltpu.VMEM((slots, ctxs // 2 + 1, 4 * half, lanes), BF16),
        pltpu.VMEM((ctxs, slots, 2 * half, 2 * HS), F32),
        pltpu.VMEM((2, ctxs // 2, slots, half, 2 * HS), BF16),
        pltpu.VMEM((ctxs // 2 - 1, 2, slots, half, 2 * HS), BF16),
        pltpu.VMEM((E, HS, count), BF16),
        pltpu.VMEM((count, width), F32),
        pltpu.VMEM((count, width), BF16),
        pltpu.VMEM((width, count), BF16),
        pltpu.VMEM((count, width), BF16),
        pltpu.VMEM((8, PANEL), F32),
        pltpu.VMEM((wide + 128, count), BF16),
        [
            reduce_scratch(shards, group, rounds, chunk_rows, PANEL, chunk_far[k])
            for k in range(chunks)
        ],
        reduce_scratch(shards, group, rounds, wos, width, False),
        [reduce_scratch(shards, group, rounds, ws, wide // 2, False) for _ in range(2)],
        reduce_scratch(shards, group, rounds, ws, 256, False),
        *[pltpu.VMEM(one.shape, one.dtype) for one in shapes_mid[0:4]],
        [pltpu.VMEM((ws, wide // 2), BF16) for _ in range(2)],
        pltpu.VMEM((ws, 256), BF16),
        pltpu.VMEM((128, width), F32),
        pltpu.SemaphoreType.DMA((22 + chunks,)),
        pltpu.SemaphoreType.DMA((RING,)),
        pltpu.SemaphoreType.DMA((arrivals,)),
    ]
    results = pl.pallas_call(
        functools.partial(layer_kernel, shards, ctxs, group, chunk_far),
        out_shape=shapes_mid,
        in_specs=[smem] + [anywhere] * 15,
        out_specs=tuple([anywhere] * 6),
        scratch_shapes=scratch,
        compiler_params=pltpu.CompilerParams(
            collective_id=0, has_side_effects=True, vmem_limit_bytes=63 * 1024 * 1024
        ),
        name="layer",
    )(
        lengths,
        tokens.reshape(count, width),
        cotangent.reshape(count, width),
        jnp.swapaxes(expert_picks, 1, 2),
        first_gain.reshape(1, ws),
        first_bias.reshape(1, ws),
        second_gain.reshape(1, ws),
        second_bias.reshape(1, ws),
        outer_bias.reshape(1, ws),
        inner_bias.reshape(1, fs),
        query_weight,
        kv_weight,
        router_weight.T,
        output_weight,
        inner_weight,
        outer_weight,
    )
    vec_shape = jax.ShapeDtypeStruct((1, ws), F32)
    shapes_out = (
        jax.ShapeDtypeStruct((count, width), BF16),
        jax.ShapeDtypeStruct((count, width), F32),
        vec_shape,
        vec_shape,
        jax.ShapeDtypeStruct(kv_weight.shape, F32),
        jax.ShapeDtypeStruct(query_weight.shape, F32),
        jax.ShapeDtypeStruct((E, ws), F32),
        jax.ShapeDtypeStruct(output_weight.shape, F32),
        vec_shape,
        vec_shape,
        jax.ShapeDtypeStruct(inner_weight.shape, F32),
        jax.ShapeDtypeStruct((1, fs), F32),
        jax.ShapeDtypeStruct(outer_weight.shape, F32),
        vec_shape,
    )
    final = pl.pallas_call(
        functools.partial(unpack_kernel, shards),
        out_shape=shapes_out,
        in_specs=[anywhere] * 6,
        out_specs=tuple([anywhere] * 14),
        scratch_shapes=[pltpu.VMEM(one.shape, one.dtype) for one in (*shapes_mid, *shapes_out)]
        + [pltpu.SemaphoreType.DMA((20 + 2 * chunks,))],
        name="unpack",
    )(*results)
    final = list(final)
    final[6] = final[6].T
    shapes = (
        tokens.shape,
        tokens.shape,
        first_gain.shape,
        first_bias.shape,
        kv_weight.shape,
        query_weight.shape,
        router_weight.shape,
        output_weight.shape,
        second_gain.shape,
        second_bias.shape,
        inner_weight.shape,
        inner_bias.shape,
        outer_weight.shape,
        outer_bias.shape,
    )
    return tuple(value.reshape(shape) for value, shape in zip(final, shapes))


def solution(mesh):
    rows = P("shard", "ctx", None)
    vec, mat = P("shard"), P("shard", None)
    return jax.shard_map(
        functools.partial(on_device, mesh.shape["shard"], mesh.shape["ctx"]),
        mesh=mesh,
        in_specs=(
            rows,
            vec,
            rows,
            vec,
            vec,
            mat,
            mat,
            mat,
            mat,
            vec,
            vec,
            mat,
            vec,
            mat,
            vec,
            rows,
        ),
        out_specs=(
            rows,
            rows,
            vec,
            vec,
            mat,
            mat,
            mat,
            mat,
            vec,
            vec,
            mat,
            vec,
            mat,
            vec,
        ),
        check_vma=False,
    )
```

```python
import functools

import jax
import jax.numpy as jnp
from jax import lax
from jax.experimental import pallas as pl
from jax.experimental.pallas import tpu as pltpu
from jax.sharding import PartitionSpec as P

HS = 64
E = 24
TOP = 8
NORM_EPS = 1e-05
NEG_LARGE = -1e30
BF16 = jnp.bfloat16
F32 = jnp.float32
PANEL = 512
UNIT = 128
GELU_C = 0.7978845608028654
GELU_A = 0.044715
MESH = pl.DeviceIdType.MESH
RING = 40
START, CORE, NEAR_A, NEAR_B, FAR_0, FAR_1, FAR_2, PASS, SHARE, END = range(10)


def dot(left, right):
    return jnp.dot(left, right, preferred_element_type=F32)


def dot_t(left, right):
    return lax.dot_general(left, right, (((1,), (1,)), ((), ())), preferred_element_type=F32)


def many(first, size, step):
    return pl.ds(pl.multiple_of(first, step), size)


class Net:
    def __init__(self, shards, ctxs, group, send_sem, recv_sem):
        self.shards, self.ctxs, self.group = shards, ctxs, group
        self.pairs = group // 2
        self.groups = ctxs // group
        self.dims = self.pairs.bit_length() - 1
        self.z = lax.axis_index("shard")
        self.i = lax.axis_index("ctx")
        self.core = self.i % 2
        self.chip = (self.i % group) // 2
        self.grp = self.i // group
        self.send_sem, self.recv_sem = send_sem, recv_sem
        self.arrivals = 0
        self.starts = 0
        self.ring = [[] for _ in range(RING)]
        flip_low = self.chip + 1 - 2 * (self.chip % 2)
        if self.dims == 2:
            flip_high = self.chip + 2 - 4 * (self.chip // 2)
            self.chip_a = self.core * flip_high + (1 - self.core) * flip_low
            self.chip_b = self.core * flip_low + (1 - self.core) * flip_high
            self.chip_ab = self.pairs - 1 - self.chip
        elif self.dims == 1:
            self.chip_b = flip_low

    def far(self, step):
        return (self.z + step) % self.shards

    def src(self, step):
        return (self.z + self.shards - step) % self.shards

    def peer(self, chip):
        return self.grp * self.group + chip * 2 + self.core

    def sibling(self):
        return self.i + 1 - 2 * self.core

    def copy(self, src, dst, sent, arrived, z, i):
        return pltpu.make_async_remote_copy(
            src_ref=src,
            dst_ref=dst,
            send_sem=self.send_sem.at[sent],
            recv_sem=self.recv_sem.at[arrived],
            device_id={"shard": z, "ctx": i},
            device_id_type=MESH,
        )

    def arrival(self):
        self.arrivals += 1
        return self.arrivals - 1

    def send(self, src, dst, arrived, z, i):
        slot = self.starts % RING
        self.starts += 1
        if self.ring[slot]:
            self.left(self.ring[slot])
        one = self.ring[slot] = [self.copy(src, dst, slot, arrived, z, i)]
        one[0].start()
        return one

    def left(self, one):
        if one:
            one.pop().wait_send()

    def wait(self, arrived, dst):
        self.copy(dst, dst, 0, arrived, self.z, self.i).wait_recv()

    def finish(self):
        for one in self.ring:
            self.left(one)

    def greet(self):
        barrier = pltpu.get_barrier_semaphore()
        for step in range(1, self.ctxs):
            pl.semaphore_signal(
                barrier,
                inc=1,
                device_id={"shard": self.z, "ctx": (self.i + step) % self.ctxs},
                device_id_type=MESH,
            )
        for step in range(1, self.shards):
            pl.semaphore_signal(
                barrier,
                inc=1,
                device_id={"shard": self.far(step), "ctx": self.i},
                device_id_type=MESH,
            )

    def greeted(self):
        pl.semaphore_wait(pltpu.get_barrier_semaphore(), self.ctxs + self.shards - 2)


class Spread:
    def __init__(self, net, refs, all_of, at_once=False, straight=False):
        self.net, self.refs, self.all_of, self.at_once = net, refs, all_of, at_once
        self.straight = straight
        self.piece = refs[0].shape[0] // net.group
        self.half = refs[0].shape[0] // 2

    def part(self, chip):
        return many((self.net.core * self.net.pairs + chip) * self.piece, self.piece, self.piece)

    def block(self, core):
        return many(core * self.half, self.half, self.half)

    def give(self, rows, peer):
        arrived = self.net.arrival()
        for ref in self.refs:
            self.net.send(ref.at[rows], ref.at[rows], arrived, self.net.z, peer)
        return arrived

    def begin(self):
        net = self.net
        own = self.part(net.chip)
        if self.at_once:
            self.to_all = net.arrival()
            (ref,) = self.refs
            for step in range(1, net.group):
                peer = net.grp * net.group + (net.i + step) % net.group
                net.send(ref.at[own], ref.at[own], self.to_all, net.z, peer)
            return
        if net.dims == 2:
            self.to_a = self.give(own, net.peer(net.chip_a))
        if net.dims:
            self.to_b = self.give(own, net.peer(net.chip_b))
        if net.dims == 2 and self.straight:
            self.on = self.give(own, net.peer(net.chip_ab))

    def pass_on(self):
        net = self.net
        if net.dims == 2 and not self.straight:
            got = self.part(net.chip_a)
            net.wait(self.to_a, self.all_of(got))
            self.on = self.give(got, net.peer(net.chip_b))

    def share(self):
        net = self.net
        if net.dims:
            net.wait(self.to_b, self.all_of(self.part(net.chip_b)))
        if net.dims == 2:
            if self.straight:
                net.wait(self.to_a, self.all_of(self.part(net.chip_a)))
            net.wait(self.on, self.all_of(self.part(net.chip_ab)))
        self.cross()

    def cross(self):
        self.to_core = self.give(self.block(self.net.core), self.net.sibling())

    def end(self):
        if self.at_once:
            count = self.piece * (self.net.group - 1)
            self.net.wait(self.to_all, self.all_of(pl.ds(0, count)))
        else:
            self.net.wait(self.to_core, self.all_of(self.block(1 - self.net.core)))


class Gather:
    def __init__(self, net, buf, by_core=False):
        self.net, self.buf, self.by_core = net, buf, by_core
        planes = [buf.at[net.src(k)] for k in range(1, net.shards)]
        self.spread = Spread(net, planes, lambda rows: buf.at[0 : net.shards - 1, rows])
        self.rows = self.spread.block(net.core) if by_core else self.spread.part(net.chip)

    def start(self):
        net = self.net
        own = self.buf.at[net.z, self.rows]
        self.far = net.arrival()
        for k in range(1, net.shards):
            net.send(own, own, self.far, net.far(k), net.i)

    def begin(self):
        self.net.wait(self.far, self.spread.all_of(self.rows))
        if self.by_core:
            self.spread.cross()
        else:
            self.spread.begin()

    def pass_on(self):
        if not self.by_core:
            self.spread.pass_on()

    def share(self):
        if not self.by_core:
            self.spread.share()

    def end(self):
        self.spread.end()


class Absent:
    def start(self):
        pass

    begin = pass_on = share = end = start

    def to(self, name):
        pass


class Reduce:
    def __init__(self, net, buffers, out, far_first, halving, at_once, straight, store):
        self.net, self.out, self.store = net, out, store
        self.grad, self.from_core, self.from_a, self.from_b = buffers[0:4]
        self.from_group, self.from_far = buffers[4:6]
        self.far_first, self.halving = far_first, halving
        self.piece = self.grad.shape[1] // net.group
        self.half = self.grad.shape[1] // 2
        self.spread = Spread(net, [out], lambda rows: out.at[rows], at_once, straight)
        near = [(NEAR_B, self.take_b)]
        if net.dims == 2:
            near = [(NEAR_A, self.take_a)] + near
        if halving:
            rounds = net.shards.bit_length() - 1
            far = [(FAR_0 + k, functools.partial(self.take_half, k)) for k in range(rounds)]
        else:
            far = [(FAR_0, self.take_far)]
        steps = far + near if far_first else near + far
        name, step = steps[-1]
        steps[-1] = (name, functools.partial(self.last, step))
        after = [(PASS, self.spread.pass_on), (SHARE, self.spread.share)]
        after = [] if at_once else after if net.dims == 2 else after[1:]
        self.steps = [(START, self.start), (CORE, self.take_core), *steps, *after]
        self.steps.append((END, self.finish))
        far, near = [FAR_0, FAR_1, FAR_2], [NEAR_A, NEAR_B]
        order = far + near if far_first else near + far
        order = [START, CORE, *order, PASS, SHARE, END]
        self.rank = {name: k for k, name in enumerate(order)}

    def to(self, name):
        while self.steps and self.rank[self.steps[0][0]] <= self.rank[name]:
            self.steps.pop(0)[1]()

    def last(self, step):
        step()
        self.spread.begin()

    def finish(self):
        self.spread.end()
        self.store.start()

    def first(self, chip):
        return (self.net.core * self.net.pairs + chip) * self.piece

    def rows(self, chip):
        return many(self.first(chip), self.piece, self.piece)

    def planes(self, after_far):
        if after_far:
            return [(self.net.z, 0)]
        return [(s, s) for s in range(self.net.shards)]

    def add(self, first, count, planes, parts):
        lines = 16

        def one(step, carry):
            at = pl.multiple_of(step * lines, lines)
            rows = many(first + at, lines, lines)
            for here, there in planes:
                value = self.grad[here, rows].astype(F32)
                for part in parts:
                    value = value + part[there, pl.ds(at, lines)].astype(F32)
                self.grad[here, rows] = value.astype(BF16)
            return carry

        lax.fori_loop(0, count // lines, one, 0)

    def cut(self, rows, after_far):
        if after_far:
            return self.grad.at[pl.ds(self.net.z, 1), rows]
        return self.grad.at[:, rows]

    def start(self):
        net = self.net
        away = many((1 - net.core) * self.half, self.half, self.half)
        self.to_core = net.arrival()
        net.send(self.grad.at[:, away], self.from_core, self.to_core, net.z, net.sibling())

    def take_core(self):
        net = self.net
        net.wait(self.to_core, self.from_core)
        self.add(net.core * self.half, self.half, self.planes(False), [self.from_core])
        if self.far_first:
            own = many(net.core * self.half, self.half, self.half)
            self.send_far(own)
        else:
            self.send_near(False)

    def send_near(self, after_far):
        net = self.net
        if net.dims == 2:
            self.to_a = [net.arrival(), net.arrival()]
            for k, chip in ((1, net.chip_ab), (0, net.chip_a)):
                net.send(
                    self.cut(self.rows(chip), after_far),
                    self.from_a.at[k],
                    self.to_a[k],
                    net.z,
                    net.peer(net.chip_a),
                )
        elif net.dims == 1:
            self.send_b(after_far)

    def send_b(self, after_far):
        net = self.net
        self.to_b = net.arrival()
        rows = self.rows(net.chip_b)
        net.send(
            self.cut(rows, after_far), self.from_b, self.to_b, net.z, net.peer(net.chip_b)
        )

    def take_a(self):
        net = self.net
        for k, chip in ((1, net.chip_b), (0, net.chip)):
            net.wait(self.to_a[k], self.from_a.at[k])
            self.add(self.first(chip), self.piece, self.planes(self.far_first), [self.from_a.at[k]])
            if k:
                self.send_b(self.far_first)

    def take_b(self):
        net = self.net
        if net.dims:
            net.wait(self.to_b, self.from_b)
            self.add(
                self.first(net.chip), self.piece, self.planes(self.far_first), [self.from_b]
            )
        own = self.rows(net.chip)
        step, at = 1, 0
        while step < net.groups:
            peer = net.i + net.group * step * (1 - 2 * ((net.grp // step) % 2))
            arrived = net.arrival()
            one = net.send(
                self.cut(own, self.far_first), self.from_group.at[at], arrived, net.z, peer
            )
            net.wait(arrived, self.from_group.at[at])
            net.left(one)
            self.add(
                self.first(net.chip),
                self.piece,
                self.planes(self.far_first),
                [self.from_group.at[at]],
            )
            step, at = step * 2, at + 1
        if self.far_first:
            self.out[own, :] = self.grad[net.z, own]
        else:
            self.send_far(own)

    def send_far(self, own):
        net = self.net
        self.own = own
        if self.halving:
            self.send_half(0)
            return
        self.to_far = net.arrival()
        for k in range(1, net.shards):
            net.send(
                self.grad.at[pl.ds(net.far(k), 1), own],
                self.from_far.at[pl.ds(k - 1, 1)],
                self.to_far,
                net.far(k),
                net.i,
            )

    def half_at(self, turn):
        step = 1 << turn
        count = self.net.shards // (2 * step)
        return step, count, self.net.shards - 2 * count

    def send_half(self, turn):
        net = self.net
        step, count, at = self.half_at(turn)
        partner = net.z + step * (1 - 2 * ((net.z // step) % 2))
        self.to_far = net.arrival()
        for k in range(count):
            plane = partner % (2 * step) + 2 * step * k
            net.send(
                self.grad.at[pl.ds(plane, 1), self.own],
                self.from_far.at[pl.ds(at + k, 1)],
                self.to_far,
                partner,
                net.i,
            )

    def take_half(self, turn):
        net = self.net
        step, count, at = self.half_at(turn)
        parts = self.from_far.at[pl.ds(at, count)]
        net.wait(self.to_far, parts)
        planes = [(net.z % (2 * step) + 2 * step * k, k) for k in range(count)]
        first, size = (
            (net.core * self.half, self.half)
            if self.far_first
            else (self.first(net.chip), self.piece)
        )
        self.add(first, size, planes, [parts])
        if count > 1:
            self.send_half(turn + 1)
        else:
            self.far_done()

    def take_far(self):
        net = self.net
        net.wait(self.to_far, self.from_far)
        parts = [self.from_far.at[pl.ds(k, 1)] for k in range(net.shards - 1)]
        if self.far_first:
            self.add(net.core * self.half, self.half, self.planes(True), parts)
        else:
            self.add(self.first(net.chip), self.piece, self.planes(True), parts)
        self.far_done()

    def far_done(self):
        if self.far_first:
            self.send_near(True)
        else:
            self.out[self.own, :] = self.grad[self.net.z, self.own]


def reduce_scratch(shards, group, rounds, rows, wide, far_first):
    pairs = group // 2
    piece, half = rows // group, rows // 2
    planes = 1 if far_first else shards
    tiny = (1, 16, 128)
    return [
        pltpu.VMEM((shards, rows, wide), BF16),
        pltpu.VMEM((shards, half, wide), BF16),
        pltpu.VMEM((2, planes, piece, wide) if pairs == 4 else tiny, BF16),
        pltpu.VMEM((planes, piece, wide), BF16),
        pltpu.VMEM((rounds, planes, piece, wide) if rounds else tiny, BF16),
        pltpu.VMEM((shards - 1, half if far_first else piece, wide), BF16),
    ]


def layer_kernel(
    shards,
    ctxs,
    group,
    chunk_far,
    len_hbm,
    x_hbm,
    cot_hbm,
    picks_hbm,
    g1_hbm,
    b1_hbm,
    g2_hbm,
    b2_hbm,
    bo_hbm,
    bi_hbm,
    wq_hbm,
    wkv_hbm,
    wr_hbm,
    wo_hbm,
    wi_hbm,
    wout_hbm,
    out_hbm,
    gin_hbm,
    chunk_hbm,
    wo_hbm_out,
    q_hbm,
    kv_hbm,
    len_ref,
    x_ref,
    cot_ref,
    picks_ref,
    g1_ref,
    b1_ref,
    g2_ref,
    b2_ref,
    bo_ref,
    bi_ref,
    wq_st,
    wkv_st,
    wr_st,
    wi_st,
    stage,
    wk,
    wqs,
    wo,
    wc,
    vec_st,
    vecs,
    normed,
    normed_t,
    q_t,
    sel_a,
    heads_t,
    small,
    kvall,
    kvt,
    pads,
    hrow,
    linv,
    sbuf,
    ebuf,
    dkv,
    from_sib,
    from_kv,
    mixed_t,
    xhat2,
    n2,
    n2_t,
    gfin_low,
    biases,
    g_t,
    sums_c,
    sums_o,
    sums_q,
    sums_k,
    out_ref,
    gin_ref,
    chunk_out,
    wo_out,
    q_out,
    kv_out,
    vec_g,
    local_sem,
    send_sem,
    recv_sem,
):
    net = Net(shards, ctxs, group, send_sem, recv_sem)
    z, c = net.z, net.i
    tokens, width = x_ref.shape
    seg = tokens // 2
    half = seg // 2
    blocks = 2 * ctxs
    ws = width // shards
    wos = wo.shape[1]
    fs = wout_hbm.shape[0]
    scale = HS ** (-0.5)
    chunks = fs // UNIT
    panels = shards * UNIT // PANEL
    per_panel = PANEL // UNIT
    lanes = TOP * half
    wide = E * HS
    split = wide // 2
    sum_c, sum_q = [one[0] for one in sums_c], [one[0] for one in sums_q]
    sum_o, sum_k = sums_o[0], sums_k[0]
    vec_line = E
    bias_line = vec_line + 5
    per_unit = UNIT // ws
    near_steps = ctxs // 2

    def local(src, dst, at):
        return pltpu.make_async_copy(src, dst, local_sem.at[at])

    net.greet()
    wo_st, wout_st = stage.at[0:wos], stage.at[wos : wos + fs]
    resid, acc_a, acc_b = (stage.at[k * tokens : (k + 1) * tokens] for k in range(3))
    loads = {}
    for at, (src, dst) in enumerate(
        (
            (wkv_hbm, wkv_st),
            (g1_hbm, g1_ref),
            (b1_hbm, b1_ref),
            (g2_hbm, g2_ref),
            (b2_hbm, b2_ref),
            (bo_hbm, bo_ref),
            (bi_hbm, bi_ref),
            (wr_hbm, wr_st),
            (wq_hbm, wq_st),
            (x_hbm, x_ref),
            (picks_hbm, picks_ref),
            (wo_hbm, wo_st),
            (wi_hbm, wi_st),
            (wout_hbm, wout_st),
            (cot_hbm, cot_ref),
        )
    ):
        loads[id(dst)] = local(src, dst, at)
        loads[id(dst)].start()
    load_len = local(len_hbm, len_ref, 22 + chunks)
    load_len.start()
    loads[id(wkv_st)].wait()
    wk[z] = wkv_st[...].astype(BF16)
    vec_st[...] = jnp.zeros(vec_st.shape, F32)
    for row, ref in enumerate((g1_ref, b1_ref, g2_ref, b2_ref, bo_ref)):
        loads[id(ref)].wait()
        vec_st[row : row + 1, 0:ws] = ref[...]
    loads[id(bi_ref)].wait()
    for k in range(chunks):
        vec_st[5 + k : 6 + k, :] = bi_ref[:, k * UNIT : (k + 1) * UNIT]
    own_vec = vecs.at[z]
    own_vec[...] = vec_st[...].astype(BF16)
    net.greeted()
    gather_k, gather_o = Gather(net, wk, True), Gather(net, wo)
    gather_q = [Gather(net, one) for one in wqs]
    gather_c = [Gather(net, wc.at[k], k == chunks - 1) for k in range(chunks)]
    gather_k.start()
    vec_slot = net.arrival()
    for k in range(1, shards):
        net.send(own_vec, own_vec, vec_slot, net.far(k), net.i)
    loads[id(wq_st)].wait()
    loads[id(wr_st)].wait()
    for k in range(2):
        wqs[k][z, :, 0:split] = wq_st[:, k * split : (k + 1) * split].astype(BF16)
    padded = jnp.concatenate([wr_st[...], jnp.zeros((128 - E, ws), F32)], axis=0)
    wqs[1][z, :, split:] = padded.T.astype(BF16)

    loads[id(x_ref)].wait()
    x = x_ref[...].astype(F32)
    mean1 = jnp.mean(x, axis=1, keepdims=True)
    cen = x - mean1
    small[0, :, 0:1] = lax.rsqrt(jnp.mean(cen * cen, axis=1, keepdims=True) + NORM_EPS)
    small[0, :, 2:3] = mean1

    def first_hat():
        return (x_ref[...].astype(F32) - small[0, :, 2:3]) * small[0, :, 0:1]

    for ref in (wo_st, wi_st, wout_st):
        loads[id(ref)].wait()
    wo[z] = wo_st[...].astype(BF16)
    for k in range(chunks):
        wc[k, z, 0:UNIT] = wout_st[k * UNIT : (k + 1) * UNIT].astype(BF16)
        for s in range(shards):
            first = UNIT + (s // per_panel) * ws
            at = (s % per_panel) * UNIT
            wc[k, z, first : first + ws, at : at + UNIT] = wi_st[
                :, s * fs + k * UNIT : s * fs + (k + 1) * UNIT
            ].astype(BF16)
    for one in gather_q:
        one.start()
    gather_k.begin()
    load_len.wait()
    net.wait(vec_slot, vecs.at[0 : shards - 1])

    vec_all = [vecs[s].astype(F32) for s in range(shards)]

    def whole(row):
        return jnp.concatenate([one[row : row + 1, 0:ws] for one in vec_all], axis=1)

    gain1, bias1, gain2, bias2, bias_out = (whole(row) for row in range(5))
    for k in range(chunks):
        for p in range(panels):
            biases[k * panels + p : k * panels + p + 1, :] = jnp.concatenate(
                [one[5 + k : 6 + k] for one in vec_all[p * per_panel : (p + 1) * per_panel]],
                axis=1,
            )
    norm_value = first_hat() * gain1 + bias1
    normed[...] = norm_value.astype(BF16)
    normed_t[...] = norm_value.T.astype(BF16)
    gather_q[0].begin()
    def at_block(ref, block):
        return ref.at[block // 2, :, block % 2]

    def my_block(h):
        return c if h == 0 else blocks - 1 - c

    def core_blocks(ref, core):
        return ref.at[0:near_steps, :, core], ref.at[near_steps:ctxs, :, 1 - core]

    kv_slot, kv_cross, dkv_cross, dkv_near = (net.arrival() for _ in range(4))
    kv_sent = []

    def do_kvproj():
        kv_own = dot(normed[...], wk[...].reshape(width, 2 * HS)).astype(BF16)

        for h in range(2):
            block = my_block(h)
            for s in range(2):
                first = s * seg + h * half
                kvall[block // 2, s, block % 2] = kv_own[first : first + half]
        for step in range(1, near_steps):
            for block in (c, blocks - 1 - c):
                ref = at_block(kvall, block)
                kv_sent.append(net.send(ref, ref, kv_slot, z, (c + 2 * step) % ctxs))

    def do_kvcross():
        net.wait(kv_slot, kvall.at[0 : near_steps - 1])
        for part in core_blocks(kvall, net.core):
            kv_sent.append(net.send(part, part, kv_cross, z, net.sibling()))

    def do_kvwait():
        net.wait(kv_cross, kvall.at[0:near_steps])

    def do_turn():
        def turn(step, carry):
            for s in range(2):
                keys = kvall[step, s].reshape(2 * half, 2 * HS)
                kvt[step, s] = keys.astype(F32).T.astype(BF16)
                dkv[step, s] = jnp.zeros((2 * half, 2 * HS), F32)
            return carry

        lax.fori_loop(0, ctxs, turn, 0, unroll=4)

    def project_queries(part):
        def query_tile(n, carry):
            cols = many(n * 256, 256, 256)
            value = dot(normed[...], wqs[part][:, :, cols].reshape(width, 256))
            value = value.astype(BF16).astype(F32).T
            for k in range(4):
                q_t[part * (E // 2) + n * 4 + k] = value[k * HS : (k + 1) * HS]
            return carry

        lax.fori_loop(0, split // 256, query_tile, 0, unroll=True)

    def do_gates():
        logits_t = dot(normed[...], wqs[1][:, :, split:].reshape(width, 128)).T
        loads[id(picks_ref)].wait()
        picks = jnp.concatenate([picks_ref[0], picks_ref[1]], axis=1).astype(F32)
        picked = jnp.zeros((TOP, tokens), F32)
        for e in range(E):
            picked = jnp.where(picks == float(e), logits_t[e : e + 1, :], picked)
        top = jnp.max(picked, axis=0, keepdims=True)
        gexp = jnp.exp(picked - top)
        small[1, 0:TOP, 0:tokens] = gexp / jnp.sum(gexp, axis=0, keepdims=True)
        small[1, TOP : 2 * TOP, 0:tokens] = picks

    def choose(src, store):
        def one(j, carry):
            pick = small[1, pl.ds(TOP + j, 1), 0:tokens]
            value = jnp.zeros((HS, tokens), F32)
            for e in range(E):
                value = jnp.where(pick == float(e), src[e], value)
            store(j, value)
            return carry

        lax.fori_loop(0, TOP, one, 0, unroll=2)

    def spread_back(src, store):
        def one(e, carry):
            value = jnp.zeros((HS, tokens), F32)
            for j in range(TOP):
                pick = small[1, TOP + j : TOP + j + 1, 0:tokens]
                value = jnp.where(pick == e.astype(F32), src[j], value)
            store(e, value)
            return carry

        lax.fori_loop(0, E, one, 0, unroll=4)

    low_lane = lax.broadcasted_iota(jnp.int32, (HS, 2 * half), 1) < half

    def swap(one, two):
        return (
            jnp.where(low_lane, one, pltpu.roll(two, half, 1)),
            jnp.where(low_lane, pltpu.roll(one, half, 1), two),
        )

    def store_query(j, value):
        sel_a[j] = value * scale

    def do_choose():
        choose(q_t, store_query)
        for s in range(2):
            for pair in range(TOP // 2):
                halves = swap(
                    sel_a[2 * pair, :, s * seg : (s + 1) * seg],
                    sel_a[2 * pair + 1, :, s * seg : (s + 1) * seg],
                )
                for h in range(2):
                    pads[2 * s + h, 0:HS, pair * 128 : (pair + 1) * 128] = halves[h].astype(BF16)
        for sh in range(4):
            pads[sh, HS:, 0:lanes] = jnp.zeros((HS, lanes), BF16)
            pads[sh, 0:HS, lanes:] = jnp.zeros((HS, lanes), BF16)

    offset = lax.broadcasted_iota(jnp.int32, (1, lanes), 1) % half
    key_row = lax.broadcasted_iota(jnp.int32, (4 * half, lanes), 0)
    keep_scores = sbuf.shape[1] > 1

    def place(h):
        last = (blocks - c + 3) // 4
        if h == 1:
            return last, 0
        return (c + 4) // 4, last

    def fold(value, op):
        parts = [value[8 * k : 8 * k + 8] for k in range(value.shape[0] // 8)]
        while len(parts) > 1:
            parts = [op(parts[k], parts[k + 1]) for k in range(0, len(parts), 2)]
        return parts[0]

    def keys_of(step, s):
        return kvall[pl.ds(2 * step, 2), s].reshape(4 * half, 2 * HS)

    def turned(step, s, rows):
        return jnp.concatenate([kvt[2 * step + k, s, rows] for k in range(2)], axis=1)

    tops_of = {}

    def masked(step, s, h):
        limit = jnp.minimum(my_block(h) * half + offset, len_ref[s] - 1)
        scores = dot(keys_of(step, s), pads[2 * s + h, :, 0:lanes])
        return jnp.where(key_row <= limit - step * 4 * half, scores, NEG_LARGE)

    def find_tops(h):
        def score_step(step, tops):
            result = []
            for s in range(2):
                scores = masked(step, s, h)
                if keep_scores:
                    sbuf[s, step] = scores
                result.append(jnp.maximum(tops[s], fold(scores, jnp.maximum)))
            return tuple(result)

        start = jnp.full((8, lanes), NEG_LARGE, F32)
        tops = lax.fori_loop(0, place(h)[0], score_step, (start, start))
        tops_of[h] = [jnp.max(top, axis=0, keepdims=True) for top in tops]

    def weigh(h):
        count, base = place(h)
        for s in range(2):
            hrow[2 * s + h] = jnp.zeros((HS, lanes), F32)

        def value_step(step, totals):
            result = []
            for s in range(2):
                total = totals[s]
                scores = None if keep_scores else masked(step, s, h)
                for k in range(2):
                    rows = slice(2 * half * k, 2 * half * (k + 1))
                    part = sbuf[s, step, rows] if keep_scores else scores[rows]
                    expd = jnp.exp(part - tops_of[h][s])
                    ebuf[s, base + step, rows] = expd.astype(BF16)
                    total = total + fold(expd, jnp.add)
                hrow[2 * s + h] += dot(turned(step, s, slice(HS, 2 * HS)), ebuf[s, base + step])
                result.append(total)
            return tuple(result)

        start = jnp.zeros((8, lanes), F32)
        totals = lax.fori_loop(0, count, value_step, (start, start))
        for s in range(2):
            inverse = 1.0 / jnp.sum(totals[s], axis=0, keepdims=True)
            linv[2 * s + h] = jnp.broadcast_to(inverse, (8, lanes))
            hrow[2 * s + h] = hrow[2 * s + h] * inverse

    def do_mix():
        for s in range(2):
            for pair in range(TOP // 2):
                both = swap(
                    hrow[2 * s, :, pair * 128 : (pair + 1) * 128],
                    hrow[2 * s + 1, :, pair * 128 : (pair + 1) * 128],
                )
                for k in range(2):
                    heads_t[2 * pair + k, :, s * seg : (s + 1) * seg] = both[k]
        for j in range(TOP):
            sel_a[j] = heads_t[j] * small[1, j : j + 1, 0:tokens]

        def store_mixed(e, value):
            mixed_t[e] = value.astype(BF16)

        spread_back(sel_a, store_mixed)

    experts = E // shards
    row = lax.broadcasted_iota(jnp.int32, (tokens, 1), 0)
    inner_row = row % seg
    pos = jnp.where(
        inner_row < half, c * half + inner_row, blocks * half - (c + 2) * half + inner_row
    )
    valid = (pos < jnp.where(row < seg, len_ref[0], len_ref[1])).astype(F32)

    def do_project():
        acc_a[...] = x_ref[...].astype(F32)

        def project(s, carry):
            part = mixed_t[pl.ds(s * experts, experts)].reshape(wos, tokens)
            acc_a[...] += dot(part.astype(F32).T.astype(BF16), wo[s])
            return carry

        lax.fori_loop(0, shards, project, 0, unroll=True)
        residual = acc_a[...]
        resid[...] = residual
        cen = residual - jnp.mean(residual, axis=1, keepdims=True)
        rstd2 = lax.rsqrt(jnp.mean(cen * cen, axis=1, keepdims=True) + NORM_EPS)
        small[0, :, 1:2] = rstd2
        cen = cen * rstd2
        xhat2[...] = cen
        cen = cen * gain2 + bias2
        n2[...] = cen.astype(BF16)
        n2_t[...] = cen.T.astype(BF16)

        loads[id(cot_ref)].wait()
        gfin_low[...] = (cot_ref[...].astype(F32) * valid).astype(BF16)
        acc_a[...] = jnp.zeros((tokens, width), F32)
        acc_b[...] = jnp.zeros((tokens, width), F32)
        vec_g[...] = jnp.zeros(vec_g.shape, F32)

    def feed(k, p):
        rows_in = slice(UNIT + p * ws, UNIT + (p + 1) * ws)
        planes = slice(p * per_panel, (p + 1) * per_panel)
        w_in = wc[k, :, rows_in].reshape(width, PANEL)
        w_out = wc[k, planes, 0:UNIT].reshape(PANEL, width)
        line = k * panels + p
        hidden = dot(n2[...], w_in) + biases[line : line + 1, :]
        square = hidden * hidden
        tanh = jnp.tanh(GELU_C * hidden * (1.0 + GELU_A * square))
        act = (0.5 * hidden * (1.0 + tanh)).astype(BF16)
        slope = 0.5 * (1.0 + tanh) + 0.5 * GELU_C * hidden * (1.0 - tanh * tanh) * (
            1.0 + 3.0 * GELU_A * square
        )
        gfin = gfin_low[...]
        acc_a[...] += dot(act, w_out)
        grad_hidden = (slope * dot_t(gfin, w_out)).astype(BF16)
        total = jnp.sum(grad_hidden.astype(F32), axis=0, keepdims=True)
        for a in range(per_panel):
            for q in range(per_unit):
                at = bias_line + k * per_unit + q
                first = (p * per_panel + a) * ws
                vec_g[at : at + 1, first : first + ws] = total[
                    :, a * UNIT + q * ws : a * UNIT + (q + 1) * ws
                ]
        grad_outer = dot(act.astype(F32).T.astype(BF16), gfin).astype(BF16)
        sum_c[k][planes, 0:UNIT] = grad_outer.reshape(per_panel, UNIT, width)
        grad_inner = dot(n2_t[...], grad_hidden).astype(BF16)
        sum_c[k][:, rows_in] = grad_inner.reshape(shards, ws, PANEL)
        acc_b[...] += dot_t(grad_hidden, w_in)

    outs = [local(out_ref, out_hbm, 15), local(gin_ref, gin_hbm, 16)]

    def reduction(
        refs, out, hbm, at, far_first=False, halving=False, at_once=False, straight=False
    ):
        store = local(out, hbm, at)
        outs.append(store)
        return Reduce(net, refs, out, far_first, halving, at_once, straight, store)

    reduce_c = [
        reduction(sums_c[k], chunk_out.at[k], chunk_hbm.at[k], 20 + k, chunk_far[k], True)
        for k in range(chunks)
    ]
    reduce_o = reduction(sums_o, wo_out, wo_hbm_out, 17, straight=False)
    reduce_q = [
        reduction(
            sums_q[k],
            q_out[k],
            q_hbm.at[:, k * split : (k + 1) * split],
            20 + chunks + k,
            straight=True,
        )
        for k in range(2)
    ]
    reduce_k = reduction(sums_k, kv_out, kv_hbm, 19, at_once=True)

    def do_norm2():
        out_ref[...] = (valid * (resid[...] + acc_a[...] + bias_out)).astype(BF16)
        outs[0].start()
        gfin = cot_ref[...].astype(F32) * valid
        vec_g[vec_line + 4 : vec_line + 5, :] = jnp.sum(gfin, axis=0, keepdims=True)
        grad_n2 = acc_b[...]
        vec_g[vec_line + 3 : vec_line + 4, :] = jnp.sum(grad_n2, axis=0, keepdims=True)
        vec_g[vec_line + 2 : vec_line + 3, :] = jnp.sum(grad_n2 * xhat2[...], axis=0, keepdims=True)
        grad_hat = grad_n2 * gain2
        grad_hat = grad_hat - jnp.mean(grad_hat, axis=1, keepdims=True)
        grad_hat = grad_hat - xhat2[...] * jnp.mean(grad_hat * xhat2[...], axis=1, keepdims=True)
        grad_residual = gfin + grad_hat * small[0, :, 1:2]
        resid[...] = grad_residual
        n2[...] = grad_residual.astype(BF16)

    def do_branch():
        def branch(s, carry):
            part = mixed_t[pl.ds(s * experts, experts)].reshape(wos, tokens)
            sum_o[s] = dot(part, n2[...]).astype(BF16)
            grad = dot_t(wo[s], n2[...])
            q_t[pl.ds(s * experts, experts)] = grad.reshape(experts, HS, tokens)
            return carry

        lax.fori_loop(0, shards, branch, 0, unroll=2)

    def do_heads():
        def store_head_grad(j, value):
            sel_a[j] = value * small[1, pl.ds(j, 1), 0:tokens]
            small[1, pl.ds(2 * TOP + j, 1), 0:tokens] = jnp.sum(
                value * heads_t[j], axis=0, keepdims=True
            )

        choose(q_t, store_head_grad)
        gates = small[1, 0:TOP, 0:tokens]
        grad_gates = small[1, 2 * TOP : 3 * TOP, 0:tokens]
        grad_picked = gates * (grad_gates - jnp.sum(gates * grad_gates, axis=0, keepdims=True))
        picks = small[1, TOP : 2 * TOP, 0:tokens]
        g_t[wide : wide + 128, :] = jnp.zeros((128, tokens), BF16)
        grad_logits = [
            jnp.sum(jnp.where(picks == float(e), grad_picked, 0.0), axis=0, keepdims=True)
            for e in range(E)
        ]
        grad_logits += [jnp.zeros((1, tokens), F32)] * (32 - E)
        g_t[wide : wide + 32, :] = jnp.concatenate(grad_logits, axis=0).astype(BF16)
        for s in range(2):
            for pair in range(TOP // 2):
                halves = swap(
                    sel_a[2 * pair, :, s * seg : (s + 1) * seg],
                    sel_a[2 * pair + 1, :, s * seg : (s + 1) * seg],
                )
                at = pair * 128
                for h in range(2):
                    sh = 2 * s + h
                    grad = (halves[h] * linv[sh, 0:1, at : at + 128]).astype(BF16)
                    pads[sh, HS:, lanes + at : lanes + at + 128] = grad
                    linv[sh, 1:2, at : at + 128] = jnp.sum(
                        grad.astype(F32) * hrow[sh, :, at : at + 128], axis=0, keepdims=True
                    )

    def attend_back(h):
        count, base = place(h)
        deltas = [linv[2 * s + h, 1:2, :] for s in range(2)]
        for s in range(2):
            hrow[2 * s + h] = jnp.zeros((HS, lanes), F32)

        def grad_step(step, carry):
            for s in range(2):
                sh = 2 * s + h
                parts = []
                for k in range(2):
                    expd = ebuf[s, base + step, 2 * half * k : 2 * half * (k + 1)]
                    keys = kvall[2 * step + k, s].reshape(2 * half, 2 * HS)
                    grad_prob = dot(keys, pads[sh, :, lanes:])
                    parts.append((expd.astype(F32) * (grad_prob - deltas[s])).astype(BF16))
                grad_score = jnp.concatenate(parts, axis=0)
                grad = dot_t(grad_score, pads[sh, :, 0:lanes])
                grad = grad + dot_t(ebuf[s, base + step], pads[sh, :, lanes:])
                dkv[pl.ds(2 * step, 2), s] += grad.reshape(2, 2 * half, 2 * HS)
                hrow[sh] += dot(turned(step, s, slice(0, HS)), grad_score)
            return carry

        lax.fori_loop(0, count, grad_step, 0)

    def do_dsend():
        for one in kv_sent:
            net.left(one)

        def lower(step, carry):
            kvall[step] = dkv[step].astype(BF16).reshape(2, 2, half, 2 * HS)
            return carry

        lax.fori_loop(0, ctxs, lower, 0)
        for k, part in enumerate(core_blocks(kvall, 1 - net.core)):
            net.send(part, from_sib.at[k], dkv_cross, z, net.sibling())

    def do_gradq():
        for s in range(2):
            for pair in range(TOP // 2):
                both = swap(
                    hrow[2 * s, :, pair * 128 : (pair + 1) * 128],
                    hrow[2 * s + 1, :, pair * 128 : (pair + 1) * 128],
                )
                for k in range(2):
                    q_t[2 * pair + k, :, s * seg : (s + 1) * seg] = both[k] * scale

        def store_grad_query(e, value):
            g_t[many(e * HS, HS, HS), :] = value.astype(BF16)

        spread_back(q_t, store_grad_query)

    def query_grads(part):
        def query_grad(n, carry):
            rows = many(part * split + n * 256, 256, 256)
            grad = dot_t(normed_t[...], g_t[rows, :]).astype(BF16)
            sum_q[part][:, :, many(n * 256, 256, 256)] = grad.reshape(shards, ws, 256)
            return carry

        lax.fori_loop(0, split // 256, query_grad, 0, unroll=True)

    def do_dnear():
        net.wait(dkv_cross, from_sib)

        def add_sibling(step, carry):
            for k, sub in enumerate((net.core, 1 - net.core)):
                at = step + k * near_steps
                rows = many(sub * half, half, half)
                for s in range(2):
                    value = dkv[at, s, rows] + from_sib[k, step, s].astype(F32)
                    dkv[at, s, rows] = value
                    kvall[at, s, sub] = value.astype(BF16)
            return carry

        lax.fori_loop(0, near_steps, add_sibling, 0)
        for step in range(1, near_steps):
            peer = (c + 2 * step) % ctxs
            for h, block in enumerate((peer, blocks - 1 - peer)):
                net.send(at_block(kvall, block), from_kv.at[step - 1, h], dkv_near, z, peer)

    def do_ngrad():
        part = dot(wqs[0][...].reshape(width, split), g_t[0:split, :])
        part = part + dot(wqs[1][...].reshape(width, split + 128), g_t[split:, :])
        heads_t[...] = part.reshape(heads_t.shape)

    def do_dwait():
        net.wait(dkv_near, from_kv)

    def do_kvgrad():
        for h in range(2):
            block = my_block(h)
            for s in range(2):
                value = dkv[block // 2, s, many((block % 2) * half, half, half)]
                for step in range(1, near_steps):
                    value = value + from_kv[step - 1, h, s].astype(F32)
                first = s * seg + h * half
                acc_a[first : first + half, 0:128] = value
        grad_kv = acc_a[:, 0:128].T.astype(BF16)
        part = heads_t[...].reshape(width, tokens) + dot(wk[...].reshape(width, 2 * HS), grad_kv)
        grad_normed = part.T
        hat = first_hat()
        vec_g[vec_line : vec_line + 1, :] = jnp.sum(grad_normed * hat, axis=0, keepdims=True)
        vec_g[vec_line + 1 : vec_line + 2, :] = jnp.sum(grad_normed, axis=0, keepdims=True)
        value = dot_t(normed_t[...], grad_kv)
        sum_k[:, :, 0 : 2 * HS] = value.astype(BF16).reshape(shards, ws, 2 * HS)
        value = dot_t(normed_t[...], g_t[wide:, :]) + vec_g[...].T
        sum_k[:, :, 2 * HS :] = value.astype(BF16).reshape(shards, ws, 128)
        acc_b[...] = grad_normed

    def do_gin():
        hat = first_hat()
        grad_normed = acc_b[...]
        grad_hat = grad_normed * gain1
        grad_hat = grad_hat - jnp.mean(grad_hat, axis=1, keepdims=True)
        grad_hat = grad_hat - hat * jnp.mean(grad_hat * hat, axis=1, keepdims=True)
        gin_ref[...] = resid[...] + grad_hat * small[0, :, 0:1]
        outs[1].start()

    def feed_all(k):
        if k < chunks:
            for p in range(panels):
                feed(k, p)

    absent = [Absent()] * 4
    gc0, gc1, gc2, gc3 = (gather_c + absent)[0:4]
    rc0, rc1, rc2, rc3 = (reduce_c + absent)[0:4]
    (gq0, gq1), (rq0, rq1) = gather_q, reduce_q
    go, gk, ro, rk = gather_o, gather_k, reduce_o, reduce_k
    gk.end()
    do_kvproj()
    go.start()
    gq1.begin()
    gq0.pass_on()
    gc0.start()
    do_kvcross()
    gq1.pass_on()
    gc1.start()
    go.begin()
    gc2.start()
    gq0.share()
    do_kvwait()
    do_turn()
    gc0.begin()
    gq0.end()
    project_queries(0)
    gq1.share()
    gc1.begin()
    gq1.end()
    gc3.start()
    project_queries(1)
    do_gates()
    go.pass_on()
    gc2.begin()
    do_choose()
    gc0.pass_on()
    find_tops(1)
    gc1.pass_on()
    weigh(1)
    go.share()
    gc2.pass_on()
    find_tops(0)
    weigh(0)
    gc0.share()
    do_mix()
    go.end()
    do_project()
    gc1.share()
    gc0.end()
    feed_all(0)
    gc2.share()
    rc0.to(START)
    gc3.begin()
    gc3.pass_on()
    gc3.share()
    gc1.end()
    feed_all(1)
    rc1.to(START)
    gc2.end()
    feed_all(2)
    rc2.to(START)
    rc0.to(CORE)
    gc3.end()
    feed_all(3)
    rc3.to(START)
    rc1.to(CORE)
    do_norm2()
    rc2.to(CORE)
    do_branch()
    ro.to(START)
    rc3.to(CORE)
    do_heads()
    attend_back(1)
    attend_back(0)
    ro.to(CORE)
    do_dsend()
    do_gradq()
    query_grads(0)
    rq0.to(START)
    query_grads(1)
    rq1.to(START)
    rc2.to(NEAR_A)
    rc3.to(NEAR_A)
    do_dnear()
    do_ngrad()
    rc0.to(FAR_0)
    rc1.to(FAR_0)
    ro.to(NEAR_A)
    rc2.to(NEAR_B)
    rc3.to(NEAR_B)
    rq0.to(CORE)
    rq1.to(CORE)
    do_dwait()
    do_kvgrad()
    rk.to(START)
    do_gin()
    rk.to(CORE)
    rc0.to(FAR_1)
    rc1.to(FAR_1)
    ro.to(NEAR_B)
    rq0.to(NEAR_A)
    rq1.to(NEAR_A)
    rc2.to(FAR_0)
    rc3.to(FAR_0)
    rc0.to(NEAR_A)
    rc1.to(NEAR_A)
    rk.to(NEAR_A)
    rq0.to(NEAR_B)
    rq1.to(NEAR_B)
    ro.to(FAR_0)
    rc0.to(NEAR_B)
    rc1.to(NEAR_B)
    rc2.to(FAR_1)
    rc3.to(FAR_1)
    rk.to(NEAR_B)
    ro.to(PASS)
    rc0.to(PASS)
    rc1.to(PASS)
    rc2.to(PASS)
    rc3.to(PASS)
    rq0.to(FAR_0)
    rq1.to(FAR_0)
    rk.to(FAR_0)
    ro.to(SHARE)
    rc0.to(SHARE)
    rc1.to(SHARE)
    rc2.to(SHARE)
    rc3.to(SHARE)
    rq0.to(PASS)
    rq1.to(PASS)
    rc1.to(END)
    rc2.to(END)
    rc0.to(END)
    rc3.to(END)
    rq0.to(SHARE)
    rq1.to(SHARE)
    rk.to(END)
    ro.to(END)
    rq0.to(END)
    rq1.to(END)
    for one in (*reduce_c, ro, *reduce_q, rk):
        one.to(END)
    net.finish()
    for one in outs:
        one.wait()


def unpack_kernel(shards, *refs):
    ins, outs = refs[0:6], refs[6:20]
    in_st, out_st, sem = refs[20:26], refs[26:40], refs[40]
    chunks = ins[2].shape[0]
    copy = pltpu.make_async_copy
    loads = [copy(a, b, sem.at[k]) for k, (a, b) in enumerate(zip(ins, in_st)) if k != 2]
    loads.insert(2, None)
    stores = {
        k: copy(in_st[k] if k < 2 else out_st[k], outs[k], sem.at[6 + k])
        for k in range(14)
        if k != 12
    }
    chunk_in, wo_in, q_in, kv_in = in_st[2:]
    g1_ref, b1_ref, kv_ref, q_ref, r_ref, wo_ref, g2_ref, b2_ref = out_st[2:10]
    wi_ref, bi_ref, wout_ref, bo_ref = out_st[10:]
    ws, fs = q_ref.shape[0], wout_ref.shape[0]
    per_panel = PANEL // UNIT
    chunk_loads = [
        copy(ins[2].at[k], chunk_in.at[k], sem.at[20 + k]) for k in range(chunks)
    ]
    for one in chunk_loads:
        one.start()
    for k in (3, 4, 5, 1, 0):
        loads[k].start()
    for k in range(chunks):
        chunk_loads[k].wait()
        rows = slice(k * UNIT, (k + 1) * UNIT)
        wout_ref[rows, :] = chunk_in[k, 0:UNIT].astype(F32)
        stores[20 + k] = copy(wout_ref.at[rows], outs[12].at[rows], sem.at[20 + chunks + k])
        stores[20 + k].start()
        for s in range(shards):
            first = UNIT + (s // per_panel) * ws
            at = (s % per_panel) * UNIT
            wi_ref[:, s * fs + k * UNIT : s * fs + (k + 1) * UNIT] = chunk_in[
                k, first : first + ws, at : at + UNIT
            ].astype(F32)
    stores[10].start()
    loads[3].wait()
    wo_ref[...] = wo_in[...].astype(F32)
    stores[7].start()
    loads[4].wait()
    q_ref[...] = q_in[...].astype(F32)
    stores[5].start()
    loads[5].wait()
    kv_ref[...] = kv_in[:, 0 : 2 * HS].astype(F32)
    stores[4].start()
    turned = kv_in[:, 2 * HS :].astype(F32).T
    r_ref[...] = turned[0:E]
    stores[6].start()
    for row, at, ref in (
        (0, 2, g1_ref),
        (1, 3, b1_ref),
        (2, 8, g2_ref),
        (3, 9, b2_ref),
        (4, 13, bo_ref),
    ):
        ref[...] = turned[E + row : E + row + 1]
        stores[at].start()
    for line in range(fs // ws):
        bi_ref[:, line * ws : (line + 1) * ws] = turned[E + 5 + line : E + 6 + line]
    stores[11].start()
    loads[1].wait()
    stores[1].start()
    loads[0].wait()
    stores[0].start()
    for one in stores.values():
        one.wait()


def on_device(
    shards,
    ctxs,
    tokens,
    lengths,
    expert_picks,
    first_gain,
    first_bias,
    kv_weight,
    query_weight,
    router_weight,
    output_weight,
    second_gain,
    second_bias,
    inner_weight,
    inner_bias,
    outer_weight,
    outer_bias,
    cotangent,
):
    slots, seg, width = tokens.shape
    count = slots * seg
    half = seg // 2
    lanes = TOP * half
    ws = width // shards
    wos = output_weight.shape[0]
    fs = outer_weight.shape[0]
    group = min(ctxs, ws // 16, 8)
    pairs, groups = group // 2, ctxs // group
    rounds = groups.bit_length() - 1
    chunks = fs // UNIT
    panels = shards * UNIT // PANEL
    chunk_rows = UNIT + panels * ws
    wide = E * HS
    chunk_far = [k < 2 for k in range(chunks)]
    keep_scores = ctxs * seg * slots * lanes * 4 <= 8 * 1024 * 1024
    shapes_mid = (
        jax.ShapeDtypeStruct((count, width), BF16),
        jax.ShapeDtypeStruct((count, width), F32),
        jax.ShapeDtypeStruct((chunks, chunk_rows, PANEL), BF16),
        jax.ShapeDtypeStruct((wos, width), BF16),
        jax.ShapeDtypeStruct((ws, wide), BF16),
        jax.ShapeDtypeStruct((ws, 256), BF16),
    )

    anywhere = pl.BlockSpec(memory_space=pl.ANY)
    arrivals = 2 + (3 + chunks) * 5 + 1 + 4 + (4 + chunks) * (8 + rounds + shards.bit_length() - 1)
    scratch = [
        pltpu.SMEM(lengths.shape, jnp.int32),
        pltpu.VMEM((count, width), BF16),
        pltpu.VMEM((count, width), BF16),
        pltpu.VMEM((slots, TOP, seg), jnp.int32),
        *[pltpu.VMEM((1, ws), F32)] * 5,
        pltpu.VMEM((1, fs), F32),
        pltpu.VMEM(query_weight.shape, F32),
        pltpu.VMEM(kv_weight.shape, F32),
        pltpu.VMEM((E, ws), F32),
        pltpu.VMEM(inner_weight.shape, F32),
        pltpu.VMEM((max(wos + fs, 3 * count), width), F32),
        pltpu.VMEM((shards, ws, 2 * HS), BF16),
        [pltpu.VMEM((shards, ws, wide // 2 + 128 * k), BF16) for k in range(2)],
        pltpu.VMEM((shards, wos, width), BF16),
        pltpu.VMEM((chunks, shards, chunk_rows, PANEL), BF16),
        pltpu.VMEM((16, UNIT), F32),
        pltpu.VMEM((shards, 16, UNIT), BF16),
        pltpu.VMEM((count, width), BF16),
        pltpu.VMEM((width, count), BF16),
        pltpu.VMEM((E, HS, count), F32),
        pltpu.VMEM((TOP, HS, count), F32),
        pltpu.VMEM((TOP, HS, count), F32),
        pltpu.VMEM((2, count, count), F32),
        pltpu.VMEM((ctxs, slots, 2, half, 2 * HS), BF16),
        pltpu.VMEM((ctxs, slots, 2 * HS, 2 * half), BF16),
        pltpu.VMEM((4, 2 * HS, 2 * lanes), BF16),
        pltpu.VMEM((4, HS, lanes), F32),
        pltpu.VMEM((4, 8, lanes), F32),
        pltpu.VMEM((slots, ctxs // 2, 4 * half, lanes) if keep_scores else (1, 1, 8, 128), F32),
        pltpu.VMEM((slots, ctxs // 2 + 1, 4 * half, lanes), BF16),
        pltpu.VMEM((ctxs, slots, 2 * half, 2 * HS), F32),
        pltpu.VMEM((2, ctxs // 2, slots, half, 2 * HS), BF16),
        pltpu.VMEM((ctxs // 2 - 1, 2, slots, half, 2 * HS), BF16),
        pltpu.VMEM((E, HS, count), BF16),
        pltpu.VMEM((count, width), F32),
        pltpu.VMEM((count, width), BF16),
        pltpu.VMEM((width, count), BF16),
        pltpu.VMEM((count, width), BF16),
        pltpu.VMEM((8, PANEL), F32),
        pltpu.VMEM((wide + 128, count), BF16),
        [
            reduce_scratch(shards, group, rounds, chunk_rows, PANEL, chunk_far[k])
            for k in range(chunks)
        ],
        reduce_scratch(shards, group, rounds, wos, width, False),
        [reduce_scratch(shards, group, rounds, ws, wide // 2, False) for _ in range(2)],
        reduce_scratch(shards, group, rounds, ws, 256, False),
        *[pltpu.VMEM(one.shape, one.dtype) for one in shapes_mid[0:4]],
        [pltpu.VMEM((ws, wide // 2), BF16) for _ in range(2)],
        pltpu.VMEM((ws, 256), BF16),
        pltpu.VMEM((128, width), F32),
        pltpu.SemaphoreType.DMA((23 + chunks,)),
        pltpu.SemaphoreType.DMA((RING,)),
        pltpu.SemaphoreType.DMA((arrivals,)),
    ]
    results = pl.pallas_call(
        functools.partial(layer_kernel, shards, ctxs, group, chunk_far),
        out_shape=shapes_mid,
        in_specs=[anywhere] * 16,
        out_specs=tuple([anywhere] * 6),
        scratch_shapes=scratch,
        compiler_params=pltpu.CompilerParams(
            collective_id=0, has_side_effects=True, vmem_limit_bytes=63 * 1024 * 1024
        ),
        name="layer",
    )(
        lengths,
        tokens.reshape(count, width),
        cotangent.reshape(count, width),
        jnp.swapaxes(expert_picks, 1, 2),
        first_gain.reshape(1, ws),
        first_bias.reshape(1, ws),
        second_gain.reshape(1, ws),
        second_bias.reshape(1, ws),
        outer_bias.reshape(1, ws),
        inner_bias.reshape(1, fs),
        query_weight,
        kv_weight,
        router_weight.T,
        output_weight,
        inner_weight,
        outer_weight,
    )
    vec_shape = jax.ShapeDtypeStruct((1, ws), F32)
    shapes_out = (
        jax.ShapeDtypeStruct((count, width), BF16),
        jax.ShapeDtypeStruct((count, width), F32),
        vec_shape,
        vec_shape,
        jax.ShapeDtypeStruct(kv_weight.shape, F32),
        jax.ShapeDtypeStruct(query_weight.shape, F32),
        jax.ShapeDtypeStruct((E, ws), F32),
        jax.ShapeDtypeStruct(output_weight.shape, F32),
        vec_shape,
        vec_shape,
        jax.ShapeDtypeStruct(inner_weight.shape, F32),
        jax.ShapeDtypeStruct((1, fs), F32),
        jax.ShapeDtypeStruct(outer_weight.shape, F32),
        vec_shape,
    )
    final = pl.pallas_call(
        functools.partial(unpack_kernel, shards),
        out_shape=shapes_out,
        in_specs=[anywhere] * 6,
        out_specs=tuple([anywhere] * 14),
        scratch_shapes=[pltpu.VMEM(one.shape, one.dtype) for one in (*shapes_mid, *shapes_out)]
        + [pltpu.SemaphoreType.DMA((20 + 2 * chunks,))],
        name="unpack",
    )(*results)
    final = list(final)
    final[6] = final[6].T
    shapes = (
        tokens.shape,
        tokens.shape,
        first_gain.shape,
        first_bias.shape,
        kv_weight.shape,
        query_weight.shape,
        router_weight.shape,
        output_weight.shape,
        second_gain.shape,
        second_bias.shape,
        inner_weight.shape,
        inner_bias.shape,
        outer_weight.shape,
        outer_bias.shape,
    )
    return tuple(value.reshape(shape) for value, shape in zip(final, shapes))


def solution(mesh):
    rows = P("shard", "ctx", None)
    vec, mat = P("shard"), P("shard", None)
    return jax.shard_map(
        functools.partial(on_device, mesh.shape["shard"], mesh.shape["ctx"]),
        mesh=mesh,
        in_specs=(
            rows,
            vec,
            rows,
            vec,
            vec,
            mat,
            mat,
            mat,
            mat,
            vec,
            vec,
            mat,
            vec,
            mat,
            vec,
            rows,
        ),
        out_specs=(
            rows,
            rows,
            vec,
            vec,
            mat,
            mat,
            mat,
            mat,
            vec,
            vec,
            mat,
            vec,
            mat,
            vec,
        ),
        check_vma=False,
    )
```

```python
import functools

import jax
import jax.numpy as jnp
from jax import lax
from jax.experimental import pallas as pl
from jax.experimental.pallas import tpu as pltpu
from jax.sharding import PartitionSpec as P

HS = 64
E = 24
TOP = 8
NORM_EPS = 1e-05
NEG_LARGE = -1e30
BF16 = jnp.bfloat16
F32 = jnp.float32
PANEL = 512
UNIT = 128
GELU_C = 0.7978845608028654
GELU_A = 0.044715
MESH = pl.DeviceIdType.MESH
RING = 40
START, CORE, NEAR_A, NEAR_B, FAR_0, FAR_1, FAR_2, PASS, SHARE, END = range(10)


def dot(left, right):
    return jnp.dot(left, right, preferred_element_type=F32)


def dot_t(left, right):
    return lax.dot_general(left, right, (((1,), (1,)), ((), ())), preferred_element_type=F32)


def many(first, size, step):
    return pl.ds(pl.multiple_of(first, step), size)


class Net:
    def __init__(self, shards, ctxs, group, send_sem, recv_sem):
        self.shards, self.ctxs, self.group = shards, ctxs, group
        self.pairs = group // 2
        self.groups = ctxs // group
        self.dims = self.pairs.bit_length() - 1
        self.z = lax.axis_index("shard")
        self.i = lax.axis_index("ctx")
        self.core = self.i % 2
        self.chip = (self.i % group) // 2
        self.grp = self.i // group
        self.send_sem, self.recv_sem = send_sem, recv_sem
        self.arrivals = 0
        self.starts = 0
        self.ring = [[] for _ in range(RING)]
        flip_low = self.chip + 1 - 2 * (self.chip % 2)
        if self.dims == 2:
            flip_high = self.chip + 2 - 4 * (self.chip // 2)
            self.chip_a = self.core * flip_high + (1 - self.core) * flip_low
            self.chip_b = self.core * flip_low + (1 - self.core) * flip_high
            self.chip_ab = self.pairs - 1 - self.chip
        elif self.dims == 1:
            self.chip_b = flip_low

    def far(self, step):
        return (self.z + step) % self.shards

    def src(self, step):
        return (self.z + self.shards - step) % self.shards

    def peer(self, chip):
        return self.grp * self.group + chip * 2 + self.core

    def sibling(self):
        return self.i + 1 - 2 * self.core

    def copy(self, src, dst, sent, arrived, z, i):
        return pltpu.make_async_remote_copy(
            src_ref=src,
            dst_ref=dst,
            send_sem=self.send_sem.at[sent],
            recv_sem=self.recv_sem.at[arrived],
            device_id={"shard": z, "ctx": i},
            device_id_type=MESH,
        )

    def arrival(self):
        self.arrivals += 1
        return self.arrivals - 1

    def send(self, src, dst, arrived, z, i):
        slot = self.starts % RING
        self.starts += 1
        if self.ring[slot]:
            self.left(self.ring[slot])
        one = self.ring[slot] = [self.copy(src, dst, slot, arrived, z, i)]
        one[0].start()
        return one

    def left(self, one):
        if one:
            one.pop().wait_send()

    def wait(self, arrived, dst):
        self.copy(dst, dst, 0, arrived, self.z, self.i).wait_recv()

    def finish(self):
        for one in self.ring:
            self.left(one)

    def greet(self):
        barrier = pltpu.get_barrier_semaphore()
        for step in range(1, self.ctxs):
            pl.semaphore_signal(
                barrier,
                inc=1,
                device_id={"shard": self.z, "ctx": (self.i + step) % self.ctxs},
                device_id_type=MESH,
            )
        for step in range(1, self.shards):
            pl.semaphore_signal(
                barrier,
                inc=1,
                device_id={"shard": self.far(step), "ctx": self.i},
                device_id_type=MESH,
            )

    def greeted(self):
        pl.semaphore_wait(pltpu.get_barrier_semaphore(), self.ctxs + self.shards - 2)


class Spread:
    def __init__(self, net, refs, all_of, at_once=False, straight=False):
        self.net, self.refs, self.all_of, self.at_once = net, refs, all_of, at_once
        self.straight = straight
        self.piece = refs[0].shape[0] // net.group
        self.half = refs[0].shape[0] // 2

    def part(self, chip):
        return many((self.net.core * self.net.pairs + chip) * self.piece, self.piece, self.piece)

    def block(self, core):
        return many(core * self.half, self.half, self.half)

    def give(self, rows, peer):
        arrived = self.net.arrival()
        for ref in self.refs:
            self.net.send(ref.at[rows], ref.at[rows], arrived, self.net.z, peer)
        return arrived

    def begin(self):
        net = self.net
        own = self.part(net.chip)
        if self.at_once:
            self.to_all = net.arrival()
            (ref,) = self.refs
            for step in range(1, net.group):
                peer = net.grp * net.group + (net.i + step) % net.group
                net.send(ref.at[own], ref.at[own], self.to_all, net.z, peer)
            return
        if net.dims == 2:
            self.to_a = self.give(own, net.peer(net.chip_a))
        if net.dims:
            self.to_b = self.give(own, net.peer(net.chip_b))
        if net.dims == 2 and self.straight:
            self.on = self.give(own, net.peer(net.chip_ab))

    def pass_on(self):
        net = self.net
        if net.dims == 2 and not self.straight:
            got = self.part(net.chip_a)
            net.wait(self.to_a, self.all_of(got))
            self.on = self.give(got, net.peer(net.chip_b))

    def share(self):
        net = self.net
        if net.dims:
            net.wait(self.to_b, self.all_of(self.part(net.chip_b)))
        if net.dims == 2:
            if self.straight:
                net.wait(self.to_a, self.all_of(self.part(net.chip_a)))
            net.wait(self.on, self.all_of(self.part(net.chip_ab)))
        self.cross()

    def cross(self):
        self.to_core = self.give(self.block(self.net.core), self.net.sibling())

    def end(self):
        if self.at_once:
            count = self.piece * (self.net.group - 1)
            self.net.wait(self.to_all, self.all_of(pl.ds(0, count)))
        else:
            self.net.wait(self.to_core, self.all_of(self.block(1 - self.net.core)))


class Gather:
    def __init__(self, net, buf, by_core=False):
        self.net, self.buf, self.by_core = net, buf, by_core
        planes = [buf.at[net.src(k)] for k in range(1, net.shards)]
        self.spread = Spread(net, planes, lambda rows: buf.at[0 : net.shards - 1, rows])
        self.rows = self.spread.block(net.core) if by_core else self.spread.part(net.chip)

    def start(self):
        net = self.net
        own = self.buf.at[net.z, self.rows]
        self.far = net.arrival()
        for k in range(1, net.shards):
            net.send(own, own, self.far, net.far(k), net.i)

    def begin(self):
        self.net.wait(self.far, self.spread.all_of(self.rows))
        if self.by_core:
            self.spread.cross()
        else:
            self.spread.begin()

    def pass_on(self):
        if not self.by_core:
            self.spread.pass_on()

    def share(self):
        if not self.by_core:
            self.spread.share()

    def end(self):
        self.spread.end()


class Absent:
    def start(self):
        pass

    begin = pass_on = share = end = start

    def to(self, name):
        pass


class Reduce:
    def __init__(self, net, buffers, out, far_first, halving, at_once, straight, store):
        self.net, self.out, self.store = net, out, store
        self.grad, self.from_core, self.from_a, self.from_b = buffers[0:4]
        self.from_group, self.from_far = buffers[4:6]
        self.far_first, self.halving = far_first, halving
        self.piece = self.grad.shape[1] // net.group
        self.half = self.grad.shape[1] // 2
        self.spread = Spread(net, [out], lambda rows: out.at[rows], at_once, straight)
        near = [(NEAR_B, self.take_b)]
        if net.dims == 2:
            near = [(NEAR_A, self.take_a)] + near
        if halving:
            rounds = net.shards.bit_length() - 1
            far = [(FAR_0 + k, functools.partial(self.take_half, k)) for k in range(rounds)]
        else:
            far = [(FAR_0, self.take_far)]
        steps = far + near if far_first else near + far
        name, step = steps[-1]
        steps[-1] = (name, functools.partial(self.last, step))
        after = [(PASS, self.spread.pass_on), (SHARE, self.spread.share)]
        after = [] if at_once else after if net.dims == 2 else after[1:]
        self.steps = [(START, self.start), (CORE, self.take_core), *steps, *after]
        self.steps.append((END, self.finish))
        far, near = [FAR_0, FAR_1, FAR_2], [NEAR_A, NEAR_B]
        order = far + near if far_first else near + far
        order = [START, CORE, *order, PASS, SHARE, END]
        self.rank = {name: k for k, name in enumerate(order)}

    def to(self, name):
        while self.steps and self.rank[self.steps[0][0]] <= self.rank[name]:
            self.steps.pop(0)[1]()

    def last(self, step):
        step()
        self.spread.begin()

    def finish(self):
        self.spread.end()
        self.store.start()

    def first(self, chip):
        return (self.net.core * self.net.pairs + chip) * self.piece

    def rows(self, chip):
        return many(self.first(chip), self.piece, self.piece)

    def planes(self, after_far):
        if after_far:
            return [(self.net.z, 0)]
        return [(s, s) for s in range(self.net.shards)]

    def add(self, first, count, planes, parts):
        lines = 16

        def one(step, carry):
            at = pl.multiple_of(step * lines, lines)
            rows = many(first + at, lines, lines)
            for here, there in planes:
                value = self.grad[here, rows].astype(F32)
                for part in parts:
                    value = value + part[there, pl.ds(at, lines)].astype(F32)
                self.grad[here, rows] = value.astype(BF16)
            return carry

        lax.fori_loop(0, count // lines, one, 0)

    def cut(self, rows, after_far):
        if after_far:
            return self.grad.at[pl.ds(self.net.z, 1), rows]
        return self.grad.at[:, rows]

    def start(self):
        net = self.net
        away = many((1 - net.core) * self.half, self.half, self.half)
        self.to_core = net.arrival()
        net.send(self.grad.at[:, away], self.from_core, self.to_core, net.z, net.sibling())

    def take_core(self):
        net = self.net
        net.wait(self.to_core, self.from_core)
        self.add(net.core * self.half, self.half, self.planes(False), [self.from_core])
        if self.far_first:
            own = many(net.core * self.half, self.half, self.half)
            self.send_far(own)
        else:
            self.send_near(False)

    def send_near(self, after_far):
        net = self.net
        if net.dims == 2:
            self.to_a = [net.arrival(), net.arrival()]
            for k, chip in ((1, net.chip_ab), (0, net.chip_a)):
                net.send(
                    self.cut(self.rows(chip), after_far),
                    self.from_a.at[k],
                    self.to_a[k],
                    net.z,
                    net.peer(net.chip_a),
                )
        elif net.dims == 1:
            self.send_b(after_far)

    def send_b(self, after_far):
        net = self.net
        self.to_b = net.arrival()
        rows = self.rows(net.chip_b)
        net.send(
            self.cut(rows, after_far), self.from_b, self.to_b, net.z, net.peer(net.chip_b)
        )

    def take_a(self):
        net = self.net
        for k, chip in ((1, net.chip_b), (0, net.chip)):
            net.wait(self.to_a[k], self.from_a.at[k])
            self.add(self.first(chip), self.piece, self.planes(self.far_first), [self.from_a.at[k]])
            if k:
                self.send_b(self.far_first)

    def take_b(self):
        net = self.net
        if net.dims:
            net.wait(self.to_b, self.from_b)
            self.add(
                self.first(net.chip), self.piece, self.planes(self.far_first), [self.from_b]
            )
        own = self.rows(net.chip)
        step, at = 1, 0
        while step < net.groups:
            peer = net.i + net.group * step * (1 - 2 * ((net.grp // step) % 2))
            arrived = net.arrival()
            one = net.send(
                self.cut(own, self.far_first), self.from_group.at[at], arrived, net.z, peer
            )
            net.wait(arrived, self.from_group.at[at])
            net.left(one)
            self.add(
                self.first(net.chip),
                self.piece,
                self.planes(self.far_first),
                [self.from_group.at[at]],
            )
            step, at = step * 2, at + 1
        if self.far_first:
            self.out[own, :] = self.grad[net.z, own]
        else:
            self.send_far(own)

    def send_far(self, own):
        net = self.net
        self.own = own
        if self.halving:
            self.send_half(0)
            return
        self.to_far = net.arrival()
        for k in range(1, net.shards):
            net.send(
                self.grad.at[pl.ds(net.far(k), 1), own],
                self.from_far.at[pl.ds(k - 1, 1)],
                self.to_far,
                net.far(k),
                net.i,
            )

    def half_at(self, turn):
        step = 1 << turn
        count = self.net.shards // (2 * step)
        return step, count, self.net.shards - 2 * count

    def send_half(self, turn):
        net = self.net
        step, count, at = self.half_at(turn)
        partner = net.z + step * (1 - 2 * ((net.z // step) % 2))
        self.to_far = net.arrival()
        for k in range(count):
            plane = partner % (2 * step) + 2 * step * k
            net.send(
                self.grad.at[pl.ds(plane, 1), self.own],
                self.from_far.at[pl.ds(at + k, 1)],
                self.to_far,
                partner,
                net.i,
            )

    def take_half(self, turn):
        net = self.net
        step, count, at = self.half_at(turn)
        parts = self.from_far.at[pl.ds(at, count)]
        net.wait(self.to_far, parts)
        planes = [(net.z % (2 * step) + 2 * step * k, k) for k in range(count)]
        first, size = (
            (net.core * self.half, self.half)
            if self.far_first
            else (self.first(net.chip), self.piece)
        )
        self.add(first, size, planes, [parts])
        if count > 1:
            self.send_half(turn + 1)
        else:
            self.far_done()

    def take_far(self):
        net = self.net
        net.wait(self.to_far, self.from_far)
        parts = [self.from_far.at[pl.ds(k, 1)] for k in range(net.shards - 1)]
        if self.far_first:
            self.add(net.core * self.half, self.half, self.planes(True), parts)
        else:
            self.add(self.first(net.chip), self.piece, self.planes(True), parts)
        self.far_done()

    def far_done(self):
        if self.far_first:
            self.send_near(True)
        else:
            self.out[self.own, :] = self.grad[self.net.z, self.own]


def reduce_scratch(shards, group, rounds, rows, wide, far_first):
    pairs = group // 2
    piece, half = rows // group, rows // 2
    planes = 1 if far_first else shards
    tiny = (1, 16, 128)
    return [
        pltpu.VMEM((shards, rows, wide), BF16),
        pltpu.VMEM((shards, half, wide), BF16),
        pltpu.VMEM((2, planes, piece, wide) if pairs == 4 else tiny, BF16),
        pltpu.VMEM((planes, piece, wide), BF16),
        pltpu.VMEM((rounds, planes, piece, wide) if rounds else tiny, BF16),
        pltpu.VMEM((shards - 1, half if far_first else piece, wide), BF16),
    ]


def layer_kernel(
    shards,
    ctxs,
    group,
    chunk_far,
    len_hbm,
    x_hbm,
    cot_hbm,
    picks_hbm,
    g1_hbm,
    b1_hbm,
    g2_hbm,
    b2_hbm,
    bo_hbm,
    bi_hbm,
    wq_hbm,
    wkv_hbm,
    wr_hbm,
    wo_hbm,
    wi_hbm,
    wout_hbm,
    out_hbm,
    gin_hbm,
    chunk_hbm,
    wo_hbm_out,
    q_hbm,
    kv_hbm,
    len_ref,
    x_ref,
    cot_ref,
    picks_ref,
    g1_ref,
    b1_ref,
    g2_ref,
    b2_ref,
    bo_ref,
    bi_ref,
    wq_st,
    wkv_st,
    wr_st,
    wi_st,
    stage,
    wk,
    wqs,
    wo,
    wc,
    vec_st,
    vecs,
    normed,
    normed_t,
    q_t,
    sel_a,
    heads_t,
    small,
    kvall,
    kvt,
    pads,
    hrow,
    linv,
    sbuf,
    ebuf,
    dkv,
    from_sib,
    from_kv,
    mixed_t,
    xhat2,
    n2,
    n2_t,
    gfin_low,
    biases,
    g_t,
    sums_c,
    sums_o,
    sums_q,
    sums_k,
    out_ref,
    gin_ref,
    chunk_out,
    wo_out,
    q_out,
    kv_out,
    vec_g,
    local_sem,
    send_sem,
    recv_sem,
):
    net = Net(shards, ctxs, group, send_sem, recv_sem)
    z, c = net.z, net.i
    tokens, width = x_ref.shape
    seg = tokens // 2
    half = seg // 2
    blocks = 2 * ctxs
    ws = width // shards
    wos = wo.shape[1]
    fs = wout_hbm.shape[0]
    scale = HS ** (-0.5)
    chunks = fs // UNIT
    panels = shards * UNIT // PANEL
    per_panel = PANEL // UNIT
    lanes = TOP * half
    wide = E * HS
    split = wide // 2
    sum_c, sum_q = [one[0] for one in sums_c], [one[0] for one in sums_q]
    sum_o, sum_k = sums_o[0], sums_k[0]
    vec_line = E
    bias_line = vec_line + 5
    per_unit = UNIT // ws
    near_steps = ctxs // 2

    def local(src, dst, at):
        return pltpu.make_async_copy(src, dst, local_sem.at[at])

    net.greet()
    wo_st, wout_st = stage.at[0:wos], stage.at[wos : wos + fs]
    resid, acc_a, acc_b = (stage.at[k * tokens : (k + 1) * tokens] for k in range(3))
    loads = {}
    for at, (src, dst) in enumerate(
        (
            (wkv_hbm, wkv_st),
            (g1_hbm, g1_ref),
            (b1_hbm, b1_ref),
            (g2_hbm, g2_ref),
            (b2_hbm, b2_ref),
            (bo_hbm, bo_ref),
            (bi_hbm, bi_ref),
            (wr_hbm, wr_st),
            (wq_hbm, wq_st),
            (x_hbm, x_ref),
            (picks_hbm, picks_ref),
            (wo_hbm, wo_st),
            (wi_hbm, wi_st),
            (wout_hbm, wout_st),
            (cot_hbm, cot_ref),
        )
    ):
        loads[id(dst)] = local(src, dst, at)
        loads[id(dst)].start()
    load_len = local(len_hbm, len_ref, 22 + chunks)
    load_len.start()
    loads[id(wkv_st)].wait()
    wk[z] = wkv_st[...].astype(BF16)
    vec_st[...] = jnp.zeros(vec_st.shape, F32)
    for row, ref in enumerate((g1_ref, b1_ref, g2_ref, b2_ref, bo_ref)):
        loads[id(ref)].wait()
        vec_st[row : row + 1, 0:ws] = ref[...]
    loads[id(bi_ref)].wait()
    for k in range(chunks):
        vec_st[5 + k : 6 + k, :] = bi_ref[:, k * UNIT : (k + 1) * UNIT]
    own_vec = vecs.at[z]
    own_vec[...] = vec_st[...].astype(BF16)
    net.greeted()
    gather_k, gather_o = Gather(net, wk, True), Gather(net, wo)
    gather_q = [Gather(net, one) for one in wqs]
    gather_c = [Gather(net, wc.at[k], k == chunks - 1) for k in range(chunks)]
    gather_k.start()
    vec_slot = net.arrival()
    for k in range(1, shards):
        net.send(own_vec, own_vec, vec_slot, net.far(k), net.i)
    loads[id(wq_st)].wait()
    loads[id(wr_st)].wait()
    for k in range(2):
        wqs[k][z, :, 0:split] = wq_st[:, k * split : (k + 1) * split].astype(BF16)
    padded = jnp.concatenate([wr_st[...], jnp.zeros((128 - E, ws), F32)], axis=0)
    wqs[1][z, :, split:] = padded.T.astype(BF16)

    loads[id(x_ref)].wait()
    x = x_ref[...].astype(F32)
    mean1 = jnp.mean(x, axis=1, keepdims=True)
    cen = x - mean1
    small[0, :, 0:1] = lax.rsqrt(jnp.mean(cen * cen, axis=1, keepdims=True) + NORM_EPS)
    small[0, :, 2:3] = mean1

    def first_hat():
        return (x_ref[...].astype(F32) - small[0, :, 2:3]) * small[0, :, 0:1]

    for ref in (wo_st, wi_st, wout_st):
        loads[id(ref)].wait()
    wo[z] = wo_st[...].astype(BF16)
    for k in range(chunks):
        wc[k, z, 0:UNIT] = wout_st[k * UNIT : (k + 1) * UNIT].astype(BF16)
        for s in range(shards):
            first = UNIT + (s // per_panel) * ws
            at = (s % per_panel) * UNIT
            wc[k, z, first : first + ws, at : at + UNIT] = wi_st[
                :, s * fs + k * UNIT : s * fs + (k + 1) * UNIT
            ].astype(BF16)
    for one in gather_q:
        one.start()
    gather_k.begin()
    load_len.wait()
    net.wait(vec_slot, vecs.at[0 : shards - 1])

    vec_all = [vecs[s].astype(F32) for s in range(shards)]

    def whole(row):
        return jnp.concatenate([one[row : row + 1, 0:ws] for one in vec_all], axis=1)

    gain1, bias1, gain2, bias2, bias_out = (whole(row) for row in range(5))
    for k in range(chunks):
        for p in range(panels):
            biases[k * panels + p : k * panels + p + 1, :] = jnp.concatenate(
                [one[5 + k : 6 + k] for one in vec_all[p * per_panel : (p + 1) * per_panel]],
                axis=1,
            )
    norm_value = first_hat() * gain1 + bias1
    normed[...] = norm_value.astype(BF16)
    normed_t[...] = norm_value.T.astype(BF16)
    gather_q[0].begin()
    def at_block(ref, block):
        return ref.at[block // 2, :, block % 2]

    def my_block(h):
        return c if h == 0 else blocks - 1 - c

    def core_blocks(ref, core):
        return ref.at[0:near_steps, :, core], ref.at[near_steps:ctxs, :, 1 - core]

    kv_slot, kv_cross, dkv_cross, dkv_near = (net.arrival() for _ in range(4))
    kv_sent = []

    def do_kvproj():
        kv_own = dot(normed[...], wk[...].reshape(width, 2 * HS)).astype(BF16)

        for h in range(2):
            block = my_block(h)
            for s in range(2):
                first = s * seg + h * half
                kvall[block // 2, s, block % 2] = kv_own[first : first + half]
        for step in range(1, near_steps):
            for block in (c, blocks - 1 - c):
                ref = at_block(kvall, block)
                kv_sent.append(net.send(ref, ref, kv_slot, z, (c + 2 * step) % ctxs))

    def do_kvcross():
        net.wait(kv_slot, kvall.at[0 : near_steps - 1])
        for part in core_blocks(kvall, net.core):
            kv_sent.append(net.send(part, part, kv_cross, z, net.sibling()))

    def do_kvwait():
        net.wait(kv_cross, kvall.at[0:near_steps])

    def do_turn():
        def turn(step, carry):
            for s in range(2):
                keys = kvall[step, s].reshape(2 * half, 2 * HS)
                kvt[step, s] = keys.astype(F32).T.astype(BF16)
                dkv[step, s] = jnp.zeros((2 * half, 2 * HS), F32)
            return carry

        lax.fori_loop(0, ctxs, turn, 0, unroll=4)

    def project_queries(part):
        def query_tile(n, carry):
            cols = many(n * 256, 256, 256)
            value = dot(normed[...], wqs[part][:, :, cols].reshape(width, 256))
            value = value.astype(BF16).astype(F32).T
            for k in range(4):
                q_t[part * (E // 2) + n * 4 + k] = value[k * HS : (k + 1) * HS]
            return carry

        lax.fori_loop(0, split // 256, query_tile, 0, unroll=True)

    def do_gates():
        logits_t = dot(normed[...], wqs[1][:, :, split:].reshape(width, 128)).T
        loads[id(picks_ref)].wait()
        picks = jnp.concatenate([picks_ref[0], picks_ref[1]], axis=1).astype(F32)
        picked = jnp.zeros((TOP, tokens), F32)
        for e in range(E):
            picked = jnp.where(picks == float(e), logits_t[e : e + 1, :], picked)
        top = jnp.max(picked, axis=0, keepdims=True)
        gexp = jnp.exp(picked - top)
        small[1, 0:TOP, 0:tokens] = gexp / jnp.sum(gexp, axis=0, keepdims=True)
        small[1, TOP : 2 * TOP, 0:tokens] = picks

    def choose(src, store):
        def one(j, carry):
            pick = small[1, pl.ds(TOP + j, 1), 0:tokens]
            value = jnp.zeros((HS, tokens), F32)
            for e in range(E):
                value = jnp.where(pick == float(e), src[e], value)
            store(j, value)
            return carry

        lax.fori_loop(0, TOP, one, 0, unroll=2)

    def spread_back(src, store):
        def one(e, carry):
            value = jnp.zeros((HS, tokens), F32)
            for j in range(TOP):
                pick = small[1, TOP + j : TOP + j + 1, 0:tokens]
                value = jnp.where(pick == e.astype(F32), src[j], value)
            store(e, value)
            return carry

        lax.fori_loop(0, E, one, 0, unroll=4)

    low_lane = lax.broadcasted_iota(jnp.int32, (HS, 2 * half), 1) < half

    def swap(one, two):
        return (
            jnp.where(low_lane, one, pltpu.roll(two, half, 1)),
            jnp.where(low_lane, pltpu.roll(one, half, 1), two),
        )

    def store_query(j, value):
        sel_a[j] = value * scale

    def do_choose():
        choose(q_t, store_query)
        for s in range(2):
            for pair in range(TOP // 2):
                halves = swap(
                    sel_a[2 * pair, :, s * seg : (s + 1) * seg],
                    sel_a[2 * pair + 1, :, s * seg : (s + 1) * seg],
                )
                for h in range(2):
                    pads[2 * s + h, 0:HS, pair * 128 : (pair + 1) * 128] = halves[h].astype(BF16)
        for sh in range(4):
            pads[sh, HS:, 0:lanes] = jnp.zeros((HS, lanes), BF16)
            pads[sh, 0:HS, lanes:] = jnp.zeros((HS, lanes), BF16)

    offset = lax.broadcasted_iota(jnp.int32, (1, lanes), 1) % half
    key_row = lax.broadcasted_iota(jnp.int32, (4 * half, lanes), 0)
    keep_scores = sbuf.shape[1] > 1

    def place(h):
        last = (blocks - c + 3) // 4
        if h == 1:
            return last, 0
        return (c + 4) // 4, last

    def fold(value, op):
        parts = [value[8 * k : 8 * k + 8] for k in range(value.shape[0] // 8)]
        while len(parts) > 1:
            parts = [op(parts[k], parts[k + 1]) for k in range(0, len(parts), 2)]
        return parts[0]

    def keys_of(step, s):
        return kvall[pl.ds(2 * step, 2), s].reshape(4 * half, 2 * HS)

    def turned(step, s, rows):
        return jnp.concatenate([kvt[2 * step + k, s, rows] for k in range(2)], axis=1)

    tops_of = {}

    def masked(step, s, h):
        limit = jnp.minimum(my_block(h) * half + offset, len_ref[s] - 1)
        scores = dot(keys_of(step, s), pads[2 * s + h, :, 0:lanes])
        return jnp.where(key_row <= limit - step * 4 * half, scores, NEG_LARGE)

    def find_tops(h):
        def score_step(step, tops):
            result = []
            for s in range(2):
                scores = masked(step, s, h)
                if keep_scores:
                    sbuf[s, step] = scores
                result.append(jnp.maximum(tops[s], fold(scores, jnp.maximum)))
            return tuple(result)

        start = jnp.full((8, lanes), NEG_LARGE, F32)
        tops = lax.fori_loop(0, place(h)[0], score_step, (start, start))
        tops_of[h] = [jnp.max(top, axis=0, keepdims=True) for top in tops]

    def weigh(h):
        count, base = place(h)
        for s in range(2):
            hrow[2 * s + h] = jnp.zeros((HS, lanes), F32)

        def value_step(step, totals):
            result = []
            for s in range(2):
                total = totals[s]
                scores = None if keep_scores else masked(step, s, h)
                for k in range(2):
                    rows = slice(2 * half * k, 2 * half * (k + 1))
                    part = sbuf[s, step, rows] if keep_scores else scores[rows]
                    expd = jnp.exp(part - tops_of[h][s])
                    ebuf[s, base + step, rows] = expd.astype(BF16)
                    total = total + fold(expd, jnp.add)
                hrow[2 * s + h] += dot(turned(step, s, slice(HS, 2 * HS)), ebuf[s, base + step])
                result.append(total)
            return tuple(result)

        start = jnp.zeros((8, lanes), F32)
        totals = lax.fori_loop(0, count, value_step, (start, start))
        for s in range(2):
            inverse = 1.0 / jnp.sum(totals[s], axis=0, keepdims=True)
            linv[2 * s + h] = jnp.broadcast_to(inverse, (8, lanes))
            hrow[2 * s + h] = hrow[2 * s + h] * inverse

    def do_mix():
        for s in range(2):
            for pair in range(TOP // 2):
                both = swap(
                    hrow[2 * s, :, pair * 128 : (pair + 1) * 128],
                    hrow[2 * s + 1, :, pair * 128 : (pair + 1) * 128],
                )
                for k in range(2):
                    heads_t[2 * pair + k, :, s * seg : (s + 1) * seg] = both[k]
        for j in range(TOP):
            sel_a[j] = heads_t[j] * small[1, j : j + 1, 0:tokens]

        def store_mixed(e, value):
            mixed_t[e] = value.astype(BF16)

        spread_back(sel_a, store_mixed)

    experts = E // shards
    row = lax.broadcasted_iota(jnp.int32, (tokens, 1), 0)
    inner_row = row % seg
    pos = jnp.where(
        inner_row < half, c * half + inner_row, blocks * half - (c + 2) * half + inner_row
    )
    valid = (pos < jnp.where(row < seg, len_ref[0], len_ref[1])).astype(F32)

    def do_project():
        acc_a[...] = x_ref[...].astype(F32)

        def project(s, carry):
            part = mixed_t[pl.ds(s * experts, experts)].reshape(wos, tokens)
            acc_a[...] += dot(part.astype(F32).T.astype(BF16), wo[s])
            return carry

        lax.fori_loop(0, shards, project, 0, unroll=True)
        residual = acc_a[...]
        resid[...] = residual
        cen = residual - jnp.mean(residual, axis=1, keepdims=True)
        rstd2 = lax.rsqrt(jnp.mean(cen * cen, axis=1, keepdims=True) + NORM_EPS)
        small[0, :, 1:2] = rstd2
        cen = cen * rstd2
        xhat2[...] = cen
        cen = cen * gain2 + bias2
        n2[...] = cen.astype(BF16)
        n2_t[...] = cen.T.astype(BF16)

        loads[id(cot_ref)].wait()
        gfin_low[...] = (cot_ref[...].astype(F32) * valid).astype(BF16)
        acc_a[...] = jnp.zeros((tokens, width), F32)
        acc_b[...] = jnp.zeros((tokens, width), F32)
        vec_g[...] = jnp.zeros(vec_g.shape, F32)

    def feed(k, p):
        rows_in = slice(UNIT + p * ws, UNIT + (p + 1) * ws)
        planes = slice(p * per_panel, (p + 1) * per_panel)
        w_in = wc[k, :, rows_in].reshape(width, PANEL)
        w_out = wc[k, planes, 0:UNIT].reshape(PANEL, width)
        line = k * panels + p
        hidden = dot(n2[...], w_in) + biases[line : line + 1, :]
        square = hidden * hidden
        tanh = jnp.tanh(GELU_C * hidden * (1.0 + GELU_A * square))
        act = (0.5 * hidden * (1.0 + tanh)).astype(BF16)
        slope = 0.5 * (1.0 + tanh) + 0.5 * GELU_C * hidden * (1.0 - tanh * tanh) * (
            1.0 + 3.0 * GELU_A * square
        )
        gfin = gfin_low[...]
        acc_a[...] += dot(act, w_out)
        grad_hidden = (slope * dot_t(gfin, w_out)).astype(BF16)
        total = jnp.sum(grad_hidden.astype(F32), axis=0, keepdims=True)
        for a in range(per_panel):
            for q in range(per_unit):
                at = bias_line + k * per_unit + q
                first = (p * per_panel + a) * ws
                vec_g[at : at + 1, first : first + ws] = total[
                    :, a * UNIT + q * ws : a * UNIT + (q + 1) * ws
                ]
        grad_outer = dot(act.astype(F32).T.astype(BF16), gfin).astype(BF16)
        sum_c[k][planes, 0:UNIT] = grad_outer.reshape(per_panel, UNIT, width)
        grad_inner = dot(n2_t[...], grad_hidden).astype(BF16)
        sum_c[k][:, rows_in] = grad_inner.reshape(shards, ws, PANEL)
        acc_b[...] += dot_t(grad_hidden, w_in)

    outs = [local(out_ref, out_hbm, 15), local(gin_ref, gin_hbm, 16)]

    def reduction(
        refs, out, hbm, at, far_first=False, halving=False, at_once=False, straight=False
    ):
        store = local(out, hbm, at)
        outs.append(store)
        return Reduce(net, refs, out, far_first, halving, at_once, straight, store)

    reduce_c = [
        reduction(sums_c[k], chunk_out.at[k], chunk_hbm.at[k], 20 + k, chunk_far[k], True)
        for k in range(chunks)
    ]
    reduce_o = reduction(sums_o, wo_out, wo_hbm_out, 17, straight=False)
    reduce_q = [
        reduction(
            sums_q[k],
            q_out[k],
            q_hbm.at[:, k * split : (k + 1) * split],
            20 + chunks + k,
            straight=True,
        )
        for k in range(2)
    ]
    reduce_k = reduction(sums_k, kv_out, kv_hbm, 19, at_once=True)

    def do_norm2():
        out_ref[...] = (valid * (resid[...] + acc_a[...] + bias_out)).astype(BF16)
        outs[0].start()
        gfin = cot_ref[...].astype(F32) * valid
        vec_g[vec_line + 4 : vec_line + 5, :] = jnp.sum(gfin, axis=0, keepdims=True)
        grad_n2 = acc_b[...]
        vec_g[vec_line + 3 : vec_line + 4, :] = jnp.sum(grad_n2, axis=0, keepdims=True)
        vec_g[vec_line + 2 : vec_line + 3, :] = jnp.sum(grad_n2 * xhat2[...], axis=0, keepdims=True)
        grad_hat = grad_n2 * gain2
        grad_hat = grad_hat - jnp.mean(grad_hat, axis=1, keepdims=True)
        grad_hat = grad_hat - xhat2[...] * jnp.mean(grad_hat * xhat2[...], axis=1, keepdims=True)
        grad_residual = gfin + grad_hat * small[0, :, 1:2]
        resid[...] = grad_residual
        n2[...] = grad_residual.astype(BF16)

    def do_branch():
        def branch(s, carry):
            part = mixed_t[pl.ds(s * experts, experts)].reshape(wos, tokens)
            sum_o[s] = dot(part, n2[...]).astype(BF16)
            grad = dot_t(wo[s], n2[...])
            q_t[pl.ds(s * experts, experts)] = grad.reshape(experts, HS, tokens)
            return carry

        lax.fori_loop(0, shards, branch, 0, unroll=2)

    def do_heads():
        def store_head_grad(j, value):
            sel_a[j] = value * small[1, pl.ds(j, 1), 0:tokens]
            small[1, pl.ds(2 * TOP + j, 1), 0:tokens] = jnp.sum(
                value * heads_t[j], axis=0, keepdims=True
            )

        choose(q_t, store_head_grad)
        gates = small[1, 0:TOP, 0:tokens]
        grad_gates = small[1, 2 * TOP : 3 * TOP, 0:tokens]
        grad_picked = gates * (grad_gates - jnp.sum(gates * grad_gates, axis=0, keepdims=True))
        picks = small[1, TOP : 2 * TOP, 0:tokens]
        g_t[wide : wide + 128, :] = jnp.zeros((128, tokens), BF16)
        grad_logits = [
            jnp.sum(jnp.where(picks == float(e), grad_picked, 0.0), axis=0, keepdims=True)
            for e in range(E)
        ]
        grad_logits += [jnp.zeros((1, tokens), F32)] * (32 - E)
        g_t[wide : wide + 32, :] = jnp.concatenate(grad_logits, axis=0).astype(BF16)
        for s in range(2):
            for pair in range(TOP // 2):
                halves = swap(
                    sel_a[2 * pair, :, s * seg : (s + 1) * seg],
                    sel_a[2 * pair + 1, :, s * seg : (s + 1) * seg],
                )
                at = pair * 128
                for h in range(2):
                    sh = 2 * s + h
                    grad = (halves[h] * linv[sh, 0:1, at : at + 128]).astype(BF16)
                    pads[sh, HS:, lanes + at : lanes + at + 128] = grad
                    linv[sh, 1:2, at : at + 128] = jnp.sum(
                        grad.astype(F32) * hrow[sh, :, at : at + 128], axis=0, keepdims=True
                    )

    def attend_back(h):
        count, base = place(h)
        deltas = [linv[2 * s + h, 1:2, :] for s in range(2)]
        for s in range(2):
            hrow[2 * s + h] = jnp.zeros((HS, lanes), F32)

        def grad_step(step, carry):
            for s in range(2):
                sh = 2 * s + h
                parts = []
                for k in range(2):
                    expd = ebuf[s, base + step, 2 * half * k : 2 * half * (k + 1)]
                    keys = kvall[2 * step + k, s].reshape(2 * half, 2 * HS)
                    grad_prob = dot(keys, pads[sh, :, lanes:])
                    parts.append((expd.astype(F32) * (grad_prob - deltas[s])).astype(BF16))
                grad_score = jnp.concatenate(parts, axis=0)
                grad = dot_t(grad_score, pads[sh, :, 0:lanes])
                grad = grad + dot_t(ebuf[s, base + step], pads[sh, :, lanes:])
                dkv[pl.ds(2 * step, 2), s] += grad.reshape(2, 2 * half, 2 * HS)
                hrow[sh] += dot(turned(step, s, slice(0, HS)), grad_score)
            return carry

        lax.fori_loop(0, count, grad_step, 0)

    def do_dsend():
        for one in kv_sent:
            net.left(one)

        def lower(step, carry):
            kvall[step] = dkv[step].astype(BF16).reshape(2, 2, half, 2 * HS)
            return carry

        lax.fori_loop(0, ctxs, lower, 0)
        for k, part in enumerate(core_blocks(kvall, 1 - net.core)):
            net.send(part, from_sib.at[k], dkv_cross, z, net.sibling())

    def do_gradq():
        for s in range(2):
            for pair in range(TOP // 2):
                both = swap(
                    hrow[2 * s, :, pair * 128 : (pair + 1) * 128],
                    hrow[2 * s + 1, :, pair * 128 : (pair + 1) * 128],
                )
                for k in range(2):
                    q_t[2 * pair + k, :, s * seg : (s + 1) * seg] = both[k] * scale

        def store_grad_query(e, value):
            g_t[many(e * HS, HS, HS), :] = value.astype(BF16)

        spread_back(q_t, store_grad_query)

    def query_grads(part):
        def query_grad(n, carry):
            rows = many(part * split + n * 256, 256, 256)
            grad = dot_t(normed_t[...], g_t[rows, :]).astype(BF16)
            sum_q[part][:, :, many(n * 256, 256, 256)] = grad.reshape(shards, ws, 256)
            return carry

        lax.fori_loop(0, split // 256, query_grad, 0, unroll=True)

    def do_dnear():
        net.wait(dkv_cross, from_sib)

        def add_sibling(step, carry):
            for k, sub in enumerate((net.core, 1 - net.core)):
                at = step + k * near_steps
                rows = many(sub * half, half, half)
                for s in range(2):
                    value = dkv[at, s, rows] + from_sib[k, step, s].astype(F32)
                    dkv[at, s, rows] = value
                    kvall[at, s, sub] = value.astype(BF16)
            return carry

        lax.fori_loop(0, near_steps, add_sibling, 0)
        for step in range(1, near_steps):
            peer = (c + 2 * step) % ctxs
            for h, block in enumerate((peer, blocks - 1 - peer)):
                net.send(at_block(kvall, block), from_kv.at[step - 1, h], dkv_near, z, peer)

    def do_ngrad():
        part = dot(wqs[0][...].reshape(width, split), g_t[0:split, :])
        part = part + dot(wqs[1][...].reshape(width, split + 128), g_t[split:, :])
        heads_t[...] = part.reshape(heads_t.shape)

    def do_dwait():
        net.wait(dkv_near, from_kv)

    def do_kvgrad():
        for h in range(2):
            block = my_block(h)
            for s in range(2):
                value = dkv[block // 2, s, many((block % 2) * half, half, half)]
                for step in range(1, near_steps):
                    value = value + from_kv[step - 1, h, s].astype(F32)
                first = s * seg + h * half
                acc_a[first : first + half, 0:128] = value
        grad_kv = acc_a[:, 0:128].T.astype(BF16)
        part = heads_t[...].reshape(width, tokens) + dot(wk[...].reshape(width, 2 * HS), grad_kv)
        grad_normed = part.T
        hat = first_hat()
        vec_g[vec_line : vec_line + 1, :] = jnp.sum(grad_normed * hat, axis=0, keepdims=True)
        vec_g[vec_line + 1 : vec_line + 2, :] = jnp.sum(grad_normed, axis=0, keepdims=True)
        value = dot_t(normed_t[...], grad_kv)
        sum_k[:, :, 0 : 2 * HS] = value.astype(BF16).reshape(shards, ws, 2 * HS)
        value = dot_t(normed_t[...], g_t[wide:, :]) + vec_g[...].T
        sum_k[:, :, 2 * HS :] = value.astype(BF16).reshape(shards, ws, 128)
        acc_b[...] = grad_normed

    def do_gin():
        hat = first_hat()
        grad_normed = acc_b[...]
        grad_hat = grad_normed * gain1
        grad_hat = grad_hat - jnp.mean(grad_hat, axis=1, keepdims=True)
        grad_hat = grad_hat - hat * jnp.mean(grad_hat * hat, axis=1, keepdims=True)
        gin_ref[...] = resid[...] + grad_hat * small[0, :, 0:1]
        outs[1].start()

    def feed_all(k):
        if k < chunks:
            for p in range(panels):
                feed(k, p)

    absent = [Absent()] * 4
    gc0, gc1, gc2, gc3 = (gather_c + absent)[0:4]
    rc0, rc1, rc2, rc3 = (reduce_c + absent)[0:4]
    (gq0, gq1), (rq0, rq1) = gather_q, reduce_q
    go, gk, ro, rk = gather_o, gather_k, reduce_o, reduce_k
    gk.end()
    do_kvproj()
    go.start()
    gq1.begin()
    gq0.pass_on()
    gc0.start()
    do_kvcross()
    gq1.pass_on()
    gc1.start()
    go.begin()
    gc2.start()
    gq0.share()
    do_kvwait()
    do_turn()
    gc0.begin()
    gq0.end()
    project_queries(0)
    gq1.share()
    gc1.begin()
    gq1.end()
    gc3.start()
    project_queries(1)
    do_gates()
    go.pass_on()
    gc2.begin()
    do_choose()
    gc0.pass_on()
    find_tops(1)
    gc1.pass_on()
    weigh(1)
    go.share()
    gc2.pass_on()
    find_tops(0)
    weigh(0)
    gc0.share()
    do_mix()
    go.end()
    do_project()
    gc1.share()
    gc0.end()
    feed_all(0)
    gc2.share()
    rc0.to(START)
    gc3.begin()
    gc3.pass_on()
    gc3.share()
    gc1.end()
    feed_all(1)
    rc1.to(START)
    gc2.end()
    feed_all(2)
    rc2.to(START)
    rc0.to(CORE)
    gc3.end()
    feed_all(3)
    rc3.to(START)
    rc1.to(CORE)
    do_norm2()
    rc2.to(CORE)
    do_branch()
    ro.to(START)
    rc3.to(CORE)
    do_heads()
    attend_back(1)
    attend_back(0)
    ro.to(CORE)
    do_dsend()
    do_gradq()
    query_grads(0)
    rq0.to(START)
    query_grads(1)
    rq1.to(START)
    rc2.to(NEAR_A)
    rc3.to(NEAR_A)
    do_dnear()
    do_ngrad()
    rc0.to(FAR_0)
    rc1.to(FAR_0)
    ro.to(NEAR_A)
    rc2.to(NEAR_B)
    rc3.to(NEAR_B)
    rq0.to(CORE)
    rq1.to(CORE)
    do_dwait()
    do_kvgrad()
    rk.to(START)
    do_gin()
    rk.to(CORE)
    ro.to(NEAR_B)
    rc0.to(FAR_1)
    rc1.to(FAR_1)
    rq0.to(NEAR_A)
    rq1.to(NEAR_A)
    rc2.to(FAR_0)
    rc3.to(FAR_0)
    rc0.to(NEAR_A)
    rc1.to(NEAR_A)
    rk.to(NEAR_A)
    rq0.to(NEAR_B)
    rq1.to(NEAR_B)
    ro.to(FAR_0)
    rc0.to(NEAR_B)
    rc1.to(NEAR_B)
    rc2.to(FAR_1)
    rc3.to(FAR_1)
    rk.to(NEAR_B)
    ro.to(PASS)
    rc0.to(PASS)
    rc1.to(PASS)
    rc2.to(PASS)
    rc3.to(PASS)
    rq0.to(FAR_0)
    rq1.to(FAR_0)
    rk.to(FAR_0)
    ro.to(SHARE)
    rc0.to(SHARE)
    rc1.to(SHARE)
    rc2.to(SHARE)
    rc3.to(SHARE)
    rq0.to(PASS)
    rq1.to(PASS)
    rc1.to(END)
    rc2.to(END)
    rc0.to(END)
    rc3.to(END)
    rq0.to(SHARE)
    rq1.to(SHARE)
    rk.to(END)
    ro.to(END)
    rq0.to(END)
    rq1.to(END)
    for one in (*reduce_c, ro, *reduce_q, rk):
        one.to(END)
    net.finish()
    for one in outs:
        one.wait()


def unpack_kernel(shards, *refs):
    ins, outs = refs[0:6], refs[6:20]
    in_st, out_st, sem = refs[20:26], refs[26:40], refs[40]
    chunks = ins[2].shape[0]
    copy = pltpu.make_async_copy
    loads = [copy(a, b, sem.at[k]) for k, (a, b) in enumerate(zip(ins, in_st)) if k != 2]
    loads.insert(2, None)
    stores = {
        k: copy(in_st[k] if k < 2 else out_st[k], outs[k], sem.at[6 + k])
        for k in range(14)
        if k != 12
    }
    chunk_in, wo_in, q_in, kv_in = in_st[2:]
    g1_ref, b1_ref, kv_ref, q_ref, r_ref, wo_ref, g2_ref, b2_ref = out_st[2:10]
    wi_ref, bi_ref, wout_ref, bo_ref = out_st[10:]
    ws, fs = q_ref.shape[0], wout_ref.shape[0]
    per_panel = PANEL // UNIT
    chunk_loads = [
        copy(ins[2].at[k], chunk_in.at[k], sem.at[20 + k]) for k in range(chunks)
    ]
    for one in chunk_loads:
        one.start()
    for k in (3, 4, 5, 1, 0):
        loads[k].start()
    for k in range(chunks):
        chunk_loads[k].wait()
        rows = slice(k * UNIT, (k + 1) * UNIT)
        wout_ref[rows, :] = chunk_in[k, 0:UNIT].astype(F32)
        stores[20 + k] = copy(wout_ref.at[rows], outs[12].at[rows], sem.at[20 + chunks + k])
        stores[20 + k].start()
        for s in range(shards):
            first = UNIT + (s // per_panel) * ws
            at = (s % per_panel) * UNIT
            wi_ref[:, s * fs + k * UNIT : s * fs + (k + 1) * UNIT] = chunk_in[
                k, first : first + ws, at : at + UNIT
            ].astype(F32)
    stores[10].start()
    loads[3].wait()
    wo_ref[...] = wo_in[...].astype(F32)
    stores[7].start()
    loads[4].wait()
    q_ref[...] = q_in[...].astype(F32)
    stores[5].start()
    loads[5].wait()
    kv_ref[...] = kv_in[:, 0 : 2 * HS].astype(F32)
    stores[4].start()
    turned = kv_in[:, 2 * HS :].astype(F32).T
    r_ref[...] = turned[0:E]
    stores[6].start()
    for row, at, ref in (
        (0, 2, g1_ref),
        (1, 3, b1_ref),
        (2, 8, g2_ref),
        (3, 9, b2_ref),
        (4, 13, bo_ref),
    ):
        ref[...] = turned[E + row : E + row + 1]
        stores[at].start()
    for line in range(fs // ws):
        bi_ref[:, line * ws : (line + 1) * ws] = turned[E + 5 + line : E + 6 + line]
    stores[11].start()
    loads[1].wait()
    stores[1].start()
    loads[0].wait()
    stores[0].start()
    for one in stores.values():
        one.wait()


def on_device(
    shards,
    ctxs,
    tokens,
    lengths,
    expert_picks,
    first_gain,
    first_bias,
    kv_weight,
    query_weight,
    router_weight,
    output_weight,
    second_gain,
    second_bias,
    inner_weight,
    inner_bias,
    outer_weight,
    outer_bias,
    cotangent,
):
    slots, seg, width = tokens.shape
    count = slots * seg
    half = seg // 2
    lanes = TOP * half
    ws = width // shards
    wos = output_weight.shape[0]
    fs = outer_weight.shape[0]
    group = min(ctxs, ws // 16, 8)
    pairs, groups = group // 2, ctxs // group
    rounds = groups.bit_length() - 1
    chunks = fs // UNIT
    panels = shards * UNIT // PANEL
    chunk_rows = UNIT + panels * ws
    wide = E * HS
    chunk_far = [k < 2 for k in range(chunks)]
    keep_scores = ctxs * seg * slots * lanes * 4 <= 8 * 1024 * 1024
    shapes_mid = (
        jax.ShapeDtypeStruct((count, width), BF16),
        jax.ShapeDtypeStruct((count, width), F32),
        jax.ShapeDtypeStruct((chunks, chunk_rows, PANEL), BF16),
        jax.ShapeDtypeStruct((wos, width), BF16),
        jax.ShapeDtypeStruct((ws, wide), BF16),
        jax.ShapeDtypeStruct((ws, 256), BF16),
    )

    anywhere = pl.BlockSpec(memory_space=pl.ANY)
    arrivals = 2 + (3 + chunks) * 5 + 1 + 4 + (4 + chunks) * (8 + rounds + shards.bit_length() - 1)
    scratch = [
        pltpu.SMEM(lengths.shape, jnp.int32),
        pltpu.VMEM((count, width), BF16),
        pltpu.VMEM((count, width), BF16),
        pltpu.VMEM((slots, TOP, seg), jnp.int32),
        *[pltpu.VMEM((1, ws), F32)] * 5,
        pltpu.VMEM((1, fs), F32),
        pltpu.VMEM(query_weight.shape, F32),
        pltpu.VMEM(kv_weight.shape, F32),
        pltpu.VMEM((E, ws), F32),
        pltpu.VMEM(inner_weight.shape, F32),
        pltpu.VMEM((max(wos + fs, 3 * count), width), F32),
        pltpu.VMEM((shards, ws, 2 * HS), BF16),
        [pltpu.VMEM((shards, ws, wide // 2 + 128 * k), BF16) for k in range(2)],
        pltpu.VMEM((shards, wos, width), BF16),
        pltpu.VMEM((chunks, shards, chunk_rows, PANEL), BF16),
        pltpu.VMEM((16, UNIT), F32),
        pltpu.VMEM((shards, 16, UNIT), BF16),
        pltpu.VMEM((count, width), BF16),
        pltpu.VMEM((width, count), BF16),
        pltpu.VMEM((E, HS, count), F32),
        pltpu.VMEM((TOP, HS, count), F32),
        pltpu.VMEM((TOP, HS, count), F32),
        pltpu.VMEM((2, count, count), F32),
        pltpu.VMEM((ctxs, slots, 2, half, 2 * HS), BF16),
        pltpu.VMEM((ctxs, slots, 2 * HS, 2 * half), BF16),
        pltpu.VMEM((4, 2 * HS, 2 * lanes), BF16),
        pltpu.VMEM((4, HS, lanes), F32),
        pltpu.VMEM((4, 8, lanes), F32),
        pltpu.VMEM((slots, ctxs // 2, 4 * half, lanes) if keep_scores else (1, 1, 8, 128), F32),
        pltpu.VMEM((slots, ctxs // 2 + 1, 4 * half, lanes), BF16),
        pltpu.VMEM((ctxs, slots, 2 * half, 2 * HS), F32),
        pltpu.VMEM((2, ctxs // 2, slots, half, 2 * HS), BF16),
        pltpu.VMEM((ctxs // 2 - 1, 2, slots, half, 2 * HS), BF16),
        pltpu.VMEM((E, HS, count), BF16),
        pltpu.VMEM((count, width), F32),
        pltpu.VMEM((count, width), BF16),
        pltpu.VMEM((width, count), BF16),
        pltpu.VMEM((count, width), BF16),
        pltpu.VMEM((8, PANEL), F32),
        pltpu.VMEM((wide + 128, count), BF16),
        [
            reduce_scratch(shards, group, rounds, chunk_rows, PANEL, chunk_far[k])
            for k in range(chunks)
        ],
        reduce_scratch(shards, group, rounds, wos, width, False),
        [reduce_scratch(shards, group, rounds, ws, wide // 2, False) for _ in range(2)],
        reduce_scratch(shards, group, rounds, ws, 256, False),
        *[pltpu.VMEM(one.shape, one.dtype) for one in shapes_mid[0:4]],
        [pltpu.VMEM((ws, wide // 2), BF16) for _ in range(2)],
        pltpu.VMEM((ws, 256), BF16),
        pltpu.VMEM((128, width), F32),
        pltpu.SemaphoreType.DMA((23 + chunks,)),
        pltpu.SemaphoreType.DMA((RING,)),
        pltpu.SemaphoreType.DMA((arrivals,)),
    ]
    results = pl.pallas_call(
        functools.partial(layer_kernel, shards, ctxs, group, chunk_far),
        out_shape=shapes_mid,
        in_specs=[anywhere] * 16,
        out_specs=tuple([anywhere] * 6),
        scratch_shapes=scratch,
        compiler_params=pltpu.CompilerParams(
            collective_id=0, has_side_effects=True, vmem_limit_bytes=63 * 1024 * 1024
        ),
        name="layer",
    )(
        lengths,
        tokens.reshape(count, width),
        cotangent.reshape(count, width),
        jnp.swapaxes(expert_picks, 1, 2),
        first_gain.reshape(1, ws),
        first_bias.reshape(1, ws),
        second_gain.reshape(1, ws),
        second_bias.reshape(1, ws),
        outer_bias.reshape(1, ws),
        inner_bias.reshape(1, fs),
        query_weight,
        kv_weight,
        router_weight.T,
        output_weight,
        inner_weight,
        outer_weight,
    )
    vec_shape = jax.ShapeDtypeStruct((1, ws), F32)
    shapes_out = (
        jax.ShapeDtypeStruct((count, width), BF16),
        jax.ShapeDtypeStruct((count, width), F32),
        vec_shape,
        vec_shape,
        jax.ShapeDtypeStruct(kv_weight.shape, F32),
        jax.ShapeDtypeStruct(query_weight.shape, F32),
        jax.ShapeDtypeStruct((E, ws), F32),
        jax.ShapeDtypeStruct(output_weight.shape, F32),
        vec_shape,
        vec_shape,
        jax.ShapeDtypeStruct(inner_weight.shape, F32),
        jax.ShapeDtypeStruct((1, fs), F32),
        jax.ShapeDtypeStruct(outer_weight.shape, F32),
        vec_shape,
    )
    final = pl.pallas_call(
        functools.partial(unpack_kernel, shards),
        out_shape=shapes_out,
        in_specs=[anywhere] * 6,
        out_specs=tuple([anywhere] * 14),
        scratch_shapes=[pltpu.VMEM(one.shape, one.dtype) for one in (*shapes_mid, *shapes_out)]
        + [pltpu.SemaphoreType.DMA((20 + 2 * chunks,))],
        name="unpack",
    )(*results)
    final = list(final)
    final[6] = final[6].T
    shapes = (
        tokens.shape,
        tokens.shape,
        first_gain.shape,
        first_bias.shape,
        kv_weight.shape,
        query_weight.shape,
        router_weight.shape,
        output_weight.shape,
        second_gain.shape,
        second_bias.shape,
        inner_weight.shape,
        inner_bias.shape,
        outer_weight.shape,
        outer_bias.shape,
    )
    return tuple(value.reshape(shape) for value, shape in zip(final, shapes))


def solution(mesh):
    rows = P("shard", "ctx", None)
    vec, mat = P("shard"), P("shard", None)
    return jax.shard_map(
        functools.partial(on_device, mesh.shape["shard"], mesh.shape["ctx"]),
        mesh=mesh,
        in_specs=(
            rows,
            vec,
            rows,
            vec,
            vec,
            mat,
            mat,
            mat,
            mat,
            vec,
            vec,
            mat,
            vec,
            mat,
            vec,
            rows,
        ),
        out_specs=(
            rows,
            rows,
            vec,
            vec,
            mat,
            mat,
            mat,
            mat,
            vec,
            vec,
            mat,
            vec,
            mat,
            vec,
        ),
        check_vma=False,
    )
```

```python
import functools

import jax
import jax.numpy as jnp
from jax import lax
from jax.experimental import pallas as pl
from jax.experimental.pallas import tpu as pltpu
from jax.sharding import PartitionSpec as P

HS = 64
E = 24
TOP = 8
NORM_EPS = 1e-05
NEG_LARGE = -1e30
BF16 = jnp.bfloat16
F32 = jnp.float32
PANEL = 512
UNIT = 128
GELU_C = 0.7978845608028654
GELU_A = 0.044715
MESH = pl.DeviceIdType.MESH
RING = 40
START, CORE, NEAR_A, NEAR_B, FAR_0, FAR_1, FAR_2, PASS, SHARE, END = range(10)


def dot(left, right):
    return jnp.dot(left, right, preferred_element_type=F32)


def dot_t(left, right):
    return lax.dot_general(left, right, (((1,), (1,)), ((), ())), preferred_element_type=F32)


def many(first, size, step):
    return pl.ds(pl.multiple_of(first, step), size)


class Net:
    def __init__(self, shards, ctxs, group, send_sem, recv_sem):
        self.shards, self.ctxs, self.group = shards, ctxs, group
        self.pairs = group // 2
        self.groups = ctxs // group
        self.dims = self.pairs.bit_length() - 1
        self.z = lax.axis_index("shard")
        self.i = lax.axis_index("ctx")
        self.core = self.i % 2
        self.chip = (self.i % group) // 2
        self.grp = self.i // group
        self.send_sem, self.recv_sem = send_sem, recv_sem
        self.arrivals = 0
        self.starts = 0
        self.ring = [[] for _ in range(RING)]
        flip_low = self.chip + 1 - 2 * (self.chip % 2)
        if self.dims == 2:
            flip_high = self.chip + 2 - 4 * (self.chip // 2)
            self.chip_a = self.core * flip_high + (1 - self.core) * flip_low
            self.chip_b = self.core * flip_low + (1 - self.core) * flip_high
            self.chip_ab = self.pairs - 1 - self.chip
        elif self.dims == 1:
            self.chip_b = flip_low

    def far(self, step):
        return (self.z + step) % self.shards

    def src(self, step):
        return (self.z + self.shards - step) % self.shards

    def peer(self, chip):
        return self.grp * self.group + chip * 2 + self.core

    def sibling(self):
        return self.i + 1 - 2 * self.core

    def copy(self, src, dst, sent, arrived, z, i):
        return pltpu.make_async_remote_copy(
            src_ref=src,
            dst_ref=dst,
            send_sem=self.send_sem.at[sent],
            recv_sem=self.recv_sem.at[arrived],
            device_id={"shard": z, "ctx": i},
            device_id_type=MESH,
        )

    def arrival(self):
        self.arrivals += 1
        return self.arrivals - 1

    def send(self, src, dst, arrived, z, i):
        slot = self.starts % RING
        self.starts += 1
        if self.ring[slot]:
            self.left(self.ring[slot])
        one = self.ring[slot] = [self.copy(src, dst, slot, arrived, z, i)]
        one[0].start()
        return one

    def left(self, one):
        if one:
            one.pop().wait_send()

    def wait(self, arrived, dst):
        self.copy(dst, dst, 0, arrived, self.z, self.i).wait_recv()

    def finish(self):
        for one in self.ring:
            self.left(one)

    def greet(self):
        barrier = pltpu.get_barrier_semaphore()
        for step in range(1, self.ctxs):
            pl.semaphore_signal(
                barrier,
                inc=1,
                device_id={"shard": self.z, "ctx": (self.i + step) % self.ctxs},
                device_id_type=MESH,
            )
        for step in range(1, self.shards):
            pl.semaphore_signal(
                barrier,
                inc=1,
                device_id={"shard": self.far(step), "ctx": self.i},
                device_id_type=MESH,
            )

    def greeted(self):
        pl.semaphore_wait(pltpu.get_barrier_semaphore(), self.ctxs + self.shards - 2)


class Spread:
    def __init__(self, net, refs, all_of, at_once=False, straight=False):
        self.net, self.refs, self.all_of, self.at_once = net, refs, all_of, at_once
        self.straight = straight
        self.piece = refs[0].shape[0] // net.group
        self.half = refs[0].shape[0] // 2

    def part(self, chip):
        return many((self.net.core * self.net.pairs + chip) * self.piece, self.piece, self.piece)

    def block(self, core):
        return many(core * self.half, self.half, self.half)

    def give(self, rows, peer):
        arrived = self.net.arrival()
        for ref in self.refs:
            self.net.send(ref.at[rows], ref.at[rows], arrived, self.net.z, peer)
        return arrived

    def begin(self):
        net = self.net
        own = self.part(net.chip)
        if self.at_once:
            self.to_all = net.arrival()
            (ref,) = self.refs
            for step in range(1, net.group):
                peer = net.grp * net.group + (net.i + step) % net.group
                net.send(ref.at[own], ref.at[own], self.to_all, net.z, peer)
            return
        if net.dims == 2:
            self.to_a = self.give(own, net.peer(net.chip_a))
        if net.dims:
            self.to_b = self.give(own, net.peer(net.chip_b))
        if net.dims == 2 and self.straight:
            self.on = self.give(own, net.peer(net.chip_ab))

    def pass_on(self):
        net = self.net
        if net.dims == 2 and not self.straight:
            got = self.part(net.chip_a)
            net.wait(self.to_a, self.all_of(got))
            self.on = self.give(got, net.peer(net.chip_b))

    def share(self):
        net = self.net
        if net.dims:
            net.wait(self.to_b, self.all_of(self.part(net.chip_b)))
        if net.dims == 2:
            if self.straight:
                net.wait(self.to_a, self.all_of(self.part(net.chip_a)))
            net.wait(self.on, self.all_of(self.part(net.chip_ab)))
        self.cross()

    def cross(self):
        self.to_core = self.give(self.block(self.net.core), self.net.sibling())

    def end(self):
        if self.at_once:
            count = self.piece * (self.net.group - 1)
            self.net.wait(self.to_all, self.all_of(pl.ds(0, count)))
        else:
            self.net.wait(self.to_core, self.all_of(self.block(1 - self.net.core)))


class Gather:
    def __init__(self, net, buf, by_core=False, straight=False):
        self.net, self.buf, self.by_core = net, buf, by_core
        planes = [buf.at[net.src(k)] for k in range(1, net.shards)]
        self.spread = Spread(
            net, planes, lambda rows: buf.at[0 : net.shards - 1, rows], False, straight
        )
        self.rows = self.spread.block(net.core) if by_core else self.spread.part(net.chip)

    def start(self):
        net = self.net
        own = self.buf.at[net.z, self.rows]
        self.far = net.arrival()
        for k in range(1, net.shards):
            net.send(own, own, self.far, net.far(k), net.i)

    def begin(self):
        self.net.wait(self.far, self.spread.all_of(self.rows))
        if self.by_core:
            self.spread.cross()
        else:
            self.spread.begin()

    def pass_on(self):
        if not self.by_core:
            self.spread.pass_on()

    def share(self):
        if not self.by_core:
            self.spread.share()

    def end(self):
        self.spread.end()


class Absent:
    def start(self):
        pass

    begin = pass_on = share = end = start

    def to(self, name):
        pass


class Reduce:
    def __init__(self, net, buffers, out, far_first, halving, at_once, straight, store):
        self.net, self.out, self.store = net, out, store
        self.grad, self.from_core, self.from_a, self.from_b = buffers[0:4]
        self.from_group, self.from_far = buffers[4:6]
        self.far_first, self.halving = far_first, halving
        self.piece = self.grad.shape[1] // net.group
        self.half = self.grad.shape[1] // 2
        self.spread = Spread(net, [out], lambda rows: out.at[rows], at_once, straight)
        near = [(NEAR_B, self.take_b)]
        if net.dims == 2:
            near = [(NEAR_A, self.take_a)] + near
        if halving:
            rounds = net.shards.bit_length() - 1
            far = [(FAR_0 + k, functools.partial(self.take_half, k)) for k in range(rounds)]
        else:
            far = [(FAR_0, self.take_far)]
        steps = far + near if far_first else near + far
        name, step = steps[-1]
        steps[-1] = (name, functools.partial(self.last, step))
        after = [(PASS, self.spread.pass_on), (SHARE, self.spread.share)]
        after = [] if at_once else after if net.dims == 2 else after[1:]
        self.steps = [(START, self.start), (CORE, self.take_core), *steps, *after]
        self.steps.append((END, self.finish))
        far, near = [FAR_0, FAR_1, FAR_2], [NEAR_A, NEAR_B]
        order = far + near if far_first else near + far
        order = [START, CORE, *order, PASS, SHARE, END]
        self.rank = {name: k for k, name in enumerate(order)}

    def to(self, name):
        while self.steps and self.rank[self.steps[0][0]] <= self.rank[name]:
            self.steps.pop(0)[1]()

    def last(self, step):
        step()
        self.spread.begin()

    def finish(self):
        self.spread.end()
        self.store.start()

    def first(self, chip):
        return (self.net.core * self.net.pairs + chip) * self.piece

    def rows(self, chip):
        return many(self.first(chip), self.piece, self.piece)

    def planes(self, after_far):
        if after_far:
            return [(self.net.z, 0)]
        return [(s, s) for s in range(self.net.shards)]

    def add(self, first, count, planes, parts):
        lines = 16

        def one(step, carry):
            at = pl.multiple_of(step * lines, lines)
            rows = many(first + at, lines, lines)
            for here, there in planes:
                value = self.grad[here, rows].astype(F32)
                for part in parts:
                    value = value + part[there, pl.ds(at, lines)].astype(F32)
                self.grad[here, rows] = value.astype(BF16)
            return carry

        lax.fori_loop(0, count // lines, one, 0)

    def cut(self, rows, after_far):
        if after_far:
            return self.grad.at[pl.ds(self.net.z, 1), rows]
        return self.grad.at[:, rows]

    def start(self):
        net = self.net
        away = many((1 - net.core) * self.half, self.half, self.half)
        self.to_core = net.arrival()
        net.send(self.grad.at[:, away], self.from_core, self.to_core, net.z, net.sibling())

    def take_core(self):
        net = self.net
        net.wait(self.to_core, self.from_core)
        self.add(net.core * self.half, self.half, self.planes(False), [self.from_core])
        if self.far_first:
            own = many(net.core * self.half, self.half, self.half)
            self.send_far(own)
        else:
            self.send_near(False)

    def send_near(self, after_far):
        net = self.net
        if net.dims == 2:
            self.to_a = [net.arrival(), net.arrival()]
            for k, chip in ((1, net.chip_ab), (0, net.chip_a)):
                net.send(
                    self.cut(self.rows(chip), after_far),
                    self.from_a.at[k],
                    self.to_a[k],
                    net.z,
                    net.peer(net.chip_a),
                )
        elif net.dims == 1:
            self.send_b(after_far)

    def send_b(self, after_far):
        net = self.net
        self.to_b = net.arrival()
        rows = self.rows(net.chip_b)
        net.send(
            self.cut(rows, after_far), self.from_b, self.to_b, net.z, net.peer(net.chip_b)
        )

    def take_a(self):
        net = self.net
        for k, chip in ((1, net.chip_b), (0, net.chip)):
            net.wait(self.to_a[k], self.from_a.at[k])
            self.add(self.first(chip), self.piece, self.planes(self.far_first), [self.from_a.at[k]])
            if k:
                self.send_b(self.far_first)

    def take_b(self):
        net = self.net
        if net.dims:
            net.wait(self.to_b, self.from_b)
            self.add(
                self.first(net.chip), self.piece, self.planes(self.far_first), [self.from_b]
            )
        own = self.rows(net.chip)
        step, at = 1, 0
        while step < net.groups:
            peer = net.i + net.group * step * (1 - 2 * ((net.grp // step) % 2))
            arrived = net.arrival()
            one = net.send(
                self.cut(own, self.far_first), self.from_group.at[at], arrived, net.z, peer
            )
            net.wait(arrived, self.from_group.at[at])
            net.left(one)
            self.add(
                self.first(net.chip),
                self.piece,
                self.planes(self.far_first),
                [self.from_group.at[at]],
            )
            step, at = step * 2, at + 1
        if self.far_first:
            self.out[own, :] = self.grad[net.z, own]
        else:
            self.send_far(own)

    def send_far(self, own):
        net = self.net
        self.own = own
        if self.halving:
            self.send_half(0)
            return
        self.to_far = net.arrival()
        for k in range(1, net.shards):
            net.send(
                self.grad.at[pl.ds(net.far(k), 1), own],
                self.from_far.at[pl.ds(k - 1, 1)],
                self.to_far,
                net.far(k),
                net.i,
            )

    def half_at(self, turn):
        step = 1 << turn
        count = self.net.shards // (2 * step)
        return step, count, self.net.shards - 2 * count

    def send_half(self, turn):
        net = self.net
        step, count, at = self.half_at(turn)
        partner = net.z + step * (1 - 2 * ((net.z // step) % 2))
        self.to_far = net.arrival()
        for k in range(count):
            plane = partner % (2 * step) + 2 * step * k
            net.send(
                self.grad.at[pl.ds(plane, 1), self.own],
                self.from_far.at[pl.ds(at + k, 1)],
                self.to_far,
                partner,
                net.i,
            )

    def take_half(self, turn):
        net = self.net
        step, count, at = self.half_at(turn)
        parts = self.from_far.at[pl.ds(at, count)]
        net.wait(self.to_far, parts)
        planes = [(net.z % (2 * step) + 2 * step * k, k) for k in range(count)]
        first, size = (
            (net.core * self.half, self.half)
            if self.far_first
            else (self.first(net.chip), self.piece)
        )
        self.add(first, size, planes, [parts])
        if count > 1:
            self.send_half(turn + 1)
        else:
            self.far_done()

    def take_far(self):
        net = self.net
        net.wait(self.to_far, self.from_far)
        parts = [self.from_far.at[pl.ds(k, 1)] for k in range(net.shards - 1)]
        if self.far_first:
            self.add(net.core * self.half, self.half, self.planes(True), parts)
        else:
            self.add(self.first(net.chip), self.piece, self.planes(True), parts)
        self.far_done()

    def far_done(self):
        if self.far_first:
            self.send_near(True)
        else:
            self.out[self.own, :] = self.grad[self.net.z, self.own]


def reduce_scratch(shards, group, rounds, rows, wide, far_first):
    pairs = group // 2
    piece, half = rows // group, rows // 2
    planes = 1 if far_first else shards
    tiny = (1, 16, 128)
    return [
        pltpu.VMEM((shards, rows, wide), BF16),
        pltpu.VMEM((shards, half, wide), BF16),
        pltpu.VMEM((2, planes, piece, wide) if pairs == 4 else tiny, BF16),
        pltpu.VMEM((planes, piece, wide), BF16),
        pltpu.VMEM((rounds, planes, piece, wide) if rounds else tiny, BF16),
        pltpu.VMEM((shards - 1, half if far_first else piece, wide), BF16),
    ]


def layer_kernel(
    shards,
    ctxs,
    group,
    chunk_far,
    len_hbm,
    x_hbm,
    cot_hbm,
    picks_hbm,
    g1_hbm,
    b1_hbm,
    g2_hbm,
    b2_hbm,
    bo_hbm,
    bi_hbm,
    wq_hbm,
    wkv_hbm,
    wr_hbm,
    wo_hbm,
    wi_hbm,
    wout_hbm,
    out_hbm,
    gin_hbm,
    chunk_hbm,
    wo_hbm_out,
    q_hbm,
    kv_hbm,
    len_ref,
    x_ref,
    cot_ref,
    picks_ref,
    g1_ref,
    b1_ref,
    g2_ref,
    b2_ref,
    bo_ref,
    bi_ref,
    wq_st,
    wkv_st,
    wr_st,
    wi_st,
    stage,
    wk,
    wqs,
    wo,
    wc,
    vec_st,
    vecs,
    normed,
    normed_t,
    q_t,
    sel_a,
    heads_t,
    small,
    kvall,
    kvt,
    pads,
    hrow,
    linv,
    sbuf,
    ebuf,
    dkv,
    from_sib,
    from_kv,
    mixed_t,
    xhat2,
    n2,
    n2_t,
    gfin_low,
    biases,
    g_t,
    sums_c,
    sums_o,
    sums_q,
    sums_k,
    out_ref,
    gin_ref,
    chunk_out,
    wo_out,
    q_out,
    kv_out,
    vec_g,
    local_sem,
    send_sem,
    recv_sem,
):
    net = Net(shards, ctxs, group, send_sem, recv_sem)
    z, c = net.z, net.i
    tokens, width = x_ref.shape
    seg = tokens // 2
    half = seg // 2
    blocks = 2 * ctxs
    ws = width // shards
    wos = wo.shape[1]
    fs = wout_hbm.shape[0]
    scale = HS ** (-0.5)
    chunks = fs // UNIT
    panels = shards * UNIT // PANEL
    per_panel = PANEL // UNIT
    lanes = TOP * half
    wide = E * HS
    split = wide // 2
    sum_c, sum_q = [one[0] for one in sums_c], [one[0] for one in sums_q]
    sum_o, sum_k = sums_o[0], sums_k[0]
    vec_line = E
    bias_line = vec_line + 5
    per_unit = UNIT // ws
    near_steps = ctxs // 2

    def local(src, dst, at):
        return pltpu.make_async_copy(src, dst, local_sem.at[at])

    net.greet()
    wo_st, wout_st = stage.at[0:wos], stage.at[wos : wos + fs]
    resid, acc_a, acc_b = (stage.at[k * tokens : (k + 1) * tokens] for k in range(3))
    loads = {}
    for at, (src, dst) in enumerate(
        (
            (wkv_hbm, wkv_st),
            (g1_hbm, g1_ref),
            (b1_hbm, b1_ref),
            (g2_hbm, g2_ref),
            (b2_hbm, b2_ref),
            (bo_hbm, bo_ref),
            (bi_hbm, bi_ref),
            (wr_hbm, wr_st),
            (wq_hbm, wq_st),
            (x_hbm, x_ref),
            (picks_hbm, picks_ref),
            (wo_hbm, wo_st),
            (wi_hbm, wi_st),
            (wout_hbm, wout_st),
            (cot_hbm, cot_ref),
        )
    ):
        loads[id(dst)] = local(src, dst, at)
        loads[id(dst)].start()
    load_len = local(len_hbm, len_ref, 22 + chunks)
    load_len.start()
    loads[id(wkv_st)].wait()
    wk[z] = wkv_st[...].astype(BF16)
    vec_st[...] = jnp.zeros(vec_st.shape, F32)
    for row, ref in enumerate((g1_ref, b1_ref, g2_ref, b2_ref, bo_ref)):
        loads[id(ref)].wait()
        vec_st[row : row + 1, 0:ws] = ref[...]
    loads[id(bi_ref)].wait()
    for k in range(chunks):
        vec_st[5 + k : 6 + k, :] = bi_ref[:, k * UNIT : (k + 1) * UNIT]
    own_vec = vecs.at[z]
    own_vec[...] = vec_st[...].astype(BF16)
    net.greeted()
    gather_k, gather_o = Gather(net, wk, True), Gather(net, wo)
    gather_q = [Gather(net, one, False, k == 1) for k, one in enumerate(wqs)]
    gather_c = [Gather(net, wc.at[k], k == chunks - 1) for k in range(chunks)]
    gather_k.start()
    vec_slot = net.arrival()
    for k in range(1, shards):
        net.send(own_vec, own_vec, vec_slot, net.far(k), net.i)
    loads[id(wq_st)].wait()
    loads[id(wr_st)].wait()
    for k in range(2):
        wqs[k][z, :, 0:split] = wq_st[:, k * split : (k + 1) * split].astype(BF16)
    padded = jnp.concatenate([wr_st[...], jnp.zeros((128 - E, ws), F32)], axis=0)
    wqs[1][z, :, split:] = padded.T.astype(BF16)

    loads[id(x_ref)].wait()
    x = x_ref[...].astype(F32)
    mean1 = jnp.mean(x, axis=1, keepdims=True)
    cen = x - mean1
    small[0, :, 0:1] = lax.rsqrt(jnp.mean(cen * cen, axis=1, keepdims=True) + NORM_EPS)
    small[0, :, 2:3] = mean1

    def first_hat():
        return (x_ref[...].astype(F32) - small[0, :, 2:3]) * small[0, :, 0:1]

    for ref in (wo_st, wi_st, wout_st):
        loads[id(ref)].wait()
    wo[z] = wo_st[...].astype(BF16)
    for k in range(chunks):
        wc[k, z, 0:UNIT] = wout_st[k * UNIT : (k + 1) * UNIT].astype(BF16)
        for s in range(shards):
            first = UNIT + (s // per_panel) * ws
            at = (s % per_panel) * UNIT
            wc[k, z, first : first + ws, at : at + UNIT] = wi_st[
                :, s * fs + k * UNIT : s * fs + (k + 1) * UNIT
            ].astype(BF16)
    for one in gather_q:
        one.start()
    gather_k.begin()
    load_len.wait()
    net.wait(vec_slot, vecs.at[0 : shards - 1])

    vec_all = [vecs[s].astype(F32) for s in range(shards)]

    def whole(row):
        return jnp.concatenate([one[row : row + 1, 0:ws] for one in vec_all], axis=1)

    gain1, bias1, gain2, bias2, bias_out = (whole(row) for row in range(5))
    for k in range(chunks):
        for p in range(panels):
            biases[k * panels + p : k * panels + p + 1, :] = jnp.concatenate(
                [one[5 + k : 6 + k] for one in vec_all[p * per_panel : (p + 1) * per_panel]],
                axis=1,
            )
    norm_value = first_hat() * gain1 + bias1
    normed[...] = norm_value.astype(BF16)
    normed_t[...] = norm_value.T.astype(BF16)
    gather_q[0].begin()
    def at_block(ref, block):
        return ref.at[block // 2, :, block % 2]

    def my_block(h):
        return c if h == 0 else blocks - 1 - c

    def core_blocks(ref, core):
        return ref.at[0:near_steps, :, core], ref.at[near_steps:ctxs, :, 1 - core]

    kv_slot, kv_cross, dkv_cross, dkv_near = (net.arrival() for _ in range(4))
    kv_sent = []

    def do_kvproj():
        kv_own = dot(normed[...], wk[...].reshape(width, 2 * HS)).astype(BF16)

        for h in range(2):
            block = my_block(h)
            for s in range(2):
                first = s * seg + h * half
                kvall[block // 2, s, block % 2] = kv_own[first : first + half]
        for step in range(1, near_steps):
            for block in (c, blocks - 1 - c):
                ref = at_block(kvall, block)
                kv_sent.append(net.send(ref, ref, kv_slot, z, (c + 2 * step) % ctxs))

    def do_kvcross():
        net.wait(kv_slot, kvall.at[0 : near_steps - 1])
        for part in core_blocks(kvall, net.core):
            kv_sent.append(net.send(part, part, kv_cross, z, net.sibling()))

    def do_kvwait():
        net.wait(kv_cross, kvall.at[0:near_steps])

    def do_turn():
        def turn(step, carry):
            for s in range(2):
                keys = kvall[step, s].reshape(2 * half, 2 * HS)
                kvt[step, s] = keys.astype(F32).T.astype(BF16)
                dkv[step, s] = jnp.zeros((2 * half, 2 * HS), F32)
            return carry

        lax.fori_loop(0, ctxs, turn, 0, unroll=4)

    def project_queries(part):
        def query_tile(n, carry):
            cols = many(n * 256, 256, 256)
            value = dot(normed[...], wqs[part][:, :, cols].reshape(width, 256))
            value = value.astype(BF16).astype(F32).T
            for k in range(4):
                q_t[part * (E // 2) + n * 4 + k] = value[k * HS : (k + 1) * HS]
            return carry

        lax.fori_loop(0, split // 256, query_tile, 0, unroll=True)

    def do_gates():
        logits_t = dot(normed[...], wqs[1][:, :, split:].reshape(width, 128)).T
        loads[id(picks_ref)].wait()
        picks = jnp.concatenate([picks_ref[0], picks_ref[1]], axis=1).astype(F32)
        picked = jnp.zeros((TOP, tokens), F32)
        for e in range(E):
            picked = jnp.where(picks == float(e), logits_t[e : e + 1, :], picked)
        top = jnp.max(picked, axis=0, keepdims=True)
        gexp = jnp.exp(picked - top)
        small[1, 0:TOP, 0:tokens] = gexp / jnp.sum(gexp, axis=0, keepdims=True)
        small[1, TOP : 2 * TOP, 0:tokens] = picks

    def choose(src, store):
        def one(j, carry):
            pick = small[1, pl.ds(TOP + j, 1), 0:tokens]
            value = jnp.zeros((HS, tokens), F32)
            for e in range(E):
                value = jnp.where(pick == float(e), src[e], value)
            store(j, value)
            return carry

        lax.fori_loop(0, TOP, one, 0, unroll=2)

    def spread_back(src, store):
        def one(e, carry):
            value = jnp.zeros((HS, tokens), F32)
            for j in range(TOP):
                pick = small[1, TOP + j : TOP + j + 1, 0:tokens]
                value = jnp.where(pick == e.astype(F32), src[j], value)
            store(e, value)
            return carry

        lax.fori_loop(0, E, one, 0, unroll=4)

    low_lane = lax.broadcasted_iota(jnp.int32, (HS, 2 * half), 1) < half

    def swap(one, two):
        return (
            jnp.where(low_lane, one, pltpu.roll(two, half, 1)),
            jnp.where(low_lane, pltpu.roll(one, half, 1), two),
        )

    def store_query(j, value):
        sel_a[j] = value * scale

    def do_choose():
        choose(q_t, store_query)
        for s in range(2):
            for pair in range(TOP // 2):
                halves = swap(
                    sel_a[2 * pair, :, s * seg : (s + 1) * seg],
                    sel_a[2 * pair + 1, :, s * seg : (s + 1) * seg],
                )
                for h in range(2):
                    pads[2 * s + h, 0:HS, pair * 128 : (pair + 1) * 128] = halves[h].astype(BF16)
        for sh in range(4):
            pads[sh, HS:, 0:lanes] = jnp.zeros((HS, lanes), BF16)
            pads[sh, 0:HS, lanes:] = jnp.zeros((HS, lanes), BF16)

    offset = lax.broadcasted_iota(jnp.int32, (1, lanes), 1) % half
    key_row = lax.broadcasted_iota(jnp.int32, (4 * half, lanes), 0)
    keep_scores = sbuf.shape[1] > 1

    def place(h):
        last = (blocks - c + 3) // 4
        if h == 1:
            return last, 0
        return (c + 4) // 4, last

    def fold(value, op):
        parts = [value[8 * k : 8 * k + 8] for k in range(value.shape[0] // 8)]
        while len(parts) > 1:
            parts = [op(parts[k], parts[k + 1]) for k in range(0, len(parts), 2)]
        return parts[0]

    def keys_of(step, s):
        return kvall[pl.ds(2 * step, 2), s].reshape(4 * half, 2 * HS)

    def turned(step, s, rows):
        return jnp.concatenate([kvt[2 * step + k, s, rows] for k in range(2)], axis=1)

    tops_of = {}

    def masked(step, s, h):
        limit = jnp.minimum(my_block(h) * half + offset, len_ref[s] - 1)
        scores = dot(keys_of(step, s), pads[2 * s + h, :, 0:lanes])
        return jnp.where(key_row <= limit - step * 4 * half, scores, NEG_LARGE)

    def find_tops(h):
        def score_step(step, tops):
            result = []
            for s in range(2):
                scores = masked(step, s, h)
                if keep_scores:
                    sbuf[s, step] = scores
                result.append(jnp.maximum(tops[s], fold(scores, jnp.maximum)))
            return tuple(result)

        start = jnp.full((8, lanes), NEG_LARGE, F32)
        tops = lax.fori_loop(0, place(h)[0], score_step, (start, start))
        tops_of[h] = [jnp.max(top, axis=0, keepdims=True) for top in tops]

    def weigh(h):
        count, base = place(h)
        for s in range(2):
            hrow[2 * s + h] = jnp.zeros((HS, lanes), F32)

        def value_step(step, totals):
            result = []
            for s in range(2):
                total = totals[s]
                scores = None if keep_scores else masked(step, s, h)
                for k in range(2):
                    rows = slice(2 * half * k, 2 * half * (k + 1))
                    part = sbuf[s, step, rows] if keep_scores else scores[rows]
                    expd = jnp.exp(part - tops_of[h][s])
                    ebuf[s, base + step, rows] = expd.astype(BF16)
                    total = total + fold(expd, jnp.add)
                hrow[2 * s + h] += dot(turned(step, s, slice(HS, 2 * HS)), ebuf[s, base + step])
                result.append(total)
            return tuple(result)

        start = jnp.zeros((8, lanes), F32)
        totals = lax.fori_loop(0, count, value_step, (start, start))
        for s in range(2):
            inverse = 1.0 / jnp.sum(totals[s], axis=0, keepdims=True)
            linv[2 * s + h] = jnp.broadcast_to(inverse, (8, lanes))
            hrow[2 * s + h] = hrow[2 * s + h] * inverse

    def do_mix():
        for s in range(2):
            for pair in range(TOP // 2):
                both = swap(
                    hrow[2 * s, :, pair * 128 : (pair + 1) * 128],
                    hrow[2 * s + 1, :, pair * 128 : (pair + 1) * 128],
                )
                for k in range(2):
                    heads_t[2 * pair + k, :, s * seg : (s + 1) * seg] = both[k]
        for j in range(TOP):
            sel_a[j] = heads_t[j] * small[1, j : j + 1, 0:tokens]

        def store_mixed(e, value):
            mixed_t[e] = value.astype(BF16)

        spread_back(sel_a, store_mixed)

    experts = E // shards
    row = lax.broadcasted_iota(jnp.int32, (tokens, 1), 0)
    inner_row = row % seg
    pos = jnp.where(
        inner_row < half, c * half + inner_row, blocks * half - (c + 2) * half + inner_row
    )
    valid = (pos < jnp.where(row < seg, len_ref[0], len_ref[1])).astype(F32)

    def do_project():
        acc_a[...] = x_ref[...].astype(F32)

        def project(s, carry):
            part = mixed_t[pl.ds(s * experts, experts)].reshape(wos, tokens)
            acc_a[...] += dot(part.astype(F32).T.astype(BF16), wo[s])
            return carry

        lax.fori_loop(0, shards, project, 0, unroll=True)
        residual = acc_a[...]
        resid[...] = residual
        cen = residual - jnp.mean(residual, axis=1, keepdims=True)
        rstd2 = lax.rsqrt(jnp.mean(cen * cen, axis=1, keepdims=True) + NORM_EPS)
        small[0, :, 1:2] = rstd2
        cen = cen * rstd2
        xhat2[...] = cen
        cen = cen * gain2 + bias2
        n2[...] = cen.astype(BF16)
        n2_t[...] = cen.T.astype(BF16)

        loads[id(cot_ref)].wait()
        gfin_low[...] = (cot_ref[...].astype(F32) * valid).astype(BF16)
        acc_a[...] = jnp.zeros((tokens, width), F32)
        acc_b[...] = jnp.zeros((tokens, width), F32)
        vec_g[...] = jnp.zeros(vec_g.shape, F32)

    def feed(k, p):
        rows_in = slice(UNIT + p * ws, UNIT + (p + 1) * ws)
        planes = slice(p * per_panel, (p + 1) * per_panel)
        w_in = wc[k, :, rows_in].reshape(width, PANEL)
        w_out = wc[k, planes, 0:UNIT].reshape(PANEL, width)
        line = k * panels + p
        hidden = dot(n2[...], w_in) + biases[line : line + 1, :]
        square = hidden * hidden
        tanh = jnp.tanh(GELU_C * hidden * (1.0 + GELU_A * square))
        act = (0.5 * hidden * (1.0 + tanh)).astype(BF16)
        slope = 0.5 * (1.0 + tanh) + 0.5 * GELU_C * hidden * (1.0 - tanh * tanh) * (
            1.0 + 3.0 * GELU_A * square
        )
        gfin = gfin_low[...]
        acc_a[...] += dot(act, w_out)
        grad_hidden = (slope * dot_t(gfin, w_out)).astype(BF16)
        total = jnp.sum(grad_hidden.astype(F32), axis=0, keepdims=True)
        for a in range(per_panel):
            for q in range(per_unit):
                at = bias_line + k * per_unit + q
                first = (p * per_panel + a) * ws
                vec_g[at : at + 1, first : first + ws] = total[
                    :, a * UNIT + q * ws : a * UNIT + (q + 1) * ws
                ]
        grad_outer = dot(act.astype(F32).T.astype(BF16), gfin).astype(BF16)
        sum_c[k][planes, 0:UNIT] = grad_outer.reshape(per_panel, UNIT, width)
        grad_inner = dot(n2_t[...], grad_hidden).astype(BF16)
        sum_c[k][:, rows_in] = grad_inner.reshape(shards, ws, PANEL)
        acc_b[...] += dot_t(grad_hidden, w_in)

    outs = [local(out_ref, out_hbm, 15), local(gin_ref, gin_hbm, 16)]

    def reduction(
        refs, out, hbm, at, far_first=False, halving=False, at_once=False, straight=False
    ):
        store = local(out, hbm, at)
        outs.append(store)
        return Reduce(net, refs, out, far_first, halving, at_once, straight, store)

    reduce_c = [
        reduction(sums_c[k], chunk_out.at[k], chunk_hbm.at[k], 20 + k, chunk_far[k], True)
        for k in range(chunks)
    ]
    reduce_o = reduction(sums_o, wo_out, wo_hbm_out, 17, straight=False)
    reduce_q = [
        reduction(
            sums_q[k],
            q_out[k],
            q_hbm.at[:, k * split : (k + 1) * split],
            20 + chunks + k,
            straight=True,
        )
        for k in range(2)
    ]
    reduce_k = reduction(sums_k, kv_out, kv_hbm, 19, at_once=True)

    def do_norm2():
        out_ref[...] = (valid * (resid[...] + acc_a[...] + bias_out)).astype(BF16)
        outs[0].start()
        gfin = cot_ref[...].astype(F32) * valid
        vec_g[vec_line + 4 : vec_line + 5, :] = jnp.sum(gfin, axis=0, keepdims=True)
        grad_n2 = acc_b[...]
        vec_g[vec_line + 3 : vec_line + 4, :] = jnp.sum(grad_n2, axis=0, keepdims=True)
        vec_g[vec_line + 2 : vec_line + 3, :] = jnp.sum(grad_n2 * xhat2[...], axis=0, keepdims=True)
        grad_hat = grad_n2 * gain2
        grad_hat = grad_hat - jnp.mean(grad_hat, axis=1, keepdims=True)
        grad_hat = grad_hat - xhat2[...] * jnp.mean(grad_hat * xhat2[...], axis=1, keepdims=True)
        grad_residual = gfin + grad_hat * small[0, :, 1:2]
        resid[...] = grad_residual
        n2[...] = grad_residual.astype(BF16)

    def do_branch():
        def branch(s, carry):
            part = mixed_t[pl.ds(s * experts, experts)].reshape(wos, tokens)
            sum_o[s] = dot(part, n2[...]).astype(BF16)
            grad = dot_t(wo[s], n2[...])
            q_t[pl.ds(s * experts, experts)] = grad.reshape(experts, HS, tokens)
            return carry

        lax.fori_loop(0, shards, branch, 0, unroll=2)

    def do_heads():
        def store_head_grad(j, value):
            sel_a[j] = value * small[1, pl.ds(j, 1), 0:tokens]
            small[1, pl.ds(2 * TOP + j, 1), 0:tokens] = jnp.sum(
                value * heads_t[j], axis=0, keepdims=True
            )

        choose(q_t, store_head_grad)
        gates = small[1, 0:TOP, 0:tokens]
        grad_gates = small[1, 2 * TOP : 3 * TOP, 0:tokens]
        grad_picked = gates * (grad_gates - jnp.sum(gates * grad_gates, axis=0, keepdims=True))
        picks = small[1, TOP : 2 * TOP, 0:tokens]
        g_t[wide : wide + 128, :] = jnp.zeros((128, tokens), BF16)
        grad_logits = [
            jnp.sum(jnp.where(picks == float(e), grad_picked, 0.0), axis=0, keepdims=True)
            for e in range(E)
        ]
        grad_logits += [jnp.zeros((1, tokens), F32)] * (32 - E)
        g_t[wide : wide + 32, :] = jnp.concatenate(grad_logits, axis=0).astype(BF16)
        for s in range(2):
            for pair in range(TOP // 2):
                halves = swap(
                    sel_a[2 * pair, :, s * seg : (s + 1) * seg],
                    sel_a[2 * pair + 1, :, s * seg : (s + 1) * seg],
                )
                at = pair * 128
                for h in range(2):
                    sh = 2 * s + h
                    grad = (halves[h] * linv[sh, 0:1, at : at + 128]).astype(BF16)
                    pads[sh, HS:, lanes + at : lanes + at + 128] = grad
                    linv[sh, 1:2, at : at + 128] = jnp.sum(
                        grad.astype(F32) * hrow[sh, :, at : at + 128], axis=0, keepdims=True
                    )

    def attend_back(h):
        count, base = place(h)
        deltas = [linv[2 * s + h, 1:2, :] for s in range(2)]
        for s in range(2):
            hrow[2 * s + h] = jnp.zeros((HS, lanes), F32)

        def grad_step(step, carry):
            for s in range(2):
                sh = 2 * s + h
                parts = []
                for k in range(2):
                    expd = ebuf[s, base + step, 2 * half * k : 2 * half * (k + 1)]
                    keys = kvall[2 * step + k, s].reshape(2 * half, 2 * HS)
                    grad_prob = dot(keys, pads[sh, :, lanes:])
                    parts.append((expd.astype(F32) * (grad_prob - deltas[s])).astype(BF16))
                grad_score = jnp.concatenate(parts, axis=0)
                grad = dot_t(grad_score, pads[sh, :, 0:lanes])
                grad = grad + dot_t(ebuf[s, base + step], pads[sh, :, lanes:])
                dkv[pl.ds(2 * step, 2), s] += grad.reshape(2, 2 * half, 2 * HS)
                hrow[sh] += dot(turned(step, s, slice(0, HS)), grad_score)
            return carry

        lax.fori_loop(0, count, grad_step, 0)

    def do_dsend():
        for one in kv_sent:
            net.left(one)

        def lower(step, carry):
            kvall[step] = dkv[step].astype(BF16).reshape(2, 2, half, 2 * HS)
            return carry

        lax.fori_loop(0, ctxs, lower, 0)
        for k, part in enumerate(core_blocks(kvall, 1 - net.core)):
            net.send(part, from_sib.at[k], dkv_cross, z, net.sibling())

    def do_gradq():
        for s in range(2):
            for pair in range(TOP // 2):
                both = swap(
                    hrow[2 * s, :, pair * 128 : (pair + 1) * 128],
                    hrow[2 * s + 1, :, pair * 128 : (pair + 1) * 128],
                )
                for k in range(2):
                    q_t[2 * pair + k, :, s * seg : (s + 1) * seg] = both[k] * scale

        def store_grad_query(e, value):
            g_t[many(e * HS, HS, HS), :] = value.astype(BF16)

        spread_back(q_t, store_grad_query)

    def query_grads(part):
        def query_grad(n, carry):
            rows = many(part * split + n * 256, 256, 256)
            grad = dot_t(normed_t[...], g_t[rows, :]).astype(BF16)
            sum_q[part][:, :, many(n * 256, 256, 256)] = grad.reshape(shards, ws, 256)
            return carry

        lax.fori_loop(0, split // 256, query_grad, 0, unroll=True)

    def do_dnear():
        net.wait(dkv_cross, from_sib)

        def add_sibling(step, carry):
            for k, sub in enumerate((net.core, 1 - net.core)):
                at = step + k * near_steps
                rows = many(sub * half, half, half)
                for s in range(2):
                    value = dkv[at, s, rows] + from_sib[k, step, s].astype(F32)
                    dkv[at, s, rows] = value
                    kvall[at, s, sub] = value.astype(BF16)
            return carry

        lax.fori_loop(0, near_steps, add_sibling, 0)
        for step in range(1, near_steps):
            peer = (c + 2 * step) % ctxs
            for h, block in enumerate((peer, blocks - 1 - peer)):
                net.send(at_block(kvall, block), from_kv.at[step - 1, h], dkv_near, z, peer)

    def do_ngrad():
        part = dot(wqs[0][...].reshape(width, split), g_t[0:split, :])
        part = part + dot(wqs[1][...].reshape(width, split + 128), g_t[split:, :])
        heads_t[...] = part.reshape(heads_t.shape)

    def do_dwait():
        net.wait(dkv_near, from_kv)

    def do_kvgrad():
        for h in range(2):
            block = my_block(h)
            for s in range(2):
                value = dkv[block // 2, s, many((block % 2) * half, half, half)]
                for step in range(1, near_steps):
                    value = value + from_kv[step - 1, h, s].astype(F32)
                first = s * seg + h * half
                acc_a[first : first + half, 0:128] = value
        grad_kv = acc_a[:, 0:128].T.astype(BF16)
        part = heads_t[...].reshape(width, tokens) + dot(wk[...].reshape(width, 2 * HS), grad_kv)
        grad_normed = part.T
        hat = first_hat()
        vec_g[vec_line : vec_line + 1, :] = jnp.sum(grad_normed * hat, axis=0, keepdims=True)
        vec_g[vec_line + 1 : vec_line + 2, :] = jnp.sum(grad_normed, axis=0, keepdims=True)
        value = dot_t(normed_t[...], grad_kv)
        sum_k[:, :, 0 : 2 * HS] = value.astype(BF16).reshape(shards, ws, 2 * HS)
        value = dot_t(normed_t[...], g_t[wide:, :]) + vec_g[...].T
        sum_k[:, :, 2 * HS :] = value.astype(BF16).reshape(shards, ws, 128)
        acc_b[...] = grad_normed

    def do_gin():
        hat = first_hat()
        grad_normed = acc_b[...]
        grad_hat = grad_normed * gain1
        grad_hat = grad_hat - jnp.mean(grad_hat, axis=1, keepdims=True)
        grad_hat = grad_hat - hat * jnp.mean(grad_hat * hat, axis=1, keepdims=True)
        gin_ref[...] = resid[...] + grad_hat * small[0, :, 0:1]
        outs[1].start()

    def feed_all(k):
        if k < chunks:
            for p in range(panels):
                feed(k, p)

    absent = [Absent()] * 4
    gc0, gc1, gc2, gc3 = (gather_c + absent)[0:4]
    rc0, rc1, rc2, rc3 = (reduce_c + absent)[0:4]
    (gq0, gq1), (rq0, rq1) = gather_q, reduce_q
    go, gk, ro, rk = gather_o, gather_k, reduce_o, reduce_k
    gk.end()
    do_kvproj()
    go.start()
    gq1.begin()
    gq0.pass_on()
    gc0.start()
    do_kvcross()
    gq1.pass_on()
    gc1.start()
    go.begin()
    gc2.start()
    gq0.share()
    do_kvwait()
    do_turn()
    gc0.begin()
    gq0.end()
    project_queries(0)
    gq1.share()
    gc1.begin()
    gq1.end()
    gc3.start()
    project_queries(1)
    do_gates()
    go.pass_on()
    gc2.begin()
    do_choose()
    gc0.pass_on()
    find_tops(1)
    gc1.pass_on()
    weigh(1)
    go.share()
    gc2.pass_on()
    find_tops(0)
    weigh(0)
    gc0.share()
    do_mix()
    go.end()
    do_project()
    gc1.share()
    gc0.end()
    feed_all(0)
    gc2.share()
    rc0.to(START)
    gc3.begin()
    gc3.pass_on()
    gc3.share()
    gc1.end()
    feed_all(1)
    rc1.to(START)
    gc2.end()
    feed_all(2)
    rc2.to(START)
    rc0.to(CORE)
    gc3.end()
    feed_all(3)
    rc3.to(START)
    rc1.to(CORE)
    do_norm2()
    rc2.to(CORE)
    do_branch()
    ro.to(START)
    rc3.to(CORE)
    do_heads()
    attend_back(1)
    attend_back(0)
    ro.to(CORE)
    do_dsend()
    do_gradq()
    query_grads(0)
    rq0.to(START)
    query_grads(1)
    rq1.to(START)
    rc2.to(NEAR_A)
    rc3.to(NEAR_A)
    do_dnear()
    do_ngrad()
    rc0.to(FAR_0)
    rc1.to(FAR_0)
    ro.to(NEAR_A)
    rc2.to(NEAR_B)
    rc3.to(NEAR_B)
    rq0.to(CORE)
    rq1.to(CORE)
    do_dwait()
    do_kvgrad()
    rk.to(START)
    do_gin()
    rk.to(CORE)
    ro.to(NEAR_B)
    rc0.to(FAR_1)
    rc1.to(FAR_1)
    rq0.to(NEAR_A)
    rq1.to(NEAR_A)
    rc2.to(FAR_0)
    rc3.to(FAR_0)
    rc0.to(NEAR_A)
    rc1.to(NEAR_A)
    rk.to(NEAR_A)
    rq0.to(NEAR_B)
    rq1.to(NEAR_B)
    ro.to(FAR_0)
    rc0.to(NEAR_B)
    rc1.to(NEAR_B)
    rc2.to(FAR_1)
    rc3.to(FAR_1)
    rk.to(NEAR_B)
    ro.to(PASS)
    rc0.to(PASS)
    rc1.to(PASS)
    rc2.to(PASS)
    rc3.to(PASS)
    rq0.to(FAR_0)
    rq1.to(FAR_0)
    rk.to(FAR_0)
    ro.to(SHARE)
    rc0.to(SHARE)
    rc1.to(SHARE)
    rc2.to(SHARE)
    rc3.to(SHARE)
    rq0.to(PASS)
    rq1.to(PASS)
    rc1.to(END)
    rc2.to(END)
    rc0.to(END)
    rc3.to(END)
    rq0.to(SHARE)
    rq1.to(SHARE)
    rk.to(END)
    ro.to(END)
    rq0.to(END)
    rq1.to(END)
    for one in (*reduce_c, ro, *reduce_q, rk):
        one.to(END)
    net.finish()
    for one in outs:
        one.wait()


def unpack_kernel(shards, *refs):
    ins, outs = refs[0:6], refs[6:20]
    in_st, out_st, sem = refs[20:26], refs[26:40], refs[40]
    chunks = ins[2].shape[0]
    copy = pltpu.make_async_copy
    loads = [copy(a, b, sem.at[k]) for k, (a, b) in enumerate(zip(ins, in_st)) if k != 2]
    loads.insert(2, None)
    stores = {
        k: copy(in_st[k] if k < 2 else out_st[k], outs[k], sem.at[6 + k])
        for k in range(14)
        if k != 12
    }
    chunk_in, wo_in, q_in, kv_in = in_st[2:]
    g1_ref, b1_ref, kv_ref, q_ref, r_ref, wo_ref, g2_ref, b2_ref = out_st[2:10]
    wi_ref, bi_ref, wout_ref, bo_ref = out_st[10:]
    ws, fs = q_ref.shape[0], wout_ref.shape[0]
    per_panel = PANEL // UNIT
    chunk_loads = [
        copy(ins[2].at[k], chunk_in.at[k], sem.at[20 + k]) for k in range(chunks)
    ]
    for one in chunk_loads:
        one.start()
    for k in (3, 4, 5, 1, 0):
        loads[k].start()
    for k in range(chunks):
        chunk_loads[k].wait()
        rows = slice(k * UNIT, (k + 1) * UNIT)
        wout_ref[rows, :] = chunk_in[k, 0:UNIT].astype(F32)
        stores[20 + k] = copy(wout_ref.at[rows], outs[12].at[rows], sem.at[20 + chunks + k])
        stores[20 + k].start()
        for s in range(shards):
            first = UNIT + (s // per_panel) * ws
            at = (s % per_panel) * UNIT
            wi_ref[:, s * fs + k * UNIT : s * fs + (k + 1) * UNIT] = chunk_in[
                k, first : first + ws, at : at + UNIT
            ].astype(F32)
    stores[10].start()
    loads[3].wait()
    wo_ref[...] = wo_in[...].astype(F32)
    stores[7].start()
    loads[4].wait()
    q_ref[...] = q_in[...].astype(F32)
    stores[5].start()
    loads[5].wait()
    kv_ref[...] = kv_in[:, 0 : 2 * HS].astype(F32)
    stores[4].start()
    turned = kv_in[:, 2 * HS :].astype(F32).T
    r_ref[...] = turned[0:E]
    stores[6].start()
    for row, at, ref in (
        (0, 2, g1_ref),
        (1, 3, b1_ref),
        (2, 8, g2_ref),
        (3, 9, b2_ref),
        (4, 13, bo_ref),
    ):
        ref[...] = turned[E + row : E + row + 1]
        stores[at].start()
    for line in range(fs // ws):
        bi_ref[:, line * ws : (line + 1) * ws] = turned[E + 5 + line : E + 6 + line]
    stores[11].start()
    loads[1].wait()
    stores[1].start()
    loads[0].wait()
    stores[0].start()
    for one in stores.values():
        one.wait()


def on_device(
    shards,
    ctxs,
    tokens,
    lengths,
    expert_picks,
    first_gain,
    first_bias,
    kv_weight,
    query_weight,
    router_weight,
    output_weight,
    second_gain,
    second_bias,
    inner_weight,
    inner_bias,
    outer_weight,
    outer_bias,
    cotangent,
):
    slots, seg, width = tokens.shape
    count = slots * seg
    half = seg // 2
    lanes = TOP * half
    ws = width // shards
    wos = output_weight.shape[0]
    fs = outer_weight.shape[0]
    group = min(ctxs, ws // 16, 8)
    pairs, groups = group // 2, ctxs // group
    rounds = groups.bit_length() - 1
    chunks = fs // UNIT
    panels = shards * UNIT // PANEL
    chunk_rows = UNIT + panels * ws
    wide = E * HS
    chunk_far = [k < 2 for k in range(chunks)]
    keep_scores = ctxs * seg * slots * lanes * 4 <= 8 * 1024 * 1024
    shapes_mid = (
        jax.ShapeDtypeStruct((count, width), BF16),
        jax.ShapeDtypeStruct((count, width), F32),
        jax.ShapeDtypeStruct((chunks, chunk_rows, PANEL), BF16),
        jax.ShapeDtypeStruct((wos, width), BF16),
        jax.ShapeDtypeStruct((ws, wide), BF16),
        jax.ShapeDtypeStruct((ws, 256), BF16),
    )

    anywhere = pl.BlockSpec(memory_space=pl.ANY)
    arrivals = 2 + (3 + chunks) * 5 + 1 + 4 + (4 + chunks) * (8 + rounds + shards.bit_length() - 1)
    scratch = [
        pltpu.SMEM(lengths.shape, jnp.int32),
        pltpu.VMEM((count, width), BF16),
        pltpu.VMEM((count, width), BF16),
        pltpu.VMEM((slots, TOP, seg), jnp.int32),
        *[pltpu.VMEM((1, ws), F32)] * 5,
        pltpu.VMEM((1, fs), F32),
        pltpu.VMEM(query_weight.shape, F32),
        pltpu.VMEM(kv_weight.shape, F32),
        pltpu.VMEM((E, ws), F32),
        pltpu.VMEM(inner_weight.shape, F32),
        pltpu.VMEM((max(wos + fs, 3 * count), width), F32),
        pltpu.VMEM((shards, ws, 2 * HS), BF16),
        [pltpu.VMEM((shards, ws, wide // 2 + 128 * k), BF16) for k in range(2)],
        pltpu.VMEM((shards, wos, width), BF16),
        pltpu.VMEM((chunks, shards, chunk_rows, PANEL), BF16),
        pltpu.VMEM((16, UNIT), F32),
        pltpu.VMEM((shards, 16, UNIT), BF16),
        pltpu.VMEM((count, width), BF16),
        pltpu.VMEM((width, count), BF16),
        pltpu.VMEM((E, HS, count), F32),
        pltpu.VMEM((TOP, HS, count), F32),
        pltpu.VMEM((TOP, HS, count), F32),
        pltpu.VMEM((2, count, count), F32),
        pltpu.VMEM((ctxs, slots, 2, half, 2 * HS), BF16),
        pltpu.VMEM((ctxs, slots, 2 * HS, 2 * half), BF16),
        pltpu.VMEM((4, 2 * HS, 2 * lanes), BF16),
        pltpu.VMEM((4, HS, lanes), F32),
        pltpu.VMEM((4, 8, lanes), F32),
        pltpu.VMEM((slots, ctxs // 2, 4 * half, lanes) if keep_scores else (1, 1, 8, 128), F32),
        pltpu.VMEM((slots, ctxs // 2 + 1, 4 * half, lanes), BF16),
        pltpu.VMEM((ctxs, slots, 2 * half, 2 * HS), F32),
        pltpu.VMEM((2, ctxs // 2, slots, half, 2 * HS), BF16),
        pltpu.VMEM((ctxs // 2 - 1, 2, slots, half, 2 * HS), BF16),
        pltpu.VMEM((E, HS, count), BF16),
        pltpu.VMEM((count, width), F32),
        pltpu.VMEM((count, width), BF16),
        pltpu.VMEM((width, count), BF16),
        pltpu.VMEM((count, width), BF16),
        pltpu.VMEM((8, PANEL), F32),
        pltpu.VMEM((wide + 128, count), BF16),
        [
            reduce_scratch(shards, group, rounds, chunk_rows, PANEL, chunk_far[k])
            for k in range(chunks)
        ],
        reduce_scratch(shards, group, rounds, wos, width, False),
        [reduce_scratch(shards, group, rounds, ws, wide // 2, False) for _ in range(2)],
        reduce_scratch(shards, group, rounds, ws, 256, False),
        *[pltpu.VMEM(one.shape, one.dtype) for one in shapes_mid[0:4]],
        [pltpu.VMEM((ws, wide // 2), BF16) for _ in range(2)],
        pltpu.VMEM((ws, 256), BF16),
        pltpu.VMEM((128, width), F32),
        pltpu.SemaphoreType.DMA((23 + chunks,)),
        pltpu.SemaphoreType.DMA((RING,)),
        pltpu.SemaphoreType.DMA((arrivals,)),
    ]
    results = pl.pallas_call(
        functools.partial(layer_kernel, shards, ctxs, group, chunk_far),
        out_shape=shapes_mid,
        in_specs=[anywhere] * 16,
        out_specs=tuple([anywhere] * 6),
        scratch_shapes=scratch,
        compiler_params=pltpu.CompilerParams(
            collective_id=0, has_side_effects=True, vmem_limit_bytes=63 * 1024 * 1024
        ),
        name="layer",
    )(
        lengths,
        tokens.reshape(count, width),
        cotangent.reshape(count, width),
        jnp.swapaxes(expert_picks, 1, 2),
        first_gain.reshape(1, ws),
        first_bias.reshape(1, ws),
        second_gain.reshape(1, ws),
        second_bias.reshape(1, ws),
        outer_bias.reshape(1, ws),
        inner_bias.reshape(1, fs),
        query_weight,
        kv_weight,
        router_weight.T,
        output_weight,
        inner_weight,
        outer_weight,
    )
    vec_shape = jax.ShapeDtypeStruct((1, ws), F32)
    shapes_out = (
        jax.ShapeDtypeStruct((count, width), BF16),
        jax.ShapeDtypeStruct((count, width), F32),
        vec_shape,
        vec_shape,
        jax.ShapeDtypeStruct(kv_weight.shape, F32),
        jax.ShapeDtypeStruct(query_weight.shape, F32),
        jax.ShapeDtypeStruct((E, ws), F32),
        jax.ShapeDtypeStruct(output_weight.shape, F32),
        vec_shape,
        vec_shape,
        jax.ShapeDtypeStruct(inner_weight.shape, F32),
        jax.ShapeDtypeStruct((1, fs), F32),
        jax.ShapeDtypeStruct(outer_weight.shape, F32),
        vec_shape,
    )
    final = pl.pallas_call(
        functools.partial(unpack_kernel, shards),
        out_shape=shapes_out,
        in_specs=[anywhere] * 6,
        out_specs=tuple([anywhere] * 14),
        scratch_shapes=[pltpu.VMEM(one.shape, one.dtype) for one in (*shapes_mid, *shapes_out)]
        + [pltpu.SemaphoreType.DMA((20 + 2 * chunks,))],
        name="unpack",
    )(*results)
    final = list(final)
    final[6] = final[6].T
    shapes = (
        tokens.shape,
        tokens.shape,
        first_gain.shape,
        first_bias.shape,
        kv_weight.shape,
        query_weight.shape,
        router_weight.shape,
        output_weight.shape,
        second_gain.shape,
        second_bias.shape,
        inner_weight.shape,
        inner_bias.shape,
        outer_weight.shape,
        outer_bias.shape,
    )
    return tuple(value.reshape(shape) for value, shape in zip(final, shapes))


def solution(mesh):
    rows = P("shard", "ctx", None)
    vec, mat = P("shard"), P("shard", None)
    return jax.shard_map(
        functools.partial(on_device, mesh.shape["shard"], mesh.shape["ctx"]),
        mesh=mesh,
        in_specs=(
            rows,
            vec,
            rows,
            vec,
            vec,
            mat,
            mat,
            mat,
            mat,
            vec,
            vec,
            mat,
            vec,
            mat,
            vec,
            rows,
        ),
        out_specs=(
            rows,
            rows,
            vec,
            vec,
            mat,
            mat,
            mat,
            mat,
            vec,
            vec,
            mat,
            vec,
            mat,
            vec,
        ),
        check_vma=False,
    )
```
